32 devices in a mesh: dp: 8 (over y, x, core), tensor: 4 (over z).
Axes of the slice: x: 2, y: 2, z: 4, core: 2. Of those that a mesh axis runs over, the one named last changes fastest.
Arguments:
- tokens: bfloat16 [2, 8, 1024, 2048], P(None, 'dp', 'tensor'), may hold values from -6 to 6
- parents: int32 [2, 8, 4], P(None, 'dp'), may hold values from 0 to 2, as said below
- cotangent: bfloat16 [2, 8, 1024, 2048], P(None, 'dp', 'tensor'), may hold values from -6 to 6
- first_gain: bfloat16 [2048], P('dp'), may hold values from 0.5 to 1.5
- first_shift: bfloat16 [2048], P('dp'), may hold values from -1.75 to 1.75
- w_query: bfloat16 [2048, 2048], P('dp', 'tensor'), may hold values from -0.125 to 0.125
- b_query: bfloat16 [32, 64], P('tensor', 'dp'), may hold values from -3 to 3
- w_key: bfloat16 [2048, 2048], P('dp', 'tensor'), may hold values from -0.125 to 0.125
- w_value: bfloat16 [2048, 2048], P('dp', 'tensor'), may hold values from -0.125 to 0.125
- b_value: bfloat16 [32, 64], P('tensor', 'dp'), may hold values from -0.3125 to 0.3125
- w_out: bfloat16 [2048, 2048], P('tensor', 'dp'), may hold values from -1 to 1
- b_out: bfloat16 [2048], P('dp'), may hold values from -1.75 to 1.75
- second_gain: bfloat16 [2048], P('dp'), may hold values from 0.5 to 1.5
- second_shift: bfloat16 [2048], P('dp'), may hold values from -1.75 to 1.75
- w_expand: bfloat16 [2048, 8192], P('dp', 'tensor'), may hold values from -0.125 to 0.125
- b_expand: bfloat16 [128, 64], P('tensor', 'dp'), may hold values from -3 to 3
- w_reduce: bfloat16 [8192, 2048], P('tensor', 'dp'), may hold values from -0.0625 to 0.0625
- b_reduce: bfloat16 [2048], P('dp'), may hold values from -1.75 to 1.75
Outputs:
- layer_out: bfloat16 [2, 8, 1024, 2048], P(None, 'dp', 'tensor')
- input_grad: bfloat16 [2, 8, 1024, 2048], P(None, 'dp', 'tensor')
- grad_first_gain: float32 [2048], P('dp')
- grad_first_shift: float32 [2048], P('dp')
- grad_w_query: float32 [2048, 2048], P('dp', 'tensor')
- grad_b_query: float32 [32, 64], P('tensor', 'dp')
- grad_w_key: float32 [2048, 2048], P('dp', 'tensor')
- grad_w_value: float32 [2048, 2048], P('dp', 'tensor')
- grad_b_value: float32 [32, 64], P('tensor', 'dp')
- grad_w_out: float32 [2048, 2048], P('tensor', 'dp')
- grad_b_out: float32 [2048], P('dp')
- grad_second_gain: float32 [2048], P('dp')
- grad_second_shift: float32 [2048], P('dp')
- grad_w_expand: float32 [2048, 8192], P('dp', 'tensor')
- grad_b_expand: float32 [128, 64], P('tensor', 'dp')
- grad_w_reduce: float32 [8192, 2048], P('tensor', 'dp')
- grad_b_reduce: float32 [2048], P('dp')
The draws below stay inside these ranges and needn't reach their ends.
Inputs may be any that keep to these rules, and one draw needn't show every extreme that they name: `parents`: block 0 of every tree names itself; every later block j names an earlier block (0 to j - 1) as its parent, so block 1 always hangs on block 0.
All inputs are finite; a program needn't handle non-finite values.
Results may differ from the reference program's by a relative error of at most 0.024.
Values may be sent and summed in bfloat16 or wider, within the bound.
A program may use at most 320 MiB of HBM per device.

```python
import math
import jax
import jax.numpy as jnp
from jax import lax

D = 2048
HEADS = 32
HEAD_DIM = 64
FF = 8192
BLOCK = 256
TREE_BLOCKS = 4
MICRO = 2
TREE_TOK = 1024
SEQS = 8


def draw_parents(key, part):
    raw_bits = jax.random.randint(key, (MICRO, SEQS, TREE_BLOCKS), 0, 1 << 20)
    place = jnp.arange(TREE_BLOCKS, dtype=jnp.int32)
    return (raw_bits % jnp.maximum(place, 1)).astype(jnp.int32)


def raised(entries, rng, source, target, blocks, factor):
    owner, partner = [(jnp.arange(entries.shape[dim]) // (entries.shape[dim] // blocks)).reshape([-1 if axis == dim else 1 for axis in range(entries.ndim)]) for dim in (source, target)]
    chosen = jax.random.permutation(rng, blocks)[partner]
    strong = (owner == chosen) | (owner == (partner + blocks // 2) % blocks)
    return jnp.where(strong, factor * entries, entries)


def block_scale(own_key, shape, shards, smallest, high):
    level = 1.0
    for position, blocks in shards:
        draws = jax.random.uniform(jax.random.fold_in(jax.random.fold_in(own_key, 6), position), (blocks,), jnp.float32, smallest / len(shards), high / len(shards))
        level = level * jnp.repeat(jnp.exp(draws), shape[position] // blocks).reshape((-1,) + (1,) * (len(shape) - 1 - position))
    return level


def bell_draw(own_key, dims, scale, bound, pieces=(), kind=jnp.bfloat16):
    values = jax.random.normal(own_key, dims, jnp.float32) * scale
    if len(pieces) > 0:
        values = block_scale(own_key, dims, pieces, -0.22, 0.18) * values
    return jnp.clip(values, min=-bound, max=bound).astype(kind)


def bell_draw_with(stream_key, extent, scale, reach, cuts, heavy, kind=jnp.bfloat16):
    entries = scale * jax.random.normal(stream_key, extent, jnp.float32)
    if cuts:
        entries = entries * block_scale(stream_key, extent, cuts, -0.22, 0.18)
    return jnp.clip(raised(entries, jax.random.fold_in(stream_key, 3), *heavy), -reach, reach).astype(kind)


def setup_inputs(seed: int = 0) -> dict:
    streams_of = jax.random.split(jax.random.key(seed), 19)
    return {
        "tokens": bell_draw_with(streams_of[0], (MICRO, SEQS, TREE_TOK, D), 1.0, 6.0, ((1, 8), (2, 4)), (1, 3, 8, 2.0)),
        "parents": draw_parents(jax.random.fold_in(streams_of[18], 71), 0),
        "cotangent": bell_draw_with(streams_of[2], (MICRO, SEQS, TREE_TOK, D), 1.0, 6.0, ((1, 8), (2, 4)), (1, 3, 8, 2.0)),
        "first_gain": jnp.clip(1.0 + 0.1 * jax.random.normal(streams_of[3], (D,), jnp.float32), 0.5, 1.5).astype(jnp.bfloat16),
        "first_shift": bell_draw(streams_of[4], (D,), 0.3, 1.75, ((0, 8),)),
        "w_query": bell_draw(streams_of[5], (D, D), D ** -0.5, 0.125, ((0, 8), (1, 4))),
        "b_query": bell_draw(streams_of[6], (HEADS, HEAD_DIM), 0.5, 3.0, ((0, 4), (1, 8))),
        "w_key": bell_draw(streams_of[7], (D, D), D ** -0.5, 0.125, ((0, 8), (1, 4))),
        "w_value": bell_draw(streams_of[8], (D, D), D ** -0.5, 0.125, ((0, 8), (1, 4))),
        "b_value": bell_draw(streams_of[9], (HEADS, HEAD_DIM), 0.05, 0.3125, ((0, 4), (1, 8))),
        "w_out": bell_draw(streams_of[10], (D, D), (max(D // 64, 1)) ** -0.5, 1.0, ((0, 4), (1, 8))),
        "b_out": bell_draw(streams_of[11], (D,), 0.3, 1.75, ((0, 8),)),
        "second_gain": jnp.clip(1.0 + 0.1 * jax.random.normal(streams_of[12], (D,), jnp.float32), 0.5, 1.5).astype(jnp.bfloat16),
        "second_shift": bell_draw(streams_of[13], (D,), 0.3, 1.75, ((0, 8),)),
        "w_expand": bell_draw(streams_of[14], (D, FF), D ** -0.5, 0.125, ((0, 8), (1, 4))),
        "b_expand": bell_draw(streams_of[15], (FF // HEAD_DIM, HEAD_DIM), 0.5, 3.0, ((0, 4), (1, 8))),
        "w_reduce": bell_draw(streams_of[16], (FF, D), FF ** -0.5, 0.0625, ((0, 4), (1, 8))),
        "b_reduce": bell_draw(streams_of[17], (D,), 0.3, 1.75, ((0, 8),)),
    }


HIGHEST = lax.Precision.HIGHEST

@jax.custom_vjp
def low(v):
    return lax.optimization_barrier(v.astype(jnp.bfloat16)).astype(jnp.float32)

@jax.custom_vjp
def low_back(v):
    return v

def low_keep(v):
    return (low(v), None)

def low_pass(kept, grad):
    return (grad,)

def back_keep(v):
    return (v, None)

def back_low(kept, grad):
    return (low(grad),)
low.defvjp(low_keep, low_pass)
low_back.defvjp(back_keep, back_low)

def matmul(left, right):
    return jnp.dot(left, right, precision=HIGHEST, preferred_element_type=jnp.float32)

def layer_norm(rows, gain, shift):
    center = rows - lax.optimization_barrier(jnp.mean(rows, -1, keepdims=True))
    spread = lax.optimization_barrier(jnp.mean(center * center, -1, keepdims=True))
    return center * lax.rsqrt(spread + 1e-05) * gain + shift

def ancestry(parent_list):
    count = parent_list.shape[0]
    blocks = jnp.arange(count, dtype=jnp.int32)
    upward = (parent_list[:, None] == blocks[None, :]).astype(jnp.float32)
    unit_matrix = jnp.eye(count, dtype=jnp.float32)
    ancestors = unit_matrix
    for hop_index in range(count):
        ancestors = jnp.maximum(unit_matrix, matmul(upward, ancestors))
    return ancestors

def visible(ancestors, first_row, row_count, total_rows, block_len):
    count = ancestors.shape[0]
    blocks = jnp.arange(count, dtype=jnp.int32)
    query_pos = first_row + jnp.arange(row_count, dtype=jnp.int32)
    key_pos = jnp.arange(total_rows, dtype=jnp.int32)
    query_hot = (query_pos[:, None] // block_len == blocks[None, :]).astype(jnp.float32)
    key_hot = (key_pos[:, None] // block_len == blocks[None, :]).astype(jnp.float32)
    linked = matmul(matmul(query_hot, ancestors), key_hot.T)
    return (linked > 0.5) & (key_pos[None, :] <= query_pos[:, None])

def forward(x_rows, params, allowed):
    first_gain, first_shift, w_query, b_query, w_key, w_value, b_value, w_out, b_out, second_gain, second_shift, w_expand, b_expand, w_reduce, b_reduce = params
    total_rows = x_rows.shape[0]
    normed_one = low(layer_norm(x_rows, first_gain, first_shift))
    query = low(low_back(matmul(normed_one, w_query) + b_query.reshape(-1)))
    key = low(low_back(matmul(normed_one, w_key)))
    value = low(low_back(matmul(normed_one, w_value) + b_value.reshape(-1)))
    query_h = query.reshape(total_rows, HEADS, HEAD_DIM)
    key_h = key.reshape(total_rows, HEADS, HEAD_DIM)
    value_h = value.reshape(total_rows, HEADS, HEAD_DIM)
    scores = jnp.einsum('qhd,khd->hqk', query_h, key_h, precision=HIGHEST) * (1.0 / math.sqrt(HEAD_DIM))
    scores = low_back(jnp.where(allowed[None], scores, -1e+30))
    probs = low(jax.nn.softmax(scores, axis=-1))
    attended = jnp.einsum('hqk,khd->qhd', probs, value_h, precision=HIGHEST).reshape(total_rows, HEADS * HEAD_DIM)
    attended = low(low_back(attended))
    hidden_one = x_rows + low_back(matmul(attended, w_out) + b_out)
    normed_two = low(layer_norm(hidden_one, second_gain, second_shift))
    pre_act = low_back(matmul(normed_two, w_expand) + b_expand.reshape(-1))
    activated = low(jax.nn.gelu(pre_act))
    return hidden_one + (matmul(activated, w_reduce) + b_reduce)

def reference(tokens, parents, cotangent, first_gain, first_shift, w_query, b_query, w_key, w_value, b_value, w_out, b_out, second_gain, second_shift, w_expand, b_expand, w_reduce, b_reduce):
    params = tuple((item.astype(jnp.float32) for item in (first_gain, first_shift, w_query, b_query, w_key, w_value, b_value, w_out, b_out, second_gain, second_shift, w_expand, b_expand, w_reduce, b_reduce)))
    tree_count = MICRO * SEQS
    inputs = tokens.reshape(tree_count, TREE_TOK, D).astype(jnp.float32)
    grads_in = cotangent.reshape(tree_count, TREE_TOK, D).astype(jnp.float32)
    parent_rows = parents.reshape(tree_count, TREE_BLOCKS)

    def one_tree(carry, item):
        x_rows, grad_rows, parent_list = item
        allowed = visible(ancestry(parent_list), 0, TREE_TOK, TREE_TOK, BLOCK)
        result, pull = jax.vjp(lambda xin, prm: forward(xin, prm, allowed), x_rows, params)
        grad_x, grad_params = pull(grad_rows)
        carry = jax.tree.map(lambda left, right: left + right, carry, grad_params)
        return (carry, (result, grad_x))
    zeros = tuple((jnp.zeros_like(item) for item in params))
    grads, (results, grad_inputs) = lax.scan(one_tree, zeros, (inputs, grads_in, parent_rows))
    layer_out = results.reshape(tokens.shape).astype(jnp.bfloat16)
    input_grad = grad_inputs.reshape(tokens.shape).astype(jnp.bfloat16)
    return (layer_out, input_grad, grads[0], grads[1], grads[2], grads[3], grads[4], grads[5], grads[6], grads[7], grads[8], grads[9], grads[10], grads[11], grads[12], grads[13], grads[14])
```

```python
import functools
import math

import jax
import jax.numpy as jnp
from jax import lax
from jax.experimental import pallas as pl
from jax.experimental.pallas import tpu as pltpu
from jax.sharding import PartitionSpec as P

HEAD_DIM = 64
BLOCK = 256

F32 = jnp.float32
BF16 = jnp.bfloat16
MESH = pl.DeviceIdType.MESH
GELU = math.sqrt(2.0 / math.pi)


def layer_norm(rows, gain, shift):
    center = rows - jnp.mean(rows, -1, keepdims=True)
    spread = jnp.mean(center * center, -1, keepdims=True)
    return center * lax.rsqrt(spread + 1e-05) * gain + shift


def chain_gather(own):
    n = lax.axis_size("tensor")
    me = lax.axis_index("tensor")
    from_left, from_right = [own], [own]
    for step in range(1, n):
        up = [(i, i + 1) for i in range(step - 1, n - 1)]
        down = [(n - 1 - i, n - 2 - i) for i in range(step - 1, n - 1)]
        from_left.append(lax.ppermute(from_left[-1], "tensor", up))
        from_right.append(lax.ppermute(from_right[-1], "tensor", down))
    full = jnp.zeros((n,) + own.shape, own.dtype)
    full = lax.dynamic_update_slice_in_dim(full, own[None], me, 0)
    for step in range(1, n):
        piece = jnp.where(me >= step, from_left[step], from_right[n - step])
        full = lax.dynamic_update_slice_in_dim(full, piece[None], lax.rem(me - step + n, n), 0)
    return full.reshape(n * own.shape[0], own.shape[1])


def line_gather(own):
    return lax.all_gather(own, "tensor", axis=0, tiled=True)


def line_scatter(parts):
    return lax.psum_scatter(parts, "tensor", scatter_dimension=0, tiled=True).astype(F32)


def far_pairs(hop):
    n = lax.axis_size("tensor")
    return [(i, (i + hop) % n) for i in range(n)]


def far_gather(own):
    n = lax.axis_size("tensor")
    return [own] + [lax.ppermute(own, "tensor", far_pairs(hop)) for hop in range(1, n)]


def far_scatter(parts):
    n = lax.axis_size("tensor")
    total = parts[0].astype(F32)
    for hop in range(1, n):
        total = total + lax.ppermute(parts[hop], "tensor", far_pairs(n - hop)).astype(F32)
    return total


def after(value, *others):
    return lax.optimization_barrier((value,) + others)[0]


PAIR = 2 * HEAD_DIM
NEVER = -1e30


def over(left, right, on_left, on_right):
    return lax.dot_general(
        left, right, (((on_left,), (on_right,)), ((), ())), preferred_element_type=F32
    )


def lane_of(shape, head):
    lane = lax.broadcasted_iota(jnp.int32, shape, 1)
    return (lane < HEAD_DIM) if head == 0 else (lane >= HEAD_DIM)


def sight(parents_ref, row, col):
    at = jnp.int32(row)
    seen = at == col
    for hop in range(row - col):
        at = parents_ref[at]
        seen = seen | (at == col)
    return jnp.where(seen, 0.0, NEVER).astype(F32)


def masked_scores(parents_ref, q_head, k_ref, row):
    scores = []
    for col in range(row + 1):
        part = over(q_head, k_ref[col * BLOCK : (col + 1) * BLOCK, :], 1, 1)
        if col == row:
            below = lax.broadcasted_iota(jnp.int32, part.shape, 1) <= lax.broadcasted_iota(
                jnp.int32, part.shape, 0
            )
            part = jnp.where(below, part, NEVER)
        else:
            part = part + sight(parents_ref, row, col)
        scores.append(part)
    return scores


def row_reduce(parts, fold, reduce):
    return reduce(functools.reduce(fold, parts), axis=-1, keepdims=True)


def attend_kernel(parents_ref, q_ref, k_ref, v_ref, out_ref):
    blocks = q_ref.shape[0] // BLOCK
    scale = 1.0 / math.sqrt(HEAD_DIM)
    for row in range(blocks):
        here = slice(row * BLOCK, (row + 1) * BLOCK)
        heads = []
        for head in range(2):
            q_head = q_ref[here, :].astype(F32) * scale
            q_head = jnp.where(lane_of(q_head.shape, head), q_head, 0.0).astype(BF16)
            scores = masked_scores(parents_ref, q_head, k_ref, row)
            top = row_reduce(scores, jnp.maximum, jnp.max)
            probs = [jnp.exp(s - top) for s in scores]
            total = row_reduce(probs, jnp.add, jnp.sum)
            out = None
            for col in range(row + 1):
                term = over(
                    probs[col].astype(BF16), v_ref[col * BLOCK : (col + 1) * BLOCK, :], 1, 0
                )
                out = term if out is None else out + term
            heads.append(out / total)
        mixed = jnp.where(lane_of(heads[0].shape, 0), heads[0], heads[1])
        out_ref[here, :] = mixed.astype(out_ref.dtype)


def attend(parents, qkv, width):
    rows = qkv.shape[0]
    pairs = width // PAIR
    spec = lambda part: pl.BlockSpec((rows, PAIR), lambda p, parents: (0, part * pairs + p))
    blocks = rows // BLOCK
    work = pairs * 2 * (blocks * (blocks + 1) // 2) * BLOCK * BLOCK
    return pl.pallas_call(
        attend_kernel,
        out_shape=jax.ShapeDtypeStruct((rows, width), BF16),
        grid_spec=pltpu.PrefetchScalarGridSpec(
            num_scalar_prefetch=1,
            grid=(pairs,),
            in_specs=[spec(0), spec(1), spec(2)],
            out_specs=pl.BlockSpec((rows, PAIR), lambda p, parents: (0, p)),
        ),
        compiler_params=pltpu.CompilerParams(vmem_limit_bytes=48 << 20),
        cost_estimate=pl.CostEstimate(
            flops=work * PAIR * 4, bytes_accessed=rows * width * 8, transcendentals=work
        ),
        name="attend",
    )(parents, qkv, qkv, qkv)


def attend_back_kernel(parents_ref, q_ref, k_ref, v_ref, g_ref, out_ref, dq_s, dk_s, dv_s):
    part = pl.program_id(1)
    blocks = q_ref.shape[0] // BLOCK
    scale = 1.0 / math.sqrt(HEAD_DIM)

    @pl.when(part == 0)
    def _():
        for row in range(blocks):
            here = slice(row * BLOCK, (row + 1) * BLOCK)
            dq_heads = []
            for head in range(2):
                lanes = lane_of((BLOCK, PAIR), head)
                q_head = jnp.where(lanes, q_ref[here, :].astype(F32) * scale, 0.0).astype(BF16)
                g_head = jnp.where(lanes, g_ref[here, :].astype(F32), 0.0).astype(BF16)
                scores = masked_scores(parents_ref, q_head, k_ref, row)
                top = row_reduce(scores, jnp.maximum, jnp.max)
                probs = [jnp.exp(s - top) for s in scores]
                rest = 1.0 / row_reduce(probs, jnp.add, jnp.sum)
                probs = [p * rest for p in probs]
                d_probs = [
                    over(g_head, v_ref[col * BLOCK : (col + 1) * BLOCK, :], 1, 1)
                    for col in range(row + 1)
                ]
                level = row_reduce([p * d for p, d in zip(probs, d_probs)], jnp.add, jnp.sum)
                dq = None
                for col in range(row + 1):
                    there = slice(col * BLOCK, (col + 1) * BLOCK)
                    d_scores = (probs[col] * (d_probs[col] - level)).astype(BF16)
                    term = over(d_scores, k_ref[there, :], 1, 0)
                    dq = term if dq is None else dq + term
                    dk = over(d_scores, q_head, 0, 0)
                    dv = over(probs[col].astype(BF16), g_head, 0, 0)
                    if row == col and head == 0:
                        dk_s[there, :] = dk
                        dv_s[there, :] = dv
                    else:
                        dk_s[there, :] += dk
                        dv_s[there, :] += dv
                dq_heads.append(dq * scale)
            dq_s[here, :] = jnp.where(lane_of((BLOCK, PAIR), 0), dq_heads[0], dq_heads[1]).astype(
                BF16
            )
        out_ref[...] = dq_s[...]

    @pl.when(part == 1)
    def _():
        out_ref[...] = dk_s[...].astype(BF16)

    @pl.when(part == 2)
    def _():
        out_ref[...] = dv_s[...].astype(BF16)


def attend_back(parents, qkv, grad, width):
    rows = qkv.shape[0]
    pairs = width // PAIR
    spec = lambda part: pl.BlockSpec((rows, PAIR), lambda p, c, parents: (0, part * pairs + p))
    blocks = rows // BLOCK
    work = pairs * 2 * (blocks * (blocks + 1) // 2) * BLOCK * BLOCK
    return pl.pallas_call(
        attend_back_kernel,
        out_shape=jax.ShapeDtypeStruct((rows, 3 * width), BF16),
        grid_spec=pltpu.PrefetchScalarGridSpec(
            num_scalar_prefetch=1,
            grid=(pairs, 3),
            in_specs=[
                spec(0),
                spec(1),
                spec(2),
                pl.BlockSpec((rows, PAIR), lambda p, c, parents: (0, p)),
            ],
            out_specs=pl.BlockSpec((rows, PAIR), lambda p, c, parents: (0, c * pairs + p)),
            scratch_shapes=[
                pltpu.VMEM((rows, PAIR), BF16),
                pltpu.VMEM((rows, PAIR), F32),
                pltpu.VMEM((rows, PAIR), F32),
            ],
        ),
        compiler_params=pltpu.CompilerParams(vmem_limit_bytes=48 << 20),
        cost_estimate=pl.CostEstimate(
            flops=work * PAIR * 10, bytes_accessed=rows * width * 14, transcendentals=work
        ),
        name="attend_back",
    )(parents, qkv, qkv, qkv, grad)


def cube_place():
    levels = lax.axis_size("dp").bit_length() - 2
    me = lax.axis_index("dp")
    core = me % 2
    flips = []
    for bit in range(1, levels + 1):
        flips.append((1 << bit) * (1 - 2 * ((me // (1 << bit)) % 2)))
    steps = [
        flips[l] * (1 - core) + flips[levels - 1 - l] * core for l in range(levels)
    ]
    return levels, me, steps, 1 - 2 * core


def ffn_kernel(
    n2_ref, dy_ref, wet_ref, wr_ref, be_ref,
    sum_ref, seq_ref, act_ref, dpre_ref,
    wet, wr, seq, dy_st, act_st, dpre_st, keep, give, core_in, fold_in,
    w_sem, own_sem, dy_sem, seq_sem, st_sem,
    ag_send, ag_recv, agc_send, agc_recv, rsc_send, rsc_recv, fold_send, fold_recv,
):
    levels, me, steps, core_step = cube_place()
    tensor = lax.axis_index("tensor")
    count = 1 << levels
    rows, model = n2_ref.shape
    units = wet_ref.shape[0]

    def at(index):
        return (index, tensor)

    def owner(piece):
        mine, other = me, me + core_step
        for l in range(levels):
            if piece >> l & 1:
                mine = mine + steps[l]
                other = other + steps[levels - 1 - l]
        return mine, other

    barrier = pltpu.get_barrier_semaphore()
    for step in steps + [core_step]:
        pl.semaphore_signal(barrier, inc=1, device_id=at(me + step), device_id_type=MESH)
    load_own = pltpu.make_async_copy(n2_ref, seq.at[0, pl.ds(0, rows)], own_sem)
    load_own.start()
    load_wet = pltpu.make_async_copy(wet_ref, wet, w_sem.at[0])
    load_wr = pltpu.make_async_copy(wr_ref, wr, w_sem.at[1])
    load_wet.start()
    load_wr.start()

    def load_dy(piece, slot):
        mine, other = owner(piece)
        out = []
        for half, index in enumerate((mine, other)):
            out.append(
                pltpu.make_async_copy(
                    dy_ref.at[pl.ds(pl.multiple_of(index * rows, rows), rows)],
                    dy_st.at[slot, pl.ds(half * rows, rows)],
                    dy_sem.at[slot, half],
                )
            )
        return out

    def remote(src, dst, send, recv, to):
        return pltpu.make_async_remote_copy(
            src_ref=src, dst_ref=dst, send_sem=send, recv_sem=recv,
            device_id=at(to), device_id_type=MESH,
        )

    def gather_copy(piece, level):
        there = piece + (1 << level)
        return remote(
            seq.at[piece, pl.ds(0, rows)], seq.at[there, pl.ds(0, rows)],
            ag_send.at[there], ag_recv.at[there], me + steps[level],
        )

    def gather_core(piece):
        return remote(
            seq.at[piece, pl.ds(0, rows)], seq.at[piece, pl.ds(rows, rows)],
            agc_send.at[piece], agc_recv.at[piece], me + core_step,
        )

    order = [0] + sorted(range(1, count), key=lambda p: (-(p.bit_length()), p))
    slots = {piece: i % 2 for i, piece in enumerate(order)}
    loads = {order[0]: load_dy(order[0], 0)}
    for c in loads[order[0]]:
        c.start()

    load_own.wait()
    pl.semaphore_wait(barrier, levels + 1)
    sends = []
    for level in range(levels):
        sends.append(gather_copy(0, level))
        sends[-1].start()
    sends.append(gather_core(0))
    sends[-1].start()
    load_wet.wait()
    load_wr.wait()

    arrived = {0}

    def take(piece):
        if piece in arrived:
            return
        low = piece - (1 << (piece.bit_length() - 1))
        gather_copy(low, piece.bit_length() - 1).wait_recv()
        arrived.add(piece)
        for level in range(piece.bit_length(), levels):
            sends.append(gather_copy(piece, level))
            sends[-1].start()
        sends.append(gather_core(piece))
        sends[-1].start()

    stores = {}
    outs = {}
    core_sends = {}
    folds = {}
    done_core = set()

    def add(piece, other):
        @pl.loop(0, rows // 16)
        def _(i):
            part = pl.ds(pl.multiple_of(i * 16, 16), 16)
            keep[piece, part] = (
                keep[piece, part].astype(F32) + other[part].astype(F32)
            ).astype(BF16)

    def add_core(piece):
        if piece in done_core:
            return
        core_copy(piece).wait_recv()
        add(piece, core_in.at[piece])
        done_core.add(piece)

    def core_copy(piece):
        return remote(
            give.at[slots[piece]], core_in.at[piece],
            rsc_send.at[piece], rsc_recv.at[piece], me + core_step,
        )

    def fold_copy(piece):
        level = piece.bit_length() - 1
        low = piece - (1 << level)
        return remote(
            keep.at[piece], fold_in.at[piece - 1],
            fold_send.at[piece - 1], fold_recv.at[piece - 1], me + steps[level],
        )

    def fold(piece):
        add_core(piece)
        for level in range(levels - 1, piece.bit_length() - 1, -1):
            above = piece + (1 << level)
            fold_copy(above).wait_recv()
            add(piece, fold_in.at[above - 1])
        if piece:
            folds[piece] = fold_copy(piece)
            folds[piece].start()

    chunk = 256
    wide = 512
    for turn, piece in enumerate(order):
        slot = turn % 2
        for earlier in range(1, piece + 1):
            take(earlier)
        gather_core(piece).wait_recv()
        for c in loads[piece]:
            c.wait()
        if turn + 1 < count:
            loads[order[turn + 1]] = load_dy(order[turn + 1], 1 - slot)
            for c in loads[order[turn + 1]]:
                c.start()
        if turn >= 2:
            for c in stores[turn - 2]:
                c.wait()
            core_sends[order[turn - 2]].wait_send()

        @pl.loop(0, units // chunk)
        def _(i):
            cols = pl.ds(pl.multiple_of(i * chunk, chunk), chunk)
            pre = over(seq[piece], wet[cols, :], 1, 1) + be_ref[:, cols]
            d_act = over(dy_st[slot], wr[cols, :], 1, 1)
            square = pre * pre
            t = jnp.tanh(GELU * pre * (1.0 + 0.044715 * square))
            act_st[slot, :, cols] = (0.5 * pre * (1.0 + t)).astype(BF16)
            slope = 0.5 * (1.0 + t) + (0.5 * GELU) * pre * (1.0 - t * t) * (
                1.0 + (3 * 0.044715) * square
            )
            dpre_st[slot, :, cols] = (d_act * slope).astype(BF16)

        @pl.loop(0, model // wide)
        def _(i):
            cols = pl.ds(pl.multiple_of(i * wide, wide), wide)
            cols_out = pl.ds(pl.multiple_of(model + i * wide, wide), wide)
            d_two = over(dpre_st[slot], wet[:, cols], 1, 0).astype(BF16)
            keep[piece, :, cols] = d_two[:rows]
            give[slot, :, cols] = d_two[rows:]
            out = over(act_st[slot], wr[:, cols], 1, 0).astype(BF16)
            keep[piece, :, cols_out] = out[:rows]
            give[slot, :, cols_out] = out[rows:]

        core_sends[piece] = core_copy(piece)
        core_sends[piece].start()
        mine, other = owner(piece)
        stores[turn] = []
        for half, index in enumerate((mine, other)):
            to = pl.ds(pl.multiple_of(index * rows, rows), rows)
            part = pl.ds(half * rows, rows)
            stores[turn].append(
                pltpu.make_async_copy(act_st.at[slot, part], act_ref.at[to], st_sem.at[0, slot, half])
            )
            stores[turn].append(
                pltpu.make_async_copy(dpre_st.at[slot, part], dpre_ref.at[to], st_sem.at[1, slot, half])
            )
            stores[turn].append(
                pltpu.make_async_copy(seq.at[piece, part], seq_ref.at[to], seq_sem.at[piece, half])
            )
        for c in stores[turn]:
            c.start()
        if piece.bit_length() == levels:
            fold(piece)
    for level in range(levels - 2, -1, -1):
        for piece in range((1 << level), 2 << level):
            fold(piece)
    add_core(0)
    for level in range(levels):
        fold_copy(1 << level).wait_recv()

    @pl.loop(0, rows // 16)
    def _(i):
        part = pl.ds(pl.multiple_of(i * 16, 16), 16)
        total = keep[0, part].astype(F32)
        for level in range(levels):
            total = total + fold_in[(1 << level) - 1, part].astype(F32)
        sum_ref[part] = total

    for s in sends:
        s.wait_send()
    for turn in range(max(0, count - 2), count):
        for c in stores[turn]:
            c.wait()
        core_sends[order[turn]].wait_send()
    for s in folds.values():
        s.wait_send()


def ffn(n2, dy_all, wet, wr, bias_e):
    rows, model = n2.shape
    units = wet.shape[0]
    dp = lax.axis_size("dp")
    count = dp // 2
    dma = pltpu.SemaphoreType.DMA
    anywhere = pl.BlockSpec(memory_space=pl.ANY)
    vmem = pl.BlockSpec(memory_space=pltpu.VMEM)
    flops = 8 * dp * rows * model * units
    return pl.pallas_call(
        ffn_kernel,
        out_shape=(
            jax.ShapeDtypeStruct((rows, 2 * model), F32),
            jax.ShapeDtypeStruct((dp * rows, model), BF16),
            jax.ShapeDtypeStruct((dp * rows, units), BF16),
            jax.ShapeDtypeStruct((dp * rows, units), BF16),
        ),
        in_specs=[anywhere, anywhere, anywhere, anywhere, vmem],
        out_specs=(vmem, anywhere, anywhere, anywhere),
        scratch_shapes=[
            pltpu.VMEM((units, model), BF16),
            pltpu.VMEM((units, model), BF16),
            pltpu.VMEM((count, 2 * rows, model), BF16),
            pltpu.VMEM((2, 2 * rows, model), BF16),
            pltpu.VMEM((2, 2 * rows, units), BF16),
            pltpu.VMEM((2, 2 * rows, units), BF16),
            pltpu.VMEM((count, rows, 2 * model), BF16),
            pltpu.VMEM((2, rows, 2 * model), BF16),
            pltpu.VMEM((count, rows, 2 * model), BF16),
            pltpu.VMEM((count - 1, rows, 2 * model), BF16),
            dma((2,)), dma, dma((2, 2)), dma((count, 2)), dma((2, 2, 2)),
            dma((count,)), dma((count,)), dma((count,)), dma((count,)),
            dma((count,)), dma((count,)), dma((count - 1,)), dma((count - 1,)),
        ],
        compiler_params=pltpu.CompilerParams(
            collective_id=1, has_side_effects=True, vmem_limit_bytes=62 << 20
        ),
        cost_estimate=pl.CostEstimate(
            flops=flops, bytes_accessed=8 * dp * rows * (model + units), transcendentals=dp * rows * units
        ),
        name="ffn_plane",
    )(n2, dy_all, wet, wr, bias_e)


def body(
    tokens,
    parents,
    cotangent,
    first_gain,
    first_shift,
    w_query,
    b_query,
    w_key,
    w_value,
    b_value,
    w_out,
    b_out,
    second_gain,
    second_shift,
    w_expand,
    b_expand,
    w_reduce,
    b_reduce,
):
    micro_count = tokens.shape[0]
    dp = lax.axis_size("dp")
    tn = lax.axis_size("tensor")
    dp_me = lax.axis_index("dp")
    tn_me = lax.axis_index("tensor")
    width = w_query.shape[1]
    model = w_query.shape[0] * dp
    units = w_expand.shape[1]
    mine = units // dp
    micros = range(micro_count)

    cut = first_gain.shape[0]
    bq_rows, bq_cols = b_query.shape
    be_rows, be_cols = b_expand.shape
    be_all = lax.all_gather(b_expand.reshape(-1), "tensor", axis=0, tiled=True)
    small = jnp.concatenate(
        [first_gain, first_shift, b_out, second_gain, second_shift, b_reduce]
        + [b_query.reshape(-1), b_value.reshape(-1), be_all]
    )
    small = lax.all_gather(small, "dp", axis=0, tiled=False)
    gain_one, shift_one, bias_out, gain_two, shift_two, bias_red = [
        small[:, i * cut : (i + 1) * cut].reshape(1, model).astype(F32) for i in range(6)
    ]
    at = 6 * cut
    bias_qkv = []
    for i in range(2):
        part = small[:, at : at + bq_rows * bq_cols].reshape(dp, bq_rows, bq_cols)
        bias_qkv.append(part.transpose(1, 0, 2).reshape(1, width).astype(F32))
        at += bq_rows * bq_cols
    bias_qkv = jnp.concatenate([bias_qkv[0], jnp.zeros((1, width), F32), bias_qkv[1]], 1)
    bias_e = small[:, at:].reshape(dp, tn, dp, be_rows // dp, be_cols)
    bias_e = lax.dynamic_index_in_dim(bias_e, dp_me, 2, keepdims=False)
    bias_e = bias_e.transpose(1, 2, 0, 3).reshape(tn, mine)
    turned = [
        lax.dynamic_index_in_dim(bias_e, lax.rem(tn_me - hop + tn, tn), 0, keepdims=True)
        for hop in range(tn)
    ]
    bias_e = jnp.concatenate(turned, 1).astype(F32)

    x_low = [tokens[m, 0] for m in micros]
    dy_low = [cotangent[m, 0] for m in micros]
    rows_here = x_low[0].shape[0]
    total = rows_here * tn
    seq_x = [chain_gather(after(x_low[0], small))]
    w_attn = jnp.concatenate([w_query, w_key, w_value, w_out.T], axis=1)
    w_attn = lax.all_gather(after(w_attn, small), "dp", axis=0, tiled=True)
    w_qkv = w_attn[:, : 3 * width]
    w_ot = w_attn[:, 3 * width :]
    for m in range(1, micro_count):
        seq_x.append(line_gather(after(x_low[m], seq_x[-1])))

    ffn_w = jnp.stack([w_expand.T, w_reduce], 0)
    ffn_w = lax.all_to_all(after(ffn_w, small), "dp", split_axis=1, concat_axis=2, tiled=True)
    ffn_w = far_gather(after(ffn_w, seq_x[0]))
    w_et = jnp.concatenate([p[0] for p in ffn_w], 0)
    w_r = jnp.concatenate([p[1] for p in ffn_w], 0)

    seq_grad = [
        lax.all_gather(after(dy_low[m], w_attn), "dp", axis=0, tiled=True) for m in micros
    ]

    seq_one, qkv, attended, hidden, normed_two = [], [], [], [], []
    for m in micros:
        seq_one.append(layer_norm(seq_x[m].astype(F32), gain_one, shift_one).astype(BF16))
        qkv.append(
            (jnp.dot(seq_one[m], w_qkv, preferred_element_type=F32) + bias_qkv).astype(BF16)
        )
        attended.append(attend(parents[m, 0], qkv[m], width))
        branch = line_scatter(over(attended[m], w_ot, 1, 1).astype(BF16))
        hidden.append(x_low[m].astype(F32) + (branch + bias_out))
        normed_two.append(layer_norm(hidden[m], gain_two, shift_two).astype(BF16))

    layer_out, seq_two, activated, d_pre, d_hidden, d_branch = [], [], [], [], [], []
    g_gain_two = g_shift_two = g_bias_red = g_bias_out = g_bias_e = 0.0
    for m in micros:
        sums, seq, act, dpre = ffn(normed_two[m], seq_grad[m], w_et, w_r, bias_e)
        seq_two.append(seq)
        activated.append(act)
        d_pre.append(dpre)
        d_two = sums[:, :model]
        layer_out.append((hidden[m] + (sums[:, model:] + bias_red)).astype(BF16))
        grad32 = dy_low[m].astype(F32)
        norm_value, norm_pull = jax.vjp(layer_norm, hidden[m], gain_two, shift_two)
        d_norm, g_gain, g_shift = norm_pull(d_two)
        d_hidden.append(grad32 + d_norm)
        d_branch.append(d_hidden[m].astype(BF16))
        g_gain_two = g_gain_two + g_gain
        g_shift_two = g_shift_two + g_shift
        g_bias_red = g_bias_red + jnp.sum(grad32, 0, keepdims=True)
        g_bias_out = g_bias_out + jnp.sum(d_branch[m].astype(F32), 0, keepdims=True)
        g_bias_e = g_bias_e + jnp.sum(dpre.astype(F32), 0)

    def outer(left, right):
        out = None
        for a, b in zip(left, right):
            term = over(a, b, 0, 0)
            out = term if out is None else out + term
        return out.astype(BF16)

    g_r = outer(activated, seq_grad)
    g_et = outer(d_pre, seq_two)
    g_ffn = far_scatter(
        [
            jnp.stack([g_et[i * mine : (i + 1) * mine], g_r[i * mine : (i + 1) * mine]], 0)
            for i in range(tn)
        ]
    ).astype(BF16)
    g_ffn = lax.all_to_all(g_ffn, "dp", split_axis=2, concat_axis=1, tiled=True).astype(F32)
    g_expand = g_ffn[0].T
    g_reduce = g_ffn[1]

    input_grad, d_qkv, seq_branch = [], [], []
    g_gain_one = g_shift_one = g_bias_qkv = 0.0
    for m in micros:
        seq_branch.append(line_gather(d_branch[m]))
        d_att = jnp.dot(seq_branch[m], w_ot, preferred_element_type=F32).astype(BF16)
        d_qkv.append(attend_back(parents[m, 0], qkv[m], d_att, width))
        g_bias_qkv = g_bias_qkv + jnp.sum(d_qkv[m].astype(F32), 0)
        d_one = line_scatter(over(d_qkv[m], w_qkv, 1, 1).astype(BF16))
        first_value, first_pull = jax.vjp(
            layer_norm, x_low[m].astype(F32), gain_one, shift_one
        )
        d_x, g_gain, g_shift = first_pull(d_one)
        input_grad.append((d_hidden[m] + d_x).astype(BF16))
        g_gain_one = g_gain_one + g_gain
        g_shift_one = g_shift_one + g_shift

    g_attn = jnp.concatenate(
        [
            outer(seq_one, d_qkv),
            outer(seq_branch, attended),
        ],
        axis=1,
    )
    g_attn = lax.psum_scatter(g_attn, "dp", scatter_dimension=0, tiled=True).astype(F32)
    g_query, g_key, g_value = [g_attn[:, i * width : (i + 1) * width] for i in range(3)]
    g_out = g_attn[:, 3 * width :].T

    rows = jnp.concatenate(
        [g_gain_one, g_shift_one, g_bias_out, g_gain_two, g_shift_two, g_bias_red], 0
    ).reshape(-1)
    place = jnp.zeros((tn, width), F32)
    row_q = lax.dynamic_update_slice(place, g_bias_qkv[None, :width], (tn_me, 0)).reshape(-1)
    row_v = lax.dynamic_update_slice(place, g_bias_qkv[None, 2 * width :], (tn_me, 0)).reshape(-1)
    g_bias_e = g_bias_e.reshape(tn, 1, 1, mine)
    row_e = jnp.zeros((tn, dp, mine), F32)
    for hop in range(tn):
        row_e = lax.dynamic_update_slice(
            row_e, g_bias_e[hop], (lax.rem(tn_me - hop + tn, tn), dp_me, 0)
        )
    row_e = row_e.reshape(-1)
    sums = lax.psum(jnp.concatenate([rows, row_q, row_v, row_e]), ("dp", "tensor"))
    n_rows = 6 * model
    six = lax.dynamic_slice_in_dim(sums[:n_rows].reshape(6, model), dp_me * cut, cut, 1)

    def block(flat, row_count):
        table = flat.reshape(tn, row_count, HEAD_DIM)
        cols = HEAD_DIM // dp
        table = lax.dynamic_slice(table, (tn_me, 0, dp_me * cols), (1, row_count, cols))
        return table[0]

    heads_all = tn * width
    g_bq = block(sums[n_rows : n_rows + heads_all], bq_rows)
    g_bv = block(sums[n_rows + heads_all : n_rows + 2 * heads_all], bq_rows)
    g_be = block(sums[n_rows + 2 * heads_all :], be_rows)

    return (
        jnp.stack(layer_out, 0)[:, None],
        jnp.stack(input_grad, 0)[:, None],
        six[0],
        six[1],
        g_query,
        g_bq,
        g_key,
        g_value,
        g_bv,
        g_out,
        six[2],
        six[3],
        six[4],
        g_expand,
        g_be,
        g_reduce,
        six[5],
    )


def solution(mesh):
    in_specs = (
        P(None, "dp", "tensor", None),
        P(None, "dp", None),
        P(None, "dp", "tensor", None),
        P("dp"),
        P("dp"),
        P("dp", "tensor"),
        P("tensor", "dp"),
        P("dp", "tensor"),
        P("dp", "tensor"),
        P("tensor", "dp"),
        P("tensor", "dp"),
        P("dp"),
        P("dp"),
        P("dp"),
        P("dp", "tensor"),
        P("tensor", "dp"),
        P("tensor", "dp"),
        P("dp"),
    )
    out_specs = (
        P(None, "dp", "tensor", None),
        P(None, "dp", "tensor", None),
        P("dp"),
        P("dp"),
        P("dp", "tensor"),
        P("tensor", "dp"),
        P("dp", "tensor"),
        P("dp", "tensor"),
        P("tensor", "dp"),
        P("tensor", "dp"),
        P("dp"),
        P("dp"),
        P("dp"),
        P("dp", "tensor"),
        P("tensor", "dp"),
        P("tensor", "dp"),
        P("dp"),
    )
    return jax.shard_map(body, mesh=mesh, in_specs=in_specs, out_specs=out_specs, check_vma=False)
```

```python
import functools
import math

import jax
import jax.numpy as jnp
from jax import lax
from jax.experimental import pallas as pl
from jax.experimental.pallas import tpu as pltpu
from jax.sharding import PartitionSpec as P

HEAD_DIM = 64
BLOCK = 256

F32 = jnp.float32
BF16 = jnp.bfloat16
MESH = pl.DeviceIdType.MESH
DMA = pltpu.SemaphoreType.DMA
GELU = math.sqrt(2.0 / math.pi)


def layer_norm(rows, gain, shift):
    center = rows - jnp.mean(rows, -1, keepdims=True)
    spread = jnp.mean(center * center, -1, keepdims=True)
    return center * lax.rsqrt(spread + 1e-05) * gain + shift


def after(value, *others):
    return lax.optimization_barrier((value,) + others)[0]


def over(left, right, on_left, on_right):
    return lax.dot_general(
        left, right, (((on_left,), (on_right,)), ((), ())), preferred_element_type=F32
    )


def window(index, rows):
    return pl.ds(pl.multiple_of(index * rows, rows), rows)


def remote(src, dst, send, recv, to):
    return pltpu.make_async_remote_copy(
        src_ref=src, dst_ref=dst, send_sem=send, recv_sem=recv,
        device_id=to, device_id_type=MESH,
    )


class Line:
    def __init__(self):
        self.n = lax.axis_size("tensor")
        self.me = lax.axis_index("tensor")
        self.dp = lax.axis_index("dp")

    def at(self, index):
        return (self.dp, index)

    def greet(self, barrier):
        @pl.when(self.me > 0)
        def _():
            pl.semaphore_signal(barrier, inc=1, device_id=self.at(self.me - 1), device_id_type=MESH)

        @pl.when(self.me < self.n - 1)
        def _():
            pl.semaphore_signal(barrier, inc=1, device_id=self.at(self.me + 1), device_id_type=MESH)

    def peers(self):
        return (self.me + self.n - 1) // self.n + (2 * self.n - 2 - self.me) // self.n


class LineGather:
    def __init__(self, line, own, full, sems):
        self.line, self.own, self.full = line, own, full
        self.rows = own.shape[0]
        self.local, self.up_send, self.up_recv, self.down_send, self.down_recv = sems

    @staticmethod
    def sems(n):
        return [DMA, DMA((n - 1,)), DMA((n - 1,)), DMA((n - 1,)), DMA((n - 1,))]

    def hop(self, step, up):
        line = self.line
        if up:
            shard, to = line.me - (step - 1), line.me + 1
            send, recv = self.up_send, self.up_recv
        else:
            shard, to = line.me + (step - 1), line.me - 1
            send, recv = self.down_send, self.down_recv
        there = self.full.at[window(shard, self.rows)]
        src = self.own if step == 1 else there
        return remote(src, there, send.at[step - 1], recv.at[step - 1], line.at(to))

    def sends(self, step, up):
        line = self.line
        if up:
            return (line.me < line.n - 1) & (line.me >= step - 1)
        return (line.me > 0) & (line.me + step - 1 < line.n)

    def takes(self, step, up):
        line = self.line
        return (line.me >= step) if up else (line.me + step < line.n)

    def send(self, step):
        for up in (True, False):
            @pl.when(self.sends(step, up))
            def _():
                self.hop(step, up).start()

    def start(self):
        self.place = pltpu.make_async_copy(
            self.own, self.full.at[window(self.line.me, self.rows)], self.local
        )
        self.place.start()
        self.send(1)

    def take(self, step):
        for up in (True, False):
            @pl.when(self.takes(step, up))
            def _():
                line = self.line
                shard = (line.me - step) if up else (line.me + step)
                here = self.full.at[window(shard, self.rows)]
                send, recv = (
                    (self.up_send, self.up_recv) if up else (self.down_send, self.down_recv)
                )
                remote(
                    here, here, send.at[step - 1], recv.at[step - 1], line.at(line.me)
                ).wait_recv()
        if step < self.line.n - 1:
            self.send(step + 1)

    def finish(self):
        for step in range(1, self.line.n):
            for up in (True, False):
                @pl.when(self.sends(step, up))
                def _():
                    self.hop(step, up).wait_send()
        pltpu.make_async_copy(
            self.own, self.full.at[window(self.line.me, self.rows)], self.local
        ).wait()


class LineScatter:
    def __init__(self, line, parts, out, scratch):
        self.line, self.parts, self.out = line, parts, out
        self.rows = out.shape[0]
        (self.own, self.sum, self.come, self.load, self.own_sem, self.send_sem, self.recv_sem) = scratch

    @staticmethod
    def scratch(n, rows, d):
        return [
            pltpu.VMEM((rows, d), BF16),
            pltpu.VMEM((2, n - 1, rows, d), BF16),
            pltpu.VMEM((2, n - 1, rows, d), BF16),
            DMA((2, n - 1)), DMA, DMA((2, n - 1)), DMA((2, n - 1)),
        ]

    def sends(self, step, up):
        line = self.line
        return (line.me <= step - 1) if up else (line.n - 1 - line.me <= step - 1)

    def load_of(self, step, up):
        line = self.line
        chunk = (line.me + line.n - step) if up else (line.me - line.n + step)
        way = 0 if up else 1
        return pltpu.make_async_copy(
            self.parts.at[window(chunk, self.rows)], self.sum.at[way, step - 1], self.load.at[way, step - 1]
        )

    def hop(self, step, up):
        line, way = self.line, 0 if up else 1
        return remote(
            self.sum.at[way, step - 1], self.come.at[way, step - 1],
            self.send_sem.at[way, step - 1], self.recv_sem.at[way, step - 1],
            line.at(line.me + 1 if up else line.me - 1),
        )

    def wait_from(self, step, up):
        line, way = self.line, 0 if up else 1
        remote(
            self.come.at[way, step - 1], self.come.at[way, step - 1],
            self.send_sem.at[way, step - 1], self.recv_sem.at[way, step - 1],
            line.at(line.me),
        ).wait_recv()

    def own_load(self):
        return pltpu.make_async_copy(
            self.parts.at[window(self.line.me, self.rows)], self.own, self.own_sem
        )

    def prepare(self):
        self.own_load().start()
        for step in range(1, self.line.n):
            for up in (True, False):
                @pl.when(self.sends(step, up))
                def _():
                    self.load_of(step, up).start()

    def step(self, step):
        line = self.line
        for up in (True, False):
            way = 0 if up else 1

            @pl.when(self.sends(step, up))
            def _():
                self.load_of(step, up).wait()
                if step > 1:
                    inner = (line.me > 0) if up else (line.me < line.n - 1)

                    @pl.when(inner)
                    def _():
                        self.wait_from(step - 1, up)

                        @pl.loop(0, self.rows // 16)
                        def _(i):
                            part = window(i, 16)
                            self.sum[way, step - 1, part] = (
                                self.sum[way, step - 1, part].astype(F32)
                                + self.come[way, step - 2, part].astype(F32)
                            ).astype(BF16)

                self.hop(step, up).start()

    def finish(self):
        line, n = self.line, self.line.n
        self.own_load().wait()

        @pl.loop(0, self.rows // 16)
        def _(i):
            part = window(i, 16)
            self.out[part] = self.own[part].astype(F32)

        for up in (True, False):
            way = 0 if up else 1

            @pl.when((line.me > 0) if up else (line.me < n - 1))
            def _():
                self.wait_from(n - 1, up)

                @pl.loop(0, self.rows // 16)
                def _(i):
                    part = window(i, 16)
                    self.out[part] += self.come[way, n - 2, part].astype(F32)

        for step in range(1, n):
            for up in (True, False):
                @pl.when(self.sends(step, up))
                def _():
                    self.hop(step, up).wait_send()


class Cube:
    def __init__(self):
        self.dp = lax.axis_size("dp")
        self.levels = levels = self.dp.bit_length() - 2
        self.count = 1 << levels
        self.me = me = lax.axis_index("dp")
        self.tensor = lax.axis_index("tensor")
        core = me % 2
        flips = []
        for bit in range(1, levels + 1):
            flips.append((1 << bit) * (1 - 2 * ((me // (1 << bit)) % 2)))
        self.steps = [
            flips[l] * (1 - core) + flips[levels - 1 - l] * core for l in range(levels)
        ]
        self.core_step = 1 - 2 * core

    def at(self, index):
        return (index, self.tensor)

    def owner(self, piece):
        mine, other = self.me, self.me + self.core_step
        for l in range(self.levels):
            if piece >> l & 1:
                mine = mine + self.steps[l]
                other = other + self.steps[self.levels - 1 - l]
        return mine, other

    def greet(self, barrier):
        for step in self.steps + [self.core_step]:
            pl.semaphore_signal(
                barrier, inc=1, device_id=self.at(self.me + step), device_id_type=MESH
            )

    def peers(self):
        return self.levels + 1


class CubeGather:
    def __init__(self, cube, own, full, sems):
        self.cube, self.own, self.full = cube, own, full
        self.rows = own.shape[0]
        self.local, self.send_sem, self.recv_sem, self.core_send, self.core_recv = sems
        self.arrived, self.sent = {0}, []

    @staticmethod
    def sems(count):
        return [DMA, DMA((count,)), DMA((count,)), DMA((count,)), DMA((count,))]

    def slot(self, index):
        return self.full.at[window(index, self.rows)]

    def src(self, piece):
        return self.own if piece == 0 else self.slot(self.cube.owner(piece)[0])

    def hop(self, piece, level):
        cube, there = self.cube, piece + (1 << level)
        return remote(
            self.src(piece), self.slot(cube.owner(piece)[0]),
            self.send_sem.at[there], self.recv_sem.at[there], cube.at(cube.me + cube.steps[level]),
        )

    def core(self, piece):
        cube = self.cube
        return remote(
            self.src(piece), self.slot(cube.owner(piece)[0]),
            self.core_send.at[piece], self.core_recv.at[piece], cube.at(cube.me + cube.core_step),
        )

    def give(self, piece):
        for level in range(piece.bit_length(), self.cube.levels):
            self.sent.append(self.hop(piece, level))
            self.sent[-1].start()
        self.sent.append(self.core(piece))
        self.sent[-1].start()

    def start(self):
        self.place = pltpu.make_async_copy(self.own, self.slot(self.cube.me), self.local)
        self.place.start()
        self.give(0)

    def take(self, piece):
        if piece in self.arrived:
            return
        here = self.slot(self.cube.owner(piece)[0])
        remote(
            here, here, self.send_sem.at[piece], self.recv_sem.at[piece], self.cube.at(self.cube.me)
        ).wait_recv()
        self.arrived.add(piece)
        self.give(piece)

    def take_core(self, piece):
        here = self.slot(self.cube.owner(piece)[1])
        remote(
            here, here, self.core_send.at[piece], self.core_recv.at[piece], self.cube.at(self.cube.me)
        ).wait_recv()

    def finish(self):
        for piece in range(self.cube.count):
            self.take(piece)
            self.take_core(piece)
        for copy in self.sent:
            copy.wait_send()
        self.place.wait()


class CubeScatter:
    def __init__(self, cube, parts, out, scratch):
        self.cube, self.parts, self.out = cube, parts, out
        self.rows = out.shape[0]
        (self.keep, self.core_in, self.fold_in, self.load_sem,
         self.core_send, self.core_recv, self.send_sem, self.recv_sem) = scratch

    @staticmethod
    def scratch(count, rows, d):
        return [
            pltpu.VMEM((count, rows, d), BF16),
            pltpu.VMEM((count, rows, d), BF16),
            pltpu.VMEM((count - 1, rows, d), BF16),
            DMA((count,)), DMA((count,)), DMA((count,)), DMA((count - 1,)), DMA((count - 1,)),
        ]

    def load(self, piece):
        return pltpu.make_async_copy(
            self.parts.at[window(self.cube.owner(piece)[0], self.rows)],
            self.keep.at[piece], self.load_sem.at[piece],
        )

    def core(self, piece):
        cube = self.cube
        return remote(
            self.parts.at[window(cube.owner(piece)[1], self.rows)], self.core_in.at[piece],
            self.core_send.at[piece], self.core_recv.at[piece], cube.at(cube.me + cube.core_step),
        )

    def hop(self, piece):
        cube, level = self.cube, piece.bit_length() - 1
        return remote(
            self.keep.at[piece], self.fold_in.at[piece - 1],
            self.send_sem.at[piece - 1], self.recv_sem.at[piece - 1],
            cube.at(cube.me + cube.steps[level]),
        )

    def order(self):
        return sorted(range(self.cube.count), key=lambda p: (-(p.bit_length()), p))

    def start(self):
        for piece in self.order():
            self.core(piece).start()
            self.load(piece).start()

    def add(self, piece, other):
        @pl.loop(0, self.rows // 16)
        def _(i):
            part = window(i, 16)
            self.keep[piece, part] = (
                self.keep[piece, part].astype(F32) + other[part].astype(F32)
            ).astype(BF16)

    def fold(self, piece):
        self.load(piece).wait()
        self.core(piece).wait_recv()
        self.add(piece, self.core_in.at[piece])
        for level in range(self.cube.levels - 1, piece.bit_length() - 1, -1):
            above = piece + (1 << level)
            self.hop(above).wait_recv()
            self.add(piece, self.fold_in.at[above - 1])
        if piece:
            self.hop(piece).start()

    def finish(self):
        self.fold(0)

        @pl.loop(0, self.rows // 16)
        def _(i):
            part = window(i, 16)
            self.out[part] = self.keep[0, part].astype(F32)

        for piece in range(self.cube.count):
            self.core(piece).wait_send()
            if piece:
                self.hop(piece).wait_send()


class CubeExchange:
    def __init__(self, cube, moves, sems):
        self.cube, self.moves = cube, moves
        self.send_sem, self.recv_sem, self.local = sems

    @staticmethod
    def sems(dp, moves):
        return [DMA((moves, dp)), DMA((moves, dp)), DMA((moves,))]

    def copies(self):
        cube = self.cube
        out = []
        for k in range(1, cube.dp):
            to = (cube.me + k) % cube.dp
            for m, (src, dst) in enumerate(self.moves):
                out.append(
                    remote(src(to), dst(cube.me), self.send_sem.at[m, k], self.recv_sem.at[m, k], cube.at(to))
                )
        return out

    def locals(self):
        return [
            pltpu.make_async_copy(src(self.cube.me), dst(self.cube.me), self.local.at[m])
            for m, (src, dst) in enumerate(self.moves)
        ]

    def start(self):
        for copy in self.copies() + self.locals():
            copy.start()

    def finish(self):
        cube = self.cube
        for copy in self.copies():
            copy.wait_send()
        for k in range(1, cube.dp):
            of = (cube.me - k + cube.dp) % cube.dp
            for m, (src, dst) in enumerate(self.moves):
                here = dst(of)
                remote(here, here, self.send_sem.at[m, k], self.recv_sem.at[m, k], cube.at(of)).wait_recv()
        for copy in self.locals():
            copy.wait()


ANY = pl.BlockSpec(memory_space=pl.ANY)
VMEM = pl.BlockSpec(memory_space=pltpu.VMEM)


def front_kernel(x_ref, w_ref, we_ref, wr_ref, small_ref, seq_ref, w_out, we_out, wr_out, small_out, *sems):
    line, cube = Line(), Cube()
    gather = LineGather(line, x_ref, seq_ref, sems[:5])
    weights = CubeGather(cube, w_ref, w_out, sems[5:10])
    mine = wr_out.shape[0]
    rows, cols = we_ref.shape[0], wr_ref.shape[1]
    tile = small_ref.shape[0]
    moves = [
        (lambda d: small_ref, lambda d: small_out.at[window(d, tile)]),
        (lambda d: wr_ref.at[window(d, mine)], lambda d: wr_out.at[:, window(d, cols)]),
        (lambda d: we_ref.at[:, window(d, mine)], lambda d: we_out.at[window(d, rows)]),
    ]
    swap = CubeExchange(cube, moves if mine % 128 == 0 else moves[:2], sems[10:13])
    barrier = pltpu.get_barrier_semaphore()
    line.greet(barrier)
    for k in range(1, cube.dp):
        pl.semaphore_signal(
            barrier, inc=1, device_id=cube.at((cube.me + k) % cube.dp), device_id_type=MESH
        )
    pl.semaphore_wait(barrier, cube.dp - 1 + line.peers())
    gather.start()
    weights.start()
    gather.take(1)
    for piece in range(1, cube.count):
        if piece.bit_length() < cube.levels:
            weights.take(piece)
    swap.start()
    gather.take(2)
    for piece in range(1, cube.count):
        weights.take(piece)
    for step in range(3, line.n):
        gather.take(step)
    weights.finish()
    swap.finish()
    gather.finish()


def front(x, w, w_e, w_r, small):
    dp, n = lax.axis_size("dp"), lax.axis_size("tensor")
    rows, model = x.shape
    outs = pl.pallas_call(
        front_kernel,
        out_shape=(
            jax.ShapeDtypeStruct((n * rows, model), BF16),
            jax.ShapeDtypeStruct((dp * w.shape[0], w.shape[1]), BF16),
            jax.ShapeDtypeStruct((dp * w_e.shape[0], w_e.shape[1] // dp), BF16),
            jax.ShapeDtypeStruct((w_r.shape[0] // dp, w_r.shape[1] * dp), BF16),
            jax.ShapeDtypeStruct((dp * small.shape[0], small.shape[1]), BF16),
        ),
        in_specs=[ANY] * 5,
        out_specs=(ANY,) * 5,
        scratch_shapes=LineGather.sems(n) + CubeGather.sems(dp // 2) + CubeExchange.sems(dp, 3),
        compiler_params=pltpu.CompilerParams(collective_id=0, has_side_effects=True),
        cost_estimate=pl.CostEstimate(flops=80 * 10**9, bytes_accessed=10**7, transcendentals=0),
        name="front",
    )(x, w, w_e, w_r, small)
    seq, w_all, e_all, r_all, small_all = outs
    if r_all.shape[0] % 128:
        e_all = lax.all_to_all(w_e, "dp", split_axis=1, concat_axis=0, tiled=True)
    return seq, w_all, e_all, r_all, small_all


def sum_kernel(lines, *refs):
    line, cube = Line(), Cube()
    total = len([r for r in refs if r is not None])
    extra = 1 if total - 2 * lines - 7 * lines > 0 else 0
    ins, outs = refs[: lines + extra], refs[lines + extra : 2 * (lines + extra)]
    scratch = refs[2 * (lines + extra) :]
    sums = [
        LineScatter(line, ins[i], outs[i], scratch[7 * i : 7 * i + 7]) for i in range(lines)
    ]
    plane = CubeScatter(cube, ins[lines], outs[lines], scratch[7 * lines :]) if extra else None
    for s in sums:
        s.prepare()
    barrier = pltpu.get_barrier_semaphore()
    line.greet(barrier)
    if extra:
        cube.greet(barrier)
    pl.semaphore_wait(barrier, line.peers() + (cube.peers() if extra else 0))
    if extra:
        plane.start()
    pieces = [p for p in plane.order() if p] if extra else []
    per = -(-len(pieces) // (line.n - 1))
    for step in range(1, line.n):
        for s in sums:
            s.step(step)
        for piece in pieces[:per]:
            plane.fold(piece)
        pieces = pieces[per:]
    if extra:
        plane.finish()
    for s in sums:
        s.finish()


def line_sums(parts, plane_parts, collective_id):
    dp, n = lax.axis_size("dp"), lax.axis_size("tensor")
    rows, d = parts[0].shape[0] // n, parts[0].shape[1]
    out_shape = [jax.ShapeDtypeStruct((rows, d), F32) for _ in parts]
    scratch = []
    for _ in parts:
        scratch += LineScatter.scratch(n, rows, d)
    operands = list(parts)
    if plane_parts is not None:
        rows_p, d_p = plane_parts.shape[0] // dp, plane_parts.shape[1]
        out_shape.append(jax.ShapeDtypeStruct((rows_p, d_p), F32))
        scratch += CubeScatter.scratch(dp // 2, rows_p, d_p)
        operands.append(plane_parts)
    return pl.pallas_call(
        functools.partial(sum_kernel, len(parts)),
        out_shape=tuple(out_shape),
        in_specs=[ANY] * len(operands),
        out_specs=(VMEM,) * len(operands),
        scratch_shapes=scratch,
        compiler_params=pltpu.CompilerParams(
            collective_id=collective_id, has_side_effects=True, vmem_limit_bytes=60 << 20
        ),
        cost_estimate=pl.CostEstimate(flops=80 * 10**9, bytes_accessed=10**7, transcendentals=0),
        name="line_sums",
    )(*operands)


PAIR = 2 * HEAD_DIM
NEVER = -1e30


def lane_of(shape, head):
    lane = lax.broadcasted_iota(jnp.int32, shape, 1)
    return (lane < HEAD_DIM) if head == 0 else (lane >= HEAD_DIM)


def sight(parents_ref, row, col):
    at = jnp.int32(row)
    seen = at == col
    for hop in range(row - col):
        at = parents_ref[at]
        seen = seen | (at == col)
    return jnp.where(seen, 0.0, NEVER).astype(F32)


def masked_scores(parents_ref, q_head, k_ref, row):
    scores = []
    for col in range(row + 1):
        part = over(q_head, k_ref[col * BLOCK : (col + 1) * BLOCK, :], 1, 1)
        if col == row:
            below = lax.broadcasted_iota(jnp.int32, part.shape, 1) <= lax.broadcasted_iota(
                jnp.int32, part.shape, 0
            )
            part = jnp.where(below, part, NEVER)
        else:
            part = part + sight(parents_ref, row, col)
        scores.append(part)
    return scores


def row_reduce(parts, fold, reduce):
    return reduce(functools.reduce(fold, parts), axis=-1, keepdims=True)


def attend_kernel(parents_ref, q_ref, k_ref, v_ref, out_ref):
    blocks = q_ref.shape[0] // BLOCK
    scale = 1.0 / math.sqrt(HEAD_DIM)
    for row in range(blocks):
        here = slice(row * BLOCK, (row + 1) * BLOCK)
        heads = []
        for head in range(2):
            q_head = q_ref[here, :].astype(F32) * scale
            q_head = jnp.where(lane_of(q_head.shape, head), q_head, 0.0).astype(BF16)
            scores = masked_scores(parents_ref, q_head, k_ref, row)
            top = row_reduce(scores, jnp.maximum, jnp.max)
            probs = [jnp.exp(s - top) for s in scores]
            total = row_reduce(probs, jnp.add, jnp.sum)
            out = None
            for col in range(row + 1):
                term = over(
                    probs[col].astype(BF16), v_ref[col * BLOCK : (col + 1) * BLOCK, :], 1, 0
                )
                out = term if out is None else out + term
            heads.append(out / total)
        mixed = jnp.where(lane_of(heads[0].shape, 0), heads[0], heads[1])
        out_ref[here, :] = mixed.astype(out_ref.dtype)


def attend(parents, qkv, width):
    rows = qkv.shape[0]
    pairs = width // PAIR
    spec = lambda part: pl.BlockSpec((rows, PAIR), lambda p, parents: (0, part * pairs + p))
    blocks = rows // BLOCK
    work = pairs * 2 * (blocks * (blocks + 1) // 2) * BLOCK * BLOCK
    return pl.pallas_call(
        attend_kernel,
        out_shape=jax.ShapeDtypeStruct((rows, width), BF16),
        grid_spec=pltpu.PrefetchScalarGridSpec(
            num_scalar_prefetch=1,
            grid=(pairs,),
            in_specs=[spec(0), spec(1), spec(2)],
            out_specs=pl.BlockSpec((rows, PAIR), lambda p, parents: (0, p)),
        ),
        compiler_params=pltpu.CompilerParams(vmem_limit_bytes=48 << 20),
        cost_estimate=pl.CostEstimate(
            flops=work * PAIR * 24, bytes_accessed=rows * width * 8, transcendentals=work
        ),
        name="attend",
    )(parents, qkv, qkv, qkv)


def attend_back_kernel(host, parents_ref, q_ref, k_ref, v_ref, g_ref, *refs):
    if host:
        own_ref, out_ref, full_ref, dq_s, dk_s, dv_s = refs[:6]
        line = Line()
        gather = LineGather(line, own_ref, full_ref, refs[6:])
        pair, pairs = pl.program_id(0), pl.num_programs(0)

        @pl.when((pair == 0) & (pl.program_id(1) == 0))
        def _():
            barrier = pltpu.get_barrier_semaphore()
            line.greet(barrier)
            pl.semaphore_wait(barrier, line.peers())
            gather.start()

        @pl.when((pair == pairs - 1) & (pl.program_id(1) == 0))
        def _():
            gather.take(1)

    else:
        out_ref, dq_s, dk_s, dv_s = refs
    part = pl.program_id(1)
    blocks = q_ref.shape[0] // BLOCK
    scale = 1.0 / math.sqrt(HEAD_DIM)

    @pl.when(part == 0)
    def _():
        for row in range(blocks):
            here = slice(row * BLOCK, (row + 1) * BLOCK)
            dq_heads = []
            for head in range(2):
                lanes = lane_of((BLOCK, PAIR), head)
                q_head = jnp.where(lanes, q_ref[here, :].astype(F32) * scale, 0.0).astype(BF16)
                g_head = jnp.where(lanes, g_ref[here, :].astype(F32), 0.0).astype(BF16)
                scores = masked_scores(parents_ref, q_head, k_ref, row)
                top = row_reduce(scores, jnp.maximum, jnp.max)
                probs = [jnp.exp(s - top) for s in scores]
                rest = 1.0 / row_reduce(probs, jnp.add, jnp.sum)
                probs = [p * rest for p in probs]
                d_probs = [
                    over(g_head, v_ref[col * BLOCK : (col + 1) * BLOCK, :], 1, 1)
                    for col in range(row + 1)
                ]
                level = row_reduce([p * d for p, d in zip(probs, d_probs)], jnp.add, jnp.sum)
                dq = None
                for col in range(row + 1):
                    there = slice(col * BLOCK, (col + 1) * BLOCK)
                    d_scores = (probs[col] * (d_probs[col] - level)).astype(BF16)
                    term = over(d_scores, k_ref[there, :], 1, 0)
                    dq = term if dq is None else dq + term
                    dk = over(d_scores, q_head, 0, 0)
                    dv = over(probs[col].astype(BF16), g_head, 0, 0)
                    if row == col and head == 0:
                        dk_s[there, :] = dk
                        dv_s[there, :] = dv
                    else:
                        dk_s[there, :] += dk
                        dv_s[there, :] += dv
                dq_heads.append(dq * scale)
            dq_s[here, :] = jnp.where(lane_of((BLOCK, PAIR), 0), dq_heads[0], dq_heads[1]).astype(
                BF16
            )
        out_ref[...] = dq_s[...]

    @pl.when(part == 1)
    def _():
        out_ref[...] = dk_s[...].astype(BF16)

    @pl.when(part == 2)
    def _():
        out_ref[...] = dv_s[...].astype(BF16)

    if host:

        @pl.when((pair == pairs - 1) & (part == 2))
        def _():
            for step in range(2, line.n):
                gather.take(step)
            gather.finish()


def attend_back(parents, qkv, grad, width, own=None):
    rows = qkv.shape[0]
    pairs = width // PAIR
    spec = lambda part: pl.BlockSpec((rows, PAIR), lambda p, c, parents: (0, part * pairs + p))
    blocks = rows // BLOCK
    work = pairs * 2 * (blocks * (blocks + 1) // 2) * BLOCK * BLOCK
    host = own is not None
    out_shape = [jax.ShapeDtypeStruct((rows, 3 * width), BF16)]
    out_specs = [pl.BlockSpec((rows, PAIR), lambda p, c, parents: (0, c * pairs + p))]
    sems = []
    params = dict(vmem_limit_bytes=48 << 20)
    if host:
        n = lax.axis_size("tensor")
        out_shape.append(jax.ShapeDtypeStruct((n * own.shape[0], own.shape[1]), BF16))
        out_specs.append(ANY)
        sems = LineGather.sems(n)
        params.update(collective_id=4, has_side_effects=True)
    out = pl.pallas_call(
        functools.partial(attend_back_kernel, host),
        out_shape=out_shape,
        grid_spec=pltpu.PrefetchScalarGridSpec(
            num_scalar_prefetch=1,
            grid=(pairs, 3),
            in_specs=[
                spec(0),
                spec(1),
                spec(2),
                pl.BlockSpec((rows, PAIR), lambda p, c, parents: (0, p)),
            ]
            + [ANY] * host,
            out_specs=out_specs,
            scratch_shapes=[
                pltpu.VMEM((rows, PAIR), BF16),
                pltpu.VMEM((rows, PAIR), F32),
                pltpu.VMEM((rows, PAIR), F32),
            ]
            + sems,
        ),
        compiler_params=pltpu.CompilerParams(**params),
        cost_estimate=pl.CostEstimate(
            flops=work * PAIR * 60, bytes_accessed=rows * width * 14, transcendentals=work
        ),
        name="attend_back",
    )(parents, qkv, qkv, qkv, grad, *([own] if host else []))
    return out if host else out[0]


def ffn_kernel(host, n2_ref, dy_ref, we_ref, wr_ref, be_ref, *refs):
    if host:
        line_own, refs = refs[0], refs[1:]
    sum_ref, seq_ref, act_ref, dpre_ref = refs[:4]
    refs = refs[4:]
    if host:
        line_full, refs = refs[0], refs[1:]
    we, wr, seq, dy_st, act_st, dpre_st, keep, give, core_in, fold_in = refs[:10]
    w_sem, own_sem, dy_sem, seq_sem, st_sem = refs[10:15]
    ag_send, ag_recv, agc_send, agc_recv, rsc_send, rsc_recv, fold_send, fold_recv = refs[15:23]
    cube = Cube()
    levels, me, steps, core_step = cube.levels, cube.me, cube.steps, cube.core_step
    count, at, owner = cube.count, cube.at, cube.owner
    rows, model = n2_ref.shape
    units = wr_ref.shape[0]
    barrier = pltpu.get_barrier_semaphore()
    cube.greet(barrier)
    hosted = []
    if host:
        line = Line()
        line.greet(barrier)
        gather = LineGather(line, line_own, line_full, refs[23:])
    load_own = pltpu.make_async_copy(n2_ref, seq.at[0, pl.ds(0, rows)], own_sem)
    load_own.start()
    parts = we_ref.shape[0] // model
    mine_units = we_ref.shape[1]
    loads_w = [pltpu.make_async_copy(wr_ref, wr, w_sem.at[parts])]
    for part in range(parts):
        loads_w.append(
            pltpu.make_async_copy(
                we_ref.at[pl.ds(part * model, model)],
                we.at[:, pl.ds(part * mine_units, mine_units)],
                w_sem.at[part],
            )
        )
    for c in loads_w:
        c.start()

    def load_dy(piece, slot):
        mine, other = owner(piece)
        out = []
        for half, index in enumerate((mine, other)):
            out.append(
                pltpu.make_async_copy(
                    dy_ref.at[pl.ds(pl.multiple_of(index * rows, rows), rows)],
                    dy_st.at[slot, pl.ds(half * rows, rows)],
                    dy_sem.at[slot, half],
                )
            )
        return out

    def gather_copy(piece, level):
        there = piece + (1 << level)
        return remote(
            seq.at[piece, pl.ds(0, rows)], seq.at[there, pl.ds(0, rows)],
            ag_send.at[there], ag_recv.at[there], at(me + steps[level]),
        )

    def gather_core(piece):
        return remote(
            seq.at[piece, pl.ds(0, rows)], seq.at[piece, pl.ds(rows, rows)],
            agc_send.at[piece], agc_recv.at[piece], at(me + core_step),
        )

    order = [0] + sorted(range(1, count), key=lambda p: (-(p.bit_length()), p))
    slots = {piece: i % 2 for i, piece in enumerate(order)}
    loads = {order[0]: load_dy(order[0], 0)}
    for c in loads[order[0]]:
        c.start()

    load_own.wait()
    pl.semaphore_wait(barrier, cube.peers() + (line.peers() if host else 0))
    if host:
        gather.start()
    sends = []
    for level in range(levels):
        sends.append(gather_copy(0, level))
        sends[-1].start()
    sends.append(gather_core(0))
    sends[-1].start()
    for c in loads_w:
        c.wait()

    arrived = {0}

    def take(piece):
        if piece in arrived:
            return
        low = piece - (1 << (piece.bit_length() - 1))
        gather_copy(low, piece.bit_length() - 1).wait_recv()
        arrived.add(piece)
        for level in range(piece.bit_length(), levels):
            sends.append(gather_copy(piece, level))
            sends[-1].start()
        sends.append(gather_core(piece))
        sends[-1].start()

    stores = {}
    outs = {}
    core_sends = {}
    folds = {}
    done_core = set()

    def add(piece, other):
        @pl.loop(0, rows // 16)
        def _(i):
            part = pl.ds(pl.multiple_of(i * 16, 16), 16)
            keep[piece, part] = (
                keep[piece, part].astype(F32) + other[part].astype(F32)
            ).astype(BF16)

    def add_core(piece):
        if piece in done_core:
            return
        core_copy(piece).wait_recv()
        add(piece, core_in.at[piece])
        done_core.add(piece)

    def core_copy(piece):
        return remote(
            give.at[slots[piece]], core_in.at[piece],
            rsc_send.at[piece], rsc_recv.at[piece], at(me + core_step),
        )

    def fold_copy(piece):
        level = piece.bit_length() - 1
        low = piece - (1 << level)
        return remote(
            keep.at[piece], fold_in.at[piece - 1],
            fold_send.at[piece - 1], fold_recv.at[piece - 1], at(me + steps[level]),
        )

    def fold(piece):
        add_core(piece)
        for level in range(levels - 1, piece.bit_length() - 1, -1):
            above = piece + (1 << level)
            fold_copy(above).wait_recv()
            add(piece, fold_in.at[above - 1])
        if piece:
            folds[piece] = fold_copy(piece)
            folds[piece].start()

    chunk = 256
    wide = 512
    for turn, piece in enumerate(order):
        slot = turn % 2
        for earlier in range(1, piece + 1):
            take(earlier)
        gather_core(piece).wait_recv()
        for c in loads[piece]:
            c.wait()
        if turn + 1 < count:
            loads[order[turn + 1]] = load_dy(order[turn + 1], 1 - slot)
            for c in loads[order[turn + 1]]:
                c.start()
        if turn >= 2:
            for c in stores[turn - 2]:
                c.wait()
            core_sends[order[turn - 2]].wait_send()

        @pl.loop(0, units // chunk)
        def _(i):
            cols = pl.ds(pl.multiple_of(i * chunk, chunk), chunk)
            pre = over(seq[piece], we[:, cols], 1, 0) + be_ref[:, cols]
            d_act = over(dy_st[slot], wr[cols, :], 1, 1)
            square = pre * pre
            t = jnp.tanh(GELU * pre * (1.0 + 0.044715 * square))
            act_st[slot, :, cols] = (0.5 * pre * (1.0 + t)).astype(BF16)
            slope = 0.5 * (1.0 + t) + (0.5 * GELU) * pre * (1.0 - t * t) * (
                1.0 + (3 * 0.044715) * square
            )
            dpre_st[slot, :, cols] = (d_act * slope).astype(BF16)

        @pl.loop(0, model // wide)
        def _(i):
            cols = pl.ds(pl.multiple_of(i * wide, wide), wide)
            cols_out = pl.ds(pl.multiple_of(model + i * wide, wide), wide)
            d_two = over(dpre_st[slot], we[cols, :], 1, 1).astype(BF16)
            keep[piece, :, cols] = d_two[:rows]
            give[slot, :, cols] = d_two[rows:]
            out = over(act_st[slot], wr[:, cols], 1, 0).astype(BF16)
            keep[piece, :, cols_out] = out[:rows]
            give[slot, :, cols_out] = out[rows:]

        if host and turn < line.n - 1:
            gather.take(turn + 1)
        core_sends[piece] = core_copy(piece)
        core_sends[piece].start()
        mine, other = owner(piece)
        stores[turn] = []
        for half, index in enumerate((mine, other)):
            to = pl.ds(pl.multiple_of(index * rows, rows), rows)
            part = pl.ds(half * rows, rows)
            stores[turn].append(
                pltpu.make_async_copy(act_st.at[slot, part], act_ref.at[to], st_sem.at[0, slot, half])
            )
            stores[turn].append(
                pltpu.make_async_copy(dpre_st.at[slot, part], dpre_ref.at[to], st_sem.at[1, slot, half])
            )
            stores[turn].append(
                pltpu.make_async_copy(seq.at[piece, part], seq_ref.at[to], seq_sem.at[piece, half])
            )
        for c in stores[turn]:
            c.start()
        if piece.bit_length() == levels:
            fold(piece)
    for level in range(levels - 2, -1, -1):
        for piece in range((1 << level), 2 << level):
            fold(piece)
    add_core(0)
    for level in range(levels):
        fold_copy(1 << level).wait_recv()

    @pl.loop(0, rows // 16)
    def _(i):
        part = pl.ds(pl.multiple_of(i * 16, 16), 16)
        total = keep[0, part].astype(F32)
        for level in range(levels):
            total = total + fold_in[(1 << level) - 1, part].astype(F32)
        sum_ref[part] = total

    if host:
        for step in range(count + 1, line.n):
            gather.take(step)
        gather.finish()
    for s in sends:
        s.wait_send()
    for turn in range(max(0, count - 2), count):
        for c in stores[turn]:
            c.wait()
        core_sends[order[turn]].wait_send()
    for s in folds.values():
        s.wait_send()


def ffn(n2, dy_all, we, wr, bias_e, own=None):
    host = own is not None
    n = lax.axis_size("tensor")
    rows, model = n2.shape
    units = wr.shape[0]
    dp = lax.axis_size("dp")
    count = dp // 2
    dma, anywhere, vmem = DMA, ANY, VMEM
    operands = [n2, dy_all, we, wr, bias_e] + [own] * host
    lines = [jax.ShapeDtypeStruct((n * rows, model), BF16)] * host
    flops = 36 * dp * rows * model * units
    return pl.pallas_call(
        functools.partial(ffn_kernel, host),
        out_shape=(
            jax.ShapeDtypeStruct((rows, 2 * model), F32),
            jax.ShapeDtypeStruct((dp * rows, model), BF16),
            jax.ShapeDtypeStruct((dp * rows, units), BF16),
            jax.ShapeDtypeStruct((dp * rows, units), BF16),
            *lines,
        ),
        in_specs=[anywhere, anywhere, anywhere, anywhere, vmem] + [anywhere] * host,
        out_specs=(vmem, anywhere, anywhere, anywhere) + (anywhere,) * host,
        scratch_shapes=[
            pltpu.VMEM((model, units), BF16),
            pltpu.VMEM((units, model), BF16),
            pltpu.VMEM((count, 2 * rows, model), BF16),
            pltpu.VMEM((2, 2 * rows, model), BF16),
            pltpu.VMEM((2, 2 * rows, units), BF16),
            pltpu.VMEM((2, 2 * rows, units), BF16),
            pltpu.VMEM((count, rows, 2 * model), BF16),
            pltpu.VMEM((2, rows, 2 * model), BF16),
            pltpu.VMEM((count, rows, 2 * model), BF16),
            pltpu.VMEM((count - 1, rows, 2 * model), BF16),
            dma((n + 1,)), dma, dma((2, 2)), dma((count, 2)), dma((2, 2, 2)),
            dma((count,)), dma((count,)), dma((count,)), dma((count,)),
            dma((count,)), dma((count,)), dma((count - 1,)), dma((count - 1,)),
        ]
        + (LineGather.sems(n) if host else []),
        compiler_params=pltpu.CompilerParams(
            collective_id=2 if host else 1, has_side_effects=True, vmem_limit_bytes=62 << 20
        ),
        cost_estimate=pl.CostEstimate(
            flops=flops, bytes_accessed=8 * dp * rows * (model + units), transcendentals=dp * rows * units
        ),
        name="ffn_plane",
    )(*operands)


def body(
    tokens,
    parents,
    cotangent,
    first_gain,
    first_shift,
    w_query,
    b_query,
    w_key,
    w_value,
    b_value,
    w_out,
    b_out,
    second_gain,
    second_shift,
    w_expand,
    b_expand,
    w_reduce,
    b_reduce,
):
    dp = lax.axis_size("dp")
    tn = lax.axis_size("tensor")
    dp_me = lax.axis_index("dp")
    tn_me = lax.axis_index("tensor")
    width = w_query.shape[1]
    model = w_query.shape[0] * dp
    units = w_expand.shape[1]
    mine = units // dp
    micros = range(tokens.shape[0])
    last = tokens.shape[0] - 1
    x_low = [tokens[m, 0] for m in micros]
    dy_low = [cotangent[m, 0] for m in micros]
    rows_here = x_low[0].shape[0]
    total = rows_here * tn

    cut = first_gain.shape[0]
    bq_rows, bq_cols = b_query.shape
    be_rows, be_cols = b_expand.shape
    small = jnp.concatenate(
        [first_gain, first_shift, b_out, second_gain, second_shift, b_reduce]
        + [b_query.reshape(-1), b_value.reshape(-1), b_expand.reshape(-1)]
    )
    used = small.shape[0]
    small = jnp.pad(small, (0, -used % 2048)).reshape(-1, 128)
    w_attn = jnp.concatenate([w_query, w_key, w_value, w_out.T], axis=1)
    seq_x0, w_attn, w_e, w_r, small = front(x_low[0], w_attn, w_expand, w_reduce, small)
    w_qkv = w_attn[:, : 3 * width]
    w_ot = w_attn[:, 3 * width :]
    small = small.reshape(dp, -1)[:, :used]
    gain_one, shift_one, bias_out, gain_two, shift_two, bias_red = [
        small[:, i * cut : (i + 1) * cut].reshape(1, model).astype(F32) for i in range(6)
    ]
    at = 6 * cut
    bias_qkv = []
    for i in range(2):
        part = small[:, at : at + bq_rows * bq_cols].reshape(dp, bq_rows, bq_cols)
        bias_qkv.append(part.transpose(1, 0, 2).reshape(1, width).astype(F32))
        at += bq_rows * bq_cols
    bias_qkv = jnp.concatenate([bias_qkv[0], jnp.zeros((1, width), F32), bias_qkv[1]], 1)
    bias_e = small[:, at:].reshape(dp, dp, be_rows // dp, be_cols)
    bias_e = lax.dynamic_index_in_dim(bias_e, dp_me, 1, keepdims=False)
    bias_e = lax.all_gather(bias_e.transpose(1, 0, 2).reshape(1, mine), "tensor", axis=1, tiled=True)
    bias_e = bias_e.astype(F32)

    seq_grad = [lax.all_gather(dy_low[0], "dp", axis=0, tiled=True)]
    seq_x = [seq_x0]
    for m in micros[1:]:
        seq_x.append(lax.all_gather(after(x_low[m], seq_x[-1]), "tensor", axis=0, tiled=True))
    side = 0 if mine % 128 == 0 else 1
    w_e = lax.all_gather(after(w_e, seq_x[-1]), "tensor", axis=side, tiled=True)
    w_r = lax.all_gather(after(w_r, w_e), "tensor", axis=0, tiled=True)
    for m in micros[1:]:
        seq_grad.append(lax.all_gather(after(dy_low[m], w_r), "dp", axis=0, tiled=True))

    normal_one, seq_one, qkv, attended, hidden, normed_two = [], [], [], [], [], []
    for m in micros:
        normal_one.append(layer_norm(seq_x[m].astype(F32), 1.0, 0.0))
        seq_one.append((normal_one[m] * gain_one + shift_one).astype(BF16))
        qkv.append(
            (jnp.dot(seq_one[m], w_qkv, preferred_element_type=F32) + bias_qkv).astype(BF16)
        )
        attended.append(attend(parents[m, 0], qkv[m], width))
        branch = line_sums([over(attended[m], w_ot, 1, 1).astype(BF16)], None, 3)[0]
        hidden.append(x_low[m].astype(F32) + (branch + bias_out))
        normed_two.append(layer_norm(hidden[m], gain_two, shift_two).astype(BF16))

    layer_out, seq_two, activated, d_pre, d_hidden, d_branch, seq_branch = [], [], [], [], [], [], []
    g_gain_two = g_shift_two = g_bias_red = g_bias_out = g_bias_e = 0.0
    for m in micros:
        own = d_branch[m - 1] if m else None
        sums, seq, act, dpre, *line = ffn(normed_two[m], seq_grad[m], w_e, w_r, bias_e, own)
        seq_branch += line
        seq_two.append(seq)
        activated.append(act)
        d_pre.append(dpre)
        d_two = sums[:, :model]
        layer_out.append((hidden[m] + (sums[:, model:] + bias_red)).astype(BF16))
        grad32 = dy_low[m].astype(F32)
        norm_value, norm_pull = jax.vjp(layer_norm, hidden[m], gain_two, shift_two)
        d_norm, g_gain, g_shift = norm_pull(d_two)
        d_hidden.append(grad32 + d_norm)
        d_branch.append(d_hidden[m].astype(BF16))
        g_gain_two = g_gain_two + g_gain
        g_shift_two = g_shift_two + g_shift
        g_bias_red = g_bias_red + jnp.sum(grad32, 0, keepdims=True)
        g_bias_out = g_bias_out + jnp.sum(d_branch[m].astype(F32), 0, keepdims=True)
        g_bias_e = g_bias_e + jnp.sum(dpre.astype(F32), 0)

    def outer(left, right):
        out = None
        for a, b in zip(left, right):
            term = over(a, b, 0, 0)
            out = term if out is None else out + term
        return out.astype(BF16)

    g_r = outer(activated, seq_grad)
    g_r_sum = lax.psum_scatter(g_r, "tensor", scatter_dimension=0, tiled=True)

    d_qkv, d_one = [], []
    g_gain_one = g_shift_one = g_bias_qkv = 0.0
    for m in micros:
        d_att = jnp.dot(seq_branch[m], w_ot, preferred_element_type=F32).astype(BF16)
        if m < last:
            d_att = after(d_att, g_r)
            d, full = attend_back(parents[m, 0], qkv[m], d_att, width, d_branch[m + 1])
            seq_branch.append(full)
        else:
            g_et = outer(d_pre, seq_two)
            g_et_sum = lax.psum_scatter(after(g_et, g_r_sum), "tensor", scatter_dimension=0, tiled=True)
            d_att = after(d_att, g_et)
            d = attend_back(parents[m, 0], qkv[m], d_att, width)
        d_qkv.append(d)
        g_bias_qkv = g_bias_qkv + jnp.sum(d.astype(F32), 0)
        d_one.append(over(d, w_qkv, 1, 1).astype(BF16))
        part = d_one[m].astype(F32)
        g_gain_one = g_gain_one + jnp.sum(part * normal_one[m], 0, keepdims=True)
        g_shift_one = g_shift_one + jnp.sum(part, 0, keepdims=True)

    rows = jnp.concatenate(
        [g_gain_one, g_shift_one, g_bias_out, g_gain_two, g_shift_two, g_bias_red], 0
    ).reshape(-1)
    place = jnp.zeros((tn, width), F32)
    row_q = lax.dynamic_update_slice(place, g_bias_qkv[None, :width], (tn_me, 0)).reshape(-1)
    row_v = lax.dynamic_update_slice(place, g_bias_qkv[None, 2 * width :], (tn_me, 0)).reshape(-1)
    row_e = lax.dynamic_update_slice(
        jnp.zeros((tn, dp, mine), F32), g_bias_e.reshape(tn, 1, mine), (0, dp_me, 0)
    ).reshape(-1)
    sums = lax.psum(jnp.concatenate([rows, row_q, row_v, row_e]), ("dp", "tensor"))
    n_rows = 6 * model
    six = lax.dynamic_slice_in_dim(sums[:n_rows].reshape(6, model), dp_me * cut, cut, 1)

    def block(flat, row_count):
        table = flat.reshape(tn, row_count, HEAD_DIM)
        cols = HEAD_DIM // dp
        table = lax.dynamic_slice(table, (tn_me, 0, dp_me * cols), (1, row_count, cols))
        return table[0]

    heads_all = tn * width
    g_bq = block(sums[n_rows : n_rows + heads_all], bq_rows)
    g_bv = block(sums[n_rows + heads_all : n_rows + 2 * heads_all], bq_rows)
    g_be = block(sums[n_rows + 2 * heads_all :], be_rows)

    g_ffn = jnp.stack([g_et_sum, g_r_sum], 0)
    g_ffn = lax.all_to_all(g_ffn, "dp", split_axis=2, concat_axis=1, tiled=True).astype(F32)
    g_expand = g_ffn[0].T
    g_reduce = g_ffn[1]

    g_attn = jnp.concatenate([outer(seq_one, d_qkv), outer(seq_branch, attended)], axis=1)
    *d_one, g_attn = line_sums(d_one, g_attn, 5)
    g_query, g_key, g_value = [g_attn[:, i * width : (i + 1) * width] for i in range(3)]
    g_out = g_attn[:, 3 * width :].T
    input_grad = []
    for m in micros:
        first_value, first_pull = jax.vjp(
            lambda rows: layer_norm(rows, gain_one, shift_one), x_low[m].astype(F32)
        )
        input_grad.append((d_hidden[m] + first_pull(d_one[m])[0]).astype(BF16))

    return (
        jnp.stack(layer_out, 0)[:, None],
        jnp.stack(input_grad, 0)[:, None],
        six[0],
        six[1],
        g_query,
        g_bq,
        g_key,
        g_value,
        g_bv,
        g_out,
        six[2],
        six[3],
        six[4],
        g_expand,
        g_be,
        g_reduce,
        six[5],
    )


def solution(mesh):
    in_specs = (
        P(None, "dp", "tensor", None),
        P(None, "dp", None),
        P(None, "dp", "tensor", None),
        P("dp"),
        P("dp"),
        P("dp", "tensor"),
        P("tensor", "dp"),
        P("dp", "tensor"),
        P("dp", "tensor"),
        P("tensor", "dp"),
        P("tensor", "dp"),
        P("dp"),
        P("dp"),
        P("dp"),
        P("dp", "tensor"),
        P("tensor", "dp"),
        P("tensor", "dp"),
        P("dp"),
    )
    out_specs = (
        P(None, "dp", "tensor", None),
        P(None, "dp", "tensor", None),
        P("dp"),
        P("dp"),
        P("dp", "tensor"),
        P("tensor", "dp"),
        P("dp", "tensor"),
        P("dp", "tensor"),
        P("tensor", "dp"),
        P("tensor", "dp"),
        P("dp"),
        P("dp"),
        P("dp"),
        P("dp", "tensor"),
        P("tensor", "dp"),
        P("tensor", "dp"),
        P("dp"),
    )
    return jax.shard_map(body, mesh=mesh, in_specs=in_specs, out_specs=out_specs, check_vma=False)
```

```python
import functools
import math

import jax
import jax.numpy as jnp
from jax import lax
from jax.experimental import pallas as pl
from jax.experimental.pallas import tpu as pltpu
from jax.sharding import PartitionSpec as P

HEAD_DIM = 64
BLOCK = 256

F32 = jnp.float32
BF16 = jnp.bfloat16
MESH = pl.DeviceIdType.MESH
DMA = pltpu.SemaphoreType.DMA
GELU = math.sqrt(2.0 / math.pi)


def layer_norm(rows, gain, shift):
    center = rows - jnp.mean(rows, -1, keepdims=True)
    spread = jnp.mean(center * center, -1, keepdims=True)
    return center * lax.rsqrt(spread + 1e-05) * gain + shift


def after(value, *others):
    return lax.optimization_barrier((value,) + others)[0]


def over(left, right, on_left, on_right):
    return lax.dot_general(
        left, right, (((on_left,), (on_right,)), ((), ())), preferred_element_type=F32
    )


def window(index, rows):
    return pl.ds(pl.multiple_of(index * rows, rows), rows)


def remote(src, dst, send, recv, to):
    return pltpu.make_async_remote_copy(
        src_ref=src, dst_ref=dst, send_sem=send, recv_sem=recv,
        device_id=to, device_id_type=MESH,
    )


class Line:
    def __init__(self):
        self.n = lax.axis_size("tensor")
        self.me = lax.axis_index("tensor")
        self.dp = lax.axis_index("dp")

    def at(self, index):
        return (self.dp, index)

    def greet(self, barrier):
        @pl.when(self.me > 0)
        def _():
            pl.semaphore_signal(barrier, inc=1, device_id=self.at(self.me - 1), device_id_type=MESH)

        @pl.when(self.me < self.n - 1)
        def _():
            pl.semaphore_signal(barrier, inc=1, device_id=self.at(self.me + 1), device_id_type=MESH)

    def peers(self):
        return (self.me + self.n - 1) // self.n + (2 * self.n - 2 - self.me) // self.n


class LineGather:
    def __init__(self, line, own, full, sems):
        self.line, self.own, self.full = line, own, full
        self.rows = own.shape[0]
        self.local, self.up_send, self.up_recv, self.down_send, self.down_recv = sems

    @staticmethod
    def sems(n):
        return [DMA, DMA((n - 1,)), DMA((n - 1,)), DMA((n - 1,)), DMA((n - 1,))]

    def hop(self, step, up):
        line = self.line
        if up:
            shard, to = line.me - (step - 1), line.me + 1
            send, recv = self.up_send, self.up_recv
        else:
            shard, to = line.me + (step - 1), line.me - 1
            send, recv = self.down_send, self.down_recv
        there = self.full.at[window(shard, self.rows)]
        src = self.own if step == 1 else there
        return remote(src, there, send.at[step - 1], recv.at[step - 1], line.at(to))

    def sends(self, step, up):
        line = self.line
        if up:
            return (line.me < line.n - 1) & (line.me >= step - 1)
        return (line.me > 0) & (line.me + step - 1 < line.n)

    def takes(self, step, up):
        line = self.line
        return (line.me >= step) if up else (line.me + step < line.n)

    def send(self, step):
        for up in (True, False):
            @pl.when(self.sends(step, up))
            def _():
                self.hop(step, up).start()

    def start(self):
        self.place = pltpu.make_async_copy(
            self.own, self.full.at[window(self.line.me, self.rows)], self.local
        )
        self.place.start()
        self.send(1)

    def take(self, step):
        for up in (True, False):
            @pl.when(self.takes(step, up))
            def _():
                line = self.line
                shard = (line.me - step) if up else (line.me + step)
                here = self.full.at[window(shard, self.rows)]
                send, recv = (
                    (self.up_send, self.up_recv) if up else (self.down_send, self.down_recv)
                )
                remote(
                    here, here, send.at[step - 1], recv.at[step - 1], line.at(line.me)
                ).wait_recv()
        if step < self.line.n - 1:
            self.send(step + 1)

    def finish(self):
        for step in range(1, self.line.n):
            for up in (True, False):
                @pl.when(self.sends(step, up))
                def _():
                    self.hop(step, up).wait_send()
        pltpu.make_async_copy(
            self.own, self.full.at[window(self.line.me, self.rows)], self.local
        ).wait()


class LineScatter:
    def __init__(self, line, parts, out, scratch):
        self.line, self.parts, self.out = line, parts, out
        self.rows = out.shape[0]
        (self.own, self.sum, self.come, self.load, self.own_sem, self.send_sem, self.recv_sem) = scratch

    @staticmethod
    def scratch(n, rows, d):
        return [
            pltpu.VMEM((rows, d), BF16),
            pltpu.VMEM((2, n - 1, rows, d), BF16),
            pltpu.VMEM((2, n - 1, rows, d), BF16),
            DMA((2, n - 1)), DMA, DMA((2, n - 1)), DMA((2, n - 1)),
        ]

    def sends(self, step, up):
        line = self.line
        return (line.me <= step - 1) if up else (line.n - 1 - line.me <= step - 1)

    def load_of(self, step, up):
        line = self.line
        chunk = (line.me + line.n - step) if up else (line.me - line.n + step)
        way = 0 if up else 1
        return pltpu.make_async_copy(
            self.parts.at[window(chunk, self.rows)], self.sum.at[way, step - 1], self.load.at[way, step - 1]
        )

    def hop(self, step, up):
        line, way = self.line, 0 if up else 1
        return remote(
            self.sum.at[way, step - 1], self.come.at[way, step - 1],
            self.send_sem.at[way, step - 1], self.recv_sem.at[way, step - 1],
            line.at(line.me + 1 if up else line.me - 1),
        )

    def wait_from(self, step, up):
        line, way = self.line, 0 if up else 1
        remote(
            self.come.at[way, step - 1], self.come.at[way, step - 1],
            self.send_sem.at[way, step - 1], self.recv_sem.at[way, step - 1],
            line.at(line.me),
        ).wait_recv()

    def own_load(self):
        return pltpu.make_async_copy(
            self.parts.at[window(self.line.me, self.rows)], self.own, self.own_sem
        )

    def prepare(self):
        self.own_load().start()
        for step in range(1, self.line.n):
            for up in (True, False):
                @pl.when(self.sends(step, up))
                def _():
                    self.load_of(step, up).start()

    def step(self, step):
        line = self.line
        for up in (True, False):
            way = 0 if up else 1

            @pl.when(self.sends(step, up))
            def _():
                self.load_of(step, up).wait()
                if step > 1:
                    inner = (line.me > 0) if up else (line.me < line.n - 1)

                    @pl.when(inner)
                    def _():
                        self.wait_from(step - 1, up)

                        @pl.loop(0, self.rows // 16)
                        def _(i):
                            part = window(i, 16)
                            self.sum[way, step - 1, part] = (
                                self.sum[way, step - 1, part].astype(F32)
                                + self.come[way, step - 2, part].astype(F32)
                            ).astype(BF16)

                self.hop(step, up).start()

    def finish(self):
        line, n = self.line, self.line.n
        self.own_load().wait()

        @pl.loop(0, self.rows // 16)
        def _(i):
            part = window(i, 16)
            self.out[part] = self.own[part].astype(F32)

        for up in (True, False):
            way = 0 if up else 1

            @pl.when((line.me > 0) if up else (line.me < n - 1))
            def _():
                self.wait_from(n - 1, up)

                @pl.loop(0, self.rows // 16)
                def _(i):
                    part = window(i, 16)
                    self.out[part] += self.come[way, n - 2, part].astype(F32)

        for step in range(1, n):
            for up in (True, False):
                @pl.when(self.sends(step, up))
                def _():
                    self.hop(step, up).wait_send()


class Cube:
    def __init__(self):
        self.dp = lax.axis_size("dp")
        self.levels = levels = self.dp.bit_length() - 2
        self.count = 1 << levels
        self.me = me = lax.axis_index("dp")
        self.tensor = lax.axis_index("tensor")
        core = me % 2
        flips = []
        for bit in range(1, levels + 1):
            flips.append((1 << bit) * (1 - 2 * ((me // (1 << bit)) % 2)))
        self.steps = [
            flips[l] * (1 - core) + flips[levels - 1 - l] * core for l in range(levels)
        ]
        self.core_step = 1 - 2 * core

    def at(self, index):
        return (index, self.tensor)

    def owner(self, piece):
        mine, other = self.me, self.me + self.core_step
        for l in range(self.levels):
            if piece >> l & 1:
                mine = mine + self.steps[l]
                other = other + self.steps[self.levels - 1 - l]
        return mine, other

    def greet(self, barrier):
        for step in self.steps + [self.core_step]:
            pl.semaphore_signal(
                barrier, inc=1, device_id=self.at(self.me + step), device_id_type=MESH
            )

    def peers(self):
        return self.levels + 1


class CubeGather:
    def __init__(self, cube, own, full, sems):
        self.cube, self.own, self.full = cube, own, full
        self.rows = own.shape[0]
        self.local, self.send_sem, self.recv_sem, self.core_send, self.core_recv = sems
        self.arrived, self.sent = {0}, []

    @staticmethod
    def sems(count):
        return [DMA, DMA((count,)), DMA((count,)), DMA((count,)), DMA((count,))]

    def slot(self, index):
        return self.full.at[window(index, self.rows)]

    def src(self, piece):
        return self.own if piece == 0 else self.slot(self.cube.owner(piece)[0])

    def hop(self, piece, level):
        cube, there = self.cube, piece + (1 << level)
        return remote(
            self.src(piece), self.slot(cube.owner(piece)[0]),
            self.send_sem.at[there], self.recv_sem.at[there], cube.at(cube.me + cube.steps[level]),
        )

    def core(self, piece):
        cube = self.cube
        return remote(
            self.src(piece), self.slot(cube.owner(piece)[0]),
            self.core_send.at[piece], self.core_recv.at[piece], cube.at(cube.me + cube.core_step),
        )

    def give(self, piece):
        for level in range(piece.bit_length(), self.cube.levels):
            self.sent.append(self.hop(piece, level))
            self.sent[-1].start()
        self.sent.append(self.core(piece))
        self.sent[-1].start()

    def start(self):
        self.place = pltpu.make_async_copy(self.own, self.slot(self.cube.me), self.local)
        self.place.start()
        self.give(0)

    def take(self, piece):
        if piece in self.arrived:
            return
        here = self.slot(self.cube.owner(piece)[0])
        remote(
            here, here, self.send_sem.at[piece], self.recv_sem.at[piece], self.cube.at(self.cube.me)
        ).wait_recv()
        self.arrived.add(piece)
        self.give(piece)

    def take_core(self, piece):
        here = self.slot(self.cube.owner(piece)[1])
        remote(
            here, here, self.core_send.at[piece], self.core_recv.at[piece], self.cube.at(self.cube.me)
        ).wait_recv()

    def finish(self):
        for piece in range(self.cube.count):
            self.take(piece)
            self.take_core(piece)
        for copy in self.sent:
            copy.wait_send()
        self.place.wait()


class CubeScatter:
    def __init__(self, cube, parts, out, scratch):
        self.cube, self.parts, self.out = cube, parts, out
        self.rows = out.shape[0]
        (self.keep, self.core_in, self.fold_in, self.load_sem,
         self.core_send, self.core_recv, self.send_sem, self.recv_sem) = scratch

    @staticmethod
    def scratch(count, rows, d):
        return [
            pltpu.VMEM((count, rows, d), BF16),
            pltpu.VMEM((count, rows, d), BF16),
            pltpu.VMEM((count - 1, rows, d), BF16),
            DMA((count,)), DMA((count,)), DMA((count,)), DMA((count - 1,)), DMA((count - 1,)),
        ]

    def load(self, piece):
        return pltpu.make_async_copy(
            self.parts.at[window(self.cube.owner(piece)[0], self.rows)],
            self.keep.at[piece], self.load_sem.at[piece],
        )

    def core(self, piece):
        cube = self.cube
        return remote(
            self.parts.at[window(cube.owner(piece)[1], self.rows)], self.core_in.at[piece],
            self.core_send.at[piece], self.core_recv.at[piece], cube.at(cube.me + cube.core_step),
        )

    def hop(self, piece):
        cube, level = self.cube, piece.bit_length() - 1
        return remote(
            self.keep.at[piece], self.fold_in.at[piece - 1],
            self.send_sem.at[piece - 1], self.recv_sem.at[piece - 1],
            cube.at(cube.me + cube.steps[level]),
        )

    def order(self):
        return sorted(range(self.cube.count), key=lambda p: (-(p.bit_length()), p))

    def start(self):
        for piece in self.order():
            self.core(piece).start()
            self.load(piece).start()

    def add(self, piece, other):
        @pl.loop(0, self.rows // 16)
        def _(i):
            part = window(i, 16)
            self.keep[piece, part] = (
                self.keep[piece, part].astype(F32) + other[part].astype(F32)
            ).astype(BF16)

    def fold(self, piece):
        self.load(piece).wait()
        self.core(piece).wait_recv()
        self.add(piece, self.core_in.at[piece])
        for level in range(self.cube.levels - 1, piece.bit_length() - 1, -1):
            above = piece + (1 << level)
            self.hop(above).wait_recv()
            self.add(piece, self.fold_in.at[above - 1])
        if piece:
            self.hop(piece).start()

    def finish(self):
        self.fold(0)

        @pl.loop(0, self.rows // 16)
        def _(i):
            part = window(i, 16)
            self.out[part] = self.keep[0, part].astype(F32)

        for piece in range(self.cube.count):
            self.core(piece).wait_send()
            if piece:
                self.hop(piece).wait_send()


class CubeExchange:
    def __init__(self, cube, moves, sems):
        self.cube, self.moves = cube, moves
        self.send_sem, self.recv_sem, self.local = sems

    @staticmethod
    def sems(dp, moves):
        return [DMA((moves, dp)), DMA((moves, dp)), DMA((moves,))]

    def copies(self):
        cube = self.cube
        out = []
        for k in range(1, cube.dp):
            to = (cube.me + k) % cube.dp
            for m, (src, dst) in enumerate(self.moves):
                out.append(
                    remote(src(to), dst(cube.me), self.send_sem.at[m, k], self.recv_sem.at[m, k], cube.at(to))
                )
        return out

    def locals(self):
        return [
            pltpu.make_async_copy(src(self.cube.me), dst(self.cube.me), self.local.at[m])
            for m, (src, dst) in enumerate(self.moves)
        ]

    def start(self):
        for copy in self.copies() + self.locals():
            copy.start()

    def finish(self):
        cube = self.cube
        for copy in self.copies():
            copy.wait_send()
        for k in range(1, cube.dp):
            of = (cube.me - k + cube.dp) % cube.dp
            for m, (src, dst) in enumerate(self.moves):
                here = dst(of)
                remote(here, here, self.send_sem.at[m, k], self.recv_sem.at[m, k], cube.at(of)).wait_recv()
        for copy in self.locals():
            copy.wait()


ANY = pl.BlockSpec(memory_space=pl.ANY)
VMEM = pl.BlockSpec(memory_space=pltpu.VMEM)


def front_kernel(x_ref, w_ref, we_ref, wr_ref, small_ref, seq_ref, w_out, we_out, wr_out, small_out, *sems):
    line, cube = Line(), Cube()
    gather = LineGather(line, x_ref, seq_ref, sems[:5])
    weights = CubeGather(cube, w_ref, w_out, sems[5:10])
    mine = wr_out.shape[0]
    rows, cols = we_ref.shape[0], wr_ref.shape[1]
    tile = small_ref.shape[0]
    moves = [
        (lambda d: small_ref, lambda d: small_out.at[window(d, tile)]),
        (lambda d: wr_ref.at[window(d, mine)], lambda d: wr_out.at[:, window(d, cols)]),
        (lambda d: we_ref.at[:, window(d, mine)], lambda d: we_out.at[window(d, rows)]),
    ]
    swap = CubeExchange(cube, moves if mine % 128 == 0 else moves[:2], sems[10:13])
    barrier = pltpu.get_barrier_semaphore()
    line.greet(barrier)
    for k in range(1, cube.dp):
        pl.semaphore_signal(
            barrier, inc=1, device_id=cube.at((cube.me + k) % cube.dp), device_id_type=MESH
        )
    pl.semaphore_wait(barrier, cube.dp - 1 + line.peers())
    gather.start()
    weights.start()
    gather.take(1)
    for piece in range(1, cube.count):
        if piece.bit_length() < cube.levels:
            weights.take(piece)
    swap.start()
    gather.take(2)
    for piece in range(1, cube.count):
        weights.take(piece)
    for step in range(3, line.n):
        gather.take(step)
    weights.finish()
    swap.finish()
    gather.finish()


def front(x, w, w_e, w_r, small):
    dp, n = lax.axis_size("dp"), lax.axis_size("tensor")
    rows, model = x.shape
    outs = pl.pallas_call(
        front_kernel,
        out_shape=(
            jax.ShapeDtypeStruct((n * rows, model), BF16),
            jax.ShapeDtypeStruct((dp * w.shape[0], w.shape[1]), BF16),
            jax.ShapeDtypeStruct((dp * w_e.shape[0], w_e.shape[1] // dp), BF16),
            jax.ShapeDtypeStruct((w_r.shape[0] // dp, w_r.shape[1] * dp), BF16),
            jax.ShapeDtypeStruct((dp * small.shape[0], small.shape[1]), BF16),
        ),
        in_specs=[ANY] * 5,
        out_specs=(ANY,) * 5,
        scratch_shapes=LineGather.sems(n) + CubeGather.sems(dp // 2) + CubeExchange.sems(dp, 3),
        compiler_params=pltpu.CompilerParams(collective_id=0, has_side_effects=True),
        cost_estimate=pl.CostEstimate(flops=80 * 10**9, bytes_accessed=10**7, transcendentals=0),
        name="front",
    )(x, w, w_e, w_r, small)
    seq, w_all, e_all, r_all, small_all = outs
    if r_all.shape[0] % 128:
        e_all = lax.all_to_all(w_e, "dp", split_axis=1, concat_axis=0, tiled=True)
    return seq, w_all, e_all, r_all, small_all


class SmallSum:
    def __init__(self, line, cube, parts, out, scratch):
        self.line, self.cube, self.parts, self.out = line, cube, parts, out
        self.come, self.gather, self.sems, self.line_send, self.line_recv = (
            scratch[0], scratch[1], scratch[2:5], scratch[5], scratch[6]
        )
        moves = [(lambda d: parts.at[d], lambda d: self.come.at[d])]
        self.swap = CubeExchange(cube, moves, self.sems)

    @staticmethod
    def scratch(dp, n, rows, d):
        return [
            pltpu.VMEM((dp, rows, d), F32),
            pltpu.VMEM((n, rows, d), F32),
            *CubeExchange.sems(dp, 1),
            DMA((n,)), DMA((n,)),
        ]

    def hop(self, k):
        line = self.line
        here = self.gather.at[line.me]
        return remote(
            here, here, self.line_send.at[k], self.line_recv.at[k], line.at((line.me + k) % line.n)
        )

    def middle(self):
        self.swap.finish()
        total = self.come[0]
        for d in range(1, self.cube.dp):
            total = total + self.come[d]
        self.gather[self.line.me] = total
        for k in range(1, self.line.n):
            self.hop(k).start()

    def finish(self):
        line = self.line
        for k in range(1, line.n):
            here = self.gather.at[(line.me - k + line.n) % line.n]
            remote(
                here, here, self.line_send.at[k], self.line_recv.at[k], line.at(line.me)
            ).wait_recv()
            self.hop(k).wait_send()
        total = self.gather[0]
        for z in range(1, line.n):
            total = total + self.gather[z]
        self.out[...] = total


def sum_kernel(lines, planes, small, *refs):
    line, cube = Line(), Cube()
    count = lines + planes + small
    ins, outs, scratch = refs[:count], refs[count : 2 * count], refs[2 * count :]
    sums, folds = [], []
    for i in range(lines):
        sums.append(LineScatter(line, ins[i], outs[i], scratch[:7]))
        scratch = scratch[7:]
    for i in range(lines, lines + planes):
        folds.append(CubeScatter(cube, ins[i], outs[i], scratch[:8]))
        scratch = scratch[8:]
    barrier = pltpu.get_barrier_semaphore()
    if small:
        for k in range(1, line.n):
            pl.semaphore_signal(
                barrier, inc=1, device_id=line.at((line.me + k) % line.n), device_id_type=MESH
            )
        for k in range(1, cube.dp):
            pl.semaphore_signal(
                barrier, inc=1, device_id=cube.at((cube.me + k) % cube.dp), device_id_type=MESH
            )
    else:
        line.greet(barrier)
        if planes:
            cube.greet(barrier)
    for s in sums:
        s.prepare()
    if small:
        pl.semaphore_wait(barrier, line.n - 1 + cube.dp - 1)
        little = SmallSum(line, cube, ins[-1], outs[-1], scratch)
        little.swap.start()
    else:
        pl.semaphore_wait(barrier, line.peers() + (cube.peers() if planes else 0))
    pieces = [p for p in folds[0].order() if p] if planes else []
    per = -(-len(pieces) // (line.n - 1))
    for step in range(1, line.n):
        for s in sums:
            s.step(step)
        if step == 1:
            for f in folds:
                f.start()
            if small:
                little.middle()
        for piece in pieces[:per]:
            for f in folds:
                f.fold(piece)
        pieces = pieces[per:]
    for f in folds:
        f.finish()
    for s in sums:
        s.finish()
    if small:
        little.finish()


def all_sums(line_parts, plane_parts, small_parts, collective_id):
    dp, n = lax.axis_size("dp"), lax.axis_size("tensor")
    out_shape, scratch = [], []
    for part in line_parts:
        rows, d = part.shape[0] // n, part.shape[1]
        out_shape.append(jax.ShapeDtypeStruct((rows, d), F32))
        scratch += LineScatter.scratch(n, rows, d)
    for part in plane_parts:
        rows, d = part.shape[0] // dp, part.shape[1]
        out_shape.append(jax.ShapeDtypeStruct((rows, d), F32))
        scratch += CubeScatter.scratch(dp // 2, rows, d)
    for part in small_parts:
        rows, d = part.shape[1:]
        out_shape.append(jax.ShapeDtypeStruct((rows, d), F32))
        scratch += SmallSum.scratch(dp, n, rows, d)
    operands = list(line_parts) + list(plane_parts) + list(small_parts)
    return pl.pallas_call(
        functools.partial(sum_kernel, len(line_parts), len(plane_parts), len(small_parts)),
        out_shape=tuple(out_shape),
        in_specs=[ANY] * len(operands),
        out_specs=(VMEM,) * len(operands),
        scratch_shapes=scratch,
        compiler_params=pltpu.CompilerParams(
            collective_id=collective_id, has_side_effects=True, vmem_limit_bytes=60 << 20
        ),
        cost_estimate=pl.CostEstimate(flops=80 * 10**9, bytes_accessed=10**7, transcendentals=0),
        name="sums",
    )(*operands)


PAIR = 2 * HEAD_DIM
NEVER = -1e30


def lane_of(shape, head):
    lane = lax.broadcasted_iota(jnp.int32, shape, 1)
    return (lane < HEAD_DIM) if head == 0 else (lane >= HEAD_DIM)


def sight(parents_ref, row, col):
    at = jnp.int32(row)
    seen = at == col
    for hop in range(row - col):
        at = parents_ref[at]
        seen = seen | (at == col)
    return jnp.where(seen, 0.0, NEVER).astype(F32)


def masked_scores(parents_ref, q_head, k_ref, row):
    scores = []
    for col in range(row + 1):
        part = over(q_head, k_ref[col * BLOCK : (col + 1) * BLOCK, :], 1, 1)
        if col == row:
            below = lax.broadcasted_iota(jnp.int32, part.shape, 1) <= lax.broadcasted_iota(
                jnp.int32, part.shape, 0
            )
            part = jnp.where(below, part, NEVER)
        else:
            part = part + sight(parents_ref, row, col)
        scores.append(part)
    return scores


def row_reduce(parts, fold, reduce):
    return reduce(functools.reduce(fold, parts), axis=-1, keepdims=True)


def attend_kernel(parents_ref, q_ref, k_ref, v_ref, out_ref):
    blocks = q_ref.shape[0] // BLOCK
    scale = 1.0 / math.sqrt(HEAD_DIM)
    for row in range(blocks):
        here = slice(row * BLOCK, (row + 1) * BLOCK)
        heads = []
        for head in range(2):
            q_head = q_ref[here, :].astype(F32) * scale
            q_head = jnp.where(lane_of(q_head.shape, head), q_head, 0.0).astype(BF16)
            scores = masked_scores(parents_ref, q_head, k_ref, row)
            top = row_reduce(scores, jnp.maximum, jnp.max)
            probs = [jnp.exp(s - top) for s in scores]
            total = row_reduce(probs, jnp.add, jnp.sum)
            out = None
            for col in range(row + 1):
                term = over(
                    probs[col].astype(BF16), v_ref[col * BLOCK : (col + 1) * BLOCK, :], 1, 0
                )
                out = term if out is None else out + term
            heads.append(out / total)
        mixed = jnp.where(lane_of(heads[0].shape, 0), heads[0], heads[1])
        out_ref[here, :] = mixed.astype(out_ref.dtype)


def attend(parents, qkv, width):
    rows = qkv.shape[0]
    pairs = width // PAIR
    spec = lambda part: pl.BlockSpec((rows, PAIR), lambda p, parents: (0, part * pairs + p))
    blocks = rows // BLOCK
    work = pairs * 2 * (blocks * (blocks + 1) // 2) * BLOCK * BLOCK
    return pl.pallas_call(
        attend_kernel,
        out_shape=jax.ShapeDtypeStruct((rows, width), BF16),
        grid_spec=pltpu.PrefetchScalarGridSpec(
            num_scalar_prefetch=1,
            grid=(pairs,),
            in_specs=[spec(0), spec(1), spec(2)],
            out_specs=pl.BlockSpec((rows, PAIR), lambda p, parents: (0, p)),
        ),
        compiler_params=pltpu.CompilerParams(vmem_limit_bytes=48 << 20),
        cost_estimate=pl.CostEstimate(
            flops=work * PAIR * 24, bytes_accessed=rows * width * 8, transcendentals=work
        ),
        name="attend",
    )(parents, qkv, qkv, qkv)


def attend_back_kernel(host, parents_ref, q_ref, k_ref, v_ref, g_ref, *refs):
    if host:
        own_ref, out_ref, full_ref, dq_s, dk_s, dv_s = refs[:6]
        line = Line()
        gather = LineGather(line, own_ref, full_ref, refs[6:])
        pair, pairs = pl.program_id(0), pl.num_programs(0)

        @pl.when((pair == 0) & (pl.program_id(1) == 0))
        def _():
            barrier = pltpu.get_barrier_semaphore()
            line.greet(barrier)
            pl.semaphore_wait(barrier, line.peers())
            gather.start()

        @pl.when((pair == pairs - 1) & (pl.program_id(1) == 0))
        def _():
            gather.take(1)

    else:
        out_ref, dq_s, dk_s, dv_s = refs
    part = pl.program_id(1)
    blocks = q_ref.shape[0] // BLOCK
    scale = 1.0 / math.sqrt(HEAD_DIM)

    @pl.when(part == 0)
    def _():
        for row in range(blocks):
            here = slice(row * BLOCK, (row + 1) * BLOCK)
            dq_heads = []
            for head in range(2):
                lanes = lane_of((BLOCK, PAIR), head)
                q_head = jnp.where(lanes, q_ref[here, :].astype(F32) * scale, 0.0).astype(BF16)
                g_head = jnp.where(lanes, g_ref[here, :].astype(F32), 0.0).astype(BF16)
                scores = masked_scores(parents_ref, q_head, k_ref, row)
                top = row_reduce(scores, jnp.maximum, jnp.max)
                probs = [jnp.exp(s - top) for s in scores]
                rest = 1.0 / row_reduce(probs, jnp.add, jnp.sum)
                probs = [p * rest for p in probs]
                d_probs = [
                    over(g_head, v_ref[col * BLOCK : (col + 1) * BLOCK, :], 1, 1)
                    for col in range(row + 1)
                ]
                level = row_reduce([p * d for p, d in zip(probs, d_probs)], jnp.add, jnp.sum)
                dq = None
                for col in range(row + 1):
                    there = slice(col * BLOCK, (col + 1) * BLOCK)
                    d_scores = (probs[col] * (d_probs[col] - level)).astype(BF16)
                    term = over(d_scores, k_ref[there, :], 1, 0)
                    dq = term if dq is None else dq + term
                    dk = over(d_scores, q_head, 0, 0)
                    dv = over(probs[col].astype(BF16), g_head, 0, 0)
                    if row == col and head == 0:
                        dk_s[there, :] = dk
                        dv_s[there, :] = dv
                    else:
                        dk_s[there, :] += dk
                        dv_s[there, :] += dv
                dq_heads.append(dq * scale)
            dq_s[here, :] = jnp.where(lane_of((BLOCK, PAIR), 0), dq_heads[0], dq_heads[1]).astype(
                BF16
            )
        out_ref[...] = dq_s[...]

    @pl.when(part == 1)
    def _():
        out_ref[...] = dk_s[...].astype(BF16)

    @pl.when(part == 2)
    def _():
        out_ref[...] = dv_s[...].astype(BF16)

    if host:

        @pl.when((pair == pairs - 1) & (part == 2))
        def _():
            for step in range(2, line.n):
                gather.take(step)
            gather.finish()


def attend_back(parents, qkv, grad, width, own=None):
    rows = qkv.shape[0]
    pairs = width // PAIR
    spec = lambda part: pl.BlockSpec((rows, PAIR), lambda p, c, parents: (0, part * pairs + p))
    blocks = rows // BLOCK
    work = pairs * 2 * (blocks * (blocks + 1) // 2) * BLOCK * BLOCK
    host = own is not None
    out_shape = [jax.ShapeDtypeStruct((rows, 3 * width), BF16)]
    out_specs = [pl.BlockSpec((rows, PAIR), lambda p, c, parents: (0, c * pairs + p))]
    sems = []
    params = dict(vmem_limit_bytes=48 << 20)
    if host:
        n = lax.axis_size("tensor")
        out_shape.append(jax.ShapeDtypeStruct((n * own.shape[0], own.shape[1]), BF16))
        out_specs.append(ANY)
        sems = LineGather.sems(n)
        params.update(collective_id=4, has_side_effects=True)
    out = pl.pallas_call(
        functools.partial(attend_back_kernel, host),
        out_shape=out_shape,
        grid_spec=pltpu.PrefetchScalarGridSpec(
            num_scalar_prefetch=1,
            grid=(pairs, 3),
            in_specs=[
                spec(0),
                spec(1),
                spec(2),
                pl.BlockSpec((rows, PAIR), lambda p, c, parents: (0, p)),
            ]
            + [ANY] * host,
            out_specs=out_specs,
            scratch_shapes=[
                pltpu.VMEM((rows, PAIR), BF16),
                pltpu.VMEM((rows, PAIR), F32),
                pltpu.VMEM((rows, PAIR), F32),
            ]
            + sems,
        ),
        compiler_params=pltpu.CompilerParams(**params),
        cost_estimate=pl.CostEstimate(
            flops=work * PAIR * 60, bytes_accessed=rows * width * 14, transcendentals=work
        ),
        name="attend_back",
    )(parents, qkv, qkv, qkv, grad, *([own] if host else []))
    return out if host else out[0]


def ffn_kernel(host, n2_ref, dy_ref, we_ref, wr_ref, be_ref, *refs):
    if host:
        line_own, refs = refs[0], refs[1:]
    sum_ref, seq_ref, act_ref, dpre_ref, part_ref = refs[:5]
    refs = refs[5:]
    if host:
        line_full, refs = refs[0], refs[1:]
    we, wr, seq, dy_st, act_st, dpre_st, part_st, keep, give, core_in, fold_in = refs[:11]
    refs = refs[1:]
    w_sem, own_sem, dy_sem, seq_sem, st_sem = refs[10:15]
    ag_send, ag_recv, agc_send, agc_recv, rsc_send, rsc_recv, fold_send, fold_recv = refs[15:23]
    cube = Cube()
    levels, me, steps, core_step = cube.levels, cube.me, cube.steps, cube.core_step
    count, at, owner = cube.count, cube.at, cube.owner
    rows, model = n2_ref.shape
    units = wr_ref.shape[0]
    barrier = pltpu.get_barrier_semaphore()
    cube.greet(barrier)
    hosted = []
    if host:
        line = Line()
        line.greet(barrier)
        gather = LineGather(line, line_own, line_full, refs[23:])
    load_own = pltpu.make_async_copy(n2_ref, seq.at[0, pl.ds(0, rows)], own_sem)
    load_own.start()
    parts = we_ref.shape[0] // model
    mine_units = we_ref.shape[1]
    loads_w = [pltpu.make_async_copy(wr_ref, wr, w_sem.at[parts])]
    for part in range(parts):
        loads_w.append(
            pltpu.make_async_copy(
                we_ref.at[pl.ds(part * model, model)],
                we.at[:, pl.ds(part * mine_units, mine_units)],
                w_sem.at[part],
            )
        )
    for c in loads_w:
        c.start()

    def load_dy(piece, slot):
        mine, other = owner(piece)
        out = []
        for half, index in enumerate((mine, other)):
            out.append(
                pltpu.make_async_copy(
                    dy_ref.at[pl.ds(pl.multiple_of(index * rows, rows), rows)],
                    dy_st.at[slot, pl.ds(half * rows, rows)],
                    dy_sem.at[slot, half],
                )
            )
        return out

    def gather_copy(piece, level):
        there = piece + (1 << level)
        return remote(
            seq.at[piece, pl.ds(0, rows)], seq.at[there, pl.ds(0, rows)],
            ag_send.at[there], ag_recv.at[there], at(me + steps[level]),
        )

    def gather_core(piece):
        return remote(
            seq.at[piece, pl.ds(0, rows)], seq.at[piece, pl.ds(rows, rows)],
            agc_send.at[piece], agc_recv.at[piece], at(me + core_step),
        )

    order = [0] + sorted(range(1, count), key=lambda p: (-(p.bit_length()), p))
    slots = {piece: i % 2 for i, piece in enumerate(order)}
    loads = {order[0]: load_dy(order[0], 0)}
    for c in loads[order[0]]:
        c.start()

    load_own.wait()
    pl.semaphore_wait(barrier, cube.peers() + (line.peers() if host else 0))
    if host:
        gather.start()
    sends = []
    for level in range(levels):
        sends.append(gather_copy(0, level))
        sends[-1].start()
    sends.append(gather_core(0))
    sends[-1].start()
    for c in loads_w:
        c.wait()

    arrived = {0}

    def take(piece):
        if piece in arrived:
            return
        low = piece - (1 << (piece.bit_length() - 1))
        gather_copy(low, piece.bit_length() - 1).wait_recv()
        arrived.add(piece)
        for level in range(piece.bit_length(), levels):
            sends.append(gather_copy(piece, level))
            sends[-1].start()
        sends.append(gather_core(piece))
        sends[-1].start()

    stores = {}
    outs = {}
    core_sends = {}
    folds = {}
    done_core = set()

    def add(piece, other):
        @pl.loop(0, rows // 16)
        def _(i):
            part = pl.ds(pl.multiple_of(i * 16, 16), 16)
            keep[piece, part] = (
                keep[piece, part].astype(F32) + other[part].astype(F32)
            ).astype(BF16)

    def add_core(piece):
        if piece in done_core:
            return
        core_copy(piece).wait_recv()
        add(piece, core_in.at[piece])
        done_core.add(piece)

    def core_copy(piece):
        return remote(
            give.at[slots[piece]], core_in.at[piece],
            rsc_send.at[piece], rsc_recv.at[piece], at(me + core_step),
        )

    def fold_copy(piece):
        level = piece.bit_length() - 1
        low = piece - (1 << level)
        return remote(
            keep.at[piece], fold_in.at[piece - 1],
            fold_send.at[piece - 1], fold_recv.at[piece - 1], at(me + steps[level]),
        )

    def fold(piece):
        add_core(piece)
        for level in range(levels - 1, piece.bit_length() - 1, -1):
            above = piece + (1 << level)
            fold_copy(above).wait_recv()
            add(piece, fold_in.at[above - 1])
        if piece:
            folds[piece] = fold_copy(piece)
            folds[piece].start()

    chunk = 256
    wide = 512
    for turn, piece in enumerate(order):
        slot = turn % 2
        for earlier in range(1, piece + 1):
            take(earlier)
        gather_core(piece).wait_recv()
        for c in loads[piece]:
            c.wait()
        if turn + 1 < count:
            loads[order[turn + 1]] = load_dy(order[turn + 1], 1 - slot)
            for c in loads[order[turn + 1]]:
                c.start()
        if turn >= 2:
            for c in stores[turn - 2]:
                c.wait()
            core_sends[order[turn - 2]].wait_send()

        @pl.loop(0, units // chunk)
        def _(i):
            cols = pl.ds(pl.multiple_of(i * chunk, chunk), chunk)
            pre = over(seq[piece], we[:, cols], 1, 0) + be_ref[:, cols]
            d_act = over(dy_st[slot], wr[cols, :], 1, 1)
            square = pre * pre
            t = jnp.tanh(GELU * pre * (1.0 + 0.044715 * square))
            act_st[slot, :, cols] = (0.5 * pre * (1.0 + t)).astype(BF16)
            slope = 0.5 * (1.0 + t) + (0.5 * GELU) * pre * (1.0 - t * t) * (
                1.0 + (3 * 0.044715) * square
            )
            dpre_st[slot, :, cols] = (d_act * slope).astype(BF16)

        @pl.loop(0, model // wide)
        def _(i):
            cols = pl.ds(pl.multiple_of(i * wide, wide), wide)
            d_two = over(dpre_st[slot], we[cols, :], 1, 1).astype(BF16)
            keep[piece, :, cols] = d_two[:rows]
            give[slot, :, cols] = d_two[rows:]
            out = over(act_st[slot], wr[:, cols], 1, 0).astype(BF16)
            part_st[slot, :, cols] = out

        if host and turn < line.n - 1:
            gather.take(turn + 1)
        core_sends[piece] = core_copy(piece)
        core_sends[piece].start()
        mine, other = owner(piece)
        stores[turn] = []
        for half, index in enumerate((mine, other)):
            to = pl.ds(pl.multiple_of(index * rows, rows), rows)
            part = pl.ds(half * rows, rows)
            stores[turn].append(
                pltpu.make_async_copy(act_st.at[slot, part], act_ref.at[to], st_sem.at[0, slot, half])
            )
            stores[turn].append(
                pltpu.make_async_copy(dpre_st.at[slot, part], dpre_ref.at[to], st_sem.at[1, slot, half])
            )
            stores[turn].append(
                pltpu.make_async_copy(part_st.at[slot, part], part_ref.at[to], st_sem.at[2, slot, half])
            )
            stores[turn].append(
                pltpu.make_async_copy(seq.at[piece, part], seq_ref.at[to], seq_sem.at[piece, half])
            )
        for c in stores[turn]:
            c.start()
        if piece.bit_length() == levels:
            fold(piece)
    for level in range(levels - 2, -1, -1):
        for piece in range((1 << level), 2 << level):
            fold(piece)
    add_core(0)
    for level in range(levels):
        fold_copy(1 << level).wait_recv()

    @pl.loop(0, rows // 16)
    def _(i):
        part = pl.ds(pl.multiple_of(i * 16, 16), 16)
        total = keep[0, part].astype(F32)
        for level in range(levels):
            total = total + fold_in[(1 << level) - 1, part].astype(F32)
        sum_ref[part] = total

    if host:
        for step in range(count + 1, line.n):
            gather.take(step)
        gather.finish()
    for s in sends:
        s.wait_send()
    for turn in range(max(0, count - 2), count):
        for c in stores[turn]:
            c.wait()
        core_sends[order[turn]].wait_send()
    for s in folds.values():
        s.wait_send()


def ffn(n2, dy_all, we, wr, bias_e, own=None):
    host = own is not None
    n = lax.axis_size("tensor")
    rows, model = n2.shape
    units = wr.shape[0]
    dp = lax.axis_size("dp")
    count = dp // 2
    dma, anywhere, vmem = DMA, ANY, VMEM
    operands = [n2, dy_all, we, wr, bias_e] + [own] * host
    lines = [jax.ShapeDtypeStruct((n * rows, model), BF16)] * host
    flops = 36 * dp * rows * model * units
    return pl.pallas_call(
        functools.partial(ffn_kernel, host),
        out_shape=(
            jax.ShapeDtypeStruct((rows, model), F32),
            jax.ShapeDtypeStruct((dp * rows, model), BF16),
            jax.ShapeDtypeStruct((dp * rows, units), BF16),
            jax.ShapeDtypeStruct((dp * rows, units), BF16),
            jax.ShapeDtypeStruct((dp * rows, model), BF16),
            *lines,
        ),
        in_specs=[anywhere, anywhere, anywhere, anywhere, vmem] + [anywhere] * host,
        out_specs=(vmem, anywhere, anywhere, anywhere, anywhere) + (anywhere,) * host,
        scratch_shapes=[
            pltpu.VMEM((model, units), BF16),
            pltpu.VMEM((units, model), BF16),
            pltpu.VMEM((count, 2 * rows, model), BF16),
            pltpu.VMEM((2, 2 * rows, model), BF16),
            pltpu.VMEM((2, 2 * rows, units), BF16),
            pltpu.VMEM((2, 2 * rows, units), BF16),
            pltpu.VMEM((2, 2 * rows, model), BF16),
            pltpu.VMEM((count, rows, model), BF16),
            pltpu.VMEM((2, rows, model), BF16),
            pltpu.VMEM((count, rows, model), BF16),
            pltpu.VMEM((count - 1, rows, model), BF16),
            dma((n + 1,)), dma, dma((2, 2)), dma((count, 2)), dma((3, 2, 2)),
            dma((count,)), dma((count,)), dma((count,)), dma((count,)),
            dma((count,)), dma((count,)), dma((count - 1,)), dma((count - 1,)),
        ]
        + (LineGather.sems(n) if host else []),
        compiler_params=pltpu.CompilerParams(
            collective_id=2 if host else 1, has_side_effects=True, vmem_limit_bytes=62 << 20
        ),
        cost_estimate=pl.CostEstimate(
            flops=flops, bytes_accessed=8 * dp * rows * (model + units), transcendentals=dp * rows * units
        ),
        name="ffn_plane",
    )(*operands)


def body(
    tokens,
    parents,
    cotangent,
    first_gain,
    first_shift,
    w_query,
    b_query,
    w_key,
    w_value,
    b_value,
    w_out,
    b_out,
    second_gain,
    second_shift,
    w_expand,
    b_expand,
    w_reduce,
    b_reduce,
):
    dp = lax.axis_size("dp")
    tn = lax.axis_size("tensor")
    dp_me = lax.axis_index("dp")
    tn_me = lax.axis_index("tensor")
    width = w_query.shape[1]
    model = w_query.shape[0] * dp
    units = w_expand.shape[1]
    mine = units // dp
    micros = range(tokens.shape[0])
    last = tokens.shape[0] - 1
    x_low = [tokens[m, 0] for m in micros]
    dy_low = [cotangent[m, 0] for m in micros]
    rows_here = x_low[0].shape[0]
    total = rows_here * tn

    cut = first_gain.shape[0]
    bq_rows, bq_cols = b_query.shape
    be_rows, be_cols = b_expand.shape
    small = jnp.concatenate(
        [first_gain, first_shift, b_out, second_gain, second_shift, b_reduce]
        + [b_query.reshape(-1), b_value.reshape(-1), b_expand.reshape(-1)]
    )
    used = small.shape[0]
    small = jnp.pad(small, (0, -used % 2048)).reshape(-1, 128)
    w_attn = jnp.concatenate([w_query, w_key, w_value, w_out.T], axis=1)
    seq_x0, w_attn, w_e, w_r, small = front(x_low[0], w_attn, w_expand, w_reduce, small)
    w_qkv = w_attn[:, : 3 * width]
    w_ot = w_attn[:, 3 * width :]
    small = small.reshape(dp, -1)[:, :used]
    gain_one, shift_one, bias_out, gain_two, shift_two, bias_red = [
        small[:, i * cut : (i + 1) * cut].reshape(1, model).astype(F32) for i in range(6)
    ]
    at = 6 * cut
    bias_qkv = []
    for i in range(2):
        part = small[:, at : at + bq_rows * bq_cols].reshape(dp, bq_rows, bq_cols)
        bias_qkv.append(part.transpose(1, 0, 2).reshape(1, width).astype(F32))
        at += bq_rows * bq_cols
    bias_qkv = jnp.concatenate([bias_qkv[0], jnp.zeros((1, width), F32), bias_qkv[1]], 1)
    bias_e = small[:, at:].reshape(dp, dp, be_rows // dp, be_cols)
    bias_e = lax.dynamic_index_in_dim(bias_e, dp_me, 1, keepdims=False)
    bias_e = lax.all_gather(bias_e.transpose(1, 0, 2).reshape(1, mine), "tensor", axis=1, tiled=True)
    bias_e = bias_e.astype(F32)

    seq_grad = [lax.all_gather(dy_low[0], "dp", axis=0, tiled=True)]
    seq_x = [seq_x0]
    for m in micros[1:]:
        seq_x.append(lax.all_gather(after(x_low[m], seq_x0, seq_grad[0]), "tensor", axis=0, tiled=True))

    normal_one, seq_one, qkv, attended, hidden, normed_two = [], [], [], [], [], []
    for m in micros:
        normal_one.append(layer_norm(seq_x[m].astype(F32), 1.0, 0.0))
        seq_one.append((normal_one[m] * gain_one + shift_one).astype(BF16))
        qkv.append(
            (jnp.dot(seq_one[m], w_qkv, preferred_element_type=F32) + bias_qkv).astype(BF16)
        )
        attended.append(attend(parents[m, 0], qkv[m], width))
        if m == 0:
            side = 0 if mine % 128 == 0 else 1
            w_e = lax.all_gather(after(w_e, qkv[m]), "tensor", axis=side, tiled=True)
            w_r = lax.all_gather(after(w_r, attended[m]), "tensor", axis=0, tiled=True)
        else:
            seq_grad.append(lax.all_gather(after(dy_low[m], attended[m]), "dp", axis=0, tiled=True))
        branch = all_sums([over(attended[m], w_ot, 1, 1).astype(BF16)], [], [], 3)[0]
        hidden.append(x_low[m].astype(F32) + (branch + bias_out))
        normed_two.append(layer_norm(hidden[m], gain_two, shift_two).astype(BF16))

    out_part, seq_two, activated, d_pre, d_hidden, d_branch, seq_branch = [], [], [], [], [], [], []
    g_gain_two = g_shift_two = g_bias_red = g_bias_out = g_bias_e = 0.0
    for m in micros:
        own = d_branch[m - 1] if m else None
        d_two, seq, act, dpre, part, *line = ffn(normed_two[m], seq_grad[m], w_e, w_r, bias_e, own)
        seq_branch += line
        seq_two.append(seq)
        activated.append(act)
        d_pre.append(dpre)
        out_part.append(part)
        grad32 = dy_low[m].astype(F32)
        norm_value, norm_pull = jax.vjp(layer_norm, hidden[m], gain_two, shift_two)
        d_norm, g_gain, g_shift = norm_pull(d_two)
        d_hidden.append(grad32 + d_norm)
        d_branch.append(d_hidden[m].astype(BF16))
        g_gain_two = g_gain_two + g_gain
        g_shift_two = g_shift_two + g_shift
        g_bias_red = g_bias_red + jnp.sum(grad32, 0, keepdims=True)
        g_bias_out = g_bias_out + jnp.sum(d_branch[m].astype(F32), 0, keepdims=True)
        g_bias_e = g_bias_e + jnp.sum(dpre.astype(F32), 0)

    def outer(left, right):
        out = None
        for a, b in zip(left, right):
            term = over(a, b, 0, 0)
            out = term if out is None else out + term
        return out.astype(BF16)

    g_r = outer(activated, seq_grad)
    g_r_sum = lax.psum_scatter(g_r, "tensor", scatter_dimension=0, tiled=True)

    d_qkv, d_one = [], []
    g_gain_one = g_shift_one = g_bias_qkv = 0.0
    for m in micros:
        d_att = jnp.dot(seq_branch[m], w_ot, preferred_element_type=F32).astype(BF16)
        if m < last:
            d_att = after(d_att, g_r)
            d, full = attend_back(parents[m, 0], qkv[m], d_att, width, d_branch[m + 1])
            seq_branch.append(full)
        else:
            g_et = outer(d_pre, seq_two)
            g_et_sum = lax.psum_scatter(g_et, "tensor", scatter_dimension=0, tiled=True)
            d_att = after(d_att, g_et)
            d = attend_back(parents[m, 0], qkv[m], d_att, width)
        d_qkv.append(d)
        g_bias_qkv = g_bias_qkv + jnp.sum(d.astype(F32), 0)
        d_one.append(over(d, w_qkv, 1, 1).astype(BF16))
        part = d_one[m].astype(F32)
        g_gain_one = g_gain_one + jnp.sum(part * normal_one[m], 0, keepdims=True)
        g_shift_one = g_shift_one + jnp.sum(part, 0, keepdims=True)

    rows = jnp.concatenate(
        [g_gain_one, g_shift_one, g_bias_out, g_gain_two, g_shift_two, g_bias_red], 0
    )
    rows = rows.reshape(6, dp, cut).transpose(1, 0, 2).reshape(dp, 6 * cut)
    row_qv = jnp.concatenate([g_bias_qkv[:width], g_bias_qkv[2 * width :]])
    row_qv = row_qv.reshape(2 * bq_rows, dp, bq_cols).transpose(1, 0, 2)[:, None]
    row_qv = lax.dynamic_update_slice(
        jnp.zeros((dp, tn, 2 * bq_rows, bq_cols), F32), row_qv, (0, tn_me, 0, 0)
    ).reshape(dp, -1)
    row_e = g_bias_e.reshape(tn, be_rows // dp, dp, be_cols).transpose(2, 0, 1, 3)[:, :, None]
    row_e = lax.dynamic_update_slice(
        jnp.zeros((dp, tn, dp, be_rows // dp, be_cols), F32), row_e, (0, 0, dp_me, 0, 0)
    ).reshape(dp, -1)
    little = jnp.concatenate([rows, row_qv, row_e], 1)
    little = jnp.pad(little, ((0, 0), (0, -little.shape[1] % 1024))).reshape(dp, -1, 128)

    g_ffn = jnp.stack([g_et_sum, g_r_sum], 0)
    g_ffn = lax.all_to_all(g_ffn, "dp", split_axis=2, concat_axis=1, tiled=True).astype(F32)
    g_expand = g_ffn[0].T
    g_reduce = g_ffn[1]

    g_attn = jnp.concatenate([outer(seq_one, d_qkv), outer(seq_branch, attended)], axis=1)
    out_sum = [
        lax.psum_scatter(after(part, d_qkv[last]), "dp", scatter_dimension=0, tiled=True).astype(F32)
        for part in out_part[:last]
    ]
    sums = all_sums(d_one, [g_attn, out_part[last]], [little], 5)
    d_one, (g_attn, out_last, little) = sums[: last + 1], sums[last + 1 :]
    out_sum.append(out_last)
    layer_out = [(hidden[m] + (out_sum[m] + bias_red)).astype(BF16) for m in micros]
    little = little.reshape(-1)
    six = little[: 6 * cut].reshape(6, cut)
    at = 6 * cut
    g_bqv = little[at : at + tn * 2 * bq_rows * bq_cols].reshape(tn, 2 * bq_rows, bq_cols)
    g_bqv = lax.dynamic_index_in_dim(g_bqv, tn_me, 0, keepdims=False)
    g_bq, g_bv = g_bqv[:bq_rows], g_bqv[bq_rows:]
    at += tn * 2 * bq_rows * bq_cols
    g_be = little[at : at + tn * be_rows * be_cols].reshape(tn, be_rows, be_cols)
    g_be = lax.dynamic_index_in_dim(g_be, tn_me, 0, keepdims=False)
    g_query, g_key, g_value = [g_attn[:, i * width : (i + 1) * width] for i in range(3)]
    g_out = g_attn[:, 3 * width :].T
    input_grad = []
    for m in micros:
        first_value, first_pull = jax.vjp(
            lambda rows: layer_norm(rows, gain_one, shift_one), x_low[m].astype(F32)
        )
        input_grad.append((d_hidden[m] + first_pull(d_one[m])[0]).astype(BF16))

    return (
        jnp.stack(layer_out, 0)[:, None],
        jnp.stack(input_grad, 0)[:, None],
        six[0],
        six[1],
        g_query,
        g_bq,
        g_key,
        g_value,
        g_bv,
        g_out,
        six[2],
        six[3],
        six[4],
        g_expand,
        g_be,
        g_reduce,
        six[5],
    )


def solution(mesh):
    in_specs = (
        P(None, "dp", "tensor", None),
        P(None, "dp", None),
        P(None, "dp", "tensor", None),
        P("dp"),
        P("dp"),
        P("dp", "tensor"),
        P("tensor", "dp"),
        P("dp", "tensor"),
        P("dp", "tensor"),
        P("tensor", "dp"),
        P("tensor", "dp"),
        P("dp"),
        P("dp"),
        P("dp"),
        P("dp", "tensor"),
        P("tensor", "dp"),
        P("tensor", "dp"),
        P("dp"),
    )
    out_specs = (
        P(None, "dp", "tensor", None),
        P(None, "dp", "tensor", None),
        P("dp"),
        P("dp"),
        P("dp", "tensor"),
        P("tensor", "dp"),
        P("dp", "tensor"),
        P("dp", "tensor"),
        P("tensor", "dp"),
        P("tensor", "dp"),
        P("dp"),
        P("dp"),
        P("dp"),
        P("dp", "tensor"),
        P("tensor", "dp"),
        P("tensor", "dp"),
        P("dp"),
    )
    return jax.shard_map(body, mesh=mesh, in_specs=in_specs, out_specs=out_specs, check_vma=False)
```

```python
import functools
import math

import jax
import jax.numpy as jnp
from jax import lax
from jax.experimental import pallas as pl
from jax.experimental.pallas import tpu as pltpu
from jax.sharding import PartitionSpec as P

HEAD_DIM = 64
BLOCK = 256

F32 = jnp.float32
BF16 = jnp.bfloat16
MESH = pl.DeviceIdType.MESH
DMA = pltpu.SemaphoreType.DMA
GELU = math.sqrt(2.0 / math.pi)


def layer_norm(rows, gain, shift):
    center = rows - jnp.mean(rows, -1, keepdims=True)
    spread = jnp.mean(center * center, -1, keepdims=True)
    return center * lax.rsqrt(spread + 1e-05) * gain + shift


def after(value, *others):
    return lax.optimization_barrier((value,) + others)[0]


def over(left, right, on_left, on_right):
    return lax.dot_general(
        left, right, (((on_left,), (on_right,)), ((), ())), preferred_element_type=F32
    )


def window(index, rows):
    return pl.ds(pl.multiple_of(index * rows, rows), rows)


def remote(src, dst, send, recv, to):
    return pltpu.make_async_remote_copy(
        src_ref=src, dst_ref=dst, send_sem=send, recv_sem=recv,
        device_id=to, device_id_type=MESH,
    )


class Line:
    def __init__(self):
        self.n = lax.axis_size("tensor")
        self.me = lax.axis_index("tensor")
        self.dp = lax.axis_index("dp")

    def at(self, index):
        return (self.dp, index)

    def greet(self, barrier):
        @pl.when(self.me > 0)
        def _():
            pl.semaphore_signal(barrier, inc=1, device_id=self.at(self.me - 1), device_id_type=MESH)

        @pl.when(self.me < self.n - 1)
        def _():
            pl.semaphore_signal(barrier, inc=1, device_id=self.at(self.me + 1), device_id_type=MESH)

    def peers(self):
        return (self.me + self.n - 1) // self.n + (2 * self.n - 2 - self.me) // self.n


class LineGather:
    def __init__(self, line, own, full, sems):
        self.line, self.own, self.full = line, own, full
        self.rows = own.shape[0]
        self.local, self.up_send, self.up_recv, self.down_send, self.down_recv = sems

    @staticmethod
    def sems(n):
        return [DMA, DMA((n - 1,)), DMA((n - 1,)), DMA((n - 1,)), DMA((n - 1,))]

    def hop(self, step, up):
        line = self.line
        if up:
            shard, to = line.me - (step - 1), line.me + 1
            send, recv = self.up_send, self.up_recv
        else:
            shard, to = line.me + (step - 1), line.me - 1
            send, recv = self.down_send, self.down_recv
        there = self.full.at[window(shard, self.rows)]
        src = self.own if step == 1 else there
        return remote(src, there, send.at[step - 1], recv.at[step - 1], line.at(to))

    def sends(self, step, up):
        line = self.line
        if up:
            return (line.me < line.n - 1) & (line.me >= step - 1)
        return (line.me > 0) & (line.me + step - 1 < line.n)

    def takes(self, step, up):
        line = self.line
        return (line.me >= step) if up else (line.me + step < line.n)

    def send(self, step):
        for up in (True, False):
            @pl.when(self.sends(step, up))
            def _():
                self.hop(step, up).start()

    def start(self):
        self.place = pltpu.make_async_copy(
            self.own, self.full.at[window(self.line.me, self.rows)], self.local
        )
        self.place.start()
        self.send(1)

    def take(self, step):
        for up in (True, False):
            @pl.when(self.takes(step, up))
            def _():
                line = self.line
                shard = (line.me - step) if up else (line.me + step)
                here = self.full.at[window(shard, self.rows)]
                send, recv = (
                    (self.up_send, self.up_recv) if up else (self.down_send, self.down_recv)
                )
                remote(
                    here, here, send.at[step - 1], recv.at[step - 1], line.at(line.me)
                ).wait_recv()
        if step < self.line.n - 1:
            self.send(step + 1)

    def finish(self):
        for step in range(1, self.line.n):
            for up in (True, False):
                @pl.when(self.sends(step, up))
                def _():
                    self.hop(step, up).wait_send()
        pltpu.make_async_copy(
            self.own, self.full.at[window(self.line.me, self.rows)], self.local
        ).wait()


class LineScatter:
    def __init__(self, line, parts, out, scratch):
        self.line, self.parts, self.out = line, parts, out
        self.rows = out.shape[0]
        (self.own, self.sum, self.come, self.load, self.own_sem, self.send_sem, self.recv_sem) = scratch

    @staticmethod
    def scratch(n, rows, d):
        return [
            pltpu.VMEM((rows, d), BF16),
            pltpu.VMEM((2, n - 1, rows, d), BF16),
            pltpu.VMEM((2, n - 1, rows, d), BF16),
            DMA((2, n - 1)), DMA, DMA((2, n - 1)), DMA((2, n - 1)),
        ]

    def sends(self, step, up):
        line = self.line
        return (line.me <= step - 1) if up else (line.n - 1 - line.me <= step - 1)

    def load_of(self, step, up):
        line = self.line
        chunk = (line.me + line.n - step) if up else (line.me - line.n + step)
        way = 0 if up else 1
        return pltpu.make_async_copy(
            self.parts.at[window(chunk, self.rows)], self.sum.at[way, step - 1], self.load.at[way, step - 1]
        )

    def hop(self, step, up):
        line, way = self.line, 0 if up else 1
        return remote(
            self.sum.at[way, step - 1], self.come.at[way, step - 1],
            self.send_sem.at[way, step - 1], self.recv_sem.at[way, step - 1],
            line.at(line.me + 1 if up else line.me - 1),
        )

    def wait_from(self, step, up):
        line, way = self.line, 0 if up else 1
        remote(
            self.come.at[way, step - 1], self.come.at[way, step - 1],
            self.send_sem.at[way, step - 1], self.recv_sem.at[way, step - 1],
            line.at(line.me),
        ).wait_recv()

    def own_load(self):
        return pltpu.make_async_copy(
            self.parts.at[window(self.line.me, self.rows)], self.own, self.own_sem
        )

    def prepare(self):
        self.own_load().start()
        for step in range(1, self.line.n):
            for up in (True, False):
                @pl.when(self.sends(step, up))
                def _():
                    self.load_of(step, up).start()

    def step(self, step):
        line = self.line
        for up in (True, False):
            way = 0 if up else 1

            @pl.when(self.sends(step, up))
            def _():
                self.load_of(step, up).wait()
                if step > 1:
                    inner = (line.me > 0) if up else (line.me < line.n - 1)

                    @pl.when(inner)
                    def _():
                        self.wait_from(step - 1, up)

                        @pl.loop(0, self.rows // 16)
                        def _(i):
                            part = window(i, 16)
                            self.sum[way, step - 1, part] = (
                                self.sum[way, step - 1, part].astype(F32)
                                + self.come[way, step - 2, part].astype(F32)
                            ).astype(BF16)

                self.hop(step, up).start()

    def finish(self):
        line, n = self.line, self.line.n
        self.own_load().wait()

        @pl.loop(0, self.rows // 16)
        def _(i):
            part = window(i, 16)
            self.out[part] = self.own[part].astype(F32)

        for up in (True, False):
            way = 0 if up else 1

            @pl.when((line.me > 0) if up else (line.me < n - 1))
            def _():
                self.wait_from(n - 1, up)

                @pl.loop(0, self.rows // 16)
                def _(i):
                    part = window(i, 16)
                    self.out[part] += self.come[way, n - 2, part].astype(F32)

        for step in range(1, n):
            for up in (True, False):
                @pl.when(self.sends(step, up))
                def _():
                    self.hop(step, up).wait_send()


class Cube:
    def __init__(self):
        self.dp = lax.axis_size("dp")
        self.levels = levels = self.dp.bit_length() - 2
        self.count = 1 << levels
        self.me = me = lax.axis_index("dp")
        self.tensor = lax.axis_index("tensor")
        core = me % 2
        flips = []
        for bit in range(1, levels + 1):
            flips.append((1 << bit) * (1 - 2 * ((me // (1 << bit)) % 2)))
        self.steps = [
            flips[l] * (1 - core) + flips[levels - 1 - l] * core for l in range(levels)
        ]
        self.core_step = 1 - 2 * core

    def at(self, index):
        return (index, self.tensor)

    def owner(self, piece):
        mine, other = self.me, self.me + self.core_step
        for l in range(self.levels):
            if piece >> l & 1:
                mine = mine + self.steps[l]
                other = other + self.steps[self.levels - 1 - l]
        return mine, other

    def greet(self, barrier):
        for step in self.steps + [self.core_step]:
            pl.semaphore_signal(
                barrier, inc=1, device_id=self.at(self.me + step), device_id_type=MESH
            )

    def peers(self):
        return self.levels + 1


class CubeGather:
    def __init__(self, cube, own, full, sems):
        self.cube, self.own, self.full = cube, own, full
        self.rows = own.shape[0]
        self.local, self.send_sem, self.recv_sem, self.core_send, self.core_recv = sems
        self.arrived, self.sent = {0}, []

    @staticmethod
    def sems(count):
        return [DMA, DMA((count,)), DMA((count,)), DMA((count,)), DMA((count,))]

    def slot(self, index):
        return self.full.at[window(index, self.rows)]

    def src(self, piece):
        return self.own if piece == 0 else self.slot(self.cube.owner(piece)[0])

    def hop(self, piece, level):
        cube, there = self.cube, piece + (1 << level)
        return remote(
            self.src(piece), self.slot(cube.owner(piece)[0]),
            self.send_sem.at[there], self.recv_sem.at[there], cube.at(cube.me + cube.steps[level]),
        )

    def core(self, piece):
        cube = self.cube
        return remote(
            self.src(piece), self.slot(cube.owner(piece)[0]),
            self.core_send.at[piece], self.core_recv.at[piece], cube.at(cube.me + cube.core_step),
        )

    def give(self, piece):
        for level in range(piece.bit_length(), self.cube.levels):
            self.sent.append(self.hop(piece, level))
            self.sent[-1].start()
        self.sent.append(self.core(piece))
        self.sent[-1].start()

    def start(self):
        self.place = pltpu.make_async_copy(self.own, self.slot(self.cube.me), self.local)
        self.place.start()
        self.give(0)

    def take(self, piece):
        if piece in self.arrived:
            return
        here = self.slot(self.cube.owner(piece)[0])
        remote(
            here, here, self.send_sem.at[piece], self.recv_sem.at[piece], self.cube.at(self.cube.me)
        ).wait_recv()
        self.arrived.add(piece)
        self.give(piece)

    def take_core(self, piece):
        here = self.slot(self.cube.owner(piece)[1])
        remote(
            here, here, self.core_send.at[piece], self.core_recv.at[piece], self.cube.at(self.cube.me)
        ).wait_recv()

    def finish(self):
        for piece in range(self.cube.count):
            self.take(piece)
            self.take_core(piece)
        for copy in self.sent:
            copy.wait_send()
        self.place.wait()


class CubeScatter:
    def __init__(self, cube, parts, out, scratch):
        self.cube, self.parts, self.out = cube, parts, out
        self.rows = out.shape[0]
        (self.keep, self.core_in, self.fold_in, self.load_sem,
         self.core_send, self.core_recv, self.send_sem, self.recv_sem) = scratch

    @staticmethod
    def scratch(count, rows, d):
        return [
            pltpu.VMEM((count, rows, d), BF16),
            pltpu.VMEM((count, rows, d), BF16),
            pltpu.VMEM((count - 1, rows, d), BF16),
            DMA((count,)), DMA((count,)), DMA((count,)), DMA((count - 1,)), DMA((count - 1,)),
        ]

    def load(self, piece):
        return pltpu.make_async_copy(
            self.parts.at[window(self.cube.owner(piece)[0], self.rows)],
            self.keep.at[piece], self.load_sem.at[piece],
        )

    def core(self, piece):
        cube = self.cube
        return remote(
            self.parts.at[window(cube.owner(piece)[1], self.rows)], self.core_in.at[piece],
            self.core_send.at[piece], self.core_recv.at[piece], cube.at(cube.me + cube.core_step),
        )

    def hop(self, piece):
        cube, level = self.cube, piece.bit_length() - 1
        return remote(
            self.keep.at[piece], self.fold_in.at[piece - 1],
            self.send_sem.at[piece - 1], self.recv_sem.at[piece - 1],
            cube.at(cube.me + cube.steps[level]),
        )

    def order(self):
        return sorted(range(self.cube.count), key=lambda p: (-(p.bit_length()), p))

    def start(self):
        for piece in self.order():
            self.core(piece).start()
            self.load(piece).start()

    def add(self, piece, other):
        @pl.loop(0, self.rows // 16)
        def _(i):
            part = window(i, 16)
            self.keep[piece, part] = (
                self.keep[piece, part].astype(F32) + other[part].astype(F32)
            ).astype(BF16)

    def fold(self, piece):
        self.load(piece).wait()
        self.core(piece).wait_recv()
        self.add(piece, self.core_in.at[piece])
        for level in range(self.cube.levels - 1, piece.bit_length() - 1, -1):
            above = piece + (1 << level)
            self.hop(above).wait_recv()
            self.add(piece, self.fold_in.at[above - 1])
        if piece:
            self.hop(piece).start()

    def finish(self):
        self.fold(0)

        @pl.loop(0, self.rows // 16)
        def _(i):
            part = window(i, 16)
            self.out[part] = self.keep[0, part].astype(F32)

        for piece in range(self.cube.count):
            self.core(piece).wait_send()
            if piece:
                self.hop(piece).wait_send()


class CubeExchange:
    def __init__(self, cube, moves, sems):
        self.cube, self.moves = cube, moves
        self.send_sem, self.recv_sem, self.local = sems

    @staticmethod
    def sems(dp, moves):
        return [DMA((moves, dp)), DMA((moves, dp)), DMA((moves,))]

    def copies(self):
        cube = self.cube
        out = []
        for k in range(1, cube.dp):
            to = (cube.me + k) % cube.dp
            for m, (src, dst) in enumerate(self.moves):
                out.append(
                    remote(src(to), dst(cube.me), self.send_sem.at[m, k], self.recv_sem.at[m, k], cube.at(to))
                )
        return out

    def locals(self):
        return [
            pltpu.make_async_copy(src(self.cube.me), dst(self.cube.me), self.local.at[m])
            for m, (src, dst) in enumerate(self.moves)
        ]

    def start(self):
        for copy in self.copies() + self.locals():
            copy.start()

    def finish(self):
        cube = self.cube
        for copy in self.copies():
            copy.wait_send()
        for k in range(1, cube.dp):
            of = (cube.me - k + cube.dp) % cube.dp
            for m, (src, dst) in enumerate(self.moves):
                here = dst(of)
                remote(here, here, self.send_sem.at[m, k], self.recv_sem.at[m, k], cube.at(of)).wait_recv()
        for copy in self.locals():
            copy.wait()


ANY = pl.BlockSpec(memory_space=pl.ANY)
VMEM = pl.BlockSpec(memory_space=pltpu.VMEM)


def front_kernel(x_ref, w_ref, we_ref, wr_ref, small_ref, seq_ref, w_out, we_out, wr_out, small_out, *sems):
    line, cube = Line(), Cube()
    gather = LineGather(line, x_ref, seq_ref, sems[:5])
    weights = CubeGather(cube, w_ref, w_out, sems[5:10])
    mine = wr_out.shape[0]
    rows, cols = we_ref.shape[0], wr_ref.shape[1]
    tile = small_ref.shape[0]
    moves = [
        (lambda d: small_ref, lambda d: small_out.at[window(d, tile)]),
        (lambda d: wr_ref.at[window(d, mine)], lambda d: wr_out.at[:, window(d, cols)]),
        (lambda d: we_ref.at[:, window(d, mine)], lambda d: we_out.at[window(d, rows)]),
    ]
    swap = CubeExchange(cube, moves if mine % 128 == 0 else moves[:2], sems[10:13])
    barrier = pltpu.get_barrier_semaphore()
    line.greet(barrier)
    for k in range(1, cube.dp):
        pl.semaphore_signal(
            barrier, inc=1, device_id=cube.at((cube.me + k) % cube.dp), device_id_type=MESH
        )
    pl.semaphore_wait(barrier, cube.dp - 1 + line.peers())
    gather.start()
    weights.start()
    gather.take(1)
    for piece in range(1, cube.count):
        if piece.bit_length() < cube.levels:
            weights.take(piece)
    swap.start()
    gather.take(2)
    for piece in range(1, cube.count):
        weights.take(piece)
    for step in range(3, line.n):
        gather.take(step)
    weights.finish()
    swap.finish()
    gather.finish()


def front(x, w, w_e, w_r, small):
    dp, n = lax.axis_size("dp"), lax.axis_size("tensor")
    rows, model = x.shape
    outs = pl.pallas_call(
        front_kernel,
        out_shape=(
            jax.ShapeDtypeStruct((n * rows, model), BF16),
            jax.ShapeDtypeStruct((dp * w.shape[0], w.shape[1]), BF16),
            jax.ShapeDtypeStruct((dp * w_e.shape[0], w_e.shape[1] // dp), BF16),
            jax.ShapeDtypeStruct((w_r.shape[0] // dp, w_r.shape[1] * dp), BF16),
            jax.ShapeDtypeStruct((dp * small.shape[0], small.shape[1]), BF16),
        ),
        in_specs=[ANY] * 5,
        out_specs=(ANY,) * 5,
        scratch_shapes=LineGather.sems(n) + CubeGather.sems(dp // 2) + CubeExchange.sems(dp, 3),
        compiler_params=pltpu.CompilerParams(collective_id=0, has_side_effects=True),
        cost_estimate=pl.CostEstimate(flops=80 * 10**9, bytes_accessed=10**7, transcendentals=0),
        name="front",
    )(x, w, w_e, w_r, small)
    seq, w_all, e_all, r_all, small_all = outs
    if r_all.shape[0] % 128:
        e_all = lax.all_to_all(w_e, "dp", split_axis=1, concat_axis=0, tiled=True)
    return seq, w_all, e_all, r_all, small_all


class SmallSum:
    def __init__(self, line, cube, parts, out, scratch):
        self.line, self.cube, self.parts, self.out = line, cube, parts, out
        self.come, self.gather, self.sems, self.line_send, self.line_recv = (
            scratch[0], scratch[1], scratch[2:5], scratch[5], scratch[6]
        )
        moves = [(lambda d: parts.at[d], lambda d: self.come.at[d])]
        self.swap = CubeExchange(cube, moves, self.sems)

    @staticmethod
    def scratch(dp, n, rows, d):
        return [
            pltpu.VMEM((dp, rows, d), F32),
            pltpu.VMEM((n, rows, d), F32),
            *CubeExchange.sems(dp, 1),
            DMA((n,)), DMA((n,)),
        ]

    def hop(self, k):
        line = self.line
        here = self.gather.at[line.me]
        return remote(
            here, here, self.line_send.at[k], self.line_recv.at[k], line.at((line.me + k) % line.n)
        )

    def middle(self):
        self.swap.finish()
        total = self.come[0]
        for d in range(1, self.cube.dp):
            total = total + self.come[d]
        self.gather[self.line.me] = total
        for k in range(1, self.line.n):
            self.hop(k).start()

    def finish(self):
        line = self.line
        for k in range(1, line.n):
            here = self.gather.at[(line.me - k + line.n) % line.n]
            remote(
                here, here, self.line_send.at[k], self.line_recv.at[k], line.at(line.me)
            ).wait_recv()
            self.hop(k).wait_send()
        total = self.gather[0]
        for z in range(1, line.n):
            total = total + self.gather[z]
        self.out[...] = total


def sum_kernel(counts, *refs):
    lines, planes, gathers, swaps, small = counts
    line, cube = Line(), Cube()
    count = sum(counts)
    ins, outs, scratch = refs[:count], refs[count : 2 * count], list(refs[2 * count :])

    def take(number):
        taken = tuple(scratch[:number])
        del scratch[:number]
        return taken

    pairs = list(zip(ins, outs))
    sums = [LineScatter(line, *pairs.pop(0), take(7)) for _ in range(lines)]
    folds = [CubeScatter(cube, *pairs.pop(0), take(8)) for _ in range(planes)]
    lanes = [LineGather(line, *pairs.pop(0), take(5)) for _ in range(gathers)]
    moves = []
    for _ in range(swaps):
        src, dst = pairs.pop(0)
        rows, cols = src.shape[0], dst.shape[1]
        moves.append(
            (
                lambda d, src=src, cols=cols: src.at[:, window(d, cols)],
                lambda d, dst=dst, rows=rows: dst.at[window(d, rows)],
            )
        )
    swap = CubeExchange(cube, moves, take(3)) if swaps else None
    little = SmallSum(line, cube, *pairs.pop(0), take(7)) if small else None
    barrier = pltpu.get_barrier_semaphore()
    peers = 0
    if small:
        for k in range(1, line.n):
            pl.semaphore_signal(
                barrier, inc=1, device_id=line.at((line.me + k) % line.n), device_id_type=MESH
            )
        peers = line.n - 1
    elif lines or gathers:
        line.greet(barrier)
        peers = line.peers()
    if small or swaps:
        for k in range(1, cube.dp):
            pl.semaphore_signal(
                barrier, inc=1, device_id=cube.at((cube.me + k) % cube.dp), device_id_type=MESH
            )
        peers = peers + cube.dp - 1
    elif planes:
        cube.greet(barrier)
        peers = peers + cube.peers()
    for s in sums:
        s.prepare()
    pl.semaphore_wait(barrier, peers)
    if small:
        little.swap.start()
    for lane in lanes:
        lane.start()
    pieces = [p for p in folds[0].order() if p] if planes else []
    per = -(-len(pieces) // (line.n - 1))
    for step in range(1, line.n):
        for s in sums:
            s.step(step)
        if step > 1:
            for lane in lanes:
                lane.take(step - 1)
        if step == 1:
            for f in folds:
                f.start()
            if small:
                little.middle()
        for piece in pieces[:per]:
            for f in folds:
                f.fold(piece)
        pieces = pieces[per:]
        if step == 1 and swaps:
            swap.start()
    for f in folds:
        f.finish()
    for lane in lanes:
        lane.take(line.n - 1)
        lane.finish()
    for s in sums:
        s.finish()
    if swaps:
        swap.finish()
    if small:
        little.finish()


def exchange(collective_id, lines=(), planes=(), gathers=(), swaps=(), small=()):
    dp, n = lax.axis_size("dp"), lax.axis_size("tensor")
    out_shape, out_specs, scratch = [], [], []
    for part in lines:
        rows, d = part.shape[0] // n, part.shape[1]
        out_shape.append(jax.ShapeDtypeStruct((rows, d), F32))
        out_specs.append(VMEM)
        scratch += LineScatter.scratch(n, rows, d)
    for part in planes:
        rows, d = part.shape[0] // dp, part.shape[1]
        out_shape.append(jax.ShapeDtypeStruct((rows, d), F32))
        out_specs.append(VMEM)
        scratch += CubeScatter.scratch(dp // 2, rows, d)
    for part in gathers:
        rows, d = part.shape
        out_shape.append(jax.ShapeDtypeStruct((n * rows, d), BF16))
        out_specs.append(ANY)
        scratch += LineGather.sems(n)
    for part in swaps:
        rows, d = part.shape
        out_shape.append(jax.ShapeDtypeStruct((dp * rows, d // dp), BF16))
        out_specs.append(ANY)
    if swaps:
        scratch += CubeExchange.sems(dp, len(swaps))
    for part in small:
        rows, d = part.shape[1:]
        out_shape.append(jax.ShapeDtypeStruct((rows, d), F32))
        out_specs.append(VMEM)
        scratch += SmallSum.scratch(dp, n, rows, d)
    counts = tuple(len(g) for g in (lines, planes, gathers, swaps, small))
    operands = [part for group in (lines, planes, gathers, swaps, small) for part in group]
    return pl.pallas_call(
        functools.partial(sum_kernel, counts),
        out_shape=tuple(out_shape),
        in_specs=[ANY] * len(operands),
        out_specs=tuple(out_specs),
        scratch_shapes=scratch,
        compiler_params=pltpu.CompilerParams(
            collective_id=collective_id, has_side_effects=True, vmem_limit_bytes=60 << 20
        ),
        cost_estimate=pl.CostEstimate(flops=80 * 10**9, bytes_accessed=10**7, transcendentals=0),
        name="exchange",
    )(*operands)


PAIR = 2 * HEAD_DIM
NEVER = -1e30


def lane_of(shape, head):
    lane = lax.broadcasted_iota(jnp.int32, shape, 1)
    return (lane < HEAD_DIM) if head == 0 else (lane >= HEAD_DIM)


def sight(parents_ref, row, col):
    at = jnp.int32(row)
    seen = at == col
    for hop in range(row - col):
        at = parents_ref[at]
        seen = seen | (at == col)
    return jnp.where(seen, 0.0, NEVER).astype(F32)


def masked_scores(parents_ref, q_head, k_ref, row):
    scores = []
    for col in range(row + 1):
        part = over(q_head, k_ref[col * BLOCK : (col + 1) * BLOCK, :], 1, 1)
        if col == row:
            below = lax.broadcasted_iota(jnp.int32, part.shape, 1) <= lax.broadcasted_iota(
                jnp.int32, part.shape, 0
            )
            part = jnp.where(below, part, NEVER)
        else:
            part = part + sight(parents_ref, row, col)
        scores.append(part)
    return scores


def row_reduce(parts, fold, reduce):
    return reduce(functools.reduce(fold, parts), axis=-1, keepdims=True)


def attend_kernel(parents_ref, q_ref, k_ref, v_ref, out_ref):
    blocks = q_ref.shape[0] // BLOCK
    scale = 1.0 / math.sqrt(HEAD_DIM)
    for row in range(blocks):
        here = slice(row * BLOCK, (row + 1) * BLOCK)
        heads = []
        for head in range(2):
            q_head = q_ref[here, :].astype(F32) * scale
            q_head = jnp.where(lane_of(q_head.shape, head), q_head, 0.0).astype(BF16)
            scores = masked_scores(parents_ref, q_head, k_ref, row)
            top = row_reduce(scores, jnp.maximum, jnp.max)
            probs = [jnp.exp(s - top) for s in scores]
            total = row_reduce(probs, jnp.add, jnp.sum)
            out = None
            for col in range(row + 1):
                term = over(
                    probs[col].astype(BF16), v_ref[col * BLOCK : (col + 1) * BLOCK, :], 1, 0
                )
                out = term if out is None else out + term
            heads.append(out / total)
        mixed = jnp.where(lane_of(heads[0].shape, 0), heads[0], heads[1])
        out_ref[here, :] = mixed.astype(out_ref.dtype)


def attend(parents, qkv, width):
    rows = qkv.shape[0]
    pairs = width // PAIR
    spec = lambda part: pl.BlockSpec((rows, PAIR), lambda p, parents: (0, part * pairs + p))
    blocks = rows // BLOCK
    work = pairs * 2 * (blocks * (blocks + 1) // 2) * BLOCK * BLOCK
    return pl.pallas_call(
        attend_kernel,
        out_shape=jax.ShapeDtypeStruct((rows, width), BF16),
        grid_spec=pltpu.PrefetchScalarGridSpec(
            num_scalar_prefetch=1,
            grid=(pairs,),
            in_specs=[spec(0), spec(1), spec(2)],
            out_specs=pl.BlockSpec((rows, PAIR), lambda p, parents: (0, p)),
        ),
        compiler_params=pltpu.CompilerParams(vmem_limit_bytes=48 << 20),
        cost_estimate=pl.CostEstimate(
            flops=work * PAIR * 24, bytes_accessed=rows * width * 8, transcendentals=work
        ),
        name="attend",
    )(parents, qkv, qkv, qkv)


def attend_back_kernel(parents_ref, q_ref, k_ref, v_ref, g_ref, out_ref, dq_s, dk_s, dv_s):
    part = pl.program_id(1)
    blocks = q_ref.shape[0] // BLOCK
    scale = 1.0 / math.sqrt(HEAD_DIM)

    @pl.when(part == 0)
    def _():
        for row in range(blocks):
            here = slice(row * BLOCK, (row + 1) * BLOCK)
            dq_heads = []
            for head in range(2):
                lanes = lane_of((BLOCK, PAIR), head)
                q_head = jnp.where(lanes, q_ref[here, :].astype(F32) * scale, 0.0).astype(BF16)
                g_head = jnp.where(lanes, g_ref[here, :].astype(F32), 0.0).astype(BF16)
                scores = masked_scores(parents_ref, q_head, k_ref, row)
                top = row_reduce(scores, jnp.maximum, jnp.max)
                probs = [jnp.exp(s - top) for s in scores]
                rest = 1.0 / row_reduce(probs, jnp.add, jnp.sum)
                probs = [p * rest for p in probs]
                d_probs = [
                    over(g_head, v_ref[col * BLOCK : (col + 1) * BLOCK, :], 1, 1)
                    for col in range(row + 1)
                ]
                level = row_reduce([p * d for p, d in zip(probs, d_probs)], jnp.add, jnp.sum)
                dq = None
                for col in range(row + 1):
                    there = slice(col * BLOCK, (col + 1) * BLOCK)
                    d_scores = (probs[col] * (d_probs[col] - level)).astype(BF16)
                    term = over(d_scores, k_ref[there, :], 1, 0)
                    dq = term if dq is None else dq + term
                    dk = over(d_scores, q_head, 0, 0)
                    dv = over(probs[col].astype(BF16), g_head, 0, 0)
                    if row == col and head == 0:
                        dk_s[there, :] = dk
                        dv_s[there, :] = dv
                    else:
                        dk_s[there, :] += dk
                        dv_s[there, :] += dv
                dq_heads.append(dq * scale)
            dq_s[here, :] = jnp.where(lane_of((BLOCK, PAIR), 0), dq_heads[0], dq_heads[1]).astype(
                BF16
            )
        out_ref[...] = dq_s[...]

    @pl.when(part == 1)
    def _():
        out_ref[...] = dk_s[...].astype(BF16)

    @pl.when(part == 2)
    def _():
        out_ref[...] = dv_s[...].astype(BF16)


def attend_back(parents, qkv, grad, width):
    rows = qkv.shape[0]
    pairs = width // PAIR
    spec = lambda part: pl.BlockSpec((rows, PAIR), lambda p, c, parents: (0, part * pairs + p))
    blocks = rows // BLOCK
    work = pairs * 2 * (blocks * (blocks + 1) // 2) * BLOCK * BLOCK
    return pl.pallas_call(
        attend_back_kernel,
        out_shape=jax.ShapeDtypeStruct((rows, 3 * width), BF16),
        grid_spec=pltpu.PrefetchScalarGridSpec(
            num_scalar_prefetch=1,
            grid=(pairs, 3),
            in_specs=[
                spec(0),
                spec(1),
                spec(2),
                pl.BlockSpec((rows, PAIR), lambda p, c, parents: (0, p)),
            ],
            out_specs=pl.BlockSpec((rows, PAIR), lambda p, c, parents: (0, c * pairs + p)),
            scratch_shapes=[
                pltpu.VMEM((rows, PAIR), BF16),
                pltpu.VMEM((rows, PAIR), F32),
                pltpu.VMEM((rows, PAIR), F32),
            ],
        ),
        compiler_params=pltpu.CompilerParams(vmem_limit_bytes=48 << 20),
        cost_estimate=pl.CostEstimate(
            flops=work * PAIR * 60, bytes_accessed=rows * width * 14, transcendentals=work
        ),
        name="attend_back",
    )(parents, qkv, qkv, qkv, grad)


def ffn_kernel(host, n2_ref, dy_ref, we_ref, wr_ref, be_ref, *refs):
    if host:
        line_own, refs = refs[0], refs[1:]
    sum_ref, seq_ref, act_ref, dpre_ref, part_ref = refs[:5]
    refs = refs[5:]
    if host:
        line_full, refs = refs[0], refs[1:]
    we, wr, seq, dy_st, act_st, dpre_st, part_st, keep, give, core_in, fold_in = refs[:11]
    refs = refs[1:]
    w_sem, own_sem, dy_sem, seq_sem, st_sem = refs[10:15]
    ag_send, ag_recv, agc_send, agc_recv, rsc_send, rsc_recv, fold_send, fold_recv = refs[15:23]
    cube = Cube()
    levels, me, steps, core_step = cube.levels, cube.me, cube.steps, cube.core_step
    count, at, owner = cube.count, cube.at, cube.owner
    rows, model = n2_ref.shape
    units = wr_ref.shape[0]
    barrier = pltpu.get_barrier_semaphore()
    cube.greet(barrier)
    hosted = []
    if host:
        line = Line()
        line.greet(barrier)
        aside = LineScatter(line, line_own, line_full, refs[23:])
        aside.prepare()
    load_own = pltpu.make_async_copy(n2_ref, seq.at[0, pl.ds(0, rows)], own_sem)
    load_own.start()
    parts = we_ref.shape[0] // model
    mine_units = we_ref.shape[1]
    loads_w = [pltpu.make_async_copy(wr_ref, wr, w_sem.at[parts])]
    for part in range(parts):
        loads_w.append(
            pltpu.make_async_copy(
                we_ref.at[pl.ds(part * model, model)],
                we.at[:, pl.ds(part * mine_units, mine_units)],
                w_sem.at[part],
            )
        )
    for c in loads_w:
        c.start()

    def load_dy(piece, slot):
        mine, other = owner(piece)
        out = []
        for half, index in enumerate((mine, other)):
            out.append(
                pltpu.make_async_copy(
                    dy_ref.at[pl.ds(pl.multiple_of(index * rows, rows), rows)],
                    dy_st.at[slot, pl.ds(half * rows, rows)],
                    dy_sem.at[slot, half],
                )
            )
        return out

    def gather_copy(piece, level):
        there = piece + (1 << level)
        return remote(
            seq.at[piece, pl.ds(0, rows)], seq.at[there, pl.ds(0, rows)],
            ag_send.at[there], ag_recv.at[there], at(me + steps[level]),
        )

    def gather_core(piece):
        return remote(
            seq.at[piece, pl.ds(0, rows)], seq.at[piece, pl.ds(rows, rows)],
            agc_send.at[piece], agc_recv.at[piece], at(me + core_step),
        )

    order = [0] + sorted(range(1, count), key=lambda p: (-(p.bit_length()), p))
    slots = {piece: i % 2 for i, piece in enumerate(order)}
    loads = {order[0]: load_dy(order[0], 0)}
    for c in loads[order[0]]:
        c.start()

    load_own.wait()
    pl.semaphore_wait(barrier, cube.peers() + (line.peers() if host else 0))
    if host:
        aside.step(1)
    sends = []
    for level in range(levels):
        sends.append(gather_copy(0, level))
        sends[-1].start()
    sends.append(gather_core(0))
    sends[-1].start()
    for c in loads_w:
        c.wait()

    arrived = {0}

    def take(piece):
        if piece in arrived:
            return
        low = piece - (1 << (piece.bit_length() - 1))
        gather_copy(low, piece.bit_length() - 1).wait_recv()
        arrived.add(piece)
        for level in range(piece.bit_length(), levels):
            sends.append(gather_copy(piece, level))
            sends[-1].start()
        sends.append(gather_core(piece))
        sends[-1].start()

    stores = {}
    outs = {}
    core_sends = {}
    folds = {}
    done_core = set()

    def add(piece, other):
        @pl.loop(0, rows // 16)
        def _(i):
            part = pl.ds(pl.multiple_of(i * 16, 16), 16)
            keep[piece, part] = (
                keep[piece, part].astype(F32) + other[part].astype(F32)
            ).astype(BF16)

    def add_core(piece):
        if piece in done_core:
            return
        core_copy(piece).wait_recv()
        add(piece, core_in.at[piece])
        done_core.add(piece)

    def core_copy(piece):
        return remote(
            give.at[slots[piece]], core_in.at[piece],
            rsc_send.at[piece], rsc_recv.at[piece], at(me + core_step),
        )

    def fold_copy(piece):
        level = piece.bit_length() - 1
        low = piece - (1 << level)
        return remote(
            keep.at[piece], fold_in.at[piece - 1],
            fold_send.at[piece - 1], fold_recv.at[piece - 1], at(me + steps[level]),
        )

    def fold(piece):
        add_core(piece)
        for level in range(levels - 1, piece.bit_length() - 1, -1):
            above = piece + (1 << level)
            fold_copy(above).wait_recv()
            add(piece, fold_in.at[above - 1])
        if piece:
            folds[piece] = fold_copy(piece)
            folds[piece].start()

    chunk = 256
    wide = 512
    for turn, piece in enumerate(order):
        slot = turn % 2
        for earlier in range(1, piece + 1):
            take(earlier)
        gather_core(piece).wait_recv()
        for c in loads[piece]:
            c.wait()
        if turn + 1 < count:
            loads[order[turn + 1]] = load_dy(order[turn + 1], 1 - slot)
            for c in loads[order[turn + 1]]:
                c.start()
        if turn >= 2:
            for c in stores[turn - 2]:
                c.wait()
            core_sends[order[turn - 2]].wait_send()

        @pl.loop(0, units // chunk)
        def _(i):
            cols = pl.ds(pl.multiple_of(i * chunk, chunk), chunk)
            pre = over(seq[piece], we[:, cols], 1, 0) + be_ref[:, cols]
            d_act = over(dy_st[slot], wr[cols, :], 1, 1)
            square = pre * pre
            t = jnp.tanh(GELU * pre * (1.0 + 0.044715 * square))
            act_st[slot, :, cols] = (0.5 * pre * (1.0 + t)).astype(BF16)
            slope = 0.5 * (1.0 + t) + (0.5 * GELU) * pre * (1.0 - t * t) * (
                1.0 + (3 * 0.044715) * square
            )
            dpre_st[slot, :, cols] = (d_act * slope).astype(BF16)

        @pl.loop(0, model // wide)
        def _(i):
            cols = pl.ds(pl.multiple_of(i * wide, wide), wide)
            d_two = over(dpre_st[slot], we[cols, :], 1, 1).astype(BF16)
            keep[piece, :, cols] = d_two[:rows]
            give[slot, :, cols] = d_two[rows:]
            out = over(act_st[slot], wr[:, cols], 1, 0).astype(BF16)
            part_st[slot, :, cols] = out

        if host and turn < line.n - 2:
            aside.step(turn + 2)
        core_sends[piece] = core_copy(piece)
        core_sends[piece].start()
        mine, other = owner(piece)
        stores[turn] = []
        for half, index in enumerate((mine, other)):
            to = pl.ds(pl.multiple_of(index * rows, rows), rows)
            part = pl.ds(half * rows, rows)
            stores[turn].append(
                pltpu.make_async_copy(act_st.at[slot, part], act_ref.at[to], st_sem.at[0, slot, half])
            )
            stores[turn].append(
                pltpu.make_async_copy(dpre_st.at[slot, part], dpre_ref.at[to], st_sem.at[1, slot, half])
            )
            stores[turn].append(
                pltpu.make_async_copy(part_st.at[slot, part], part_ref.at[to], st_sem.at[2, slot, half])
            )
            stores[turn].append(
                pltpu.make_async_copy(seq.at[piece, part], seq_ref.at[to], seq_sem.at[piece, half])
            )
        for c in stores[turn]:
            c.start()
        if piece.bit_length() == levels:
            fold(piece)
    for level in range(levels - 2, -1, -1):
        for piece in range((1 << level), 2 << level):
            fold(piece)
    add_core(0)
    for level in range(levels):
        fold_copy(1 << level).wait_recv()

    @pl.loop(0, rows // 16)
    def _(i):
        part = pl.ds(pl.multiple_of(i * 16, 16), 16)
        total = keep[0, part].astype(F32)
        for level in range(levels):
            total = total + fold_in[(1 << level) - 1, part].astype(F32)
        sum_ref[part] = total

    if host:
        for step in range(count + 2, line.n):
            aside.step(step)
        aside.finish()
    for s in sends:
        s.wait_send()
    for turn in range(max(0, count - 2), count):
        for c in stores[turn]:
            c.wait()
        core_sends[order[turn]].wait_send()
    for s in folds.values():
        s.wait_send()


def ffn(n2, dy_all, we, wr, bias_e, own=None):
    host = own is not None
    n = lax.axis_size("tensor")
    rows, model = n2.shape
    units = wr.shape[0]
    dp = lax.axis_size("dp")
    count = dp // 2
    dma, anywhere, vmem = DMA, ANY, VMEM
    operands = [n2, dy_all, we, wr, bias_e] + [own] * host
    lines = [jax.ShapeDtypeStruct((rows, model), F32)] * host
    flops = 36 * dp * rows * model * units
    return pl.pallas_call(
        functools.partial(ffn_kernel, host),
        out_shape=(
            jax.ShapeDtypeStruct((rows, model), F32),
            jax.ShapeDtypeStruct((dp * rows, model), BF16),
            jax.ShapeDtypeStruct((dp * rows, units), BF16),
            jax.ShapeDtypeStruct((dp * rows, units), BF16),
            jax.ShapeDtypeStruct((dp * rows, model), BF16),
            *lines,
        ),
        in_specs=[anywhere, anywhere, anywhere, anywhere, vmem] + [anywhere] * host,
        out_specs=(vmem, anywhere, anywhere, anywhere, anywhere) + (vmem,) * host,
        scratch_shapes=[
            pltpu.VMEM((model, units), BF16),
            pltpu.VMEM((units, model), BF16),
            pltpu.VMEM((count, 2 * rows, model), BF16),
            pltpu.VMEM((2, 2 * rows, model), BF16),
            pltpu.VMEM((2, 2 * rows, units), BF16),
            pltpu.VMEM((2, 2 * rows, units), BF16),
            pltpu.VMEM((2, 2 * rows, model), BF16),
            pltpu.VMEM((count, rows, model), BF16),
            pltpu.VMEM((2, rows, model), BF16),
            pltpu.VMEM((count, rows, model), BF16),
            pltpu.VMEM((count - 1, rows, model), BF16),
            dma((n + 1,)), dma, dma((2, 2)), dma((count, 2)), dma((3, 2, 2)),
            dma((count,)), dma((count,)), dma((count,)), dma((count,)),
            dma((count,)), dma((count,)), dma((count - 1,)), dma((count - 1,)),
        ]
        + (LineScatter.scratch(n, rows, model) if host else []),
        compiler_params=pltpu.CompilerParams(
            collective_id=2 if host else 1, has_side_effects=True, vmem_limit_bytes=62 << 20
        ),
        cost_estimate=pl.CostEstimate(
            flops=flops, bytes_accessed=8 * dp * rows * (model + units), transcendentals=dp * rows * units
        ),
        name="ffn_plane",
    )(*operands)


def body(
    tokens,
    parents,
    cotangent,
    first_gain,
    first_shift,
    w_query,
    b_query,
    w_key,
    w_value,
    b_value,
    w_out,
    b_out,
    second_gain,
    second_shift,
    w_expand,
    b_expand,
    w_reduce,
    b_reduce,
):
    dp = lax.axis_size("dp")
    tn = lax.axis_size("tensor")
    dp_me = lax.axis_index("dp")
    tn_me = lax.axis_index("tensor")
    width = w_query.shape[1]
    model = w_query.shape[0] * dp
    units = w_expand.shape[1]
    mine = units // dp
    micros = range(tokens.shape[0])
    last = tokens.shape[0] - 1
    x_low = [tokens[m, 0] for m in micros]
    dy_low = [cotangent[m, 0] for m in micros]
    rows_here = x_low[0].shape[0]
    total = rows_here * tn

    cut = first_gain.shape[0]
    bq_rows, bq_cols = b_query.shape
    be_rows, be_cols = b_expand.shape
    small = jnp.concatenate(
        [first_gain, first_shift, b_out, second_gain, second_shift, b_reduce]
        + [b_query.reshape(-1), b_value.reshape(-1), b_expand.reshape(-1)]
    )
    used = small.shape[0]
    small = jnp.pad(small, (0, -used % 2048)).reshape(-1, 128)
    w_attn = jnp.concatenate([w_query, w_key, w_value, w_out.T], axis=1)
    seq_x0, w_attn, w_e, w_r, small = front(x_low[0], w_attn, w_expand, w_reduce, small)
    w_qkv = w_attn[:, : 3 * width]
    w_ot = w_attn[:, 3 * width :]
    small = small.reshape(dp, -1)[:, :used]
    gain_one, shift_one, bias_out, gain_two, shift_two, bias_red = [
        small[:, i * cut : (i + 1) * cut].reshape(1, model).astype(F32) for i in range(6)
    ]
    at = 6 * cut
    bias_qkv = []
    for i in range(2):
        part = small[:, at : at + bq_rows * bq_cols].reshape(dp, bq_rows, bq_cols)
        bias_qkv.append(part.transpose(1, 0, 2).reshape(1, width).astype(F32))
        at += bq_rows * bq_cols
    bias_qkv = jnp.concatenate([bias_qkv[0], jnp.zeros((1, width), F32), bias_qkv[1]], 1)
    bias_e = small[:, at:].reshape(dp, dp, be_rows // dp, be_cols)
    bias_e = lax.dynamic_index_in_dim(bias_e, dp_me, 1, keepdims=False)
    bias_e = lax.all_gather(bias_e.transpose(1, 0, 2).reshape(1, mine), "tensor", axis=1, tiled=True)
    bias_e = bias_e.astype(F32)

    seq_grad = [lax.all_gather(dy_low[0], "dp", axis=0, tiled=True)]
    seq_x = [seq_x0]
    side = 0 if mine % 128 == 0 else 1
    w_e = lax.all_gather(after(w_e, seq_grad[0]), "tensor", axis=side, tiled=True)

    normal_one, seq_one, qkv, attended, hidden, normed_two = [], [], [], [], [], []
    out_part, seq_two, activated, d_pre, d_hidden, d_branch, seq_branch = [], [], [], [], [], [], []
    d_qkv, d_one, out_sum = [], [], []
    g_gain_two = g_shift_two = g_bias_red = g_bias_out = g_bias_e = 0.0
    g_gain_one = g_shift_one = g_bias_qkv = 0.0
    for m in micros:
        normal_one.append(layer_norm(seq_x[m].astype(F32), 1.0, 0.0))
        seq_one.append((normal_one[m] * gain_one + shift_one).astype(BF16))
        qkv.append(
            (jnp.dot(seq_one[m], w_qkv, preferred_element_type=F32) + bias_qkv).astype(BF16)
        )
        if m == 0:
            w_r = lax.all_gather(after(w_r, qkv[m]), "tensor", axis=0, tiled=True)
        attended.append(attend(parents[m, 0], qkv[m], width))
        branch = over(attended[m], w_ot, 1, 1).astype(BF16)
        if m < last:
            next_x = lax.all_gather(after(x_low[m + 1], branch), "tensor", axis=0, tiled=True)
        if m == 0:
            (branch,) = exchange(3, lines=[branch])
        else:
            branch, full = exchange(4, lines=[branch], gathers=[d_branch[m - 1]])
            seq_branch.append(full)
        hidden.append(x_low[m].astype(F32) + (branch + bias_out))
        normed_two.append(layer_norm(hidden[m], gain_two, shift_two).astype(BF16))
        if m < last:
            seq_grad.append(
                lax.all_gather(after(dy_low[m + 1], normed_two[m]), "dp", axis=0, tiled=True)
            )

        def attention_back(k):
            d_att = jnp.dot(seq_branch[k], w_ot, preferred_element_type=F32).astype(BF16)
            d_qkv.append(attend_back(parents[k, 0], qkv[k], d_att, width))
            d_one.append(over(d_qkv[k], w_qkv, 1, 1).astype(BF16))
            part = d_one[k].astype(F32)
            return (
                jnp.sum(part * normal_one[k], 0, keepdims=True),
                jnp.sum(part, 0, keepdims=True),
                jnp.sum(d_qkv[k].astype(F32), 0),
            )

        own = None
        if m:
            part, attended[m] = lax.optimization_barrier((out_part[m - 1], attended[m]))
            part = lax.psum_scatter(part, "dp", scatter_dimension=0, tiled=True)
            normed_two[m], part = lax.optimization_barrier((normed_two[m], part))
            out_sum.append(part.astype(F32))
            gain, shift, bias = attention_back(m - 1)
            g_gain_one, g_shift_one = g_gain_one + gain, g_shift_one + shift
            g_bias_qkv = g_bias_qkv + bias
            own = d_one[m - 1]

        d_two, seq, act, dpre, part, *line = ffn(normed_two[m], seq_grad[m], w_e, w_r, bias_e, own)
        if m:
            d_one[m - 1] = line[0]
        seq_two.append(seq)
        activated.append(act)
        d_pre.append(dpre)
        out_part.append(part)
        grad32 = dy_low[m].astype(F32)
        norm_value, norm_pull = jax.vjp(layer_norm, hidden[m], gain_two, shift_two)
        d_norm, g_gain, g_shift = norm_pull(d_two)
        d_hidden.append(grad32 + d_norm)
        d_branch.append(d_hidden[m].astype(BF16))
        g_gain_two = g_gain_two + g_gain
        g_shift_two = g_shift_two + g_shift
        g_bias_red = g_bias_red + jnp.sum(grad32, 0, keepdims=True)
        g_bias_out = g_bias_out + jnp.sum(d_branch[m].astype(F32), 0, keepdims=True)
        g_bias_e = g_bias_e + jnp.sum(dpre.astype(F32), 0)
        if m < last:
            seq_x.append(after(next_x, d_branch[m]))

    def outer(left, right):
        out = None
        for a, b in zip(left, right):
            term = over(a, b, 0, 0)
            out = term if out is None else out + term
        return out.astype(BF16)

    seq_branch.append(lax.all_gather(d_branch[last], "tensor", axis=0, tiled=True))
    g_r = outer(activated, seq_grad)
    g_r = lax.psum_scatter(after(g_r, d_branch[last]), "tensor", scatter_dimension=0, tiled=True)
    g_et = outer(d_pre, seq_two)
    g_et_sum = lax.psum_scatter(g_et, "tensor", scatter_dimension=0, tiled=True)
    seq_branch[last] = after(seq_branch[last], g_et)
    gain, shift, bias = attention_back(last)
    g_gain_one, g_shift_one = g_gain_one + gain, g_shift_one + shift
    g_bias_qkv = g_bias_qkv + bias

    rows = jnp.concatenate(
        [g_gain_one, g_shift_one, g_bias_out, g_gain_two, g_shift_two, g_bias_red], 0
    )
    rows = rows.reshape(6, dp, cut).transpose(1, 0, 2).reshape(dp, 6 * cut)
    row_qv = jnp.concatenate([g_bias_qkv[:width], g_bias_qkv[2 * width :]])
    row_qv = row_qv.reshape(2 * bq_rows, dp, bq_cols).transpose(1, 0, 2)[:, None]
    row_qv = lax.dynamic_update_slice(
        jnp.zeros((dp, tn, 2 * bq_rows, bq_cols), F32), row_qv, (0, tn_me, 0, 0)
    ).reshape(dp, -1)
    row_e = g_bias_e.reshape(tn, be_rows // dp, dp, be_cols).transpose(2, 0, 1, 3)[:, :, None]
    row_e = lax.dynamic_update_slice(
        jnp.zeros((dp, tn, dp, be_rows // dp, be_cols), F32), row_e, (0, 0, dp_me, 0, 0)
    ).reshape(dp, -1)
    little = jnp.concatenate([rows, row_qv, row_e], 1)
    little = jnp.pad(little, ((0, 0), (0, -little.shape[1] % 1024))).reshape(dp, -1, 128)

    g_attn = jnp.concatenate([outer(seq_one, d_qkv), outer(seq_branch, attended)], axis=1)
    d_one[last], g_attn, out_last, g_reduce, little = exchange(
        5, lines=[d_one[last]], planes=[g_attn, out_part[last]], swaps=[g_r], small=[little]
    )
    out_sum.append(out_last)
    (g_expand,) = exchange(6, swaps=[after(g_et_sum, little)])
    g_expand = g_expand.T.astype(F32)
    g_reduce = g_reduce.astype(F32)
    g_query, g_key, g_value = [g_attn[:, i * width : (i + 1) * width] for i in range(3)]
    g_out = g_attn[:, 3 * width :].T
    layer_out = [(hidden[m] + (out_sum[m] + bias_red)).astype(BF16) for m in micros]
    little = little.reshape(-1)
    six = little[: 6 * cut].reshape(6, cut)
    at = 6 * cut
    g_bqv = little[at : at + tn * 2 * bq_rows * bq_cols].reshape(tn, 2 * bq_rows, bq_cols)
    g_bqv = lax.dynamic_index_in_dim(g_bqv, tn_me, 0, keepdims=False)
    g_bq, g_bv = g_bqv[:bq_rows], g_bqv[bq_rows:]
    at += tn * 2 * bq_rows * bq_cols
    g_be = little[at : at + tn * be_rows * be_cols].reshape(tn, be_rows, be_cols)
    g_be = lax.dynamic_index_in_dim(g_be, tn_me, 0, keepdims=False)
    input_grad = []
    for m in micros:
        first_value, first_pull = jax.vjp(
            lambda rows: layer_norm(rows, gain_one, shift_one), x_low[m].astype(F32)
        )
        input_grad.append((d_hidden[m] + first_pull(d_one[m])[0]).astype(BF16))

    return (
        jnp.stack(layer_out, 0)[:, None],
        jnp.stack(input_grad, 0)[:, None],
        six[0],
        six[1],
        g_query,
        g_bq,
        g_key,
        g_value,
        g_bv,
        g_out,
        six[2],
        six[3],
        six[4],
        g_expand,
        g_be,
        g_reduce,
        six[5],
    )


def solution(mesh):
    in_specs = (
        P(None, "dp", "tensor", None),
        P(None, "dp", None),
        P(None, "dp", "tensor", None),
        P("dp"),
        P("dp"),
        P("dp", "tensor"),
        P("tensor", "dp"),
        P("dp", "tensor"),
        P("dp", "tensor"),
        P("tensor", "dp"),
        P("tensor", "dp"),
        P("dp"),
        P("dp"),
        P("dp"),
        P("dp", "tensor"),
        P("tensor", "dp"),
        P("tensor", "dp"),
        P("dp"),
    )
    out_specs = (
        P(None, "dp", "tensor", None),
        P(None, "dp", "tensor", None),
        P("dp"),
        P("dp"),
        P("dp", "tensor"),
        P("tensor", "dp"),
        P("dp", "tensor"),
        P("dp", "tensor"),
        P("tensor", "dp"),
        P("tensor", "dp"),
        P("dp"),
        P("dp"),
        P("dp"),
        P("dp", "tensor"),
        P("tensor", "dp"),
        P("tensor", "dp"),
        P("dp"),
    )
    return jax.shard_map(body, mesh=mesh, in_specs=in_specs, out_specs=out_specs, check_vma=False)
```

```python
import functools
import math

import jax
import jax.numpy as jnp
from jax import lax
from jax.experimental import pallas as pl
from jax.experimental.pallas import tpu as pltpu
from jax.sharding import PartitionSpec as P

HEAD_DIM = 64
BLOCK = 256

F32 = jnp.float32
BF16 = jnp.bfloat16
MESH = pl.DeviceIdType.MESH
DMA = pltpu.SemaphoreType.DMA
GELU = math.sqrt(2.0 / math.pi)


def layer_norm(rows, gain, shift):
    center = rows - jnp.mean(rows, -1, keepdims=True)
    spread = jnp.mean(center * center, -1, keepdims=True)
    return center * lax.rsqrt(spread + 1e-05) * gain + shift


def after(value, *others):
    return lax.optimization_barrier((value,) + others)[0]


def over(left, right, on_left, on_right):
    return lax.dot_general(
        left, right, (((on_left,), (on_right,)), ((), ())), preferred_element_type=F32
    )


def window(index, rows):
    return pl.ds(pl.multiple_of(index * rows, rows), rows)


def remote(src, dst, send, recv, to):
    return pltpu.make_async_remote_copy(
        src_ref=src, dst_ref=dst, send_sem=send, recv_sem=recv,
        device_id=to, device_id_type=MESH,
    )


class Line:
    def __init__(self):
        self.n = lax.axis_size("tensor")
        self.me = lax.axis_index("tensor")
        self.dp = lax.axis_index("dp")

    def at(self, index):
        return (self.dp, index)

    def greet(self, barrier):
        @pl.when(self.me > 0)
        def _():
            pl.semaphore_signal(barrier, inc=1, device_id=self.at(self.me - 1), device_id_type=MESH)

        @pl.when(self.me < self.n - 1)
        def _():
            pl.semaphore_signal(barrier, inc=1, device_id=self.at(self.me + 1), device_id_type=MESH)

    def peers(self):
        return (self.me + self.n - 1) // self.n + (2 * self.n - 2 - self.me) // self.n


class LineGather:
    def __init__(self, line, own, full, sems):
        self.line, self.own, self.full = line, own, full
        self.rows = own.shape[0]
        self.local, self.up_send, self.up_recv, self.down_send, self.down_recv = sems

    @staticmethod
    def sems(n):
        return [DMA, DMA((n - 1,)), DMA((n - 1,)), DMA((n - 1,)), DMA((n - 1,))]

    def hop(self, step, up):
        line = self.line
        if up:
            shard, to = line.me - (step - 1), line.me + 1
            send, recv = self.up_send, self.up_recv
        else:
            shard, to = line.me + (step - 1), line.me - 1
            send, recv = self.down_send, self.down_recv
        there = self.full.at[window(shard, self.rows)]
        src = self.own if step == 1 else there
        return remote(src, there, send.at[step - 1], recv.at[step - 1], line.at(to))

    def sends(self, step, up):
        line = self.line
        if up:
            return (line.me < line.n - 1) & (line.me >= step - 1)
        return (line.me > 0) & (line.me + step - 1 < line.n)

    def takes(self, step, up):
        line = self.line
        return (line.me >= step) if up else (line.me + step < line.n)

    def send(self, step):
        for up in (True, False):
            @pl.when(self.sends(step, up))
            def _():
                self.hop(step, up).start()

    def start(self):
        self.place = pltpu.make_async_copy(
            self.own, self.full.at[window(self.line.me, self.rows)], self.local
        )
        self.place.start()
        self.send(1)

    def take(self, step):
        for up in (True, False):
            @pl.when(self.takes(step, up))
            def _():
                line = self.line
                shard = (line.me - step) if up else (line.me + step)
                here = self.full.at[window(shard, self.rows)]
                send, recv = (
                    (self.up_send, self.up_recv) if up else (self.down_send, self.down_recv)
                )
                remote(
                    here, here, send.at[step - 1], recv.at[step - 1], line.at(line.me)
                ).wait_recv()
        if step < self.line.n - 1:
            self.send(step + 1)

    def finish(self):
        for step in range(1, self.line.n):
            for up in (True, False):
                @pl.when(self.sends(step, up))
                def _():
                    self.hop(step, up).wait_send()
        pltpu.make_async_copy(
            self.own, self.full.at[window(self.line.me, self.rows)], self.local
        ).wait()


class LineScatter:
    def __init__(self, line, parts, out, scratch):
        self.line, self.parts, self.out = line, parts, out
        self.rows = out.shape[0]
        (self.own, self.sum, self.come, self.load, self.own_sem, self.send_sem, self.recv_sem) = scratch

    @staticmethod
    def scratch(n, rows, d):
        return [
            pltpu.VMEM((rows, d), BF16),
            pltpu.VMEM((2, n - 1, rows, d), BF16),
            pltpu.VMEM((2, n - 1, rows, d), BF16),
            DMA((2, n - 1)), DMA, DMA((2, n - 1)), DMA((2, n - 1)),
        ]

    def sends(self, step, up):
        line = self.line
        return (line.me <= step - 1) if up else (line.n - 1 - line.me <= step - 1)

    def load_of(self, step, up):
        line = self.line
        chunk = (line.me + line.n - step) if up else (line.me - line.n + step)
        way = 0 if up else 1
        return pltpu.make_async_copy(
            self.parts.at[window(chunk, self.rows)], self.sum.at[way, step - 1], self.load.at[way, step - 1]
        )

    def hop(self, step, up):
        line, way = self.line, 0 if up else 1
        return remote(
            self.sum.at[way, step - 1], self.come.at[way, step - 1],
            self.send_sem.at[way, step - 1], self.recv_sem.at[way, step - 1],
            line.at(line.me + 1 if up else line.me - 1),
        )

    def wait_from(self, step, up):
        line, way = self.line, 0 if up else 1
        remote(
            self.come.at[way, step - 1], self.come.at[way, step - 1],
            self.send_sem.at[way, step - 1], self.recv_sem.at[way, step - 1],
            line.at(line.me),
        ).wait_recv()

    def own_load(self):
        return pltpu.make_async_copy(
            self.parts.at[window(self.line.me, self.rows)], self.own, self.own_sem
        )

    def prepare(self):
        self.own_load().start()
        for step in range(1, self.line.n):
            for up in (True, False):
                @pl.when(self.sends(step, up))
                def _():
                    self.load_of(step, up).start()

    def step(self, step):
        line = self.line
        for up in (True, False):
            way = 0 if up else 1

            @pl.when(self.sends(step, up))
            def _():
                self.load_of(step, up).wait()
                if step > 1:
                    inner = (line.me > 0) if up else (line.me < line.n - 1)

                    @pl.when(inner)
                    def _():
                        self.wait_from(step - 1, up)

                        @pl.loop(0, self.rows // 16)
                        def _(i):
                            part = window(i, 16)
                            self.sum[way, step - 1, part] = (
                                self.sum[way, step - 1, part].astype(F32)
                                + self.come[way, step - 2, part].astype(F32)
                            ).astype(BF16)

                if step > 1:

                    @pl.when(self.sends(step - 1, up))
                    def _():
                        self.hop(step - 1, up).wait_send()

                self.hop(step, up).start()

    def finish(self):
        line, n = self.line, self.line.n
        self.own_load().wait()

        @pl.loop(0, self.rows // 16)
        def _(i):
            part = window(i, 16)
            self.out[part] = self.own[part].astype(F32)

        for up in (True, False):
            way = 0 if up else 1

            @pl.when((line.me > 0) if up else (line.me < n - 1))
            def _():
                self.wait_from(n - 1, up)

                @pl.loop(0, self.rows // 16)
                def _(i):
                    part = window(i, 16)
                    self.out[part] += self.come[way, n - 2, part].astype(F32)

        for up in (True, False):
            @pl.when(self.sends(n - 1, up))
            def _():
                self.hop(n - 1, up).wait_send()


class Cube:
    def __init__(self):
        self.dp = lax.axis_size("dp")
        self.levels = levels = self.dp.bit_length() - 2
        self.count = 1 << levels
        self.me = me = lax.axis_index("dp")
        self.tensor = lax.axis_index("tensor")
        core = me % 2
        flips = []
        for bit in range(1, levels + 1):
            flips.append((1 << bit) * (1 - 2 * ((me // (1 << bit)) % 2)))
        self.steps = [
            flips[l] * (1 - core) + flips[levels - 1 - l] * core for l in range(levels)
        ]
        self.core_step = 1 - 2 * core

    def at(self, index):
        return (index, self.tensor)

    def owner(self, piece):
        mine, other = self.me, self.me + self.core_step
        for l in range(self.levels):
            if piece >> l & 1:
                mine = mine + self.steps[l]
                other = other + self.steps[self.levels - 1 - l]
        return mine, other

    def greet(self, barrier):
        for step in self.steps + [self.core_step]:
            pl.semaphore_signal(
                barrier, inc=1, device_id=self.at(self.me + step), device_id_type=MESH
            )

    def peers(self):
        return self.levels + 1


class CubeGather:
    def __init__(self, cube, own, full, sems):
        self.cube, self.own, self.full = cube, own, full
        self.rows = own.shape[0]
        self.local, self.send_sem, self.recv_sem, self.core_send, self.core_recv = sems
        self.arrived, self.sent = {0}, []

    @staticmethod
    def sems(count):
        return [DMA, DMA((count,)), DMA((count,)), DMA((count,)), DMA((count,))]

    def slot(self, index):
        return self.full.at[window(index, self.rows)]

    def src(self, piece):
        return self.own if piece == 0 else self.slot(self.cube.owner(piece)[0])

    def hop(self, piece, level):
        cube, there = self.cube, piece + (1 << level)
        return remote(
            self.src(piece), self.slot(cube.owner(piece)[0]),
            self.send_sem.at[there], self.recv_sem.at[there], cube.at(cube.me + cube.steps[level]),
        )

    def core(self, piece):
        cube = self.cube
        return remote(
            self.src(piece), self.slot(cube.owner(piece)[0]),
            self.core_send.at[piece], self.core_recv.at[piece], cube.at(cube.me + cube.core_step),
        )

    def give(self, piece):
        for level in range(piece.bit_length(), self.cube.levels):
            self.sent.append(self.hop(piece, level))
            self.sent[-1].start()
        self.sent.append(self.core(piece))
        self.sent[-1].start()

    def start(self):
        self.place = pltpu.make_async_copy(self.own, self.slot(self.cube.me), self.local)
        self.place.start()
        self.give(0)

    def take(self, piece):
        if piece in self.arrived:
            return
        here = self.slot(self.cube.owner(piece)[0])
        remote(
            here, here, self.send_sem.at[piece], self.recv_sem.at[piece], self.cube.at(self.cube.me)
        ).wait_recv()
        self.arrived.add(piece)
        self.give(piece)

    def take_core(self, piece):
        here = self.slot(self.cube.owner(piece)[1])
        remote(
            here, here, self.core_send.at[piece], self.core_recv.at[piece], self.cube.at(self.cube.me)
        ).wait_recv()

    def finish(self):
        for piece in range(self.cube.count):
            self.take(piece)
            self.take_core(piece)
        for copy in self.sent:
            copy.wait_send()
        self.place.wait()


class CubeScatter:
    def __init__(self, cube, parts, out, scratch):
        self.cube, self.parts, self.out = cube, parts, out
        self.rows = out.shape[0]
        (self.keep, self.core_in, self.fold_in, self.load_sem,
         self.core_send, self.core_recv, self.send_sem, self.recv_sem) = scratch

    @staticmethod
    def scratch(count, rows, d):
        return [
            pltpu.VMEM((count, rows, d), BF16),
            pltpu.VMEM((count, rows, d), BF16),
            pltpu.VMEM((count - 1, rows, d), BF16),
            DMA((count,)), DMA((count,)), DMA((count,)), DMA((count - 1,)), DMA((count - 1,)),
        ]

    def load(self, piece):
        return pltpu.make_async_copy(
            self.parts.at[window(self.cube.owner(piece)[0], self.rows)],
            self.keep.at[piece], self.load_sem.at[piece],
        )

    def core(self, piece):
        cube = self.cube
        return remote(
            self.parts.at[window(cube.owner(piece)[1], self.rows)], self.core_in.at[piece],
            self.core_send.at[piece], self.core_recv.at[piece], cube.at(cube.me + cube.core_step),
        )

    def hop(self, piece):
        cube, level = self.cube, piece.bit_length() - 1
        return remote(
            self.keep.at[piece], self.fold_in.at[piece - 1],
            self.send_sem.at[piece - 1], self.recv_sem.at[piece - 1],
            cube.at(cube.me + cube.steps[level]),
        )

    def order(self):
        return sorted(range(self.cube.count), key=lambda p: (-(p.bit_length()), p))

    def start(self):
        for piece in self.order():
            self.core(piece).start()
            self.load(piece).start()

    def add(self, piece, other):
        @pl.loop(0, self.rows // 16)
        def _(i):
            part = window(i, 16)
            self.keep[piece, part] = (
                self.keep[piece, part].astype(F32) + other[part].astype(F32)
            ).astype(BF16)

    def fold(self, piece):
        self.load(piece).wait()
        self.core(piece).wait_recv()
        self.add(piece, self.core_in.at[piece])
        for level in range(self.cube.levels - 1, piece.bit_length() - 1, -1):
            above = piece + (1 << level)
            self.hop(above).wait_recv()
            self.add(piece, self.fold_in.at[above - 1])
        if piece:
            self.hop(piece).start()

    def finish(self):
        self.fold(0)

        @pl.loop(0, self.rows // 16)
        def _(i):
            part = window(i, 16)
            self.out[part] = self.keep[0, part].astype(F32)

        for piece in range(self.cube.count):
            self.core(piece).wait_send()
            if piece:
                self.hop(piece).wait_send()


class CubeExchange:
    def __init__(self, cube, moves, sems):
        self.cube, self.moves = cube, moves
        self.send_sem, self.recv_sem, self.local = sems

    @staticmethod
    def sems(dp, moves):
        return [DMA((moves, dp)), DMA((moves, dp)), DMA((moves,))]

    def copies(self):
        cube = self.cube
        out = []
        for k in range(1, cube.dp):
            to = (cube.me + k) % cube.dp
            for m, (src, dst) in enumerate(self.moves):
                out.append(
                    remote(src(to), dst(cube.me), self.send_sem.at[m, k], self.recv_sem.at[m, k], cube.at(to))
                )
        return out

    def locals(self):
        return [
            pltpu.make_async_copy(src(self.cube.me), dst(self.cube.me), self.local.at[m])
            for m, (src, dst) in enumerate(self.moves)
        ]

    def start(self):
        for copy in self.copies() + self.locals():
            copy.start()

    def finish(self):
        cube = self.cube
        for copy in self.copies():
            copy.wait_send()
        for k in range(1, cube.dp):
            of = (cube.me - k + cube.dp) % cube.dp
            for m, (src, dst) in enumerate(self.moves):
                here = dst(of)
                remote(here, here, self.send_sem.at[m, k], self.recv_sem.at[m, k], cube.at(of)).wait_recv()
        for copy in self.locals():
            copy.wait()


ANY = pl.BlockSpec(memory_space=pl.ANY)
VMEM = pl.BlockSpec(memory_space=pltpu.VMEM)


def front_kernel(x_ref, w_ref, we_ref, wr_ref, small_ref, seq_ref, w_out, we_out, wr_out, small_out, *sems):
    line, cube = Line(), Cube()
    gather = LineGather(line, x_ref, seq_ref, sems[:5])
    weights = CubeGather(cube, w_ref, w_out, sems[5:10])
    mine = wr_out.shape[0]
    rows, cols = we_ref.shape[0], wr_ref.shape[1]
    tile = small_ref.shape[0]
    moves = [
        (lambda d: small_ref, lambda d: small_out.at[window(d, tile)]),
        (lambda d: wr_ref.at[window(d, mine)], lambda d: wr_out.at[:, window(d, cols)]),
        (lambda d: we_ref.at[:, window(d, mine)], lambda d: we_out.at[window(d, rows)]),
    ]
    swap = CubeExchange(cube, moves if mine % 128 == 0 else moves[:2], sems[10:13])
    barrier = pltpu.get_barrier_semaphore()
    line.greet(barrier)
    for k in range(1, cube.dp):
        pl.semaphore_signal(
            barrier, inc=1, device_id=cube.at((cube.me + k) % cube.dp), device_id_type=MESH
        )
    pl.semaphore_wait(barrier, cube.dp - 1 + line.peers())
    gather.start()
    weights.start()
    gather.take(1)
    for piece in range(1, cube.count):
        if piece.bit_length() < cube.levels:
            weights.take(piece)
    swap.start()
    gather.take(2)
    for piece in range(1, cube.count):
        weights.take(piece)
    for step in range(3, line.n):
        gather.take(step)
    weights.finish()
    swap.finish()
    gather.finish()


def front(x, w, w_e, w_r, small):
    dp, n = lax.axis_size("dp"), lax.axis_size("tensor")
    rows, model = x.shape
    outs = pl.pallas_call(
        front_kernel,
        out_shape=(
            jax.ShapeDtypeStruct((n * rows, model), BF16),
            jax.ShapeDtypeStruct((dp * w.shape[0], w.shape[1]), BF16),
            jax.ShapeDtypeStruct((dp * w_e.shape[0], w_e.shape[1] // dp), BF16),
            jax.ShapeDtypeStruct((w_r.shape[0] // dp, w_r.shape[1] * dp), BF16),
            jax.ShapeDtypeStruct((dp * small.shape[0], small.shape[1]), BF16),
        ),
        in_specs=[ANY] * 5,
        out_specs=(ANY,) * 5,
        scratch_shapes=LineGather.sems(n) + CubeGather.sems(dp // 2) + CubeExchange.sems(dp, 3),
        compiler_params=pltpu.CompilerParams(collective_id=0, has_side_effects=True),
        cost_estimate=pl.CostEstimate(flops=80 * 10**9, bytes_accessed=10**7, transcendentals=0),
        name="front",
    )(x, w, w_e, w_r, small)
    seq, w_all, e_all, r_all, small_all = outs
    if r_all.shape[0] % 128:
        e_all = lax.all_to_all(w_e, "dp", split_axis=1, concat_axis=0, tiled=True)
    return seq, w_all, e_all, r_all, small_all


class SmallSum:
    def __init__(self, line, cube, parts, out, scratch):
        self.line, self.cube, self.parts, self.out = line, cube, parts, out
        self.come, self.gather, self.sems, self.line_send, self.line_recv = (
            scratch[0], scratch[1], scratch[2:5], scratch[5], scratch[6]
        )
        moves = [(lambda d: parts.at[d], lambda d: self.come.at[d])]
        self.swap = CubeExchange(cube, moves, self.sems)

    @staticmethod
    def scratch(dp, n, rows, d):
        return [
            pltpu.VMEM((dp, rows, d), F32),
            pltpu.VMEM((n, rows, d), F32),
            *CubeExchange.sems(dp, 1),
            DMA((n,)), DMA((n,)),
        ]

    def hop(self, k):
        line = self.line
        here = self.gather.at[line.me]
        return remote(
            here, here, self.line_send.at[k], self.line_recv.at[k], line.at((line.me + k) % line.n)
        )

    def middle(self):
        self.swap.finish()
        total = self.come[0]
        for d in range(1, self.cube.dp):
            total = total + self.come[d]
        self.gather[self.line.me] = total
        for k in range(1, self.line.n):
            self.hop(k).start()

    def finish(self):
        line = self.line
        for k in range(1, line.n):
            here = self.gather.at[(line.me - k + line.n) % line.n]
            remote(
                here, here, self.line_send.at[k], self.line_recv.at[k], line.at(line.me)
            ).wait_recv()
            self.hop(k).wait_send()
        total = self.gather[0]
        for z in range(1, line.n):
            total = total + self.gather[z]
        self.out[...] = total


def sum_kernel(counts, *refs):
    lines, planes, gathers, cubes, swaps, small = counts
    line, cube = Line(), Cube()
    count = sum(counts)
    ins, outs, scratch = refs[:count], refs[count : 2 * count], list(refs[2 * count :])

    def take(number):
        taken = tuple(scratch[:number])
        del scratch[:number]
        return taken

    pairs = list(zip(ins, outs))
    sums = [LineScatter(line, *pairs.pop(0), take(7)) for _ in range(lines)]
    folds = [CubeScatter(cube, *pairs.pop(0), take(8)) for _ in range(planes)]
    lanes = [LineGather(line, *pairs.pop(0), take(5)) for _ in range(gathers)]
    wholes = [CubeGather(cube, *pairs.pop(0), take(5)) for _ in range(cubes)]
    moves = []
    for _ in range(swaps):
        src, dst = pairs.pop(0)
        rows, cols = src.shape[0], dst.shape[1]
        moves.append(
            (
                lambda d, src=src, cols=cols: src.at[:, window(d, cols)],
                lambda d, dst=dst, rows=rows: dst.at[window(d, rows)],
            )
        )
    swap = CubeExchange(cube, moves, take(3)) if swaps else None
    little = SmallSum(line, cube, *pairs.pop(0), take(7)) if small else None
    barrier = pltpu.get_barrier_semaphore()
    peers = 0
    if small:
        for k in range(1, line.n):
            pl.semaphore_signal(
                barrier, inc=1, device_id=line.at((line.me + k) % line.n), device_id_type=MESH
            )
        peers = line.n - 1
    elif lines or gathers:
        line.greet(barrier)
        peers = line.peers()
    if small or swaps:
        for k in range(1, cube.dp):
            pl.semaphore_signal(
                barrier, inc=1, device_id=cube.at((cube.me + k) % cube.dp), device_id_type=MESH
            )
        peers = peers + cube.dp - 1
    elif planes or cubes:
        cube.greet(barrier)
        peers = peers + cube.peers()
    for s in sums:
        s.prepare()
    pl.semaphore_wait(barrier, peers)
    if small:
        little.swap.start()
    for s in sums:
        s.step(1)
    for lane in lanes:
        lane.start()
    for whole in wholes[:1]:
        whole.start()
    pieces = [p for p in folds[0].order() if p] if planes else []
    per = -(-len(pieces) // (line.n - 1))
    for step in range(1, line.n):
        if step > 1:
            for s in sums:
                s.step(step)
            for lane in lanes:
                lane.take(step - 1)
        if step == 1:
            for f in folds:
                f.start()
            if small:
                little.middle()
        for piece in pieces[:per]:
            for f in folds:
                f.fold(piece)
        pieces = pieces[per:]
        if step == 1 and swaps:
            swap.start()
        for whole in wholes[step - 1 : step]:
            whole.finish()
        for whole in wholes[step : step + 1]:
            whole.start()
    for f in folds:
        f.finish()
    for lane in lanes:
        lane.take(line.n - 1)
        lane.finish()
    for s in sums:
        s.finish()
    if swaps:
        swap.finish()
    if small:
        little.finish()


def exchange(collective_id, lines=(), planes=(), gathers=(), cubes=(), swaps=(), small=()):
    dp, n = lax.axis_size("dp"), lax.axis_size("tensor")
    out_shape, out_specs, scratch = [], [], []
    for part in lines:
        rows, d = part.shape[0] // n, part.shape[1]
        out_shape.append(jax.ShapeDtypeStruct((rows, d), F32))
        out_specs.append(VMEM)
        scratch += LineScatter.scratch(n, rows, d)
    for part in planes:
        rows, d = part.shape[0] // dp, part.shape[1]
        out_shape.append(jax.ShapeDtypeStruct((rows, d), F32))
        out_specs.append(VMEM)
        scratch += CubeScatter.scratch(dp // 2, rows, d)
    for part in gathers:
        rows, d = part.shape
        out_shape.append(jax.ShapeDtypeStruct((n * rows, d), BF16))
        out_specs.append(ANY)
        scratch += LineGather.sems(n)
    for part in cubes:
        rows, d = part.shape
        out_shape.append(jax.ShapeDtypeStruct((dp * rows, d), BF16))
        out_specs.append(ANY)
        scratch += CubeGather.sems(dp // 2)
    for part in swaps:
        rows, d = part.shape
        out_shape.append(jax.ShapeDtypeStruct((dp * rows, d // dp), BF16))
        out_specs.append(ANY)
    if swaps:
        scratch += CubeExchange.sems(dp, len(swaps))
    for part in small:
        rows, d = part.shape[1:]
        out_shape.append(jax.ShapeDtypeStruct((rows, d), F32))
        out_specs.append(VMEM)
        scratch += SmallSum.scratch(dp, n, rows, d)
    counts = tuple(len(g) for g in (lines, planes, gathers, cubes, swaps, small))
    operands = [part for group in (lines, planes, gathers, cubes, swaps, small) for part in group]
    return pl.pallas_call(
        functools.partial(sum_kernel, counts),
        out_shape=tuple(out_shape),
        in_specs=[ANY] * len(operands),
        out_specs=tuple(out_specs),
        scratch_shapes=scratch,
        compiler_params=pltpu.CompilerParams(
            collective_id=collective_id, has_side_effects=True, vmem_limit_bytes=60 << 20
        ),
        cost_estimate=pl.CostEstimate(flops=80 * 10**9, bytes_accessed=10**7, transcendentals=0),
        name="exchange",
    )(*operands)


PAIR = 2 * HEAD_DIM
NEVER = -1e30


def lane_of(shape, head):
    lane = lax.broadcasted_iota(jnp.int32, shape, 1)
    return (lane < HEAD_DIM) if head == 0 else (lane >= HEAD_DIM)


def sight(parents_ref, row, col):
    at = jnp.int32(row)
    seen = at == col
    for hop in range(row - col):
        at = parents_ref[at]
        seen = seen | (at == col)
    return jnp.where(seen, 0.0, NEVER).astype(F32)


def masked_scores(parents_ref, q_head, k_ref, row):
    scores = []
    for col in range(row + 1):
        part = over(q_head, k_ref[col * BLOCK : (col + 1) * BLOCK, :], 1, 1)
        if col == row:
            below = lax.broadcasted_iota(jnp.int32, part.shape, 1) <= lax.broadcasted_iota(
                jnp.int32, part.shape, 0
            )
            part = jnp.where(below, part, NEVER)
        else:
            part = part + sight(parents_ref, row, col)
        scores.append(part)
    return scores


def row_reduce(parts, fold, reduce):
    return reduce(functools.reduce(fold, parts), axis=-1, keepdims=True)


def attend_kernel(parents_ref, q_ref, k_ref, v_ref, out_ref):
    blocks = q_ref.shape[0] // BLOCK
    scale = 1.0 / math.sqrt(HEAD_DIM)
    for row in range(blocks):
        here = slice(row * BLOCK, (row + 1) * BLOCK)
        heads = []
        for head in range(2):
            q_head = q_ref[here, :].astype(F32) * scale
            q_head = jnp.where(lane_of(q_head.shape, head), q_head, 0.0).astype(BF16)
            scores = masked_scores(parents_ref, q_head, k_ref, row)
            top = row_reduce(scores, jnp.maximum, jnp.max)
            probs = [jnp.exp(s - top) for s in scores]
            total = row_reduce(probs, jnp.add, jnp.sum)
            out = None
            for col in range(row + 1):
                term = over(
                    probs[col].astype(BF16), v_ref[col * BLOCK : (col + 1) * BLOCK, :], 1, 0
                )
                out = term if out is None else out + term
            heads.append(out / total)
        mixed = jnp.where(lane_of(heads[0].shape, 0), heads[0], heads[1])
        out_ref[here, :] = mixed.astype(out_ref.dtype)


def attend(parents, qkv, width):
    rows = qkv.shape[0]
    pairs = width // PAIR
    spec = lambda part: pl.BlockSpec((rows, PAIR), lambda p, parents: (0, part * pairs + p))
    blocks = rows // BLOCK
    work = pairs * 2 * (blocks * (blocks + 1) // 2) * BLOCK * BLOCK
    return pl.pallas_call(
        attend_kernel,
        out_shape=jax.ShapeDtypeStruct((rows, width), BF16),
        grid_spec=pltpu.PrefetchScalarGridSpec(
            num_scalar_prefetch=1,
            grid=(pairs,),
            in_specs=[spec(0), spec(1), spec(2)],
            out_specs=pl.BlockSpec((rows, PAIR), lambda p, parents: (0, p)),
        ),
        compiler_params=pltpu.CompilerParams(vmem_limit_bytes=48 << 20),
        cost_estimate=pl.CostEstimate(
            flops=work * PAIR * 24, bytes_accessed=rows * width * 8, transcendentals=work
        ),
        name="attend",
    )(parents, qkv, qkv, qkv)


def attend_back_kernel(parents_ref, q_ref, k_ref, v_ref, g_ref, out_ref, dq_s, dk_s, dv_s):
    part = pl.program_id(1)
    blocks = q_ref.shape[0] // BLOCK
    scale = 1.0 / math.sqrt(HEAD_DIM)

    @pl.when(part == 0)
    def _():
        for row in range(blocks):
            here = slice(row * BLOCK, (row + 1) * BLOCK)
            dq_heads = []
            for head in range(2):
                lanes = lane_of((BLOCK, PAIR), head)
                q_head = jnp.where(lanes, q_ref[here, :].astype(F32) * scale, 0.0).astype(BF16)
                g_head = jnp.where(lanes, g_ref[here, :].astype(F32), 0.0).astype(BF16)
                scores = masked_scores(parents_ref, q_head, k_ref, row)
                top = row_reduce(scores, jnp.maximum, jnp.max)
                probs = [jnp.exp(s - top) for s in scores]
                rest = 1.0 / row_reduce(probs, jnp.add, jnp.sum)
                probs = [p * rest for p in probs]
                d_probs = [
                    over(g_head, v_ref[col * BLOCK : (col + 1) * BLOCK, :], 1, 1)
                    for col in range(row + 1)
                ]
                level = row_reduce([p * d for p, d in zip(probs, d_probs)], jnp.add, jnp.sum)
                dq = None
                for col in range(row + 1):
                    there = slice(col * BLOCK, (col + 1) * BLOCK)
                    d_scores = (probs[col] * (d_probs[col] - level)).astype(BF16)
                    term = over(d_scores, k_ref[there, :], 1, 0)
                    dq = term if dq is None else dq + term
                    dk = over(d_scores, q_head, 0, 0)
                    dv = over(probs[col].astype(BF16), g_head, 0, 0)
                    if row == col and head == 0:
                        dk_s[there, :] = dk
                        dv_s[there, :] = dv
                    else:
                        dk_s[there, :] += dk
                        dv_s[there, :] += dv
                dq_heads.append(dq * scale)
            dq_s[here, :] = jnp.where(lane_of((BLOCK, PAIR), 0), dq_heads[0], dq_heads[1]).astype(
                BF16
            )
        out_ref[...] = dq_s[...]

    @pl.when(part == 1)
    def _():
        out_ref[...] = dk_s[...].astype(BF16)

    @pl.when(part == 2)
    def _():
        out_ref[...] = dv_s[...].astype(BF16)


def attend_back(parents, qkv, grad, width):
    rows = qkv.shape[0]
    pairs = width // PAIR
    spec = lambda part: pl.BlockSpec((rows, PAIR), lambda p, c, parents: (0, part * pairs + p))
    blocks = rows // BLOCK
    work = pairs * 2 * (blocks * (blocks + 1) // 2) * BLOCK * BLOCK
    return pl.pallas_call(
        attend_back_kernel,
        out_shape=jax.ShapeDtypeStruct((rows, 3 * width), BF16),
        grid_spec=pltpu.PrefetchScalarGridSpec(
            num_scalar_prefetch=1,
            grid=(pairs, 3),
            in_specs=[
                spec(0),
                spec(1),
                spec(2),
                pl.BlockSpec((rows, PAIR), lambda p, c, parents: (0, p)),
            ],
            out_specs=pl.BlockSpec((rows, PAIR), lambda p, c, parents: (0, c * pairs + p)),
            scratch_shapes=[
                pltpu.VMEM((rows, PAIR), BF16),
                pltpu.VMEM((rows, PAIR), F32),
                pltpu.VMEM((rows, PAIR), F32),
            ],
        ),
        compiler_params=pltpu.CompilerParams(vmem_limit_bytes=48 << 20),
        cost_estimate=pl.CostEstimate(
            flops=work * PAIR * 60, bytes_accessed=rows * width * 14, transcendentals=work
        ),
        name="attend_back",
    )(parents, qkv, qkv, qkv, grad)


def ffn_kernel(host, n2_ref, dy_ref, we_ref, wr_ref, be_ref, *refs):
    if host:
        line_own, refs = refs[0], refs[1:]
    sum_ref, seq_ref, act_ref, dpre_ref, part_ref = refs[:5]
    refs = refs[5:]
    if host:
        line_full, refs = refs[0], refs[1:]
    we, wr, seq, dy_st, act_st, dpre_st, part_st, keep, give, core_in, fold_in = refs[:11]
    refs = refs[1:]
    w_sem, own_sem, dy_sem, seq_sem, st_sem = refs[10:15]
    ag_send, ag_recv, agc_send, agc_recv, rsc_send, rsc_recv, fold_send, fold_recv = refs[15:23]
    cube = Cube()
    levels, me, steps, core_step = cube.levels, cube.me, cube.steps, cube.core_step
    count, at, owner = cube.count, cube.at, cube.owner
    rows, model = n2_ref.shape
    units = wr_ref.shape[0]
    barrier = pltpu.get_barrier_semaphore()
    cube.greet(barrier)
    hosted = []
    if host:
        line = Line()
        line.greet(barrier)
        aside = LineScatter(line, line_own, line_full, refs[23:])
        aside.prepare()
    load_own = pltpu.make_async_copy(n2_ref, seq.at[0, pl.ds(0, rows)], own_sem)
    load_own.start()
    parts = we_ref.shape[0] // model
    mine_units = we_ref.shape[1]
    loads_w = [pltpu.make_async_copy(wr_ref, wr, w_sem.at[parts])]
    for part in range(parts):
        loads_w.append(
            pltpu.make_async_copy(
                we_ref.at[pl.ds(part * model, model)],
                we.at[:, pl.ds(part * mine_units, mine_units)],
                w_sem.at[part],
            )
        )
    for c in loads_w:
        c.start()

    def load_dy(piece, slot):
        mine, other = owner(piece)
        out = []
        for half, index in enumerate((mine, other)):
            out.append(
                pltpu.make_async_copy(
                    dy_ref.at[pl.ds(pl.multiple_of(index * rows, rows), rows)],
                    dy_st.at[slot, pl.ds(half * rows, rows)],
                    dy_sem.at[slot, half],
                )
            )
        return out

    def gather_copy(piece, level):
        there = piece + (1 << level)
        return remote(
            seq.at[piece, pl.ds(0, rows)], seq.at[there, pl.ds(0, rows)],
            ag_send.at[there], ag_recv.at[there], at(me + steps[level]),
        )

    def gather_core(piece):
        return remote(
            seq.at[piece, pl.ds(0, rows)], seq.at[piece, pl.ds(rows, rows)],
            agc_send.at[piece], agc_recv.at[piece], at(me + core_step),
        )

    order = [0] + sorted(range(1, count), key=lambda p: (-(p.bit_length()), p))
    slots = {piece: i % 2 for i, piece in enumerate(order)}
    loads = {order[0]: load_dy(order[0], 0)}
    for c in loads[order[0]]:
        c.start()

    load_own.wait()
    pl.semaphore_wait(barrier, cube.peers() + (line.peers() if host else 0))
    if host:
        aside.step(1)
    sends = []
    for level in range(levels):
        sends.append(gather_copy(0, level))
        sends[-1].start()
    sends.append(gather_core(0))
    sends[-1].start()
    for c in loads_w:
        c.wait()

    arrived = {0}

    def take(piece):
        if piece in arrived:
            return
        low = piece - (1 << (piece.bit_length() - 1))
        gather_copy(low, piece.bit_length() - 1).wait_recv()
        arrived.add(piece)
        for level in range(piece.bit_length(), levels):
            sends.append(gather_copy(piece, level))
            sends[-1].start()
        sends.append(gather_core(piece))
        sends[-1].start()

    stores = {}
    outs = {}
    core_sends = {}
    folds = {}
    done_core = set()

    def add(piece, other):
        @pl.loop(0, rows // 16)
        def _(i):
            part = pl.ds(pl.multiple_of(i * 16, 16), 16)
            keep[piece, part] = (
                keep[piece, part].astype(F32) + other[part].astype(F32)
            ).astype(BF16)

    def add_core(piece):
        if piece in done_core:
            return
        core_copy(piece).wait_recv()
        add(piece, core_in.at[piece])
        done_core.add(piece)

    def core_copy(piece):
        return remote(
            give.at[slots[piece]], core_in.at[piece],
            rsc_send.at[piece], rsc_recv.at[piece], at(me + core_step),
        )

    def fold_copy(piece):
        level = piece.bit_length() - 1
        low = piece - (1 << level)
        return remote(
            keep.at[piece], fold_in.at[piece - 1],
            fold_send.at[piece - 1], fold_recv.at[piece - 1], at(me + steps[level]),
        )

    def fold(piece):
        add_core(piece)
        for level in range(levels - 1, piece.bit_length() - 1, -1):
            above = piece + (1 << level)
            fold_copy(above).wait_recv()
            add(piece, fold_in.at[above - 1])
        if piece:
            folds[piece] = fold_copy(piece)
            folds[piece].start()

    chunk = 256
    wide = 512
    for turn, piece in enumerate(order):
        slot = turn % 2
        for earlier in range(1, piece + 1):
            take(earlier)
        gather_core(piece).wait_recv()
        for c in loads[piece]:
            c.wait()
        if turn + 1 < count:
            loads[order[turn + 1]] = load_dy(order[turn + 1], 1 - slot)
            for c in loads[order[turn + 1]]:
                c.start()
        if turn >= 2:
            for c in stores[turn - 2]:
                c.wait()
            core_sends[order[turn - 2]].wait_send()

        @pl.loop(0, units // chunk)
        def _(i):
            cols = pl.ds(pl.multiple_of(i * chunk, chunk), chunk)
            pre = over(seq[piece], we[:, cols], 1, 0) + be_ref[:, cols]
            d_act = over(dy_st[slot], wr[cols, :], 1, 1)
            square = pre * pre
            t = jnp.tanh(GELU * pre * (1.0 + 0.044715 * square))
            act_st[slot, :, cols] = (0.5 * pre * (1.0 + t)).astype(BF16)
            slope = 0.5 * (1.0 + t) + (0.5 * GELU) * pre * (1.0 - t * t) * (
                1.0 + (3 * 0.044715) * square
            )
            dpre_st[slot, :, cols] = (d_act * slope).astype(BF16)

        @pl.loop(0, model // wide)
        def _(i):
            cols = pl.ds(pl.multiple_of(i * wide, wide), wide)
            d_two = over(dpre_st[slot], we[cols, :], 1, 1).astype(BF16)
            keep[piece, :, cols] = d_two[:rows]
            give[slot, :, cols] = d_two[rows:]
            out = over(act_st[slot], wr[:, cols], 1, 0).astype(BF16)
            part_st[slot, :, cols] = out

        if host and turn < line.n - 2:
            aside.step(turn + 2)
        core_sends[piece] = core_copy(piece)
        core_sends[piece].start()
        mine, other = owner(piece)
        stores[turn] = []
        for half, index in enumerate((mine, other)):
            to = pl.ds(pl.multiple_of(index * rows, rows), rows)
            part = pl.ds(half * rows, rows)
            stores[turn].append(
                pltpu.make_async_copy(act_st.at[slot, part], act_ref.at[to], st_sem.at[0, slot, half])
            )
            stores[turn].append(
                pltpu.make_async_copy(dpre_st.at[slot, part], dpre_ref.at[to], st_sem.at[1, slot, half])
            )
            stores[turn].append(
                pltpu.make_async_copy(part_st.at[slot, part], part_ref.at[to], st_sem.at[2, slot, half])
            )
            stores[turn].append(
                pltpu.make_async_copy(seq.at[piece, part], seq_ref.at[to], seq_sem.at[piece, half])
            )
        for c in stores[turn]:
            c.start()
        if piece.bit_length() == levels:
            fold(piece)
    for level in range(levels - 2, -1, -1):
        for piece in range((1 << level), 2 << level):
            fold(piece)
    add_core(0)
    for level in range(levels):
        fold_copy(1 << level).wait_recv()

    @pl.loop(0, rows // 16)
    def _(i):
        part = pl.ds(pl.multiple_of(i * 16, 16), 16)
        total = keep[0, part].astype(F32)
        for level in range(levels):
            total = total + fold_in[(1 << level) - 1, part].astype(F32)
        sum_ref[part] = total

    if host:
        for step in range(count + 2, line.n):
            aside.step(step)
        aside.finish()
    for s in sends:
        s.wait_send()
    for turn in range(max(0, count - 2), count):
        for c in stores[turn]:
            c.wait()
        core_sends[order[turn]].wait_send()
    for s in folds.values():
        s.wait_send()


def ffn(n2, dy_all, we, wr, bias_e, own=None):
    host = own is not None
    n = lax.axis_size("tensor")
    rows, model = n2.shape
    units = wr.shape[0]
    dp = lax.axis_size("dp")
    count = dp // 2
    dma, anywhere, vmem = DMA, ANY, VMEM
    operands = [n2, dy_all, we, wr, bias_e] + [own] * host
    lines = [jax.ShapeDtypeStruct((rows, model), F32)] * host
    flops = 36 * dp * rows * model * units
    return pl.pallas_call(
        functools.partial(ffn_kernel, host),
        out_shape=(
            jax.ShapeDtypeStruct((rows, model), F32),
            jax.ShapeDtypeStruct((dp * rows, model), BF16),
            jax.ShapeDtypeStruct((dp * rows, units), BF16),
            jax.ShapeDtypeStruct((dp * rows, units), BF16),
            jax.ShapeDtypeStruct((dp * rows, model), BF16),
            *lines,
        ),
        in_specs=[anywhere, anywhere, anywhere, anywhere, vmem] + [anywhere] * host,
        out_specs=(vmem, anywhere, anywhere, anywhere, anywhere) + (vmem,) * host,
        scratch_shapes=[
            pltpu.VMEM((model, units), BF16),
            pltpu.VMEM((units, model), BF16),
            pltpu.VMEM((count, 2 * rows, model), BF16),
            pltpu.VMEM((2, 2 * rows, model), BF16),
            pltpu.VMEM((2, 2 * rows, units), BF16),
            pltpu.VMEM((2, 2 * rows, units), BF16),
            pltpu.VMEM((2, 2 * rows, model), BF16),
            pltpu.VMEM((count, rows, model), BF16),
            pltpu.VMEM((2, rows, model), BF16),
            pltpu.VMEM((count, rows, model), BF16),
            pltpu.VMEM((count - 1, rows, model), BF16),
            dma((n + 1,)), dma, dma((2, 2)), dma((count, 2)), dma((3, 2, 2)),
            dma((count,)), dma((count,)), dma((count,)), dma((count,)),
            dma((count,)), dma((count,)), dma((count - 1,)), dma((count - 1,)),
        ]
        + (LineScatter.scratch(n, rows, model) if host else []),
        compiler_params=pltpu.CompilerParams(
            collective_id=2 if host else 1, has_side_effects=True, vmem_limit_bytes=62 << 20
        ),
        cost_estimate=pl.CostEstimate(
            flops=flops, bytes_accessed=8 * dp * rows * (model + units), transcendentals=dp * rows * units
        ),
        name="ffn_plane",
    )(*operands)


def body(
    tokens,
    parents,
    cotangent,
    first_gain,
    first_shift,
    w_query,
    b_query,
    w_key,
    w_value,
    b_value,
    w_out,
    b_out,
    second_gain,
    second_shift,
    w_expand,
    b_expand,
    w_reduce,
    b_reduce,
):
    dp = lax.axis_size("dp")
    tn = lax.axis_size("tensor")
    dp_me = lax.axis_index("dp")
    tn_me = lax.axis_index("tensor")
    width = w_query.shape[1]
    model = w_query.shape[0] * dp
    units = w_expand.shape[1]
    mine = units // dp
    micros = range(tokens.shape[0])
    last = tokens.shape[0] - 1
    x_low = [tokens[m, 0] for m in micros]
    dy_low = [cotangent[m, 0] for m in micros]
    rows_here = x_low[0].shape[0]
    total = rows_here * tn

    cut = first_gain.shape[0]
    bq_rows, bq_cols = b_query.shape
    be_rows, be_cols = b_expand.shape
    small = jnp.concatenate(
        [first_gain, first_shift, b_out, second_gain, second_shift, b_reduce]
        + [b_query.reshape(-1), b_value.reshape(-1), b_expand.reshape(-1)]
    )
    used = small.shape[0]
    small = jnp.pad(small, (0, -used % 2048)).reshape(-1, 128)
    w_attn = jnp.concatenate([w_query, w_key, w_value, w_out.T], axis=1)
    seq_x0, w_attn, w_e, w_r, small = front(x_low[0], w_attn, w_expand, w_reduce, small)
    w_qkv = w_attn[:, : 3 * width]
    w_ot = w_attn[:, 3 * width :]
    small = small.reshape(dp, -1)[:, :used]
    gain_one, shift_one, bias_out, gain_two, shift_two, bias_red = [
        small[:, i * cut : (i + 1) * cut].reshape(1, model).astype(F32) for i in range(6)
    ]
    at = 6 * cut
    bias_qkv = []
    for i in range(2):
        part = small[:, at : at + bq_rows * bq_cols].reshape(dp, bq_rows, bq_cols)
        bias_qkv.append(part.transpose(1, 0, 2).reshape(1, width).astype(F32))
        at += bq_rows * bq_cols
    bias_qkv = jnp.concatenate([bias_qkv[0], jnp.zeros((1, width), F32), bias_qkv[1]], 1)
    bias_e = small[:, at:].reshape(dp, dp, be_rows // dp, be_cols)
    bias_e = lax.dynamic_index_in_dim(bias_e, dp_me, 1, keepdims=False)
    bias_e = lax.all_gather(bias_e.transpose(1, 0, 2).reshape(1, mine), "tensor", axis=1, tiled=True)
    bias_e = bias_e.astype(F32)

    seq_x = [seq_x0]
    w_r = lax.all_gather(w_r, "tensor", axis=0, tiled=True)
    if mine % 128:
        w_e = lax.all_gather(w_e, "tensor", axis=1, tiled=True)

    normal_one, seq_one, qkv, attended, hidden, normed_two = [], [], [], [], [], []
    out_part, seq_two, activated, d_pre, d_hidden, d_branch, seq_branch = [], [], [], [], [], [], []
    d_qkv, d_one = [], []
    g_gain_two = g_shift_two = g_bias_red = g_bias_out = g_bias_e = 0.0
    g_gain_one = g_shift_one = g_bias_qkv = 0.0
    for m in micros:
        normal_one.append(layer_norm(seq_x[m].astype(F32), 1.0, 0.0))
        seq_one.append((normal_one[m] * gain_one + shift_one).astype(BF16))
        qkv.append(
            (jnp.dot(seq_one[m], w_qkv, preferred_element_type=F32) + bias_qkv).astype(BF16)
        )
        attended.append(attend(parents[m, 0], qkv[m], width))
        branch = over(attended[m], w_ot, 1, 1).astype(BF16)
        if m == 0:
            others = [w_e] if mine % 128 == 0 else []
            branch, *full = exchange(3, lines=[branch], gathers=others, cubes=dy_low)
            w_e = full[0] if others else w_e
            seq_grad = full[len(others) :]
        else:
            branch = lax.psum_scatter(branch, "tensor", scatter_dimension=0, tiled=True).astype(F32)
        if m < last:
            next_x, branch = lax.optimization_barrier((x_low[m + 1], branch))
            next_x = lax.all_gather(next_x, "tensor", axis=0, tiled=True)
        hidden.append(x_low[m].astype(F32) + (branch + bias_out))
        normed_two.append(layer_norm(hidden[m], gain_two, shift_two).astype(BF16))

        def attention_back(k):
            d_att = jnp.dot(seq_branch[k], w_ot, preferred_element_type=F32).astype(BF16)
            d_qkv.append(attend_back(parents[k, 0], qkv[k], d_att, width))
            d_one.append(over(d_qkv[k], w_qkv, 1, 1).astype(BF16))
            part = d_one[k].astype(F32)
            return (
                jnp.sum(part * normal_one[k], 0, keepdims=True),
                jnp.sum(part, 0, keepdims=True),
                jnp.sum(d_qkv[k].astype(F32), 0),
            )

        own = None
        if m:
            seq_branch.append(lax.all_gather(d_branch[m - 1], "tensor", axis=0, tiled=True))
            g_r = over(activated[m - 1], seq_grad[m - 1], 0, 0) + (g_r if m > 1 else 0.0)
            g_et = over(d_pre[m - 1], seq_two[m - 1], 0, 0) + (g_et if m > 1 else 0.0)
            normed_two[m], g_r, g_et = lax.optimization_barrier((normed_two[m], g_r, g_et))
            gain, shift, bias = attention_back(m - 1)
            g_gain_one, g_shift_one = g_gain_one + gain, g_shift_one + shift
            g_bias_qkv = g_bias_qkv + bias
            own = d_one[m - 1]

        d_two, seq, act, dpre, part, *line = ffn(normed_two[m], seq_grad[m], w_e, w_r, bias_e, own)
        if m:
            d_one[m - 1] = line[0]
        seq_two.append(seq)
        activated.append(act)
        d_pre.append(dpre)
        out_part.append(part)
        grad32 = dy_low[m].astype(F32)
        norm_value, norm_pull = jax.vjp(layer_norm, hidden[m], gain_two, shift_two)
        d_norm, g_gain, g_shift = norm_pull(d_two)
        d_hidden.append(grad32 + d_norm)
        d_branch.append(d_hidden[m].astype(BF16))
        g_gain_two = g_gain_two + g_gain
        g_shift_two = g_shift_two + g_shift
        g_bias_red = g_bias_red + jnp.sum(grad32, 0, keepdims=True)
        g_bias_out = g_bias_out + jnp.sum(d_branch[m].astype(F32), 0, keepdims=True)
        g_bias_e = g_bias_e + jnp.sum(dpre.astype(F32), 0)
        if m < last:
            next_x, d_branch[m] = lax.optimization_barrier((next_x, d_branch[m]))
            seq_x.append(next_x)

    def outer(left, right):
        out = None
        for a, b in zip(left, right):
            term = over(a, b, 0, 0)
            out = term if out is None else out + term
        return out.astype(BF16)

    def closing(so_far, left, right):
        term = over(left, right, 0, 0)
        return (term if last == 0 else so_far + term).astype(BF16)

    g_r = closing(g_r, activated[last], seq_grad[last])
    branch_last, g_r = lax.optimization_barrier((d_branch[last], g_r))
    g_r = lax.psum_scatter(g_r, "tensor", scatter_dimension=0, tiled=True)
    *out_sum, full = exchange(4, planes=out_part, gathers=[branch_last])
    full, dpre = lax.optimization_barrier((full, d_pre[last]))
    g_et = closing(g_et, dpre, seq_two[last])
    full, g_et, g_r = lax.optimization_barrier((full, g_et, g_r))
    g_et = lax.psum_scatter(g_et, "tensor", scatter_dimension=0, tiled=True)
    seq_branch.append(full)
    gain, shift, bias = attention_back(last)
    g_gain_one, g_shift_one = g_gain_one + gain, g_shift_one + shift
    g_bias_qkv = g_bias_qkv + bias

    rows = jnp.concatenate(
        [g_gain_one, g_shift_one, g_bias_out, g_gain_two, g_shift_two, g_bias_red], 0
    )
    rows = rows.reshape(6, dp, cut).transpose(1, 0, 2).reshape(dp, 6 * cut)
    row_qv = jnp.concatenate([g_bias_qkv[:width], g_bias_qkv[2 * width :]])
    row_qv = row_qv.reshape(2 * bq_rows, dp, bq_cols).transpose(1, 0, 2)[:, None]
    row_qv = lax.dynamic_update_slice(
        jnp.zeros((dp, tn, 2 * bq_rows, bq_cols), F32), row_qv, (0, tn_me, 0, 0)
    ).reshape(dp, -1)
    row_e = g_bias_e.reshape(tn, be_rows // dp, dp, be_cols).transpose(2, 0, 1, 3)[:, :, None]
    row_e = lax.dynamic_update_slice(
        jnp.zeros((dp, tn, dp, be_rows // dp, be_cols), F32), row_e, (0, 0, dp_me, 0, 0)
    ).reshape(dp, -1)
    little = jnp.concatenate([rows, row_qv, row_e], 1)
    little = jnp.pad(little, ((0, 0), (0, -little.shape[1] % 1024))).reshape(dp, -1, 128)

    g_attn = jnp.concatenate([outer(seq_one, d_qkv), outer(seq_branch, attended)], axis=1)
    d_one[last], g_attn, g_reduce, g_expand, little = exchange(
        5, lines=[d_one[last]], planes=[g_attn], swaps=[g_r, g_et], small=[little]
    )
    g_expand = g_expand.T.astype(F32)
    g_reduce = g_reduce.astype(F32)
    g_query, g_key, g_value = [g_attn[:, i * width : (i + 1) * width] for i in range(3)]
    g_out = g_attn[:, 3 * width :].T
    layer_out = [(hidden[m] + (out_sum[m] + bias_red)).astype(BF16) for m in micros]
    little = little.reshape(-1)
    six = little[: 6 * cut].reshape(6, cut)
    at = 6 * cut
    g_bqv = little[at : at + tn * 2 * bq_rows * bq_cols].reshape(tn, 2 * bq_rows, bq_cols)
    g_bqv = lax.dynamic_index_in_dim(g_bqv, tn_me, 0, keepdims=False)
    g_bq, g_bv = g_bqv[:bq_rows], g_bqv[bq_rows:]
    at += tn * 2 * bq_rows * bq_cols
    g_be = little[at : at + tn * be_rows * be_cols].reshape(tn, be_rows, be_cols)
    g_be = lax.dynamic_index_in_dim(g_be, tn_me, 0, keepdims=False)
    input_grad = []
    for m in micros:
        first_value, first_pull = jax.vjp(
            lambda rows: layer_norm(rows, gain_one, shift_one), x_low[m].astype(F32)
        )
        input_grad.append((d_hidden[m] + first_pull(d_one[m])[0]).astype(BF16))

    return (
        jnp.stack(layer_out, 0)[:, None],
        jnp.stack(input_grad, 0)[:, None],
        six[0],
        six[1],
        g_query,
        g_bq,
        g_key,
        g_value,
        g_bv,
        g_out,
        six[2],
        six[3],
        six[4],
        g_expand,
        g_be,
        g_reduce,
        six[5],
    )


def solution(mesh):
    in_specs = (
        P(None, "dp", "tensor", None),
        P(None, "dp", None),
        P(None, "dp", "tensor", None),
        P("dp"),
        P("dp"),
        P("dp", "tensor"),
        P("tensor", "dp"),
        P("dp", "tensor"),
        P("dp", "tensor"),
        P("tensor", "dp"),
        P("tensor", "dp"),
        P("dp"),
        P("dp"),
        P("dp"),
        P("dp", "tensor"),
        P("tensor", "dp"),
        P("tensor", "dp"),
        P("dp"),
    )
    out_specs = (
        P(None, "dp", "tensor", None),
        P(None, "dp", "tensor", None),
        P("dp"),
        P("dp"),
        P("dp", "tensor"),
        P("tensor", "dp"),
        P("dp", "tensor"),
        P("dp", "tensor"),
        P("tensor", "dp"),
        P("tensor", "dp"),
        P("dp"),
        P("dp"),
        P("dp"),
        P("dp", "tensor"),
        P("tensor", "dp"),
        P("tensor", "dp"),
        P("dp"),
    )
    return jax.shard_map(body, mesh=mesh, in_specs=in_specs, out_specs=out_specs, check_vma=False)
```

```python
import functools
import math

import jax
import jax.numpy as jnp
from jax import lax
from jax.experimental import pallas as pl
from jax.experimental.pallas import tpu as pltpu
from jax.sharding import PartitionSpec as P

HEAD_DIM = 64
BLOCK = 256

F32 = jnp.float32
BF16 = jnp.bfloat16
MESH = pl.DeviceIdType.MESH
DMA = pltpu.SemaphoreType.DMA
GELU = math.sqrt(2.0 / math.pi)


def layer_norm(rows, gain, shift):
    center = rows - jnp.mean(rows, -1, keepdims=True)
    spread = jnp.mean(center * center, -1, keepdims=True)
    return center * lax.rsqrt(spread + 1e-05) * gain + shift


def after(value, *others):
    return lax.optimization_barrier((value,) + others)[0]


def over(left, right, on_left, on_right):
    return lax.dot_general(
        left, right, (((on_left,), (on_right,)), ((), ())), preferred_element_type=F32
    )


def window(index, rows):
    return pl.ds(pl.multiple_of(index * rows, rows), rows)


def remote(src, dst, send, recv, to):
    return pltpu.make_async_remote_copy(
        src_ref=src, dst_ref=dst, send_sem=send, recv_sem=recv,
        device_id=to, device_id_type=MESH,
    )


class Line:
    def __init__(self):
        self.n = lax.axis_size("tensor")
        self.me = lax.axis_index("tensor")
        self.dp = lax.axis_index("dp")

    def at(self, index):
        return (self.dp, index)

    def greet(self, barrier):
        @pl.when(self.me > 0)
        def _():
            pl.semaphore_signal(barrier, inc=1, device_id=self.at(self.me - 1), device_id_type=MESH)

        @pl.when(self.me < self.n - 1)
        def _():
            pl.semaphore_signal(barrier, inc=1, device_id=self.at(self.me + 1), device_id_type=MESH)

    @property
    def size(self):
        return self.n

    def greet_all(self, barrier):
        for k in range(1, self.n):
            pl.semaphore_signal(
                barrier, inc=1, device_id=self.at((self.me + k) % self.n), device_id_type=MESH
            )

    def peers(self):
        return (self.me + self.n - 1) // self.n + (2 * self.n - 2 - self.me) // self.n


class LineGather:
    def __init__(self, line, own, full, sems):
        self.line, self.own, self.full = line, own, full
        self.side = own.shape[0] == full.shape[0]
        self.local, self.up_send, self.up_recv, self.down_send, self.down_recv = sems

    @staticmethod
    def sems(n):
        return [DMA, DMA((n - 1,)), DMA((n - 1,)), DMA((n - 1,)), DMA((n - 1,))]

    def slot(self, index):
        if self.side:
            return self.full.at[:, window(index, self.own.shape[1])]
        return self.full.at[window(index, self.own.shape[0])]

    def hop(self, step, up):
        line = self.line
        if up:
            shard, to = line.me - (step - 1), line.me + 1
            send, recv = self.up_send, self.up_recv
        else:
            shard, to = line.me + (step - 1), line.me - 1
            send, recv = self.down_send, self.down_recv
        there = self.slot(shard)
        src = self.own if step == 1 else there
        return remote(src, there, send.at[step - 1], recv.at[step - 1], line.at(to))

    def sends(self, step, up):
        line = self.line
        if up:
            return (line.me < line.n - 1) & (line.me >= step - 1)
        return (line.me > 0) & (line.me + step - 1 < line.n)

    def takes(self, step, up):
        line = self.line
        return (line.me >= step) if up else (line.me + step < line.n)

    def send(self, step):
        for up in (True, False):
            @pl.when(self.sends(step, up))
            def _():
                self.hop(step, up).start()

    def start(self):
        pltpu.make_async_copy(self.own, self.slot(self.line.me), self.local).start()
        self.send(1)

    def take(self, step):
        for up in (True, False):
            @pl.when(self.takes(step, up))
            def _():
                line = self.line
                shard = (line.me - step) if up else (line.me + step)
                here = self.slot(shard)
                send, recv = (
                    (self.up_send, self.up_recv) if up else (self.down_send, self.down_recv)
                )
                remote(
                    here, here, send.at[step - 1], recv.at[step - 1], line.at(line.me)
                ).wait_recv()
        if step < self.line.n - 1:
            self.send(step + 1)

    def finish(self):
        for step in range(1, self.line.n):
            for up in (True, False):
                @pl.when(self.sends(step, up))
                def _():
                    self.hop(step, up).wait_send()
        pltpu.make_async_copy(self.own, self.slot(self.line.me), self.local).wait()


class LineScatter:
    def __init__(self, line, parts, out, scratch):
        self.line, self.parts, self.out = line, parts, out
        self.rows = out.shape[0]
        (self.own, self.sum, self.come, self.load, self.own_sem, self.send_sem, self.recv_sem) = scratch

    @staticmethod
    def scratch(n, rows, d):
        return [
            pltpu.VMEM((rows, d), BF16),
            pltpu.VMEM((2, n - 1, rows, d), BF16),
            pltpu.VMEM((2, n - 1, rows, d), BF16),
            DMA((2, n - 1)), DMA, DMA((2, n - 1)), DMA((2, n - 1)),
        ]

    def sends(self, step, up):
        line = self.line
        return (line.me <= step - 1) if up else (line.n - 1 - line.me <= step - 1)

    def load_of(self, step, up):
        line = self.line
        chunk = (line.me + line.n - step) if up else (line.me - line.n + step)
        way = 0 if up else 1
        return pltpu.make_async_copy(
            self.parts.at[window(chunk, self.rows)], self.sum.at[way, step - 1], self.load.at[way, step - 1]
        )

    def hop(self, step, up):
        line, way = self.line, 0 if up else 1
        return remote(
            self.sum.at[way, step - 1], self.come.at[way, step - 1],
            self.send_sem.at[way, step - 1], self.recv_sem.at[way, step - 1],
            line.at(line.me + 1 if up else line.me - 1),
        )

    def wait_from(self, step, up):
        line, way = self.line, 0 if up else 1
        remote(
            self.come.at[way, step - 1], self.come.at[way, step - 1],
            self.send_sem.at[way, step - 1], self.recv_sem.at[way, step - 1],
            line.at(line.me),
        ).wait_recv()

    def own_load(self):
        return pltpu.make_async_copy(
            self.parts.at[window(self.line.me, self.rows)], self.own, self.own_sem
        )

    def prepare(self):
        self.own_load().start()
        for step in range(1, self.line.n):
            for up in (True, False):
                @pl.when(self.sends(step, up))
                def _():
                    self.load_of(step, up).start()

    def step(self, step):
        line = self.line
        for up in (True, False):
            way = 0 if up else 1

            @pl.when(self.sends(step, up))
            def _():
                self.load_of(step, up).wait()
                if step > 1:
                    inner = (line.me > 0) if up else (line.me < line.n - 1)

                    @pl.when(inner)
                    def _():
                        self.wait_from(step - 1, up)

                        @pl.loop(0, self.rows // 16)
                        def _(i):
                            part = window(i, 16)
                            self.sum[way, step - 1, part] = (
                                self.sum[way, step - 1, part].astype(F32)
                                + self.come[way, step - 2, part].astype(F32)
                            ).astype(BF16)

                if step > 1:

                    @pl.when(self.sends(step - 1, up))
                    def _():
                        self.hop(step - 1, up).wait_send()

                self.hop(step, up).start()

    def finish(self):
        line, n = self.line, self.line.n
        self.own_load().wait()

        @pl.loop(0, self.rows // 16)
        def _(i):
            part = window(i, 16)
            self.out[part] = self.own[part].astype(F32)

        for up in (True, False):
            way = 0 if up else 1

            @pl.when((line.me > 0) if up else (line.me < n - 1))
            def _():
                self.wait_from(n - 1, up)

                @pl.loop(0, self.rows // 16)
                def _(i):
                    part = window(i, 16)
                    self.out[part] += self.come[way, n - 2, part].astype(F32)

        for up in (True, False):
            @pl.when(self.sends(n - 1, up))
            def _():
                self.hop(n - 1, up).wait_send()


class Cube:
    def __init__(self):
        self.dp = lax.axis_size("dp")
        self.levels = levels = self.dp.bit_length() - 2
        self.count = 1 << levels
        self.me = me = lax.axis_index("dp")
        self.tensor = lax.axis_index("tensor")
        core = me % 2
        flips = []
        for bit in range(1, levels + 1):
            flips.append((1 << bit) * (1 - 2 * ((me // (1 << bit)) % 2)))
        self.steps = [
            flips[l] * (1 - core) + flips[levels - 1 - l] * core for l in range(levels)
        ]
        self.core_step = 1 - 2 * core

    def at(self, index):
        return (index, self.tensor)

    def owner(self, piece):
        mine, other = self.me, self.me + self.core_step
        for l in range(self.levels):
            if piece >> l & 1:
                mine = mine + self.steps[l]
                other = other + self.steps[self.levels - 1 - l]
        return mine, other

    def greet(self, barrier):
        for step in self.steps + [self.core_step]:
            pl.semaphore_signal(
                barrier, inc=1, device_id=self.at(self.me + step), device_id_type=MESH
            )

    @property
    def size(self):
        return self.dp

    def greet_all(self, barrier):
        for k in range(1, self.dp):
            pl.semaphore_signal(
                barrier, inc=1, device_id=self.at((self.me + k) % self.dp), device_id_type=MESH
            )

    def peers(self):
        return self.levels + 1


class CubeGather:
    def __init__(self, cube, own, full, sems):
        self.cube, self.own, self.full = cube, own, full
        self.rows = own.shape[0]
        self.local, self.send_sem, self.recv_sem, self.core_send, self.core_recv = sems
        self.arrived, self.sent = {0}, []

    @staticmethod
    def sems(count):
        return [DMA, DMA((count,)), DMA((count,)), DMA((count,)), DMA((count,))]

    def slot(self, index):
        return self.full.at[window(index, self.rows)]

    def src(self, piece):
        return self.own if piece == 0 else self.slot(self.cube.owner(piece)[0])

    def hop(self, piece, level):
        cube, there = self.cube, piece + (1 << level)
        return remote(
            self.src(piece), self.slot(cube.owner(piece)[0]),
            self.send_sem.at[there], self.recv_sem.at[there], cube.at(cube.me + cube.steps[level]),
        )

    def core(self, piece):
        cube = self.cube
        return remote(
            self.src(piece), self.slot(cube.owner(piece)[0]),
            self.core_send.at[piece], self.core_recv.at[piece], cube.at(cube.me + cube.core_step),
        )

    def give(self, piece):
        for level in range(piece.bit_length(), self.cube.levels):
            self.sent.append(self.hop(piece, level))
            self.sent[-1].start()
        self.sent.append(self.core(piece))
        self.sent[-1].start()

    def start(self):
        self.place = pltpu.make_async_copy(self.own, self.slot(self.cube.me), self.local)
        self.place.start()
        self.give(0)

    def take(self, piece):
        if piece in self.arrived:
            return
        here = self.slot(self.cube.owner(piece)[0])
        remote(
            here, here, self.send_sem.at[piece], self.recv_sem.at[piece], self.cube.at(self.cube.me)
        ).wait_recv()
        self.arrived.add(piece)
        self.give(piece)

    def take_core(self, piece):
        here = self.slot(self.cube.owner(piece)[1])
        remote(
            here, here, self.core_send.at[piece], self.core_recv.at[piece], self.cube.at(self.cube.me)
        ).wait_recv()

    def finish(self):
        for piece in range(self.cube.count):
            self.take(piece)
            self.take_core(piece)
        for copy in self.sent:
            copy.wait_send()
        self.place.wait()


class CubeScatter:
    def __init__(self, cube, parts, out, scratch):
        self.cube, self.parts, self.out = cube, parts, out
        self.rows = out.shape[0]
        (self.keep, self.core_in, self.fold_in, self.load_sem,
         self.core_send, self.core_recv, self.send_sem, self.recv_sem) = scratch

    @staticmethod
    def scratch(count, rows, d):
        return [
            pltpu.VMEM((count, rows, d), BF16),
            pltpu.VMEM((count, rows, d), BF16),
            pltpu.VMEM((count - 1, rows, d), BF16),
            DMA((count,)), DMA((count,)), DMA((count,)), DMA((count - 1,)), DMA((count - 1,)),
        ]

    def load(self, piece):
        return pltpu.make_async_copy(
            self.parts.at[window(self.cube.owner(piece)[0], self.rows)],
            self.keep.at[piece], self.load_sem.at[piece],
        )

    def core(self, piece):
        cube = self.cube
        return remote(
            self.parts.at[window(cube.owner(piece)[1], self.rows)], self.core_in.at[piece],
            self.core_send.at[piece], self.core_recv.at[piece], cube.at(cube.me + cube.core_step),
        )

    def hop(self, piece):
        cube, level = self.cube, piece.bit_length() - 1
        return remote(
            self.keep.at[piece], self.fold_in.at[piece - 1],
            self.send_sem.at[piece - 1], self.recv_sem.at[piece - 1],
            cube.at(cube.me + cube.steps[level]),
        )

    def order(self):
        return sorted(range(self.cube.count), key=lambda p: (-(p.bit_length()), p))

    def start(self):
        for piece in self.order():
            self.core(piece).start()
            self.load(piece).start()

    def add(self, piece, other):
        @pl.loop(0, self.rows // 16)
        def _(i):
            part = window(i, 16)
            self.keep[piece, part] = (
                self.keep[piece, part].astype(F32) + other[part].astype(F32)
            ).astype(BF16)

    def fold(self, piece):
        self.load(piece).wait()
        self.core(piece).wait_recv()
        self.add(piece, self.core_in.at[piece])
        for level in range(self.cube.levels - 1, piece.bit_length() - 1, -1):
            above = piece + (1 << level)
            self.hop(above).wait_recv()
            self.add(piece, self.fold_in.at[above - 1])
        if piece:
            self.hop(piece).start()

    def finish(self):
        self.fold(0)

        @pl.loop(0, self.rows // 16)
        def _(i):
            part = window(i, 16)
            self.out[part] = self.keep[0, part].astype(F32)

        for piece in range(self.cube.count):
            self.core(piece).wait_send()
            if piece:
                self.hop(piece).wait_send()


class Swap:
    def __init__(self, place, moves, sems):
        self.place, self.moves = place, moves
        self.send_sem, self.recv_sem, self.local = sems

    @staticmethod
    def sems(size, moves):
        return [DMA((moves, size)), DMA((moves, size)), DMA((moves,))]

    def copies(self):
        place = self.place
        out = []
        for k in range(1, place.size):
            to = (place.me + k) % place.size
            for m, (src, dst) in enumerate(self.moves):
                out.append(
                    remote(src(to), dst(place.me), self.send_sem.at[m, k], self.recv_sem.at[m, k], place.at(to))
                )
        return out

    def locals(self):
        return [
            pltpu.make_async_copy(src(self.place.me), dst(self.place.me), self.local.at[m])
            for m, (src, dst) in enumerate(self.moves)
        ]

    def start(self):
        for copy in self.copies() + self.locals():
            copy.start()

    def finish(self):
        place = self.place
        for copy in self.copies():
            copy.wait_send()
        for k in range(1, place.size):
            of = (place.me - k + place.size) % place.size
            for m, (src, dst) in enumerate(self.moves):
                here = dst(of)
                remote(here, here, self.send_sem.at[m, k], self.recv_sem.at[m, k], place.at(of)).wait_recv()
        for copy in self.locals():
            copy.wait()


def rows_to_side(src, dst):
    rows, cols = dst.shape[0], src.shape[1]
    return (lambda d: src.at[window(d, rows)], lambda d: dst.at[:, window(d, cols)])


def side_to_rows(src, dst):
    rows, cols = src.shape[0], dst.shape[1]
    return (lambda d: src.at[:, window(d, cols)], lambda d: dst.at[window(d, rows)])


ANY = pl.BlockSpec(memory_space=pl.ANY)
VMEM = pl.BlockSpec(memory_space=pltpu.VMEM)


def front_kernel(
    x_ref, w_ref, wo_ref, we_ref, wr_ref, small_ref,
    seq_ref, w_out, wo_line, wo_out, we_out, wr_out, small_out, *sems
):
    line, cube = Line(), Cube()
    gather = LineGather(line, x_ref, seq_ref, sems[:5])
    wide = LineGather(line, wo_ref, wo_line, sems[5:10])
    weights = CubeGather(cube, w_ref, w_out, sems[10:15])
    outer = CubeGather(cube, wo_line, wo_out, sems[15:20])
    tile = small_ref.shape[0]
    moves = [
        (lambda d: small_ref, lambda d: small_out.at[window(d, tile)]),
        rows_to_side(wr_ref, wr_out),
    ]
    if wr_out.shape[0] % 128 == 0:
        moves.append(side_to_rows(we_ref, we_out))
    swap = Swap(cube, moves, sems[20:23])
    barrier = pltpu.get_barrier_semaphore()
    line.greet(barrier)
    cube.greet_all(barrier)
    pl.semaphore_wait(barrier, cube.dp - 1 + line.peers())
    wide.start()
    gather.start()
    weights.start()
    wide.take(1)
    wide.take(2)
    gather.take(1)
    for step in range(3, line.n):
        wide.take(step)
    for piece in range(1, cube.count):
        if piece.bit_length() < cube.levels:
            weights.take(piece)
    wide.finish()
    outer.start()
    swap.start()
    gather.take(2)
    for piece in range(1, cube.count):
        weights.take(piece)
    for piece in range(1, cube.count):
        outer.take(piece)
    for step in range(3, line.n):
        gather.take(step)
    weights.finish()
    outer.finish()
    swap.finish()
    gather.finish()


def front(x, w, w_o, w_e, w_r, small):
    dp, n = lax.axis_size("dp"), lax.axis_size("tensor")
    rows, model = x.shape
    seq, w_all, _, o_all, e_all, r_all, small_all = pl.pallas_call(
        front_kernel,
        out_shape=(
            jax.ShapeDtypeStruct((n * rows, model), BF16),
            jax.ShapeDtypeStruct((dp * w.shape[0], w.shape[1]), BF16),
            jax.ShapeDtypeStruct((w_o.shape[0], n * w_o.shape[1]), BF16),
            jax.ShapeDtypeStruct((dp * w_o.shape[0], n * w_o.shape[1]), BF16),
            jax.ShapeDtypeStruct((dp * w_e.shape[0], w_e.shape[1] // dp), BF16),
            jax.ShapeDtypeStruct((w_r.shape[0] // dp, w_r.shape[1] * dp), BF16),
            jax.ShapeDtypeStruct((dp * small.shape[0], small.shape[1]), BF16),
        ),
        in_specs=[ANY] * 6,
        out_specs=(ANY,) * 7,
        scratch_shapes=2 * LineGather.sems(n) + 2 * CubeGather.sems(dp // 2) + Swap.sems(dp, 3),
        compiler_params=pltpu.CompilerParams(collective_id=0, has_side_effects=True),
        cost_estimate=pl.CostEstimate(flops=80 * 10**9, bytes_accessed=10**7, transcendentals=0),
        name="front",
    )(x, w, w_o, w_e, w_r, small)
    if r_all.shape[0] % 128:
        e_all = lax.all_to_all(w_e, "dp", split_axis=1, concat_axis=0, tiled=True)
    return seq, w_all, o_all, e_all, r_all, small_all


class SmallSum:
    def __init__(self, line, cube, parts, out, scratch):
        self.line, self.cube, self.parts, self.out = line, cube, parts, out
        self.come, self.gather, self.sems, self.line_send, self.line_recv = (
            scratch[0], scratch[1], scratch[2:5], scratch[5], scratch[6]
        )
        moves = [(lambda d: parts.at[d], lambda d: self.come.at[d])]
        self.swap = Swap(cube, moves, self.sems)

    @staticmethod
    def scratch(dp, n, rows, d):
        return [
            pltpu.VMEM((dp, rows, d), F32),
            pltpu.VMEM((n, rows, d), F32),
            *Swap.sems(dp, 1),
            DMA((n,)), DMA((n,)),
        ]

    def hop(self, k):
        line = self.line
        here = self.gather.at[line.me]
        return remote(
            here, here, self.line_send.at[k], self.line_recv.at[k], line.at((line.me + k) % line.n)
        )

    def middle(self):
        self.swap.finish()
        total = self.come[0]
        for d in range(1, self.cube.dp):
            total = total + self.come[d]
        self.gather[self.line.me] = total
        for k in range(1, self.line.n):
            self.hop(k).start()

    def finish(self):
        line = self.line
        for k in range(1, line.n):
            here = self.gather.at[(line.me - k + line.n) % line.n]
            remote(
                here, here, self.line_send.at[k], self.line_recv.at[k], line.at(line.me)
            ).wait_recv()
            self.hop(k).wait_send()
        total = self.gather[0]
        for z in range(1, line.n):
            total = total + self.gather[z]
        self.out[...] = total


def exchange_kernel(counts, *refs):
    lines, planes, gathers, cubes, swaps, outs, backs, small = counts
    line, cube = Line(), Cube()
    count = sum(counts)
    pairs, scratch = list(zip(refs[:count], refs[count : 2 * count])), list(refs[2 * count :])

    def take(number):
        taken = tuple(scratch[:number])
        del scratch[:number]
        return taken

    sums = [LineScatter(line, *pairs.pop(0), take(7)) for _ in range(lines)]
    folds = [CubeScatter(cube, *pairs.pop(0), take(8)) for _ in range(planes)]
    lanes = [LineGather(line, *pairs.pop(0), take(5)) for _ in range(gathers)]
    wholes = [CubeGather(cube, *pairs.pop(0), take(5)) for _ in range(cubes)]
    moves = [side_to_rows(*pairs.pop(0)) for _ in range(swaps)]
    swap = Swap(cube, moves, take(3)) if swaps else None
    turns = [rows_to_side(*pairs.pop(0)) for _ in range(outs)]
    turns += [side_to_rows(*pairs.pop(0)) for _ in range(backs)]
    turn = Swap(line, turns, take(3)) if turns else None
    little = SmallSum(line, cube, *pairs.pop(0), take(7)) if small else None
    barrier = pltpu.get_barrier_semaphore()
    peers = 0
    if small or turns:
        line.greet_all(barrier)
        peers = line.n - 1
    elif lines or gathers:
        line.greet(barrier)
        peers = line.peers()
    if small or swaps:
        cube.greet_all(barrier)
        peers = peers + cube.dp - 1
    elif planes or cubes:
        cube.greet(barrier)
        peers = peers + cube.peers()
    for s in sums:
        s.prepare()
    pl.semaphore_wait(barrier, peers)
    if turns:
        turn.start()
    if small:
        little.swap.start()
    for s in sums:
        s.step(1)
    for lane in lanes:
        lane.start()
    for whole in wholes[:1]:
        whole.start()
    for f in folds:
        f.start()
    if small:
        little.middle()
    pieces = [p for p in folds[0].order() if p] if planes else []
    per = -(-len(pieces) // (line.n - 1))
    for step in range(1, line.n):
        for whole in wholes[step - 1 : step]:
            for piece in range(1, cube.count):
                if piece.bit_length() < cube.levels:
                    whole.take(piece)
        if step > 1:
            for s in sums:
                s.step(step)
            for lane in lanes:
                lane.take(step - 1)
        for piece in pieces[:per]:
            for f in folds:
                f.fold(piece)
        pieces = pieces[per:]
        if step == 1 and swaps:
            swap.start()
        for whole in wholes[step - 1 : step]:
            whole.finish()
        for whole in wholes[step : step + 1]:
            whole.start()
    for f in folds:
        f.finish()
    for lane in lanes:
        lane.take(line.n - 1)
        lane.finish()
    for s in sums:
        s.finish()
    if turns:
        turn.finish()
    if swaps:
        swap.finish()
    if small:
        little.finish()


def exchange(
    collective_id, lines=(), planes=(), gathers=(), cubes=(), swaps=(), outs=(), backs=(), small=()
):
    dp, n = lax.axis_size("dp"), lax.axis_size("tensor")
    groups = (lines, planes, gathers, cubes, swaps, outs, backs, small)
    counts = tuple(len(group) for group in groups)
    operands = [part for group in groups for part in group]
    out_shape, out_specs, scratch = [], [], []

    def result(rows, d, kind, spec):
        out_shape.append(jax.ShapeDtypeStruct((rows, d), kind))
        out_specs.append(spec)

    for part in lines:
        rows, d = part.shape[0] // n, part.shape[1]
        result(rows, d, F32, VMEM)
        scratch += LineScatter.scratch(n, rows, d)
    for part in planes:
        rows, d = part.shape[0] // dp, part.shape[1]
        result(rows, d, F32, VMEM)
        scratch += CubeScatter.scratch(dp // 2, rows, d)
    for part in gathers:
        result(n * part.shape[0], part.shape[1], BF16, ANY)
        scratch += LineGather.sems(n)
    for part in cubes:
        result(dp * part.shape[0], part.shape[1], BF16, ANY)
        scratch += CubeGather.sems(dp // 2)
    for part in swaps:
        result(dp * part.shape[0], part.shape[1] // dp, BF16, ANY)
    if swaps:
        scratch += Swap.sems(dp, len(swaps))
    for part in outs:
        result(part.shape[0] // n, part.shape[1] * n, BF16, ANY)
    for part in backs:
        result(part.shape[0] * n, part.shape[1] // n, BF16, ANY)
    if outs or backs:
        scratch += Swap.sems(n, len(outs) + len(backs))
    for part in small:
        rows, d = part.shape[1:]
        result(rows, d, F32, VMEM)
        scratch += SmallSum.scratch(dp, n, rows, d)
    return pl.pallas_call(
        functools.partial(exchange_kernel, counts),
        out_shape=tuple(out_shape),
        in_specs=[ANY] * len(operands),
        out_specs=tuple(out_specs),
        scratch_shapes=scratch,
        compiler_params=pltpu.CompilerParams(
            collective_id=collective_id, has_side_effects=True, vmem_limit_bytes=60 << 20
        ),
        cost_estimate=pl.CostEstimate(flops=80 * 10**9, bytes_accessed=10**7, transcendentals=0),
        name="exchange",
    )(*operands)


PAIR = 2 * HEAD_DIM
NEVER = -1e30


def lane_of(shape, head):
    lane = lax.broadcasted_iota(jnp.int32, shape, 1)
    return (lane < HEAD_DIM) if head == 0 else (lane >= HEAD_DIM)


def sight(parents_ref, row, col):
    at = jnp.int32(row)
    seen = at == col
    for hop in range(row - col):
        at = parents_ref[at]
        seen = seen | (at == col)
    return jnp.where(seen, 0.0, NEVER).astype(F32)


def masked_scores(parents_ref, q_head, k_ref, row):
    scores = []
    for col in range(row + 1):
        part = over(q_head, k_ref[col * BLOCK : (col + 1) * BLOCK, :], 1, 1)
        if col == row:
            below = lax.broadcasted_iota(jnp.int32, part.shape, 1) <= lax.broadcasted_iota(
                jnp.int32, part.shape, 0
            )
            part = jnp.where(below, part, NEVER)
        else:
            part = part + sight(parents_ref, row, col)
        scores.append(part)
    return scores


def row_reduce(parts, fold, reduce):
    return reduce(functools.reduce(fold, parts), axis=-1, keepdims=True)


def attend_kernel(parents_ref, q_ref, k_ref, v_ref, out_ref):
    blocks = q_ref.shape[0] // BLOCK
    scale = 1.0 / math.sqrt(HEAD_DIM)
    for row in range(blocks):
        here = slice(row * BLOCK, (row + 1) * BLOCK)
        heads = []
        for head in range(2):
            q_head = q_ref[here, :].astype(F32) * scale
            q_head = jnp.where(lane_of(q_head.shape, head), q_head, 0.0).astype(BF16)
            scores = masked_scores(parents_ref, q_head, k_ref, row)
            top = row_reduce(scores, jnp.maximum, jnp.max)
            probs = [jnp.exp(s - top) for s in scores]
            total = row_reduce(probs, jnp.add, jnp.sum)
            out = None
            for col in range(row + 1):
                term = over(
                    probs[col].astype(BF16), v_ref[col * BLOCK : (col + 1) * BLOCK, :], 1, 0
                )
                out = term if out is None else out + term
            heads.append(out / total)
        mixed = jnp.where(lane_of(heads[0].shape, 0), heads[0], heads[1])
        out_ref[here, :] = mixed.astype(out_ref.dtype)


def attend(parents, qkv, width):
    rows = qkv.shape[0]
    pairs = width // PAIR
    spec = lambda part: pl.BlockSpec((rows, PAIR), lambda p, parents: (0, part * pairs + p))
    blocks = rows // BLOCK
    work = pairs * 2 * (blocks * (blocks + 1) // 2) * BLOCK * BLOCK
    return pl.pallas_call(
        attend_kernel,
        out_shape=jax.ShapeDtypeStruct((rows, width), BF16),
        grid_spec=pltpu.PrefetchScalarGridSpec(
            num_scalar_prefetch=1,
            grid=(pairs,),
            in_specs=[spec(0), spec(1), spec(2)],
            out_specs=pl.BlockSpec((rows, PAIR), lambda p, parents: (0, p)),
        ),
        compiler_params=pltpu.CompilerParams(vmem_limit_bytes=48 << 20),
        cost_estimate=pl.CostEstimate(
            flops=work * PAIR * 24, bytes_accessed=rows * width * 8, transcendentals=work
        ),
        name="attend",
    )(parents, qkv, qkv, qkv)


def attend_back_kernel(parents_ref, q_ref, k_ref, v_ref, g_ref, out_ref, dq_s, dk_s, dv_s):
    part = pl.program_id(1)
    blocks = q_ref.shape[0] // BLOCK
    scale = 1.0 / math.sqrt(HEAD_DIM)

    @pl.when(part == 0)
    def _():
        for row in range(blocks):
            here = slice(row * BLOCK, (row + 1) * BLOCK)
            dq_heads = []
            for head in range(2):
                lanes = lane_of((BLOCK, PAIR), head)
                q_head = jnp.where(lanes, q_ref[here, :].astype(F32) * scale, 0.0).astype(BF16)
                g_head = jnp.where(lanes, g_ref[here, :].astype(F32), 0.0).astype(BF16)
                scores = masked_scores(parents_ref, q_head, k_ref, row)
                top = row_reduce(scores, jnp.maximum, jnp.max)
                probs = [jnp.exp(s - top) for s in scores]
                rest = 1.0 / row_reduce(probs, jnp.add, jnp.sum)
                probs = [p * rest for p in probs]
                d_probs = [
                    over(g_head, v_ref[col * BLOCK : (col + 1) * BLOCK, :], 1, 1)
                    for col in range(row + 1)
                ]
                level = row_reduce([p * d for p, d in zip(probs, d_probs)], jnp.add, jnp.sum)
                dq = None
                for col in range(row + 1):
                    there = slice(col * BLOCK, (col + 1) * BLOCK)
                    d_scores = (probs[col] * (d_probs[col] - level)).astype(BF16)
                    term = over(d_scores, k_ref[there, :], 1, 0)
                    dq = term if dq is None else dq + term
                    dk = over(d_scores, q_head, 0, 0)
                    dv = over(probs[col].astype(BF16), g_head, 0, 0)
                    if row == col and head == 0:
                        dk_s[there, :] = dk
                        dv_s[there, :] = dv
                    else:
                        dk_s[there, :] += dk
                        dv_s[there, :] += dv
                dq_heads.append(dq * scale)
            dq_s[here, :] = jnp.where(lane_of((BLOCK, PAIR), 0), dq_heads[0], dq_heads[1]).astype(
                BF16
            )
        out_ref[...] = dq_s[...]

    @pl.when(part == 1)
    def _():
        out_ref[...] = dk_s[...].astype(BF16)

    @pl.when(part == 2)
    def _():
        out_ref[...] = dv_s[...].astype(BF16)


def attend_back(parents, qkv, grad, width):
    rows = qkv.shape[0]
    pairs = width // PAIR
    spec = lambda part: pl.BlockSpec((rows, PAIR), lambda p, c, parents: (0, part * pairs + p))
    blocks = rows // BLOCK
    work = pairs * 2 * (blocks * (blocks + 1) // 2) * BLOCK * BLOCK
    return pl.pallas_call(
        attend_back_kernel,
        out_shape=jax.ShapeDtypeStruct((rows, 3 * width), BF16),
        grid_spec=pltpu.PrefetchScalarGridSpec(
            num_scalar_prefetch=1,
            grid=(pairs, 3),
            in_specs=[
                spec(0),
                spec(1),
                spec(2),
                pl.BlockSpec((rows, PAIR), lambda p, c, parents: (0, p)),
            ],
            out_specs=pl.BlockSpec((rows, PAIR), lambda p, c, parents: (0, c * pairs + p)),
            scratch_shapes=[
                pltpu.VMEM((rows, PAIR), BF16),
                pltpu.VMEM((rows, PAIR), F32),
                pltpu.VMEM((rows, PAIR), F32),
            ],
        ),
        compiler_params=pltpu.CompilerParams(vmem_limit_bytes=48 << 20),
        cost_estimate=pl.CostEstimate(
            flops=work * PAIR * 60, bytes_accessed=rows * width * 14, transcendentals=work
        ),
        name="attend_back",
    )(parents, qkv, qkv, qkv, grad)


def ffn_kernel(host, n2_ref, dy_ref, we_ref, wr_ref, be_ref, *refs):
    if host:
        line_own, refs = refs[0], refs[1:]
    sum_ref, seq_ref, act_ref, dpre_ref, part_ref = refs[:5]
    refs = refs[5:]
    if host:
        line_full, refs = refs[0], refs[1:]
    we, wr, seq, dy_st, act_st, dpre_st, part_st, keep, give, core_in, fold_in = refs[:11]
    refs = refs[1:]
    w_sem, own_sem, dy_sem, seq_sem, st_sem = refs[10:15]
    ag_send, ag_recv, agc_send, agc_recv, rsc_send, rsc_recv, fold_send, fold_recv = refs[15:23]
    cube = Cube()
    levels, me, steps, core_step = cube.levels, cube.me, cube.steps, cube.core_step
    count, at, owner = cube.count, cube.at, cube.owner
    rows, model = n2_ref.shape
    units = wr_ref.shape[0]
    barrier = pltpu.get_barrier_semaphore()
    cube.greet(barrier)
    hosted = []
    if host:
        line = Line()
        line.greet(barrier)
        aside = LineScatter(line, line_own, line_full, refs[23:])
        aside.prepare()
    load_own = pltpu.make_async_copy(n2_ref, seq.at[0, pl.ds(0, rows)], own_sem)
    load_own.start()
    parts = we_ref.shape[0] // model
    mine_units = we_ref.shape[1]
    loads_w = [pltpu.make_async_copy(wr_ref, wr, w_sem.at[parts])]
    for part in range(parts):
        loads_w.append(
            pltpu.make_async_copy(
                we_ref.at[pl.ds(part * model, model)],
                we.at[:, pl.ds(part * mine_units, mine_units)],
                w_sem.at[part],
            )
        )
    for c in loads_w:
        c.start()

    def load_dy(piece, slot):
        mine, other = owner(piece)
        out = []
        for half, index in enumerate((mine, other)):
            out.append(
                pltpu.make_async_copy(
                    dy_ref.at[pl.ds(pl.multiple_of(index * rows, rows), rows)],
                    dy_st.at[slot, pl.ds(half * rows, rows)],
                    dy_sem.at[slot, half],
                )
            )
        return out

    def gather_copy(piece, level):
        there = piece + (1 << level)
        return remote(
            seq.at[piece, pl.ds(0, rows)], seq.at[there, pl.ds(0, rows)],
            ag_send.at[there], ag_recv.at[there], at(me + steps[level]),
        )

    def gather_core(piece):
        return remote(
            seq.at[piece, pl.ds(0, rows)], seq.at[piece, pl.ds(rows, rows)],
            agc_send.at[piece], agc_recv.at[piece], at(me + core_step),
        )

    order = [0] + sorted(range(1, count), key=lambda p: (-(p.bit_length()), p))
    slots = {piece: i % 2 for i, piece in enumerate(order)}
    loads = {order[0]: load_dy(order[0], 0)}
    for c in loads[order[0]]:
        c.start()

    load_own.wait()
    pl.semaphore_wait(barrier, cube.peers() + (line.peers() if host else 0))
    if host:
        aside.step(1)
    sends = []
    for level in range(levels):
        sends.append(gather_copy(0, level))
        sends[-1].start()
    sends.append(gather_core(0))
    sends[-1].start()
    for c in loads_w:
        c.wait()

    arrived = {0}

    def take(piece):
        if piece in arrived:
            return
        low = piece - (1 << (piece.bit_length() - 1))
        gather_copy(low, piece.bit_length() - 1).wait_recv()
        arrived.add(piece)
        for level in range(piece.bit_length(), levels):
            sends.append(gather_copy(piece, level))
            sends[-1].start()
        sends.append(gather_core(piece))
        sends[-1].start()

    stores = {}
    outs = {}
    core_sends = {}
    folds = {}
    done_core = set()

    def add(piece, other):
        @pl.loop(0, rows // 16)
        def _(i):
            part = pl.ds(pl.multiple_of(i * 16, 16), 16)
            keep[piece, part] = (
                keep[piece, part].astype(F32) + other[part].astype(F32)
            ).astype(BF16)

    def add_core(piece):
        if piece in done_core:
            return
        core_copy(piece).wait_recv()
        add(piece, core_in.at[piece])
        done_core.add(piece)

    def core_copy(piece):
        return remote(
            give.at[slots[piece]], core_in.at[piece],
            rsc_send.at[piece], rsc_recv.at[piece], at(me + core_step),
        )

    def fold_copy(piece):
        level = piece.bit_length() - 1
        low = piece - (1 << level)
        return remote(
            keep.at[piece], fold_in.at[piece - 1],
            fold_send.at[piece - 1], fold_recv.at[piece - 1], at(me + steps[level]),
        )

    def fold(piece):
        add_core(piece)
        for level in range(levels - 1, piece.bit_length() - 1, -1):
            above = piece + (1 << level)
            fold_copy(above).wait_recv()
            add(piece, fold_in.at[above - 1])
        if piece:
            folds[piece] = fold_copy(piece)
            folds[piece].start()

    chunk = 256
    wide = 512
    for turn, piece in enumerate(order):
        slot = turn % 2
        for earlier in range(1, piece + 1):
            take(earlier)
        gather_core(piece).wait_recv()
        for c in loads[piece]:
            c.wait()
        if turn + 1 < count:
            loads[order[turn + 1]] = load_dy(order[turn + 1], 1 - slot)
            for c in loads[order[turn + 1]]:
                c.start()
        if turn >= 2:
            for c in stores[turn - 2]:
                c.wait()
            core_sends[order[turn - 2]].wait_send()

        @pl.loop(0, units // chunk)
        def _(i):
            cols = pl.ds(pl.multiple_of(i * chunk, chunk), chunk)
            pre = over(seq[piece], we[:, cols], 1, 0) + be_ref[:, cols]
            d_act = over(dy_st[slot], wr[cols, :], 1, 1)
            square = pre * pre
            t = jnp.tanh(GELU * pre * (1.0 + 0.044715 * square))
            act_st[slot, :, cols] = (0.5 * pre * (1.0 + t)).astype(BF16)
            slope = 0.5 * (1.0 + t) + (0.5 * GELU) * pre * (1.0 - t * t) * (
                1.0 + (3 * 0.044715) * square
            )
            dpre_st[slot, :, cols] = (d_act * slope).astype(BF16)

        @pl.loop(0, model // wide)
        def _(i):
            cols = pl.ds(pl.multiple_of(i * wide, wide), wide)
            d_two = over(dpre_st[slot], we[cols, :], 1, 1).astype(BF16)
            keep[piece, :, cols] = d_two[:rows]
            give[slot, :, cols] = d_two[rows:]
            out = over(act_st[slot], wr[:, cols], 1, 0).astype(BF16)
            part_st[slot, :, cols] = out

        if host and turn < line.n - 2:
            aside.step(turn + 2)
        core_sends[piece] = core_copy(piece)
        core_sends[piece].start()
        mine, other = owner(piece)
        stores[turn] = []
        for half, index in enumerate((mine, other)):
            to = pl.ds(pl.multiple_of(index * rows, rows), rows)
            part = pl.ds(half * rows, rows)
            stores[turn].append(
                pltpu.make_async_copy(act_st.at[slot, part], act_ref.at[to], st_sem.at[0, slot, half])
            )
            stores[turn].append(
                pltpu.make_async_copy(dpre_st.at[slot, part], dpre_ref.at[to], st_sem.at[1, slot, half])
            )
            stores[turn].append(
                pltpu.make_async_copy(part_st.at[slot, part], part_ref.at[to], st_sem.at[2, slot, half])
            )
            stores[turn].append(
                pltpu.make_async_copy(seq.at[piece, part], seq_ref.at[to], seq_sem.at[piece, half])
            )
        for c in stores[turn]:
            c.start()
        if piece.bit_length() == levels:
            fold(piece)
    for level in range(levels - 2, -1, -1):
        for piece in range((1 << level), 2 << level):
            fold(piece)
    add_core(0)
    for level in range(levels):
        fold_copy(1 << level).wait_recv()

    @pl.loop(0, rows // 16)
    def _(i):
        part = pl.ds(pl.multiple_of(i * 16, 16), 16)
        total = keep[0, part].astype(F32)
        for level in range(levels):
            total = total + fold_in[(1 << level) - 1, part].astype(F32)
        sum_ref[part] = total

    if host:
        for step in range(count + 2, line.n):
            aside.step(step)
        aside.finish()
    for s in sends:
        s.wait_send()
    for turn in range(max(0, count - 2), count):
        for c in stores[turn]:
            c.wait()
        core_sends[order[turn]].wait_send()
    for s in folds.values():
        s.wait_send()


def ffn(n2, dy_all, we, wr, bias_e, own=None):
    host = own is not None
    n = lax.axis_size("tensor")
    rows, model = n2.shape
    units = wr.shape[0]
    dp = lax.axis_size("dp")
    count = dp // 2
    dma, anywhere, vmem = DMA, ANY, VMEM
    operands = [n2, dy_all, we, wr, bias_e] + [own] * host
    lines = [jax.ShapeDtypeStruct((rows, model), F32)] * host
    flops = 36 * dp * rows * model * units
    return pl.pallas_call(
        functools.partial(ffn_kernel, host),
        out_shape=(
            jax.ShapeDtypeStruct((rows, model), F32),
            jax.ShapeDtypeStruct((dp * rows, model), BF16),
            jax.ShapeDtypeStruct((dp * rows, units), BF16),
            jax.ShapeDtypeStruct((dp * rows, units), BF16),
            jax.ShapeDtypeStruct((dp * rows, model), BF16),
            *lines,
        ),
        in_specs=[anywhere, anywhere, anywhere, anywhere, vmem] + [anywhere] * host,
        out_specs=(vmem, anywhere, anywhere, anywhere, anywhere) + (vmem,) * host,
        scratch_shapes=[
            pltpu.VMEM((model, units), BF16),
            pltpu.VMEM((units, model), BF16),
            pltpu.VMEM((count, 2 * rows, model), BF16),
            pltpu.VMEM((2, 2 * rows, model), BF16),
            pltpu.VMEM((2, 2 * rows, units), BF16),
            pltpu.VMEM((2, 2 * rows, units), BF16),
            pltpu.VMEM((2, 2 * rows, model), BF16),
            pltpu.VMEM((count, rows, model), BF16),
            pltpu.VMEM((2, rows, model), BF16),
            pltpu.VMEM((count, rows, model), BF16),
            pltpu.VMEM((count - 1, rows, model), BF16),
            dma((n + 1,)), dma, dma((2, 2)), dma((count, 2)), dma((3, 2, 2)),
            dma((count,)), dma((count,)), dma((count,)), dma((count,)),
            dma((count,)), dma((count,)), dma((count - 1,)), dma((count - 1,)),
        ]
        + (LineScatter.scratch(n, rows, model) if host else []),
        compiler_params=pltpu.CompilerParams(
            collective_id=2 if host else 1, has_side_effects=True, vmem_limit_bytes=62 << 20
        ),
        cost_estimate=pl.CostEstimate(
            flops=flops, bytes_accessed=8 * dp * rows * (model + units), transcendentals=dp * rows * units
        ),
        name="ffn_plane",
    )(*operands)


def body(
    tokens,
    parents,
    cotangent,
    first_gain,
    first_shift,
    w_query,
    b_query,
    w_key,
    w_value,
    b_value,
    w_out,
    b_out,
    second_gain,
    second_shift,
    w_expand,
    b_expand,
    w_reduce,
    b_reduce,
):
    dp = lax.axis_size("dp")
    tn = lax.axis_size("tensor")
    dp_me = lax.axis_index("dp")
    tn_me = lax.axis_index("tensor")
    width = w_query.shape[1]
    model = w_query.shape[0] * dp
    units = w_expand.shape[1]
    mine = units // dp
    micros = range(tokens.shape[0])
    last = tokens.shape[0] - 1
    x_low = [tokens[m, 0] for m in micros]
    dy_low = [cotangent[m, 0] for m in micros]
    rows_here = x_low[0].shape[0]
    total = rows_here * tn

    cut = first_gain.shape[0]
    bq_rows, bq_cols = b_query.shape
    be_rows, be_cols = b_expand.shape
    small = jnp.concatenate(
        [first_gain, first_shift, b_out, second_gain, second_shift, b_reduce]
        + [b_query.reshape(-1), b_value.reshape(-1), b_expand.reshape(-1)]
    )
    used = small.shape[0]
    small = jnp.pad(small, (0, -used % 2048)).reshape(-1, 128)
    w_qkv = jnp.concatenate([w_query, w_key, w_value], axis=1)
    seq_x0, w_qkv, w_ot, w_e, w_r, small = front(
        x_low[0], w_qkv, w_out.T, w_expand, w_reduce, small
    )
    small = small.reshape(dp, -1)[:, :used]
    gain_one, shift_one, bias_out, gain_two, shift_two, bias_red = [
        small[:, i * cut : (i + 1) * cut].reshape(1, model).astype(F32) for i in range(6)
    ]
    at = 6 * cut
    bias_qkv = []
    for i in range(2):
        part = small[:, at : at + bq_rows * bq_cols].reshape(dp, bq_rows, bq_cols)
        bias_qkv.append(part.transpose(1, 0, 2).reshape(1, width).astype(F32))
        at += bq_rows * bq_cols
    bias_qkv = jnp.concatenate([bias_qkv[0], jnp.zeros((1, width), F32), bias_qkv[1]], 1)
    bias_e = small[:, at:].reshape(dp, dp, be_rows // dp, be_cols)
    bias_e = lax.dynamic_index_in_dim(bias_e, dp_me, 1, keepdims=False)
    bias_e = bias_e.transpose(1, 0, 2).reshape(mine)
    bias_e = jnp.pad(bias_e, (0, -mine % 2048)).reshape(-1, 128)

    seq_x = [seq_x0]
    w_r = lax.all_gather(w_r, "tensor", axis=0, tiled=True)
    w_e = lax.all_gather(w_e, "tensor", axis=1 if mine % 128 else 0, tiled=True)

    normal_one, seq_one, qkv, attended, hidden, normed_two = [], [], [], [], [], []
    out_part, seq_two, activated, d_pre, d_hidden, d_branch, out_sum = [], [], [], [], [], [], []
    d_qkv, d_one, d_att, row_attended = [], [], [], []
    g_gain_two = g_shift_two = g_bias_red = g_bias_out = g_bias_e = 0.0
    g_gain_one = g_shift_one = g_bias_qkv = 0.0
    for m in micros:
        normal_one.append(layer_norm(seq_x[m].astype(F32), 1.0, 0.0))
        seq_one.append((normal_one[m] * gain_one + shift_one).astype(BF16))
        qkv.append(
            (jnp.dot(seq_one[m], w_qkv, preferred_element_type=F32) + bias_qkv).astype(BF16)
        )
        attended.append(attend(parents[m, 0], qkv[m], width))
        if m == 0:
            bias_e, *seq_grad, row_att = exchange(
                3, gathers=[bias_e], cubes=dy_low, outs=[attended[m]]
            )
            bias_e = bias_e.reshape(tn, -1)[:, :mine].reshape(1, tn * mine).astype(F32)
        else:
            part, row_att, col_grad = exchange(
                4, planes=[out_part[m - 1]], outs=[attended[m]], backs=[d_att[m - 1]]
            )
            out_sum.append(part)
            d_att[m - 1] = col_grad
        if m < last:
            next_x, row_att = lax.optimization_barrier((x_low[m + 1], row_att))
            next_x = lax.all_gather(next_x, "tensor", axis=0, tiled=True)
        row_attended.append(row_att)
        branch = over(row_att, w_ot, 1, 1)
        hidden.append(x_low[m].astype(F32) + (branch + bias_out))
        normed_two.append(layer_norm(hidden[m], gain_two, shift_two).astype(BF16))

        def attention_back(k):
            d_qkv.append(attend_back(parents[k, 0], qkv[k], d_att[k], width))
            d_one.append(over(d_qkv[k], w_qkv, 1, 1).astype(BF16))
            part = d_one[k].astype(F32)
            return (
                jnp.sum(part * normal_one[k], 0, keepdims=True),
                jnp.sum(part, 0, keepdims=True),
                jnp.sum(d_qkv[k].astype(F32), 0),
            )

        own = None
        if m:
            gain, shift, bias = attention_back(m - 1)
            g_gain_one, g_shift_one = g_gain_one + gain, g_shift_one + shift
            g_bias_qkv = g_bias_qkv + bias
            own = d_one[m - 1]

        d_two, seq, act, dpre, part, *line = ffn(normed_two[m], seq_grad[m], w_e, w_r, bias_e, own)
        if m:
            d_one[m - 1] = line[0]
        seq_two.append(seq)
        activated.append(act)
        d_pre.append(dpre)
        out_part.append(part)
        grad32 = dy_low[m].astype(F32)
        norm_value, norm_pull = jax.vjp(layer_norm, hidden[m], gain_two, shift_two)
        d_norm, g_gain, g_shift = norm_pull(d_two)
        d_hidden.append(grad32 + d_norm)
        d_branch.append(d_hidden[m].astype(BF16))
        d_att.append(jnp.dot(d_branch[m], w_ot, preferred_element_type=F32).astype(BF16))
        g_gain_two = g_gain_two + g_gain
        g_shift_two = g_shift_two + g_shift
        g_bias_red = g_bias_red + jnp.sum(grad32, 0, keepdims=True)
        g_bias_out = g_bias_out + jnp.sum(d_branch[m].astype(F32), 0, keepdims=True)
        g_bias_e = g_bias_e + jnp.sum(dpre.astype(F32), 0)
        if m < last:
            next_x, d_branch[m] = lax.optimization_barrier((next_x, d_branch[m]))
            seq_x.append(next_x)

    def outer(left, right):
        out = None
        for a, b in zip(left, right):
            term = over(a, b, 0, 0)
            out = term if out is None else out + term
        return out.astype(BF16)

    g_r = outer(activated, seq_grad)
    d_att[last], g_r = lax.optimization_barrier((d_att[last], g_r))
    g_r = lax.psum_scatter(g_r, "tensor", scatter_dimension=0, tiled=True)
    g_ot = outer(d_branch, row_attended)
    g_ot, d_att[last] = exchange(6, planes=[g_ot], backs=[d_att[last]])
    g_et = outer(d_pre, seq_two)
    g_et, g_r = lax.optimization_barrier((g_et, g_r))
    g_et = lax.psum_scatter(g_et, "tensor", scatter_dimension=0, tiled=True)
    gain, shift, bias = attention_back(last)
    g_gain_one, g_shift_one = g_gain_one + gain, g_shift_one + shift
    g_bias_qkv = g_bias_qkv + bias

    rows = jnp.concatenate(
        [g_gain_one, g_shift_one, g_bias_out, g_gain_two, g_shift_two, g_bias_red], 0
    )
    rows = rows.reshape(6, dp, cut).transpose(1, 0, 2).reshape(dp, 6 * cut)
    row_qv = jnp.concatenate([g_bias_qkv[:width], g_bias_qkv[2 * width :]])
    row_qv = row_qv.reshape(2 * bq_rows, dp, bq_cols).transpose(1, 0, 2)[:, None]
    row_qv = lax.dynamic_update_slice(
        jnp.zeros((dp, tn, 2 * bq_rows, bq_cols), F32), row_qv, (0, tn_me, 0, 0)
    ).reshape(dp, -1)
    row_e = g_bias_e.reshape(tn, be_rows // dp, dp, be_cols).transpose(2, 0, 1, 3)[:, :, None]
    row_e = lax.dynamic_update_slice(
        jnp.zeros((dp, tn, dp, be_rows // dp, be_cols), F32), row_e, (0, 0, dp_me, 0, 0)
    ).reshape(dp, -1)
    little = jnp.concatenate([rows, row_qv, row_e], 1)
    little = jnp.pad(little, ((0, 0), (0, -little.shape[1] % 1024))).reshape(dp, -1, 128)

    g_qkv = outer(seq_one, d_qkv)
    g_ot = g_ot.astype(BF16).reshape(-1, tn, width).transpose(1, 0, 2).reshape(-1, width)
    d_one[last], g_ot, g_qkv, out_last, g_reduce, g_expand, little = exchange(
        5,
        lines=[d_one[last], g_ot],
        planes=[g_qkv, out_part[last]],
        swaps=[g_r, g_et],
        small=[little],
    )
    out_sum.append(out_last)
    g_query, g_key, g_value = [g_qkv[:, i * width : (i + 1) * width] for i in range(3)]
    g_out = g_ot.T
    g_expand = g_expand.T.astype(F32)
    g_reduce = g_reduce.astype(F32)
    layer_out = [(hidden[m] + (out_sum[m] + bias_red)).astype(BF16) for m in micros]
    little = little.reshape(-1)
    six = little[: 6 * cut].reshape(6, cut)
    at = 6 * cut
    g_bqv = little[at : at + tn * 2 * bq_rows * bq_cols].reshape(tn, 2 * bq_rows, bq_cols)
    g_bqv = lax.dynamic_index_in_dim(g_bqv, tn_me, 0, keepdims=False)
    g_bq, g_bv = g_bqv[:bq_rows], g_bqv[bq_rows:]
    at += tn * 2 * bq_rows * bq_cols
    g_be = little[at : at + tn * be_rows * be_cols].reshape(tn, be_rows, be_cols)
    g_be = lax.dynamic_index_in_dim(g_be, tn_me, 0, keepdims=False)
    input_grad = []
    for m in micros:
        first_value, first_pull = jax.vjp(
            lambda rows: layer_norm(rows, gain_one, shift_one), x_low[m].astype(F32)
        )
        input_grad.append((d_hidden[m] + first_pull(d_one[m])[0]).astype(BF16))

    return (
        jnp.stack(layer_out, 0)[:, None],
        jnp.stack(input_grad, 0)[:, None],
        six[0],
        six[1],
        g_query,
        g_bq,
        g_key,
        g_value,
        g_bv,
        g_out,
        six[2],
        six[3],
        six[4],
        g_expand,
        g_be,
        g_reduce,
        six[5],
    )


def solution(mesh):
    in_specs = (
        P(None, "dp", "tensor", None),
        P(None, "dp", None),
        P(None, "dp", "tensor", None),
        P("dp"),
        P("dp"),
        P("dp", "tensor"),
        P("tensor", "dp"),
        P("dp", "tensor"),
        P("dp", "tensor"),
        P("tensor", "dp"),
        P("tensor", "dp"),
        P("dp"),
        P("dp"),
        P("dp"),
        P("dp", "tensor"),
        P("tensor", "dp"),
        P("tensor", "dp"),
        P("dp"),
    )
    out_specs = (
        P(None, "dp", "tensor", None),
        P(None, "dp", "tensor", None),
        P("dp"),
        P("dp"),
        P("dp", "tensor"),
        P("tensor", "dp"),
        P("dp", "tensor"),
        P("dp", "tensor"),
        P("tensor", "dp"),
        P("tensor", "dp"),
        P("dp"),
        P("dp"),
        P("dp"),
        P("dp", "tensor"),
        P("tensor", "dp"),
        P("tensor", "dp"),
        P("dp"),
    )
    return jax.shard_map(body, mesh=mesh, in_specs=in_specs, out_specs=out_specs, check_vma=False)
```

```python
import functools
import math

import jax
import jax.numpy as jnp
from jax import lax
from jax.experimental import pallas as pl
from jax.experimental.pallas import tpu as pltpu
from jax.sharding import PartitionSpec as P

HEAD_DIM = 64
BLOCK = 256

F32 = jnp.float32
BF16 = jnp.bfloat16
MESH = pl.DeviceIdType.MESH
DMA = pltpu.SemaphoreType.DMA
GELU = math.sqrt(2.0 / math.pi)


def layer_norm(rows, gain, shift):
    center = rows - jnp.mean(rows, -1, keepdims=True)
    spread = jnp.mean(center * center, -1, keepdims=True)
    return center * lax.rsqrt(spread + 1e-05) * gain + shift


def after(value, *others):
    return lax.optimization_barrier((value,) + others)[0]


def over(left, right, on_left, on_right):
    return lax.dot_general(
        left, right, (((on_left,), (on_right,)), ((), ())), preferred_element_type=F32
    )


def window(index, rows):
    return pl.ds(pl.multiple_of(index * rows, rows), rows)


def remote(src, dst, send, recv, to):
    return pltpu.make_async_remote_copy(
        src_ref=src, dst_ref=dst, send_sem=send, recv_sem=recv,
        device_id=to, device_id_type=MESH,
    )


class Line:
    def __init__(self):
        self.n = lax.axis_size("tensor")
        self.me = lax.axis_index("tensor")
        self.dp = lax.axis_index("dp")

    def at(self, index):
        return (self.dp, index)

    def greet(self, barrier):
        @pl.when(self.me > 0)
        def _():
            pl.semaphore_signal(barrier, inc=1, device_id=self.at(self.me - 1), device_id_type=MESH)

        @pl.when(self.me < self.n - 1)
        def _():
            pl.semaphore_signal(barrier, inc=1, device_id=self.at(self.me + 1), device_id_type=MESH)

    @property
    def size(self):
        return self.n

    def greet_all(self, barrier):
        for k in range(1, self.n):
            pl.semaphore_signal(
                barrier, inc=1, device_id=self.at((self.me + k) % self.n), device_id_type=MESH
            )

    def peers(self):
        return (self.me + self.n - 1) // self.n + (2 * self.n - 2 - self.me) // self.n


class LineGather:
    def __init__(self, line, own, full, sems):
        self.line, self.own, self.full = line, own, full
        self.side = own.shape[0] == full.shape[0]
        self.local, self.up_send, self.up_recv, self.down_send, self.down_recv = sems

    @staticmethod
    def sems(n):
        return [DMA, DMA((n - 1,)), DMA((n - 1,)), DMA((n - 1,)), DMA((n - 1,))]

    def slot(self, index):
        if self.side:
            return self.full.at[:, window(index, self.own.shape[1])]
        return self.full.at[window(index, self.own.shape[0])]

    def hop(self, step, up):
        line = self.line
        if up:
            shard, to = line.me - (step - 1), line.me + 1
            send, recv = self.up_send, self.up_recv
        else:
            shard, to = line.me + (step - 1), line.me - 1
            send, recv = self.down_send, self.down_recv
        there = self.slot(shard)
        src = self.own if step == 1 else there
        return remote(src, there, send.at[step - 1], recv.at[step - 1], line.at(to))

    def sends(self, step, up):
        line = self.line
        if up:
            return (line.me < line.n - 1) & (line.me >= step - 1)
        return (line.me > 0) & (line.me + step - 1 < line.n)

    def takes(self, step, up):
        line = self.line
        return (line.me >= step) if up else (line.me + step < line.n)

    def send(self, step):
        for up in (True, False):
            @pl.when(self.sends(step, up))
            def _():
                self.hop(step, up).start()

    def start(self):
        pltpu.make_async_copy(self.own, self.slot(self.line.me), self.local).start()
        self.send(1)

    def take(self, step):
        for up in (True, False):
            @pl.when(self.takes(step, up))
            def _():
                line = self.line
                shard = (line.me - step) if up else (line.me + step)
                here = self.slot(shard)
                send, recv = (
                    (self.up_send, self.up_recv) if up else (self.down_send, self.down_recv)
                )
                remote(
                    here, here, send.at[step - 1], recv.at[step - 1], line.at(line.me)
                ).wait_recv()
        if step < self.line.n - 1:
            self.send(step + 1)

    def finish(self):
        for step in range(1, self.line.n):
            for up in (True, False):
                @pl.when(self.sends(step, up))
                def _():
                    self.hop(step, up).wait_send()
        pltpu.make_async_copy(self.own, self.slot(self.line.me), self.local).wait()


class LineScatter:
    def __init__(self, line, parts, out, scratch):
        self.line, self.parts, self.out = line, parts, out
        self.rows = out.shape[0]
        (self.own, self.sum, self.come, self.load, self.own_sem, self.send_sem, self.recv_sem) = scratch

    @staticmethod
    def scratch(n, rows, d):
        return [
            pltpu.VMEM((rows, d), BF16),
            pltpu.VMEM((2, n - 1, rows, d), BF16),
            pltpu.VMEM((2, n - 1, rows, d), BF16),
            DMA((2, n - 1)), DMA, DMA((2, n - 1)), DMA((2, n - 1)),
        ]

    def sends(self, step, up):
        line = self.line
        return (line.me <= step - 1) if up else (line.n - 1 - line.me <= step - 1)

    def load_of(self, step, up):
        line = self.line
        chunk = (line.me + line.n - step) if up else (line.me - line.n + step)
        way = 0 if up else 1
        return pltpu.make_async_copy(
            self.parts.at[window(chunk, self.rows)], self.sum.at[way, step - 1], self.load.at[way, step - 1]
        )

    def hop(self, step, up):
        line, way = self.line, 0 if up else 1
        return remote(
            self.sum.at[way, step - 1], self.come.at[way, step - 1],
            self.send_sem.at[way, step - 1], self.recv_sem.at[way, step - 1],
            line.at(line.me + 1 if up else line.me - 1),
        )

    def wait_from(self, step, up):
        line, way = self.line, 0 if up else 1
        remote(
            self.come.at[way, step - 1], self.come.at[way, step - 1],
            self.send_sem.at[way, step - 1], self.recv_sem.at[way, step - 1],
            line.at(line.me),
        ).wait_recv()

    def own_load(self):
        return pltpu.make_async_copy(
            self.parts.at[window(self.line.me, self.rows)], self.own, self.own_sem
        )

    def prepare(self):
        self.own_load().start()
        for step in range(1, self.line.n):
            for up in (True, False):
                @pl.when(self.sends(step, up))
                def _():
                    self.load_of(step, up).start()

    def step(self, step):
        line = self.line
        for up in (True, False):
            way = 0 if up else 1

            @pl.when(self.sends(step, up))
            def _():
                self.load_of(step, up).wait()
                if step > 1:
                    inner = (line.me > 0) if up else (line.me < line.n - 1)

                    @pl.when(inner)
                    def _():
                        self.wait_from(step - 1, up)

                        @pl.loop(0, self.rows // 16)
                        def _(i):
                            part = window(i, 16)
                            self.sum[way, step - 1, part] = (
                                self.sum[way, step - 1, part].astype(F32)
                                + self.come[way, step - 2, part].astype(F32)
                            ).astype(BF16)

                if step > 1:

                    @pl.when(self.sends(step - 1, up))
                    def _():
                        self.hop(step - 1, up).wait_send()

                self.hop(step, up).start()

    def finish(self):
        line, n = self.line, self.line.n
        self.own_load().wait()

        @pl.loop(0, self.rows // 16)
        def _(i):
            part = window(i, 16)
            self.out[part] = self.own[part].astype(F32)

        for up in (True, False):
            way = 0 if up else 1

            @pl.when((line.me > 0) if up else (line.me < n - 1))
            def _():
                self.wait_from(n - 1, up)

                @pl.loop(0, self.rows // 16)
                def _(i):
                    part = window(i, 16)
                    self.out[part] += self.come[way, n - 2, part].astype(F32)

        for up in (True, False):
            @pl.when(self.sends(n - 1, up))
            def _():
                self.hop(n - 1, up).wait_send()


class Cube:
    def __init__(self):
        self.dp = lax.axis_size("dp")
        self.levels = levels = self.dp.bit_length() - 2
        self.count = 1 << levels
        self.me = me = lax.axis_index("dp")
        self.tensor = lax.axis_index("tensor")
        core = me % 2
        flips = []
        for bit in range(1, levels + 1):
            flips.append((1 << bit) * (1 - 2 * ((me // (1 << bit)) % 2)))
        self.steps = [
            flips[l] * (1 - core) + flips[levels - 1 - l] * core for l in range(levels)
        ]
        self.core_step = 1 - 2 * core

    def at(self, index):
        return (index, self.tensor)

    def owner(self, piece):
        mine, other = self.me, self.me + self.core_step
        for l in range(self.levels):
            if piece >> l & 1:
                mine = mine + self.steps[l]
                other = other + self.steps[self.levels - 1 - l]
        return mine, other

    def greet(self, barrier):
        for step in self.steps + [self.core_step]:
            pl.semaphore_signal(
                barrier, inc=1, device_id=self.at(self.me + step), device_id_type=MESH
            )

    @property
    def size(self):
        return self.dp

    def greet_all(self, barrier):
        for k in range(1, self.dp):
            pl.semaphore_signal(
                barrier, inc=1, device_id=self.at((self.me + k) % self.dp), device_id_type=MESH
            )

    def peers(self):
        return self.levels + 1


class CubeGather:
    def __init__(self, cube, own, full, sems):
        self.cube, self.own, self.full = cube, own, full
        self.rows = own.shape[0]
        self.local, self.send_sem, self.recv_sem, self.core_send, self.core_recv = sems
        self.arrived, self.sent = {0}, []

    @staticmethod
    def sems(count):
        return [DMA, DMA((count,)), DMA((count,)), DMA((count,)), DMA((count,))]

    def slot(self, index):
        return self.full.at[window(index, self.rows)]

    def src(self, piece):
        return self.own if piece == 0 else self.slot(self.cube.owner(piece)[0])

    def hop(self, piece, level):
        cube, there = self.cube, piece + (1 << level)
        return remote(
            self.src(piece), self.slot(cube.owner(piece)[0]),
            self.send_sem.at[there], self.recv_sem.at[there], cube.at(cube.me + cube.steps[level]),
        )

    def core(self, piece):
        cube = self.cube
        return remote(
            self.src(piece), self.slot(cube.owner(piece)[0]),
            self.core_send.at[piece], self.core_recv.at[piece], cube.at(cube.me + cube.core_step),
        )

    def give(self, piece):
        for level in range(piece.bit_length(), self.cube.levels):
            self.sent.append(self.hop(piece, level))
            self.sent[-1].start()
        self.sent.append(self.core(piece))
        self.sent[-1].start()

    def start(self):
        self.place = pltpu.make_async_copy(self.own, self.slot(self.cube.me), self.local)
        self.place.start()
        self.give(0)

    def take(self, piece):
        if piece in self.arrived:
            return
        here = self.slot(self.cube.owner(piece)[0])
        remote(
            here, here, self.send_sem.at[piece], self.recv_sem.at[piece], self.cube.at(self.cube.me)
        ).wait_recv()
        self.arrived.add(piece)
        self.give(piece)

    def take_core(self, piece):
        here = self.slot(self.cube.owner(piece)[1])
        remote(
            here, here, self.core_send.at[piece], self.core_recv.at[piece], self.cube.at(self.cube.me)
        ).wait_recv()

    def finish(self):
        for piece in range(self.cube.count):
            self.take(piece)
            self.take_core(piece)
        for copy in self.sent:
            copy.wait_send()
        self.place.wait()


class CubeScatter:
    def __init__(self, cube, parts, out, scratch):
        self.cube, self.parts, self.out = cube, parts, out
        self.rows = out.shape[0]
        (self.keep, self.core_in, self.fold_in, self.load_sem,
         self.core_send, self.core_recv, self.send_sem, self.recv_sem) = scratch

    @staticmethod
    def scratch(count, rows, d):
        return [
            pltpu.VMEM((count, rows, d), BF16),
            pltpu.VMEM((count, rows, d), BF16),
            pltpu.VMEM((count - 1, rows, d), BF16),
            DMA((count,)), DMA((count,)), DMA((count,)), DMA((count - 1,)), DMA((count - 1,)),
        ]

    def load(self, piece):
        return pltpu.make_async_copy(
            self.parts.at[window(self.cube.owner(piece)[0], self.rows)],
            self.keep.at[piece], self.load_sem.at[piece],
        )

    def core(self, piece):
        cube = self.cube
        return remote(
            self.parts.at[window(cube.owner(piece)[1], self.rows)], self.core_in.at[piece],
            self.core_send.at[piece], self.core_recv.at[piece], cube.at(cube.me + cube.core_step),
        )

    def hop(self, piece):
        cube, level = self.cube, piece.bit_length() - 1
        return remote(
            self.keep.at[piece], self.fold_in.at[piece - 1],
            self.send_sem.at[piece - 1], self.recv_sem.at[piece - 1],
            cube.at(cube.me + cube.steps[level]),
        )

    def order(self):
        return sorted(range(self.cube.count), key=lambda p: (-(p.bit_length()), p))

    def start(self):
        for piece in self.order():
            self.core(piece).start()
            self.load(piece).start()

    def add(self, piece, other):
        @pl.loop(0, self.rows // 16)
        def _(i):
            part = window(i, 16)
            self.keep[piece, part] = (
                self.keep[piece, part].astype(F32) + other[part].astype(F32)
            ).astype(BF16)

    def fold(self, piece):
        self.load(piece).wait()
        self.core(piece).wait_recv()
        self.add(piece, self.core_in.at[piece])
        for level in range(self.cube.levels - 1, piece.bit_length() - 1, -1):
            above = piece + (1 << level)
            self.hop(above).wait_recv()
            self.add(piece, self.fold_in.at[above - 1])
        if piece:
            self.hop(piece).start()

    def finish(self):
        self.fold(0)

        @pl.loop(0, self.rows // 16)
        def _(i):
            part = window(i, 16)
            self.out[part] = self.keep[0, part].astype(F32)

        for piece in range(self.cube.count):
            self.core(piece).wait_send()
            if piece:
                self.hop(piece).wait_send()


class Swap:
    def __init__(self, place, moves, sems):
        self.place, self.moves = place, moves
        self.send_sem, self.recv_sem, self.local = sems

    @staticmethod
    def sems(size, moves):
        return [DMA((moves, size)), DMA((moves, size)), DMA((moves,))]

    def copies(self):
        place = self.place
        out = []
        for k in range(1, place.size):
            to = (place.me + k) % place.size
            for m, (src, dst) in enumerate(self.moves):
                out.append(
                    remote(src(to), dst(place.me), self.send_sem.at[m, k], self.recv_sem.at[m, k], place.at(to))
                )
        return out

    def locals(self):
        return [
            pltpu.make_async_copy(src(self.place.me), dst(self.place.me), self.local.at[m])
            for m, (src, dst) in enumerate(self.moves)
        ]

    def start(self):
        for copy in self.copies() + self.locals():
            copy.start()

    def finish(self):
        place = self.place
        for copy in self.copies():
            copy.wait_send()
        for k in range(1, place.size):
            of = (place.me - k + place.size) % place.size
            for m, (src, dst) in enumerate(self.moves):
                here = dst(of)
                remote(here, here, self.send_sem.at[m, k], self.recv_sem.at[m, k], place.at(of)).wait_recv()
        for copy in self.locals():
            copy.wait()


def rows_to_side(src, dst):
    rows, cols = dst.shape[0], src.shape[1]
    return (lambda d: src.at[window(d, rows)], lambda d: dst.at[:, window(d, cols)])


def side_to_rows(src, dst):
    rows, cols = src.shape[0], dst.shape[1]
    return (lambda d: src.at[:, window(d, cols)], lambda d: dst.at[window(d, rows)])


ANY = pl.BlockSpec(memory_space=pl.ANY)
VMEM = pl.BlockSpec(memory_space=pltpu.VMEM)


def front_kernel(
    x_ref, w_ref, wo_ref, we_ref, wr_ref, small_ref,
    seq_ref, w_out, wo_line, we_out, wr_out, small_out, *sems
):
    line, cube = Line(), Cube()
    gather = LineGather(line, x_ref, seq_ref, sems[:5])
    wide = LineGather(line, wo_ref, wo_line, sems[5:10])
    weights = CubeGather(cube, w_ref, w_out, sems[10:15])
    tile = small_ref.shape[0]
    moves = [
        (lambda d: small_ref, lambda d: small_out.at[window(d, tile)]),
        rows_to_side(wr_ref, wr_out),
    ]
    if wr_out.shape[0] % 128 == 0:
        moves.append(side_to_rows(we_ref, we_out))
    swap = Swap(cube, moves, sems[15:18])
    barrier = pltpu.get_barrier_semaphore()
    line.greet(barrier)
    cube.greet_all(barrier)
    pl.semaphore_wait(barrier, cube.dp - 1 + line.peers())
    gather.start()
    weights.start()
    gather.take(1)
    for piece in range(1, cube.count):
        if piece.bit_length() < cube.levels:
            weights.take(piece)
    swap.start()
    gather.take(2)
    wide.start()
    for piece in range(1, cube.count):
        weights.take(piece)
    wide.take(1)
    for step in range(3, line.n):
        gather.take(step)
        wide.take(step - 1)
    wide.take(line.n - 1)
    weights.finish()
    swap.finish()
    gather.finish()
    wide.finish()


def front(x, w, w_o, w_e, w_r, small):
    dp, n = lax.axis_size("dp"), lax.axis_size("tensor")
    rows, model = x.shape
    seq, w_all, o_line, e_all, r_all, small_all = pl.pallas_call(
        front_kernel,
        out_shape=(
            jax.ShapeDtypeStruct((n * rows, model), BF16),
            jax.ShapeDtypeStruct((dp * w.shape[0], w.shape[1]), BF16),
            jax.ShapeDtypeStruct((w_o.shape[0], n * w_o.shape[1]), BF16),
            jax.ShapeDtypeStruct((dp * w_e.shape[0], w_e.shape[1] // dp), BF16),
            jax.ShapeDtypeStruct((w_r.shape[0] // dp, w_r.shape[1] * dp), BF16),
            jax.ShapeDtypeStruct((dp * small.shape[0], small.shape[1]), BF16),
        ),
        in_specs=[ANY] * 6,
        out_specs=(ANY,) * 6,
        scratch_shapes=2 * LineGather.sems(n) + CubeGather.sems(dp // 2) + Swap.sems(dp, 3),
        compiler_params=pltpu.CompilerParams(collective_id=0, has_side_effects=True),
        cost_estimate=pl.CostEstimate(flops=80 * 10**9, bytes_accessed=10**7, transcendentals=0),
        name="front",
    )(x, w, w_o, w_e, w_r, small)
    if r_all.shape[0] % 128:
        e_all = lax.all_to_all(w_e, "dp", split_axis=1, concat_axis=0, tiled=True)
    return seq, w_all, o_line, e_all, r_all, small_all


class SmallSum:
    def __init__(self, line, cube, parts, out, scratch):
        self.line, self.cube, self.parts, self.out = line, cube, parts, out
        self.come, self.gather, self.sems, self.line_send, self.line_recv = (
            scratch[0], scratch[1], scratch[2:5], scratch[5], scratch[6]
        )
        moves = [(lambda d: parts.at[d], lambda d: self.come.at[d])]
        self.swap = Swap(cube, moves, self.sems)

    @staticmethod
    def scratch(dp, n, rows, d):
        return [
            pltpu.VMEM((dp, rows, d), F32),
            pltpu.VMEM((n, rows, d), F32),
            *Swap.sems(dp, 1),
            DMA((n,)), DMA((n,)),
        ]

    def hop(self, k):
        line = self.line
        here = self.gather.at[line.me]
        return remote(
            here, here, self.line_send.at[k], self.line_recv.at[k], line.at((line.me + k) % line.n)
        )

    def middle(self):
        self.swap.finish()
        total = self.come[0]
        for d in range(1, self.cube.dp):
            total = total + self.come[d]
        self.gather[self.line.me] = total
        for k in range(1, self.line.n):
            self.hop(k).start()

    def finish(self):
        line = self.line
        for k in range(1, line.n):
            here = self.gather.at[(line.me - k + line.n) % line.n]
            remote(
                here, here, self.line_send.at[k], self.line_recv.at[k], line.at(line.me)
            ).wait_recv()
            self.hop(k).wait_send()
        total = self.gather[0]
        for z in range(1, line.n):
            total = total + self.gather[z]
        self.out[...] = total


def exchange_kernel(counts, *refs):
    lines, planes, gathers, cubes, swaps, outs, backs, small = counts
    line, cube = Line(), Cube()
    count = sum(counts)
    pairs, scratch = list(zip(refs[:count], refs[count : 2 * count])), list(refs[2 * count :])

    def take(number):
        taken = tuple(scratch[:number])
        del scratch[:number]
        return taken

    sums = [LineScatter(line, *pairs.pop(0), take(7)) for _ in range(lines)]
    folds = [CubeScatter(cube, *pairs.pop(0), take(8)) for _ in range(planes)]
    lanes = [LineGather(line, *pairs.pop(0), take(5)) for _ in range(gathers)]
    wholes = [CubeGather(cube, *pairs.pop(0), take(5)) for _ in range(cubes)]
    moves = [side_to_rows(*pairs.pop(0)) for _ in range(swaps)]
    swap = Swap(cube, moves, take(3)) if swaps else None
    turns = [rows_to_side(*pairs.pop(0)) for _ in range(outs)]
    turns += [side_to_rows(*pairs.pop(0)) for _ in range(backs)]
    turn = Swap(line, turns, take(3)) if turns else None
    little = SmallSum(line, cube, *pairs.pop(0), take(7)) if small else None
    barrier = pltpu.get_barrier_semaphore()
    peers = 0
    if small or turns:
        line.greet_all(barrier)
        peers = line.n - 1
    elif lines or gathers:
        line.greet(barrier)
        peers = line.peers()
    if small or swaps:
        cube.greet_all(barrier)
        peers = peers + cube.dp - 1
    elif planes or cubes:
        cube.greet(barrier)
        peers = peers + cube.peers()
    for s in sums:
        s.prepare()
    pl.semaphore_wait(barrier, peers)
    if turns:
        turn.start()
    if small:
        little.swap.start()
    for s in sums:
        s.step(1)
    for lane in lanes:
        lane.start()
    for whole in wholes[:1]:
        whole.start()
    for f in folds:
        f.start()
    if small:
        little.middle()
    pieces = [p for p in folds[0].order() if p] if planes else []
    per = -(-len(pieces) // (line.n - 1))
    for step in range(1, line.n):
        for whole in wholes[step - 1 : step]:
            for piece in range(1, cube.count):
                if piece.bit_length() < cube.levels:
                    whole.take(piece)
        if step > 1:
            for s in sums:
                s.step(step)
            for lane in lanes:
                lane.take(step - 1)
        for piece in pieces[:per]:
            for f in folds:
                f.fold(piece)
        pieces = pieces[per:]
        if step == 1 and swaps:
            swap.start()
        for whole in wholes[step - 1 : step]:
            whole.finish()
        for whole in wholes[step : step + 1]:
            whole.start()
    for f in folds:
        f.finish()
    for lane in lanes:
        lane.take(line.n - 1)
        lane.finish()
    for s in sums:
        s.finish()
    if turns:
        turn.finish()
    if swaps:
        swap.finish()
    if small:
        little.finish()


def exchange(
    collective_id, lines=(), planes=(), gathers=(), cubes=(), swaps=(), outs=(), backs=(), small=()
):
    dp, n = lax.axis_size("dp"), lax.axis_size("tensor")
    groups = (lines, planes, gathers, cubes, swaps, outs, backs, small)
    counts = tuple(len(group) for group in groups)
    operands = [part for group in groups for part in group]
    out_shape, out_specs, scratch = [], [], []

    def result(rows, d, kind, spec):
        out_shape.append(jax.ShapeDtypeStruct((rows, d), kind))
        out_specs.append(spec)

    for part in lines:
        rows, d = part.shape[0] // n, part.shape[1]
        result(rows, d, F32, VMEM)
        scratch += LineScatter.scratch(n, rows, d)
    for part in planes:
        rows, d = part.shape[0] // dp, part.shape[1]
        result(rows, d, F32, VMEM)
        scratch += CubeScatter.scratch(dp // 2, rows, d)
    for part in gathers:
        result(n * part.shape[0], part.shape[1], BF16, ANY)
        scratch += LineGather.sems(n)
    for part in cubes:
        result(dp * part.shape[0], part.shape[1], BF16, ANY)
        scratch += CubeGather.sems(dp // 2)
    for part in swaps:
        result(dp * part.shape[0], part.shape[1] // dp, BF16, ANY)
    if swaps:
        scratch += Swap.sems(dp, len(swaps))
    for part in outs:
        result(part.shape[0] // n, part.shape[1] * n, BF16, ANY)
    for part in backs:
        result(part.shape[0] * n, part.shape[1] // n, BF16, ANY)
    if outs or backs:
        scratch += Swap.sems(n, len(outs) + len(backs))
    for part in small:
        rows, d = part.shape[1:]
        result(rows, d, F32, VMEM)
        scratch += SmallSum.scratch(dp, n, rows, d)
    return pl.pallas_call(
        functools.partial(exchange_kernel, counts),
        out_shape=tuple(out_shape),
        in_specs=[ANY] * len(operands),
        out_specs=tuple(out_specs),
        scratch_shapes=scratch,
        compiler_params=pltpu.CompilerParams(
            collective_id=collective_id, has_side_effects=True, vmem_limit_bytes=60 << 20
        ),
        cost_estimate=pl.CostEstimate(flops=80 * 10**9, bytes_accessed=10**7, transcendentals=0),
        name="exchange",
    )(*operands)


PAIR = 2 * HEAD_DIM
NEVER = -1e30


def lane_of(shape, head):
    lane = lax.broadcasted_iota(jnp.int32, shape, 1)
    return (lane < HEAD_DIM) if head == 0 else (lane >= HEAD_DIM)


def sight(parents_ref, row, col):
    at = jnp.int32(row)
    seen = at == col
    for hop in range(row - col):
        at = parents_ref[at]
        seen = seen | (at == col)
    return jnp.where(seen, 0.0, NEVER).astype(F32)


def masked_scores(parents_ref, q_head, k_ref, row):
    scores = []
    for col in range(row + 1):
        part = over(q_head, k_ref[col * BLOCK : (col + 1) * BLOCK, :], 1, 1)
        if col == row:
            below = lax.broadcasted_iota(jnp.int32, part.shape, 1) <= lax.broadcasted_iota(
                jnp.int32, part.shape, 0
            )
            part = jnp.where(below, part, NEVER)
        else:
            part = part + sight(parents_ref, row, col)
        scores.append(part)
    return scores


def row_reduce(parts, fold, reduce):
    return reduce(functools.reduce(fold, parts), axis=-1, keepdims=True)


def attend_kernel(parents_ref, q_ref, k_ref, v_ref, out_ref):
    blocks = q_ref.shape[0] // BLOCK
    scale = 1.0 / math.sqrt(HEAD_DIM)
    for row in range(blocks):
        here = slice(row * BLOCK, (row + 1) * BLOCK)
        heads = []
        for head in range(2):
            q_head = q_ref[here, :].astype(F32) * scale
            q_head = jnp.where(lane_of(q_head.shape, head), q_head, 0.0).astype(BF16)
            scores = masked_scores(parents_ref, q_head, k_ref, row)
            top = row_reduce(scores, jnp.maximum, jnp.max)
            probs = [jnp.exp(s - top) for s in scores]
            total = row_reduce(probs, jnp.add, jnp.sum)
            out = None
            for col in range(row + 1):
                term = over(
                    probs[col].astype(BF16), v_ref[col * BLOCK : (col + 1) * BLOCK, :], 1, 0
                )
                out = term if out is None else out + term
            heads.append(out / total)
        mixed = jnp.where(lane_of(heads[0].shape, 0), heads[0], heads[1])
        out_ref[here, :] = mixed.astype(out_ref.dtype)


def attend(parents, qkv, width):
    rows = qkv.shape[0]
    pairs = width // PAIR
    spec = lambda part: pl.BlockSpec((rows, PAIR), lambda p, parents: (0, part * pairs + p))
    blocks = rows // BLOCK
    work = pairs * 2 * (blocks * (blocks + 1) // 2) * BLOCK * BLOCK
    return pl.pallas_call(
        attend_kernel,
        out_shape=jax.ShapeDtypeStruct((rows, width), BF16),
        grid_spec=pltpu.PrefetchScalarGridSpec(
            num_scalar_prefetch=1,
            grid=(pairs,),
            in_specs=[spec(0), spec(1), spec(2)],
            out_specs=pl.BlockSpec((rows, PAIR), lambda p, parents: (0, p)),
        ),
        compiler_params=pltpu.CompilerParams(vmem_limit_bytes=48 << 20),
        cost_estimate=pl.CostEstimate(
            flops=work * PAIR * 24, bytes_accessed=rows * width * 8, transcendentals=work
        ),
        name="attend",
    )(parents, qkv, qkv, qkv)


def attend_back_kernel(parents_ref, q_ref, k_ref, v_ref, g_ref, out_ref, dq_s, dk_s, dv_s):
    part = pl.program_id(1)
    blocks = q_ref.shape[0] // BLOCK
    scale = 1.0 / math.sqrt(HEAD_DIM)

    @pl.when(part == 0)
    def _():
        for row in range(blocks):
            here = slice(row * BLOCK, (row + 1) * BLOCK)
            dq_heads = []
            for head in range(2):
                lanes = lane_of((BLOCK, PAIR), head)
                q_head = jnp.where(lanes, q_ref[here, :].astype(F32) * scale, 0.0).astype(BF16)
                g_head = jnp.where(lanes, g_ref[here, :].astype(F32), 0.0).astype(BF16)
                scores = masked_scores(parents_ref, q_head, k_ref, row)
                top = row_reduce(scores, jnp.maximum, jnp.max)
                probs = [jnp.exp(s - top) for s in scores]
                rest = 1.0 / row_reduce(probs, jnp.add, jnp.sum)
                probs = [p * rest for p in probs]
                d_probs = [
                    over(g_head, v_ref[col * BLOCK : (col + 1) * BLOCK, :], 1, 1)
                    for col in range(row + 1)
                ]
                level = row_reduce([p * d for p, d in zip(probs, d_probs)], jnp.add, jnp.sum)
                dq = None
                for col in range(row + 1):
                    there = slice(col * BLOCK, (col + 1) * BLOCK)
                    d_scores = (probs[col] * (d_probs[col] - level)).astype(BF16)
                    term = over(d_scores, k_ref[there, :], 1, 0)
                    dq = term if dq is None else dq + term
                    dk = over(d_scores, q_head, 0, 0)
                    dv = over(probs[col].astype(BF16), g_head, 0, 0)
                    if row == col and head == 0:
                        dk_s[there, :] = dk
                        dv_s[there, :] = dv
                    else:
                        dk_s[there, :] += dk
                        dv_s[there, :] += dv
                dq_heads.append(dq * scale)
            dq_s[here, :] = jnp.where(lane_of((BLOCK, PAIR), 0), dq_heads[0], dq_heads[1]).astype(
                BF16
            )
        out_ref[...] = dq_s[...]

    @pl.when(part == 1)
    def _():
        out_ref[...] = dk_s[...].astype(BF16)

    @pl.when(part == 2)
    def _():
        out_ref[...] = dv_s[...].astype(BF16)


def attend_back(parents, qkv, grad, width):
    rows = qkv.shape[0]
    pairs = width // PAIR
    spec = lambda part: pl.BlockSpec((rows, PAIR), lambda p, c, parents: (0, part * pairs + p))
    blocks = rows // BLOCK
    work = pairs * 2 * (blocks * (blocks + 1) // 2) * BLOCK * BLOCK
    return pl.pallas_call(
        attend_back_kernel,
        out_shape=jax.ShapeDtypeStruct((rows, 3 * width), BF16),
        grid_spec=pltpu.PrefetchScalarGridSpec(
            num_scalar_prefetch=1,
            grid=(pairs, 3),
            in_specs=[
                spec(0),
                spec(1),
                spec(2),
                pl.BlockSpec((rows, PAIR), lambda p, c, parents: (0, p)),
            ],
            out_specs=pl.BlockSpec((rows, PAIR), lambda p, c, parents: (0, c * pairs + p)),
            scratch_shapes=[
                pltpu.VMEM((rows, PAIR), BF16),
                pltpu.VMEM((rows, PAIR), F32),
                pltpu.VMEM((rows, PAIR), F32),
            ],
        ),
        compiler_params=pltpu.CompilerParams(vmem_limit_bytes=48 << 20),
        cost_estimate=pl.CostEstimate(
            flops=work * PAIR * 60, bytes_accessed=rows * width * 14, transcendentals=work
        ),
        name="attend_back",
    )(parents, qkv, qkv, qkv, grad)


def ffn_kernel(host, n2_ref, dy_ref, we_ref, wr_ref, be_ref, *refs):
    if host:
        line_own, refs = refs[0], refs[1:]
    sum_ref, seq_ref, act_ref, dpre_ref, part_ref = refs[:5]
    refs = refs[5:]
    if host:
        line_full, refs = refs[0], refs[1:]
    we, wr, seq, dy_st, act_st, dpre_st, part_st, keep, give, core_in, fold_in = refs[:11]
    refs = refs[1:]
    w_sem, own_sem, dy_sem, seq_sem, st_sem = refs[10:15]
    ag_send, ag_recv, agc_send, agc_recv, rsc_send, rsc_recv, fold_send, fold_recv = refs[15:23]
    cube = Cube()
    levels, me, steps, core_step = cube.levels, cube.me, cube.steps, cube.core_step
    count, at, owner = cube.count, cube.at, cube.owner
    rows, model = n2_ref.shape
    units = wr_ref.shape[0]
    barrier = pltpu.get_barrier_semaphore()
    cube.greet(barrier)
    hosted = []
    if host:
        line = Line()
        line.greet(barrier)
        aside = LineScatter(line, line_own, line_full, refs[23:])
        aside.prepare()
    load_own = pltpu.make_async_copy(n2_ref, seq.at[0, pl.ds(0, rows)], own_sem)
    load_own.start()
    parts = we_ref.shape[0] // model
    mine_units = we_ref.shape[1]
    loads_w = [pltpu.make_async_copy(wr_ref, wr, w_sem.at[parts])]
    for part in range(parts):
        loads_w.append(
            pltpu.make_async_copy(
                we_ref.at[pl.ds(part * model, model)],
                we.at[:, pl.ds(part * mine_units, mine_units)],
                w_sem.at[part],
            )
        )
    for c in loads_w:
        c.start()

    def load_dy(piece, slot):
        mine, other = owner(piece)
        out = []
        for half, index in enumerate((mine, other)):
            out.append(
                pltpu.make_async_copy(
                    dy_ref.at[pl.ds(pl.multiple_of(index * rows, rows), rows)],
                    dy_st.at[slot, pl.ds(half * rows, rows)],
                    dy_sem.at[slot, half],
                )
            )
        return out

    def gather_copy(piece, level):
        there = piece + (1 << level)
        return remote(
            seq.at[piece, pl.ds(0, rows)], seq.at[there, pl.ds(0, rows)],
            ag_send.at[there], ag_recv.at[there], at(me + steps[level]),
        )

    def gather_core(piece):
        return remote(
            seq.at[piece, pl.ds(0, rows)], seq.at[piece, pl.ds(rows, rows)],
            agc_send.at[piece], agc_recv.at[piece], at(me + core_step),
        )

    order = [0] + sorted(range(1, count), key=lambda p: (-(p.bit_length()), p))
    slots = {piece: i % 2 for i, piece in enumerate(order)}
    loads = {order[0]: load_dy(order[0], 0)}
    for c in loads[order[0]]:
        c.start()

    load_own.wait()
    pl.semaphore_wait(barrier, cube.peers() + (line.peers() if host else 0))
    if host:
        aside.step(1)
    sends = []
    for level in range(levels):
        sends.append(gather_copy(0, level))
        sends[-1].start()
    sends.append(gather_core(0))
    sends[-1].start()
    for c in loads_w:
        c.wait()

    arrived = {0}

    def take(piece):
        if piece in arrived:
            return
        low = piece - (1 << (piece.bit_length() - 1))
        gather_copy(low, piece.bit_length() - 1).wait_recv()
        arrived.add(piece)
        for level in range(piece.bit_length(), levels):
            sends.append(gather_copy(piece, level))
            sends[-1].start()
        sends.append(gather_core(piece))
        sends[-1].start()

    stores = {}
    outs = {}
    core_sends = {}
    folds = {}
    done_core = set()

    def add(piece, other):
        @pl.loop(0, rows // 16)
        def _(i):
            part = pl.ds(pl.multiple_of(i * 16, 16), 16)
            keep[piece, part] = (
                keep[piece, part].astype(F32) + other[part].astype(F32)
            ).astype(BF16)

    def add_core(piece):
        if piece in done_core:
            return
        core_copy(piece).wait_recv()
        add(piece, core_in.at[piece])
        done_core.add(piece)

    def core_copy(piece):
        return remote(
            give.at[slots[piece]], core_in.at[piece],
            rsc_send.at[piece], rsc_recv.at[piece], at(me + core_step),
        )

    def fold_copy(piece):
        level = piece.bit_length() - 1
        low = piece - (1 << level)
        return remote(
            keep.at[piece], fold_in.at[piece - 1],
            fold_send.at[piece - 1], fold_recv.at[piece - 1], at(me + steps[level]),
        )

    def fold(piece):
        add_core(piece)
        for level in range(levels - 1, piece.bit_length() - 1, -1):
            above = piece + (1 << level)
            fold_copy(above).wait_recv()
            add(piece, fold_in.at[above - 1])
        if piece:
            folds[piece] = fold_copy(piece)
            folds[piece].start()

    chunk = 256
    wide = 512
    for turn, piece in enumerate(order):
        slot = turn % 2
        for earlier in range(1, piece + 1):
            take(earlier)
        gather_core(piece).wait_recv()
        for c in loads[piece]:
            c.wait()
        if turn + 1 < count:
            loads[order[turn + 1]] = load_dy(order[turn + 1], 1 - slot)
            for c in loads[order[turn + 1]]:
                c.start()
        if turn >= 2:
            for c in stores[turn - 2]:
                c.wait()
            core_sends[order[turn - 2]].wait_send()

        @pl.loop(0, units // chunk)
        def _(i):
            cols = pl.ds(pl.multiple_of(i * chunk, chunk), chunk)
            pre = over(seq[piece], we[:, cols], 1, 0) + be_ref[:, cols]
            d_act = over(dy_st[slot], wr[cols, :], 1, 1)
            square = pre * pre
            t = jnp.tanh(GELU * pre * (1.0 + 0.044715 * square))
            act_st[slot, :, cols] = (0.5 * pre * (1.0 + t)).astype(BF16)
            slope = 0.5 * (1.0 + t) + (0.5 * GELU) * pre * (1.0 - t * t) * (
                1.0 + (3 * 0.044715) * square
            )
            dpre_st[slot, :, cols] = (d_act * slope).astype(BF16)

        @pl.loop(0, model // wide)
        def _(i):
            cols = pl.ds(pl.multiple_of(i * wide, wide), wide)
            d_two = over(dpre_st[slot], we[cols, :], 1, 1).astype(BF16)
            keep[piece, :, cols] = d_two[:rows]
            give[slot, :, cols] = d_two[rows:]
            out = over(act_st[slot], wr[:, cols], 1, 0).astype(BF16)
            part_st[slot, :, cols] = out

        if host and turn < line.n - 2:
            aside.step(turn + 2)
        core_sends[piece] = core_copy(piece)
        core_sends[piece].start()
        mine, other = owner(piece)
        stores[turn] = []
        for half, index in enumerate((mine, other)):
            to = pl.ds(pl.multiple_of(index * rows, rows), rows)
            part = pl.ds(half * rows, rows)
            stores[turn].append(
                pltpu.make_async_copy(act_st.at[slot, part], act_ref.at[to], st_sem.at[0, slot, half])
            )
            stores[turn].append(
                pltpu.make_async_copy(dpre_st.at[slot, part], dpre_ref.at[to], st_sem.at[1, slot, half])
            )
            stores[turn].append(
                pltpu.make_async_copy(part_st.at[slot, part], part_ref.at[to], st_sem.at[2, slot, half])
            )
            stores[turn].append(
                pltpu.make_async_copy(seq.at[piece, part], seq_ref.at[to], seq_sem.at[piece, half])
            )
        for c in stores[turn]:
            c.start()
        if piece.bit_length() == levels:
            fold(piece)
    for level in range(levels - 2, -1, -1):
        for piece in range((1 << level), 2 << level):
            fold(piece)
    add_core(0)
    for level in range(levels):
        fold_copy(1 << level).wait_recv()

    @pl.loop(0, rows // 16)
    def _(i):
        part = pl.ds(pl.multiple_of(i * 16, 16), 16)
        total = keep[0, part].astype(F32)
        for level in range(levels):
            total = total + fold_in[(1 << level) - 1, part].astype(F32)
        sum_ref[part] = total

    if host:
        for step in range(count + 2, line.n):
            aside.step(step)
        aside.finish()
    for s in sends:
        s.wait_send()
    for turn in range(max(0, count - 2), count):
        for c in stores[turn]:
            c.wait()
        core_sends[order[turn]].wait_send()
    for s in folds.values():
        s.wait_send()


def ffn(n2, dy_all, we, wr, bias_e, own=None):
    host = own is not None
    n = lax.axis_size("tensor")
    rows, model = n2.shape
    units = wr.shape[0]
    dp = lax.axis_size("dp")
    count = dp // 2
    dma, anywhere, vmem = DMA, ANY, VMEM
    operands = [n2, dy_all, we, wr, bias_e] + [own] * host
    lines = [jax.ShapeDtypeStruct((rows, model), F32)] * host
    flops = 36 * dp * rows * model * units
    return pl.pallas_call(
        functools.partial(ffn_kernel, host),
        out_shape=(
            jax.ShapeDtypeStruct((rows, model), F32),
            jax.ShapeDtypeStruct((dp * rows, model), BF16),
            jax.ShapeDtypeStruct((dp * rows, units), BF16),
            jax.ShapeDtypeStruct((dp * rows, units), BF16),
            jax.ShapeDtypeStruct((dp * rows, model), BF16),
            *lines,
        ),
        in_specs=[anywhere, anywhere, anywhere, anywhere, vmem] + [anywhere] * host,
        out_specs=(vmem, anywhere, anywhere, anywhere, anywhere) + (vmem,) * host,
        scratch_shapes=[
            pltpu.VMEM((model, units), BF16),
            pltpu.VMEM((units, model), BF16),
            pltpu.VMEM((count, 2 * rows, model), BF16),
            pltpu.VMEM((2, 2 * rows, model), BF16),
            pltpu.VMEM((2, 2 * rows, units), BF16),
            pltpu.VMEM((2, 2 * rows, units), BF16),
            pltpu.VMEM((2, 2 * rows, model), BF16),
            pltpu.VMEM((count, rows, model), BF16),
            pltpu.VMEM((2, rows, model), BF16),
            pltpu.VMEM((count, rows, model), BF16),
            pltpu.VMEM((count - 1, rows, model), BF16),
            dma((n + 1,)), dma, dma((2, 2)), dma((count, 2)), dma((3, 2, 2)),
            dma((count,)), dma((count,)), dma((count,)), dma((count,)),
            dma((count,)), dma((count,)), dma((count - 1,)), dma((count - 1,)),
        ]
        + (LineScatter.scratch(n, rows, model) if host else []),
        compiler_params=pltpu.CompilerParams(
            collective_id=2 if host else 1, has_side_effects=True, vmem_limit_bytes=62 << 20
        ),
        cost_estimate=pl.CostEstimate(
            flops=flops, bytes_accessed=8 * dp * rows * (model + units), transcendentals=dp * rows * units
        ),
        name="ffn_plane",
    )(*operands)


def body(
    tokens,
    parents,
    cotangent,
    first_gain,
    first_shift,
    w_query,
    b_query,
    w_key,
    w_value,
    b_value,
    w_out,
    b_out,
    second_gain,
    second_shift,
    w_expand,
    b_expand,
    w_reduce,
    b_reduce,
):
    dp = lax.axis_size("dp")
    tn = lax.axis_size("tensor")
    dp_me = lax.axis_index("dp")
    tn_me = lax.axis_index("tensor")
    width = w_query.shape[1]
    model = w_query.shape[0] * dp
    units = w_expand.shape[1]
    mine = units // dp
    micros = range(tokens.shape[0])
    last = tokens.shape[0] - 1
    x_low = [tokens[m, 0] for m in micros]
    dy_low = [cotangent[m, 0] for m in micros]
    rows_here = x_low[0].shape[0]
    total = rows_here * tn

    cut = first_gain.shape[0]
    bq_rows, bq_cols = b_query.shape
    be_rows, be_cols = b_expand.shape
    small = jnp.concatenate(
        [first_gain, first_shift, b_out, second_gain, second_shift, b_reduce]
        + [b_query.reshape(-1), b_value.reshape(-1), b_expand.reshape(-1)]
    )
    used = small.shape[0]
    small = jnp.pad(small, (0, -used % 2048)).reshape(-1, 128)
    w_qkv = jnp.concatenate([w_query, w_key, w_value], axis=1)
    seq_x0, w_qkv, w_ot, w_e, w_r, small = front(
        x_low[0], w_qkv, w_out.T, w_expand, w_reduce, small
    )
    small = small.reshape(dp, -1)[:, :used]
    gain_one, shift_one, bias_out, gain_two, shift_two, bias_red = [
        small[:, i * cut : (i + 1) * cut].reshape(1, model).astype(F32) for i in range(6)
    ]
    at = 6 * cut
    bias_qkv = []
    for i in range(2):
        part = small[:, at : at + bq_rows * bq_cols].reshape(dp, bq_rows, bq_cols)
        bias_qkv.append(part.transpose(1, 0, 2).reshape(1, width).astype(F32))
        at += bq_rows * bq_cols
    bias_qkv = jnp.concatenate([bias_qkv[0], jnp.zeros((1, width), F32), bias_qkv[1]], 1)
    bias_e = small[:, at:].reshape(dp, dp, be_rows // dp, be_cols)
    bias_e = lax.dynamic_index_in_dim(bias_e, dp_me, 1, keepdims=False)
    bias_e = bias_e.transpose(1, 0, 2).reshape(mine)
    bias_e = jnp.pad(bias_e, (0, -mine % 2048)).reshape(-1, 128)

    seq_x = [seq_x0]
    w_r = lax.all_gather(w_r, "tensor", axis=0, tiled=True)
    w_e = lax.all_gather(w_e, "tensor", axis=1 if mine % 128 else 0, tiled=True)

    normal_one, seq_one, qkv, attended, hidden, normed_two = [], [], [], [], [], []
    out_part, seq_two, activated, d_pre, d_hidden, d_branch, out_sum = [], [], [], [], [], [], []
    d_qkv, d_one, d_att, row_attended = [], [], [], []
    g_gain_two = g_shift_two = g_bias_red = g_bias_out = g_bias_e = 0.0
    g_gain_one = g_shift_one = g_bias_qkv = 0.0
    for m in micros:
        normal_one.append(layer_norm(seq_x[m].astype(F32), 1.0, 0.0))
        seq_one.append((normal_one[m] * gain_one + shift_one).astype(BF16))
        qkv.append(
            (jnp.dot(seq_one[m], w_qkv, preferred_element_type=F32) + bias_qkv).astype(BF16)
        )
        attended.append(attend(parents[m, 0], qkv[m], width))
        if m == 0:
            bias_e, w_ot, grad, row_att = exchange(
                3, gathers=[bias_e], cubes=[w_ot, dy_low[m]], outs=[attended[m]]
            )
            seq_grad = [grad]
            bias_e = bias_e.reshape(tn, -1)[:, :mine].reshape(1, tn * mine).astype(F32)
        else:
            part, row_att, col_grad = exchange(
                4, planes=[out_part[m - 1]], outs=[attended[m]], backs=[d_att[m - 1]]
            )
            out_sum.append(part)
            d_att[m - 1] = col_grad
        if m < last:
            next_x, row_att = lax.optimization_barrier((x_low[m + 1], row_att))
            next_x = lax.all_gather(next_x, "tensor", axis=0, tiled=True)
        row_attended.append(row_att)
        branch = over(row_att, w_ot, 1, 1)
        hidden.append(x_low[m].astype(F32) + (branch + bias_out))
        normed_two.append(layer_norm(hidden[m], gain_two, shift_two).astype(BF16))
        if m < last:
            grad, normed_two[m] = lax.optimization_barrier((dy_low[m + 1], normed_two[m]))
            seq_grad.append(lax.all_gather(grad, "dp", axis=0, tiled=True))

        def attention_back(k, awaited=None):
            d_qkv.append(attend_back(parents[k, 0], qkv[k], d_att[k], width))
            if awaited is not None:
                d_qkv[k], awaited = lax.optimization_barrier((d_qkv[k], awaited))
            d_one.append(over(d_qkv[k], w_qkv, 1, 1).astype(BF16))
            part = d_one[k].astype(F32)
            return (
                jnp.sum(part * normal_one[k], 0, keepdims=True),
                jnp.sum(part, 0, keepdims=True),
                jnp.sum(d_qkv[k].astype(F32), 0),
                awaited,
            )

        own = None
        if m:
            gain, shift, bias, _ = attention_back(m - 1)
            g_gain_one, g_shift_one = g_gain_one + gain, g_shift_one + shift
            g_bias_qkv = g_bias_qkv + bias
            own = d_one[m - 1]

        d_two, seq, act, dpre, part, *line = ffn(normed_two[m], seq_grad[m], w_e, w_r, bias_e, own)
        if m:
            d_one[m - 1] = line[0]
        seq_two.append(seq)
        activated.append(act)
        d_pre.append(dpre)
        out_part.append(part)
        grad32 = dy_low[m].astype(F32)
        norm_value, norm_pull = jax.vjp(layer_norm, hidden[m], gain_two, shift_two)
        d_norm, g_gain, g_shift = norm_pull(d_two)
        d_hidden.append(grad32 + d_norm)
        d_branch.append(d_hidden[m].astype(BF16))
        d_att.append(jnp.dot(d_branch[m], w_ot, preferred_element_type=F32).astype(BF16))
        g_gain_two = g_gain_two + g_gain
        g_shift_two = g_shift_two + g_shift
        g_bias_red = g_bias_red + jnp.sum(grad32, 0, keepdims=True)
        g_bias_out = g_bias_out + jnp.sum(d_branch[m].astype(F32), 0, keepdims=True)
        g_bias_e = g_bias_e + jnp.sum(dpre.astype(F32), 0)
        if m < last:
            next_x, d_branch[m] = lax.optimization_barrier((next_x, d_branch[m]))
            seq_x.append(next_x)

    def outer(left, right):
        out = None
        for a, b in zip(left, right):
            term = over(a, b, 0, 0)
            out = term if out is None else out + term
        return out.astype(BF16)

    g_r = outer(activated, seq_grad)
    d_att[last], g_r = lax.optimization_barrier((d_att[last], g_r))
    g_r = lax.psum_scatter(g_r, "tensor", scatter_dimension=0, tiled=True)
    g_ot = outer([jnp.concatenate(d_branch, 0)], [jnp.concatenate(row_attended, 0)])
    g_ot, d_att[last] = exchange(6, planes=[g_ot], backs=[d_att[last]])
    d_pre[last], d_att[last] = lax.optimization_barrier((d_pre[last], d_att[last]))
    g_et = outer(d_pre, seq_two)
    g_et = lax.psum_scatter(g_et, "tensor", scatter_dimension=0, tiled=True)
    gain, shift, bias, g_r = attention_back(last, g_r)
    g_gain_one, g_shift_one = g_gain_one + gain, g_shift_one + shift
    g_bias_qkv = g_bias_qkv + bias

    rows = jnp.concatenate(
        [g_gain_one, g_shift_one, g_bias_out, g_gain_two, g_shift_two, g_bias_red], 0
    )
    rows = rows.reshape(6, dp, cut).transpose(1, 0, 2).reshape(dp, 6 * cut)
    row_qv = jnp.concatenate([g_bias_qkv[:width], g_bias_qkv[2 * width :]])
    row_qv = row_qv.reshape(2 * bq_rows, dp, bq_cols).transpose(1, 0, 2)[:, None]
    row_qv = lax.dynamic_update_slice(
        jnp.zeros((dp, tn, 2 * bq_rows, bq_cols), F32), row_qv, (0, tn_me, 0, 0)
    ).reshape(dp, -1)
    row_e = g_bias_e.reshape(tn, be_rows // dp, dp, be_cols).transpose(2, 0, 1, 3)[:, :, None]
    row_e = lax.dynamic_update_slice(
        jnp.zeros((dp, tn, dp, be_rows // dp, be_cols), F32), row_e, (0, 0, dp_me, 0, 0)
    ).reshape(dp, -1)
    little = jnp.concatenate([rows, row_qv, row_e], 1)
    little = jnp.pad(little, ((0, 0), (0, -little.shape[1] % 1024))).reshape(dp, -1, 128)

    g_qkv = outer(seq_one, d_qkv)
    g_ot = g_ot.astype(BF16).reshape(-1, tn, width).transpose(1, 0, 2).reshape(-1, width)
    d_one[last], g_ot, g_qkv, out_last, g_expand, g_reduce, little = exchange(
        5,
        lines=[d_one[last], g_ot],
        planes=[g_qkv, out_part[last]],
        swaps=[g_et, g_r],
        small=[little],
    )
    out_sum.append(out_last)
    g_query, g_key, g_value = [g_qkv[:, i * width : (i + 1) * width] for i in range(3)]
    g_out = g_ot.T
    g_expand = g_expand.T.astype(F32)
    g_reduce = g_reduce.astype(F32)
    layer_out = [(hidden[m] + (out_sum[m] + bias_red)).astype(BF16) for m in micros]
    little = little.reshape(-1)
    six = little[: 6 * cut].reshape(6, cut)
    at = 6 * cut
    g_bqv = little[at : at + tn * 2 * bq_rows * bq_cols].reshape(tn, 2 * bq_rows, bq_cols)
    g_bqv = lax.dynamic_index_in_dim(g_bqv, tn_me, 0, keepdims=False)
    g_bq, g_bv = g_bqv[:bq_rows], g_bqv[bq_rows:]
    at += tn * 2 * bq_rows * bq_cols
    g_be = little[at : at + tn * be_rows * be_cols].reshape(tn, be_rows, be_cols)
    g_be = lax.dynamic_index_in_dim(g_be, tn_me, 0, keepdims=False)
    input_grad = []
    for m in micros:
        first_value, first_pull = jax.vjp(
            lambda rows: layer_norm(rows, gain_one, shift_one), x_low[m].astype(F32)
        )
        input_grad.append((d_hidden[m] + first_pull(d_one[m])[0]).astype(BF16))

    return (
        jnp.stack(layer_out, 0)[:, None],
        jnp.stack(input_grad, 0)[:, None],
        six[0],
        six[1],
        g_query,
        g_bq,
        g_key,
        g_value,
        g_bv,
        g_out,
        six[2],
        six[3],
        six[4],
        g_expand,
        g_be,
        g_reduce,
        six[5],
    )


def solution(mesh):
    in_specs = (
        P(None, "dp", "tensor", None),
        P(None, "dp", None),
        P(None, "dp", "tensor", None),
        P("dp"),
        P("dp"),
        P("dp", "tensor"),
        P("tensor", "dp"),
        P("dp", "tensor"),
        P("dp", "tensor"),
        P("tensor", "dp"),
        P("tensor", "dp"),
        P("dp"),
        P("dp"),
        P("dp"),
        P("dp", "tensor"),
        P("tensor", "dp"),
        P("tensor", "dp"),
        P("dp"),
    )
    out_specs = (
        P(None, "dp", "tensor", None),
        P(None, "dp", "tensor", None),
        P("dp"),
        P("dp"),
        P("dp", "tensor"),
        P("tensor", "dp"),
        P("dp", "tensor"),
        P("dp", "tensor"),
        P("tensor", "dp"),
        P("tensor", "dp"),
        P("dp"),
        P("dp"),
        P("dp"),
        P("dp", "tensor"),
        P("tensor", "dp"),
        P("tensor", "dp"),
        P("dp"),
    )
    return jax.shard_map(body, mesh=mesh, in_specs=in_specs, out_specs=out_specs, check_vma=False)
```

```python
import functools
import math

import jax
import jax.numpy as jnp
from jax import lax
from jax.experimental import pallas as pl
from jax.experimental.pallas import tpu as pltpu
from jax.sharding import PartitionSpec as P

HEAD_DIM = 64
BLOCK = 256

F32 = jnp.float32
BF16 = jnp.bfloat16
MESH = pl.DeviceIdType.MESH
DMA = pltpu.SemaphoreType.DMA
GELU = math.sqrt(2.0 / math.pi)


def layer_norm(rows, gain, shift):
    center = rows - jnp.mean(rows, -1, keepdims=True)
    spread = jnp.mean(center * center, -1, keepdims=True)
    return center * lax.rsqrt(spread + 1e-05) * gain + shift


def after(value, *others):
    return lax.optimization_barrier((value,) + others)[0]


def over(left, right, on_left, on_right):
    return lax.dot_general(
        left, right, (((on_left,), (on_right,)), ((), ())), preferred_element_type=F32
    )


def window(index, rows):
    return pl.ds(pl.multiple_of(index * rows, rows), rows)


def remote(src, dst, send, recv, to):
    return pltpu.make_async_remote_copy(
        src_ref=src, dst_ref=dst, send_sem=send, recv_sem=recv,
        device_id=to, device_id_type=MESH,
    )


class Line:
    def __init__(self):
        self.n = lax.axis_size("tensor")
        self.me = lax.axis_index("tensor")
        self.dp = lax.axis_index("dp")

    def at(self, index):
        return (self.dp, index)

    def greet(self, barrier):
        @pl.when(self.me > 0)
        def _():
            pl.semaphore_signal(barrier, inc=1, device_id=self.at(self.me - 1), device_id_type=MESH)

        @pl.when(self.me < self.n - 1)
        def _():
            pl.semaphore_signal(barrier, inc=1, device_id=self.at(self.me + 1), device_id_type=MESH)

    @property
    def size(self):
        return self.n

    def greet_all(self, barrier):
        for k in range(1, self.n):
            pl.semaphore_signal(
                barrier, inc=1, device_id=self.at((self.me + k) % self.n), device_id_type=MESH
            )

    def peers(self):
        return (self.me + self.n - 1) // self.n + (2 * self.n - 2 - self.me) // self.n


class LineGather:
    def __init__(self, line, own, full, sems):
        self.line, self.own, self.full = line, own, full
        self.side = own.shape[0] == full.shape[0]
        self.local, self.up_send, self.up_recv, self.down_send, self.down_recv = sems

    @staticmethod
    def sems(n):
        return [DMA, DMA((n - 1,)), DMA((n - 1,)), DMA((n - 1,)), DMA((n - 1,))]

    def slot(self, index):
        if self.side:
            return self.full.at[:, window(index, self.own.shape[1])]
        return self.full.at[window(index, self.own.shape[0])]

    def hop(self, step, up):
        line = self.line
        if up:
            shard, to = line.me - (step - 1), line.me + 1
            send, recv = self.up_send, self.up_recv
        else:
            shard, to = line.me + (step - 1), line.me - 1
            send, recv = self.down_send, self.down_recv
        there = self.slot(shard)
        src = self.own if step == 1 else there
        return remote(src, there, send.at[step - 1], recv.at[step - 1], line.at(to))

    def sends(self, step, up):
        line = self.line
        if up:
            return (line.me < line.n - 1) & (line.me >= step - 1)
        return (line.me > 0) & (line.me + step - 1 < line.n)

    def takes(self, step, up):
        line = self.line
        return (line.me >= step) if up else (line.me + step < line.n)

    def send(self, step):
        for up in (True, False):
            @pl.when(self.sends(step, up))
            def _():
                self.hop(step, up).start()

    def start(self):
        pltpu.make_async_copy(self.own, self.slot(self.line.me), self.local).start()
        self.send(1)

    def take(self, step):
        for up in (True, False):
            @pl.when(self.takes(step, up))
            def _():
                line = self.line
                shard = (line.me - step) if up else (line.me + step)
                here = self.slot(shard)
                send, recv = (
                    (self.up_send, self.up_recv) if up else (self.down_send, self.down_recv)
                )
                remote(
                    here, here, send.at[step - 1], recv.at[step - 1], line.at(line.me)
                ).wait_recv()
        if step < self.line.n - 1:
            self.send(step + 1)

    def finish(self):
        for step in range(1, self.line.n):
            for up in (True, False):
                @pl.when(self.sends(step, up))
                def _():
                    self.hop(step, up).wait_send()
        pltpu.make_async_copy(self.own, self.slot(self.line.me), self.local).wait()


class LineScatter:
    def __init__(self, line, parts, out, scratch):
        self.line, self.parts, self.out = line, parts, out
        self.rows = out.shape[0]
        (self.own, self.sum, self.come, self.load, self.own_sem, self.send_sem, self.recv_sem) = scratch

    @staticmethod
    def scratch(n, rows, d):
        return [
            pltpu.VMEM((rows, d), BF16),
            pltpu.VMEM((2, n - 1, rows, d), BF16),
            pltpu.VMEM((2, n - 1, rows, d), BF16),
            DMA((2, n - 1)), DMA, DMA((2, n - 1)), DMA((2, n - 1)),
        ]

    def sends(self, step, up):
        line = self.line
        return (line.me <= step - 1) if up else (line.n - 1 - line.me <= step - 1)

    def load_of(self, step, up):
        line = self.line
        chunk = (line.me + line.n - step) if up else (line.me - line.n + step)
        way = 0 if up else 1
        return pltpu.make_async_copy(
            self.parts.at[window(chunk, self.rows)], self.sum.at[way, step - 1], self.load.at[way, step - 1]
        )

    def hop(self, step, up):
        line, way = self.line, 0 if up else 1
        return remote(
            self.sum.at[way, step - 1], self.come.at[way, step - 1],
            self.send_sem.at[way, step - 1], self.recv_sem.at[way, step - 1],
            line.at(line.me + 1 if up else line.me - 1),
        )

    def wait_from(self, step, up):
        line, way = self.line, 0 if up else 1
        remote(
            self.come.at[way, step - 1], self.come.at[way, step - 1],
            self.send_sem.at[way, step - 1], self.recv_sem.at[way, step - 1],
            line.at(line.me),
        ).wait_recv()

    def own_load(self):
        return pltpu.make_async_copy(
            self.parts.at[window(self.line.me, self.rows)], self.own, self.own_sem
        )

    def prepare(self):
        self.own_load().start()
        for step in range(1, self.line.n):
            for up in (True, False):
                @pl.when(self.sends(step, up))
                def _():
                    self.load_of(step, up).start()

    def step(self, step):
        line = self.line
        for up in (True, False):
            way = 0 if up else 1

            @pl.when(self.sends(step, up))
            def _():
                self.load_of(step, up).wait()
                if step > 1:
                    inner = (line.me > 0) if up else (line.me < line.n - 1)

                    @pl.when(inner)
                    def _():
                        self.wait_from(step - 1, up)

                        @pl.loop(0, self.rows // 16)
                        def _(i):
                            part = window(i, 16)
                            self.sum[way, step - 1, part] = (
                                self.sum[way, step - 1, part].astype(F32)
                                + self.come[way, step - 2, part].astype(F32)
                            ).astype(BF16)

                if step > 1:

                    @pl.when(self.sends(step - 1, up))
                    def _():
                        self.hop(step - 1, up).wait_send()

                self.hop(step, up).start()

    def finish(self):
        line, n = self.line, self.line.n
        self.own_load().wait()

        @pl.loop(0, self.rows // 16)
        def _(i):
            part = window(i, 16)
            self.out[part] = self.own[part].astype(F32)

        for up in (True, False):
            way = 0 if up else 1

            @pl.when((line.me > 0) if up else (line.me < n - 1))
            def _():
                self.wait_from(n - 1, up)

                @pl.loop(0, self.rows // 16)
                def _(i):
                    part = window(i, 16)
                    self.out[part] += self.come[way, n - 2, part].astype(F32)

        for up in (True, False):
            @pl.when(self.sends(n - 1, up))
            def _():
                self.hop(n - 1, up).wait_send()


class Cube:
    def __init__(self):
        self.dp = lax.axis_size("dp")
        self.levels = levels = self.dp.bit_length() - 2
        self.count = 1 << levels
        self.me = me = lax.axis_index("dp")
        self.tensor = lax.axis_index("tensor")
        core = me % 2
        flips = []
        for bit in range(1, levels + 1):
            flips.append((1 << bit) * (1 - 2 * ((me // (1 << bit)) % 2)))
        self.steps = [
            flips[l] * (1 - core) + flips[levels - 1 - l] * core for l in range(levels)
        ]
        self.core_step = 1 - 2 * core

    def at(self, index):
        return (index, self.tensor)

    def owner(self, piece):
        mine, other = self.me, self.me + self.core_step
        for l in range(self.levels):
            if piece >> l & 1:
                mine = mine + self.steps[l]
                other = other + self.steps[self.levels - 1 - l]
        return mine, other

    def greet(self, barrier):
        for step in self.steps + [self.core_step]:
            pl.semaphore_signal(
                barrier, inc=1, device_id=self.at(self.me + step), device_id_type=MESH
            )

    @property
    def size(self):
        return self.dp

    def greet_all(self, barrier):
        for k in range(1, self.dp):
            pl.semaphore_signal(
                barrier, inc=1, device_id=self.at((self.me + k) % self.dp), device_id_type=MESH
            )

    def peers(self):
        return self.levels + 1


class CubeGather:
    def __init__(self, cube, own, full, sems):
        self.cube, self.own, self.full = cube, own, full
        self.rows = own.shape[0]
        self.local, self.send_sem, self.recv_sem, self.core_send, self.core_recv = sems
        self.arrived, self.sent = {0}, []

    @staticmethod
    def sems(count):
        return [DMA, DMA((count,)), DMA((count,)), DMA((count,)), DMA((count,))]

    def slot(self, index):
        return self.full.at[window(index, self.rows)]

    def src(self, piece):
        return self.own if piece == 0 else self.slot(self.cube.owner(piece)[0])

    def hop(self, piece, level):
        cube, there = self.cube, piece + (1 << level)
        return remote(
            self.src(piece), self.slot(cube.owner(piece)[0]),
            self.send_sem.at[there], self.recv_sem.at[there], cube.at(cube.me + cube.steps[level]),
        )

    def core(self, piece):
        cube = self.cube
        return remote(
            self.src(piece), self.slot(cube.owner(piece)[0]),
            self.core_send.at[piece], self.core_recv.at[piece], cube.at(cube.me + cube.core_step),
        )

    def give(self, piece):
        for level in range(piece.bit_length(), self.cube.levels):
            self.sent.append(self.hop(piece, level))
            self.sent[-1].start()
        self.sent.append(self.core(piece))
        self.sent[-1].start()

    def start(self):
        self.place = pltpu.make_async_copy(self.own, self.slot(self.cube.me), self.local)
        self.place.start()
        self.give(0)

    def take(self, piece):
        if piece in self.arrived:
            return
        here = self.slot(self.cube.owner(piece)[0])
        remote(
            here, here, self.send_sem.at[piece], self.recv_sem.at[piece], self.cube.at(self.cube.me)
        ).wait_recv()
        self.arrived.add(piece)
        self.give(piece)

    def take_core(self, piece):
        here = self.slot(self.cube.owner(piece)[1])
        remote(
            here, here, self.core_send.at[piece], self.core_recv.at[piece], self.cube.at(self.cube.me)
        ).wait_recv()

    def finish(self):
        for piece in range(self.cube.count):
            self.take(piece)
            self.take_core(piece)
        for copy in self.sent:
            copy.wait_send()
        self.place.wait()


class CubeScatter:
    def __init__(self, cube, parts, out, scratch):
        self.cube, self.parts, self.out = cube, parts, out
        self.rows = out.shape[0]
        (self.keep, self.core_in, self.fold_in, self.load_sem,
         self.core_send, self.core_recv, self.send_sem, self.recv_sem) = scratch

    @staticmethod
    def scratch(count, rows, d):
        return [
            pltpu.VMEM((count, rows, d), BF16),
            pltpu.VMEM((count, rows, d), BF16),
            pltpu.VMEM((count - 1, rows, d), BF16),
            DMA((count,)), DMA((count,)), DMA((count,)), DMA((count - 1,)), DMA((count - 1,)),
        ]

    def load(self, piece):
        return pltpu.make_async_copy(
            self.parts.at[window(self.cube.owner(piece)[0], self.rows)],
            self.keep.at[piece], self.load_sem.at[piece],
        )

    def core(self, piece):
        cube = self.cube
        return remote(
            self.parts.at[window(cube.owner(piece)[1], self.rows)], self.core_in.at[piece],
            self.core_send.at[piece], self.core_recv.at[piece], cube.at(cube.me + cube.core_step),
        )

    def hop(self, piece):
        cube, level = self.cube, piece.bit_length() - 1
        return remote(
            self.keep.at[piece], self.fold_in.at[piece - 1],
            self.send_sem.at[piece - 1], self.recv_sem.at[piece - 1],
            cube.at(cube.me + cube.steps[level]),
        )

    def order(self):
        return sorted(range(self.cube.count), key=lambda p: (-(p.bit_length()), p))

    def start(self):
        for piece in self.order():
            self.core(piece).start()
            self.load(piece).start()

    def add(self, piece, other):
        @pl.loop(0, self.rows // 16)
        def _(i):
            part = window(i, 16)
            self.keep[piece, part] = (
                self.keep[piece, part].astype(F32) + other[part].astype(F32)
            ).astype(BF16)

    def fold(self, piece):
        self.load(piece).wait()
        self.core(piece).wait_recv()
        self.add(piece, self.core_in.at[piece])
        for level in range(self.cube.levels - 1, piece.bit_length() - 1, -1):
            above = piece + (1 << level)
            self.hop(above).wait_recv()
            self.add(piece, self.fold_in.at[above - 1])
        if piece:
            self.hop(piece).start()

    def finish(self):
        self.fold(0)

        @pl.loop(0, self.rows // 16)
        def _(i):
            part = window(i, 16)
            self.out[part] = self.keep[0, part].astype(F32)

        for piece in range(self.cube.count):
            self.core(piece).wait_send()
            if piece:
                self.hop(piece).wait_send()


class Swap:
    def __init__(self, place, moves, sems):
        self.place, self.moves = place, moves
        self.send_sem, self.recv_sem, self.local = sems

    @staticmethod
    def sems(size, moves):
        return [DMA((moves, size)), DMA((moves, size)), DMA((moves,))]

    def copies(self):
        place = self.place
        out = []
        for k in range(1, place.size):
            to = (place.me + k) % place.size
            for m, (src, dst) in enumerate(self.moves):
                out.append(
                    remote(src(to), dst(place.me), self.send_sem.at[m, k], self.recv_sem.at[m, k], place.at(to))
                )
        return out

    def locals(self):
        return [
            pltpu.make_async_copy(src(self.place.me), dst(self.place.me), self.local.at[m])
            for m, (src, dst) in enumerate(self.moves)
        ]

    def start(self):
        for copy in self.copies() + self.locals():
            copy.start()

    def finish(self):
        place = self.place
        for copy in self.copies():
            copy.wait_send()
        for k in range(1, place.size):
            of = (place.me - k + place.size) % place.size
            for m, (src, dst) in enumerate(self.moves):
                here = dst(of)
                remote(here, here, self.send_sem.at[m, k], self.recv_sem.at[m, k], place.at(of)).wait_recv()
        for copy in self.locals():
            copy.wait()


def rows_to_side(src, dst):
    rows, cols = dst.shape[0], src.shape[1]
    return (lambda d: src.at[window(d, rows)], lambda d: dst.at[:, window(d, cols)])


def side_to_rows(src, dst):
    rows, cols = src.shape[0], dst.shape[1]
    return (lambda d: src.at[:, window(d, cols)], lambda d: dst.at[window(d, rows)])


ANY = pl.BlockSpec(memory_space=pl.ANY)
VMEM = pl.BlockSpec(memory_space=pltpu.VMEM)


def front_kernel(
    x_ref, w_ref, wo_ref, we_ref, wr_ref, small_ref,
    seq_ref, w_out, wo_line, we_out, wr_out, small_out, *sems
):
    line, cube = Line(), Cube()
    gather = LineGather(line, x_ref, seq_ref, sems[:5])
    wide = LineGather(line, wo_ref, wo_line, sems[5:10])
    weights = CubeGather(cube, w_ref, w_out, sems[10:15])
    tile = small_ref.shape[0]
    moves = [
        (lambda d: small_ref, lambda d: small_out.at[window(d, tile)]),
        rows_to_side(wr_ref, wr_out),
    ]
    if wr_out.shape[0] % 128 == 0:
        moves.append(side_to_rows(we_ref, we_out))
    swap = Swap(cube, moves, sems[15:18])
    barrier = pltpu.get_barrier_semaphore()
    line.greet(barrier)
    cube.greet_all(barrier)
    pl.semaphore_wait(barrier, cube.dp - 1 + line.peers())
    gather.start()
    weights.start()
    gather.take(1)
    for piece in range(1, cube.count):
        if piece.bit_length() < cube.levels:
            weights.take(piece)
    swap.start()
    gather.take(2)
    wide.start()
    for piece in range(1, cube.count):
        weights.take(piece)
    wide.take(1)
    for step in range(3, line.n):
        gather.take(step)
        wide.take(step - 1)
    wide.take(line.n - 1)
    weights.finish()
    swap.finish()
    gather.finish()
    wide.finish()


def front(x, w, w_o, w_e, w_r, small):
    dp, n = lax.axis_size("dp"), lax.axis_size("tensor")
    rows, model = x.shape
    seq, w_all, o_line, e_all, r_all, small_all = pl.pallas_call(
        front_kernel,
        out_shape=(
            jax.ShapeDtypeStruct((n * rows, model), BF16),
            jax.ShapeDtypeStruct((dp * w.shape[0], w.shape[1]), BF16),
            jax.ShapeDtypeStruct((w_o.shape[0], n * w_o.shape[1]), BF16),
            jax.ShapeDtypeStruct((dp * w_e.shape[0], w_e.shape[1] // dp), BF16),
            jax.ShapeDtypeStruct((w_r.shape[0] // dp, w_r.shape[1] * dp), BF16),
            jax.ShapeDtypeStruct((dp * small.shape[0], small.shape[1]), BF16),
        ),
        in_specs=[ANY] * 6,
        out_specs=(ANY,) * 6,
        scratch_shapes=2 * LineGather.sems(n) + CubeGather.sems(dp // 2) + Swap.sems(dp, 3),
        compiler_params=pltpu.CompilerParams(collective_id=0, has_side_effects=True),
        cost_estimate=pl.CostEstimate(flops=80 * 10**9, bytes_accessed=10**7, transcendentals=0),
        name="front",
    )(x, w, w_o, w_e, w_r, small)
    if r_all.shape[0] % 128:
        e_all = lax.all_to_all(w_e, "dp", split_axis=1, concat_axis=0, tiled=True)
    return seq, w_all, o_line, e_all, r_all, small_all


class SmallSum:
    def __init__(self, line, cube, parts, out, scratch):
        self.line, self.cube, self.parts, self.out = line, cube, parts, out
        self.come, self.gather, self.sems, self.line_send, self.line_recv = (
            scratch[0], scratch[1], scratch[2:5], scratch[5], scratch[6]
        )
        moves = [(lambda d: parts.at[d], lambda d: self.come.at[d])]
        self.swap = Swap(cube, moves, self.sems)

    @staticmethod
    def scratch(dp, n, rows, d):
        return [
            pltpu.VMEM((dp, rows, d), F32),
            pltpu.VMEM((n, rows, d), F32),
            *Swap.sems(dp, 1),
            DMA((n,)), DMA((n,)),
        ]

    def hop(self, k):
        line = self.line
        here = self.gather.at[line.me]
        return remote(
            here, here, self.line_send.at[k], self.line_recv.at[k], line.at((line.me + k) % line.n)
        )

    def middle(self):
        self.swap.finish()
        total = self.come[0]
        for d in range(1, self.cube.dp):
            total = total + self.come[d]
        self.gather[self.line.me] = total
        for k in range(1, self.line.n):
            self.hop(k).start()

    def finish(self):
        line = self.line
        for k in range(1, line.n):
            here = self.gather.at[(line.me - k + line.n) % line.n]
            remote(
                here, here, self.line_send.at[k], self.line_recv.at[k], line.at(line.me)
            ).wait_recv()
            self.hop(k).wait_send()
        total = self.gather[0]
        for z in range(1, line.n):
            total = total + self.gather[z]
        self.out[...] = total


def exchange_kernel(counts, *refs):
    lines, planes, gathers, cubes, swaps, outs, backs, small = counts
    line, cube = Line(), Cube()
    count = sum(counts)
    pairs, scratch = list(zip(refs[:count], refs[count : 2 * count])), list(refs[2 * count :])

    def take(number):
        taken = tuple(scratch[:number])
        del scratch[:number]
        return taken

    sums = [LineScatter(line, *pairs.pop(0), take(7)) for _ in range(lines)]
    folds = [CubeScatter(cube, *pairs.pop(0), take(8)) for _ in range(planes)]
    lanes = [LineGather(line, *pairs.pop(0), take(5)) for _ in range(gathers)]
    wholes = [CubeGather(cube, *pairs.pop(0), take(5)) for _ in range(cubes)]
    moves = [side_to_rows(*pairs.pop(0)) for _ in range(swaps)]
    swap = Swap(cube, moves, take(3)) if swaps else None
    turns = [rows_to_side(*pairs.pop(0)) for _ in range(outs)]
    turns += [side_to_rows(*pairs.pop(0)) for _ in range(backs)]
    turn = Swap(line, turns, take(3)) if turns else None
    little = SmallSum(line, cube, *pairs.pop(0), take(7)) if small else None
    barrier = pltpu.get_barrier_semaphore()
    peers = 0
    if small or turns:
        line.greet_all(barrier)
        peers = line.n - 1
    elif lines or gathers:
        line.greet(barrier)
        peers = line.peers()
    if small or swaps:
        cube.greet_all(barrier)
        peers = peers + cube.dp - 1
    elif planes or cubes:
        cube.greet(barrier)
        peers = peers + cube.peers()
    for s in sums:
        s.prepare()
    pl.semaphore_wait(barrier, peers)
    if turns:
        turn.start()
    if small:
        little.swap.start()
    for s in sums:
        s.step(1)
    for lane in lanes:
        lane.start()
    for whole in wholes[:1]:
        whole.start()
    for f in folds:
        f.start()
    if small:
        little.middle()
    pieces = [p for p in folds[0].order() if p] if planes else []
    per = -(-len(pieces) // (line.n - 1))
    for step in range(1, line.n):
        for whole in wholes[step - 1 : step]:
            for piece in range(1, cube.count):
                if piece.bit_length() < cube.levels:
                    whole.take(piece)
        if step > 1:
            for s in sums:
                s.step(step)
            for lane in lanes:
                lane.take(step - 1)
        for piece in pieces[:per]:
            for f in folds:
                f.fold(piece)
        pieces = pieces[per:]
        if step == 1 and swaps:
            swap.start()
        for whole in wholes[step - 1 : step]:
            whole.finish()
        for whole in wholes[step : step + 1]:
            whole.start()
    for f in folds:
        f.finish()
    for lane in lanes:
        lane.take(line.n - 1)
        lane.finish()
    for s in sums:
        s.finish()
    if turns:
        turn.finish()
    if swaps:
        swap.finish()
    if small:
        little.finish()


def exchange(
    collective_id, lines=(), planes=(), gathers=(), cubes=(), swaps=(), outs=(), backs=(), small=(),
    weight=80,
):
    dp, n = lax.axis_size("dp"), lax.axis_size("tensor")
    groups = (lines, planes, gathers, cubes, swaps, outs, backs, small)
    counts = tuple(len(group) for group in groups)
    operands = [part for group in groups for part in group]
    out_shape, out_specs, scratch = [], [], []

    def result(rows, d, kind, spec):
        out_shape.append(jax.ShapeDtypeStruct((rows, d), kind))
        out_specs.append(spec)

    for part in lines:
        rows, d = part.shape[0] // n, part.shape[1]
        result(rows, d, F32, VMEM)
        scratch += LineScatter.scratch(n, rows, d)
    for part in planes:
        rows, d = part.shape[0] // dp, part.shape[1]
        result(rows, d, F32, VMEM)
        scratch += CubeScatter.scratch(dp // 2, rows, d)
    for part in gathers:
        result(n * part.shape[0], part.shape[1], BF16, ANY)
        scratch += LineGather.sems(n)
    for part in cubes:
        result(dp * part.shape[0], part.shape[1], BF16, ANY)
        scratch += CubeGather.sems(dp // 2)
    for part in swaps:
        result(dp * part.shape[0], part.shape[1] // dp, BF16, ANY)
    if swaps:
        scratch += Swap.sems(dp, len(swaps))
    for part in outs:
        result(part.shape[0] // n, part.shape[1] * n, BF16, ANY)
    for part in backs:
        result(part.shape[0] * n, part.shape[1] // n, BF16, ANY)
    if outs or backs:
        scratch += Swap.sems(n, len(outs) + len(backs))
    for part in small:
        rows, d = part.shape[1:]
        result(rows, d, F32, VMEM)
        scratch += SmallSum.scratch(dp, n, rows, d)
    return pl.pallas_call(
        functools.partial(exchange_kernel, counts),
        out_shape=tuple(out_shape),
        in_specs=[ANY] * len(operands),
        out_specs=tuple(out_specs),
        scratch_shapes=scratch,
        compiler_params=pltpu.CompilerParams(
            collective_id=collective_id, has_side_effects=True, vmem_limit_bytes=60 << 20
        ),
        cost_estimate=pl.CostEstimate(flops=weight * 10**9, bytes_accessed=10**7, transcendentals=0),
        name="exchange",
    )(*operands)


PAIR = 2 * HEAD_DIM
NEVER = -1e30


def lane_of(shape, head):
    lane = lax.broadcasted_iota(jnp.int32, shape, 1)
    return (lane < HEAD_DIM) if head == 0 else (lane >= HEAD_DIM)


def sight(parents_ref, row, col):
    at = jnp.int32(row)
    seen = at == col
    for hop in range(row - col):
        at = parents_ref[at]
        seen = seen | (at == col)
    return jnp.where(seen, 0.0, NEVER).astype(F32)


def masked_scores(parents_ref, q_head, k_ref, row):
    scores = []
    for col in range(row + 1):
        part = over(q_head, k_ref[col * BLOCK : (col + 1) * BLOCK, :], 1, 1)
        if col == row:
            below = lax.broadcasted_iota(jnp.int32, part.shape, 1) <= lax.broadcasted_iota(
                jnp.int32, part.shape, 0
            )
            part = jnp.where(below, part, NEVER)
        else:
            part = part + sight(parents_ref, row, col)
        scores.append(part)
    return scores


def row_reduce(parts, fold, reduce):
    return reduce(functools.reduce(fold, parts), axis=-1, keepdims=True)


def attend_kernel(parents_ref, q_ref, k_ref, v_ref, out_ref):
    blocks = q_ref.shape[0] // BLOCK
    scale = 1.0 / math.sqrt(HEAD_DIM)
    for row in range(blocks):
        here = slice(row * BLOCK, (row + 1) * BLOCK)
        heads = []
        for head in range(2):
            q_head = q_ref[here, :].astype(F32) * scale
            q_head = jnp.where(lane_of(q_head.shape, head), q_head, 0.0).astype(BF16)
            scores = masked_scores(parents_ref, q_head, k_ref, row)
            top = row_reduce(scores, jnp.maximum, jnp.max)
            probs = [jnp.exp(s - top) for s in scores]
            total = row_reduce(probs, jnp.add, jnp.sum)
            out = None
            for col in range(row + 1):
                term = over(
                    probs[col].astype(BF16), v_ref[col * BLOCK : (col + 1) * BLOCK, :], 1, 0
                )
                out = term if out is None else out + term
            heads.append(out / total)
        mixed = jnp.where(lane_of(heads[0].shape, 0), heads[0], heads[1])
        out_ref[here, :] = mixed.astype(out_ref.dtype)


def attend(parents, qkv, width):
    rows = qkv.shape[0]
    pairs = width // PAIR
    spec = lambda part: pl.BlockSpec((rows, PAIR), lambda p, parents: (0, part * pairs + p))
    blocks = rows // BLOCK
    work = pairs * 2 * (blocks * (blocks + 1) // 2) * BLOCK * BLOCK
    return pl.pallas_call(
        attend_kernel,
        out_shape=jax.ShapeDtypeStruct((rows, width), BF16),
        grid_spec=pltpu.PrefetchScalarGridSpec(
            num_scalar_prefetch=1,
            grid=(pairs,),
            in_specs=[spec(0), spec(1), spec(2)],
            out_specs=pl.BlockSpec((rows, PAIR), lambda p, parents: (0, p)),
        ),
        compiler_params=pltpu.CompilerParams(vmem_limit_bytes=48 << 20),
        cost_estimate=pl.CostEstimate(
            flops=work * PAIR * 24, bytes_accessed=rows * width * 8, transcendentals=work
        ),
        name="attend",
    )(parents, qkv, qkv, qkv)


def attend_back_kernel(parents_ref, q_ref, k_ref, v_ref, g_ref, out_ref, dq_s, dk_s, dv_s):
    part = pl.program_id(1)
    blocks = q_ref.shape[0] // BLOCK
    scale = 1.0 / math.sqrt(HEAD_DIM)

    @pl.when(part == 0)
    def _():
        for row in range(blocks):
            here = slice(row * BLOCK, (row + 1) * BLOCK)
            dq_heads = []
            for head in range(2):
                lanes = lane_of((BLOCK, PAIR), head)
                q_head = jnp.where(lanes, q_ref[here, :].astype(F32) * scale, 0.0).astype(BF16)
                g_head = jnp.where(lanes, g_ref[here, :].astype(F32), 0.0).astype(BF16)
                scores = masked_scores(parents_ref, q_head, k_ref, row)
                top = row_reduce(scores, jnp.maximum, jnp.max)
                probs = [jnp.exp(s - top) for s in scores]
                rest = 1.0 / row_reduce(probs, jnp.add, jnp.sum)
                probs = [p * rest for p in probs]
                d_probs = [
                    over(g_head, v_ref[col * BLOCK : (col + 1) * BLOCK, :], 1, 1)
                    for col in range(row + 1)
                ]
                level = row_reduce([p * d for p, d in zip(probs, d_probs)], jnp.add, jnp.sum)
                dq = None
                for col in range(row + 1):
                    there = slice(col * BLOCK, (col + 1) * BLOCK)
                    d_scores = (probs[col] * (d_probs[col] - level)).astype(BF16)
                    term = over(d_scores, k_ref[there, :], 1, 0)
                    dq = term if dq is None else dq + term
                    dk = over(d_scores, q_head, 0, 0)
                    dv = over(probs[col].astype(BF16), g_head, 0, 0)
                    if row == col and head == 0:
                        dk_s[there, :] = dk
                        dv_s[there, :] = dv
                    else:
                        dk_s[there, :] += dk
                        dv_s[there, :] += dv
                dq_heads.append(dq * scale)
            dq_s[here, :] = jnp.where(lane_of((BLOCK, PAIR), 0), dq_heads[0], dq_heads[1]).astype(
                BF16
            )
        out_ref[...] = dq_s[...]

    @pl.when(part == 1)
    def _():
        out_ref[...] = dk_s[...].astype(BF16)

    @pl.when(part == 2)
    def _():
        out_ref[...] = dv_s[...].astype(BF16)


def attend_back(parents, qkv, grad, width):
    rows = qkv.shape[0]
    pairs = width // PAIR
    spec = lambda part: pl.BlockSpec((rows, PAIR), lambda p, c, parents: (0, part * pairs + p))
    blocks = rows // BLOCK
    work = pairs * 2 * (blocks * (blocks + 1) // 2) * BLOCK * BLOCK
    return pl.pallas_call(
        attend_back_kernel,
        out_shape=jax.ShapeDtypeStruct((rows, 3 * width), BF16),
        grid_spec=pltpu.PrefetchScalarGridSpec(
            num_scalar_prefetch=1,
            grid=(pairs, 3),
            in_specs=[
                spec(0),
                spec(1),
                spec(2),
                pl.BlockSpec((rows, PAIR), lambda p, c, parents: (0, p)),
            ],
            out_specs=pl.BlockSpec((rows, PAIR), lambda p, c, parents: (0, c * pairs + p)),
            scratch_shapes=[
                pltpu.VMEM((rows, PAIR), BF16),
                pltpu.VMEM((rows, PAIR), F32),
                pltpu.VMEM((rows, PAIR), F32),
            ],
        ),
        compiler_params=pltpu.CompilerParams(vmem_limit_bytes=48 << 20),
        cost_estimate=pl.CostEstimate(
            flops=work * PAIR * 60, bytes_accessed=rows * width * 14, transcendentals=work
        ),
        name="attend_back",
    )(parents, qkv, qkv, qkv, grad)


def ffn_kernel(host, n2_ref, dy_ref, we_ref, wr_ref, be_ref, *refs):
    if host:
        line_own, refs = refs[0], refs[1:]
    sum_ref, act_ref, dpre_ref, part_ref = refs[:4]
    refs = refs[4:]
    if host:
        line_full, refs = refs[0], refs[1:]
    we, wr, seq_st, dy_st, act_st, dpre_st, part_st, keep, give, core_in, fold_in = refs[:11]
    w_sem, load_sem, st_sem, rsc_send, rsc_recv, fold_send, fold_recv = refs[11:18]
    cube = Cube()
    levels, count, owner = cube.levels, cube.count, cube.owner
    rows, model = sum_ref.shape
    units = wr_ref.shape[0]
    barrier = pltpu.get_barrier_semaphore()
    cube.greet(barrier)
    if host:
        line = Line()
        line.greet(barrier)
        aside = LineScatter(line, line_own, line_full, refs[18:])
        aside.prepare()
    parts = we_ref.shape[0] // model
    mine_units = we_ref.shape[1]
    loads_w = [pltpu.make_async_copy(wr_ref, wr, w_sem.at[parts])]
    for part in range(parts):
        loads_w.append(
            pltpu.make_async_copy(
                we_ref.at[pl.ds(part * model, model)],
                we.at[:, pl.ds(part * mine_units, mine_units)],
                w_sem.at[part],
            )
        )

    def load(piece, slot):
        out = []
        for half, index in enumerate(owner(piece)):
            for kind, (ref, stage) in enumerate(((n2_ref, seq_st), (dy_ref, dy_st))):
                out.append(
                    pltpu.make_async_copy(
                        ref.at[window(index, rows)],
                        stage.at[slot, pl.ds(half * rows, rows)],
                        load_sem.at[kind, slot, half],
                    )
                )
        return out

    order = sorted(range(count), key=lambda p: (-(p.bit_length()), p))
    slots = {piece: i % 2 for i, piece in enumerate(order)}
    loads = {order[0]: load(order[0], 0)}
    for c in loads[order[0]] + loads_w:
        c.start()
    pl.semaphore_wait(barrier, cube.peers() + (line.peers() if host else 0))
    if host:
        aside.step(1)
    for c in loads_w:
        c.wait()
    stores, core_sends, folds = {}, {}, {}

    def add(piece, other):
        @pl.loop(0, rows // 16)
        def _(i):
            part = window(i, 16)
            keep[piece, part] = (
                keep[piece, part].astype(F32) + other[part].astype(F32)
            ).astype(BF16)

    def core_copy(piece):
        return remote(
            give.at[slots[piece]], core_in.at[piece],
            rsc_send.at[piece], rsc_recv.at[piece], cube.at(cube.me + cube.core_step),
        )

    def fold_copy(piece):
        return remote(
            keep.at[piece], fold_in.at[piece - 1], fold_send.at[piece - 1], fold_recv.at[piece - 1],
            cube.at(cube.me + cube.steps[piece.bit_length() - 1]),
        )

    def fold(piece):
        core_copy(piece).wait_recv()
        add(piece, core_in.at[piece])
        for level in range(levels - 1, piece.bit_length() - 1, -1):
            above = piece + (1 << level)
            fold_copy(above).wait_recv()
            add(piece, fold_in.at[above - 1])
        folds[piece] = fold_copy(piece)
        folds[piece].start()

    chunk = 256
    wide = 512
    for turn, piece in enumerate(order):
        slot = turn % 2
        for c in loads[piece]:
            c.wait()
        if turn + 1 < count:
            loads[order[turn + 1]] = load(order[turn + 1], 1 - slot)
            for c in loads[order[turn + 1]]:
                c.start()
        if turn >= 2:
            for c in stores[turn - 2]:
                c.wait()
            core_sends[order[turn - 2]].wait_send()

        @pl.loop(0, units // chunk)
        def _(i):
            cols = window(i, chunk)
            pre = over(seq_st[slot], we[:, cols], 1, 0) + be_ref[:, cols]
            d_act = over(dy_st[slot], wr[cols, :], 1, 1)
            square = pre * pre
            t = jnp.tanh(GELU * pre * (1.0 + 0.044715 * square))
            act_st[slot, :, cols] = (0.5 * pre * (1.0 + t)).astype(BF16)
            slope = 0.5 * (1.0 + t) + (0.5 * GELU) * pre * (1.0 - t * t) * (
                1.0 + (3 * 0.044715) * square
            )
            dpre_st[slot, :, cols] = (d_act * slope).astype(BF16)

        if turn:
            fold(order[turn - 1])

        @pl.loop(0, model // wide)
        def _(i):
            cols = window(i, wide)
            d_two = over(dpre_st[slot], we[cols, :], 1, 1).astype(BF16)
            keep[piece, :, cols] = d_two[:rows]
            give[slot, :, cols] = d_two[rows:]
            part_st[slot, :, cols] = over(act_st[slot], wr[:, cols], 1, 0).astype(BF16)

        core_sends[piece] = core_copy(piece)
        core_sends[piece].start()
        stores[turn] = []
        for half, index in enumerate(owner(piece)):
            to, part = window(index, rows), pl.ds(half * rows, rows)
            for kind, (stage, ref) in enumerate(
                ((act_st, act_ref), (dpre_st, dpre_ref), (part_st, part_ref))
            ):
                stores[turn].append(
                    pltpu.make_async_copy(stage.at[slot, part], ref.at[to], st_sem.at[kind, slot, half])
                )
        for c in stores[turn]:
            c.start()
        if host and turn < line.n - 2:
            aside.step(turn + 2)
    core_copy(0).wait_recv()
    for level in range(levels):
        fold_copy(1 << level).wait_recv()

    @pl.loop(0, rows // 16)
    def _(i):
        part = window(i, 16)
        total = keep[0, part].astype(F32) + core_in[0, part].astype(F32)
        for level in range(levels):
            total = total + fold_in[(1 << level) - 1, part].astype(F32)
        sum_ref[part] = total

    if host:
        for step in range(count + 2, line.n):
            aside.step(step)
        aside.finish()
    for turn in range(max(0, count - 2), count):
        for c in stores[turn]:
            c.wait()
        core_sends[order[turn]].wait_send()
    for s in folds.values():
        s.wait_send()


def ffn(n2, dy, we, wr, bias_e, own=None):
    host = own is not None
    n, dp = lax.axis_size("tensor"), lax.axis_size("dp")
    rows, model = n2.shape[0] // dp, n2.shape[1]
    units, count = wr.shape[0], dp // 2
    operands = [n2, dy, we, wr, bias_e] + [own] * host
    flops = 30 * dp * rows * model * units
    return pl.pallas_call(
        functools.partial(ffn_kernel, host),
        out_shape=(
            jax.ShapeDtypeStruct((rows, model), F32),
            jax.ShapeDtypeStruct((dp * rows, units), BF16),
            jax.ShapeDtypeStruct((dp * rows, units), BF16),
            jax.ShapeDtypeStruct((dp * rows, model), BF16),
            *[jax.ShapeDtypeStruct((rows, model), F32)] * host,
        ),
        in_specs=[ANY] * 4 + [VMEM] + [ANY] * host,
        out_specs=(VMEM, ANY, ANY, ANY) + (VMEM,) * host,
        scratch_shapes=[
            pltpu.VMEM((model, units), BF16),
            pltpu.VMEM((units, model), BF16),
            pltpu.VMEM((2, 2 * rows, model), BF16),
            pltpu.VMEM((2, 2 * rows, model), BF16),
            pltpu.VMEM((2, 2 * rows, units), BF16),
            pltpu.VMEM((2, 2 * rows, units), BF16),
            pltpu.VMEM((2, 2 * rows, model), BF16),
            pltpu.VMEM((count, rows, model), BF16),
            pltpu.VMEM((2, rows, model), BF16),
            pltpu.VMEM((count, rows, model), BF16),
            pltpu.VMEM((count - 1, rows, model), BF16),
            DMA((n + 1,)), DMA((2, 2, 2)), DMA((3, 2, 2)),
            DMA((count,)), DMA((count,)), DMA((count - 1,)), DMA((count - 1,)),
        ]
        + (LineScatter.scratch(n, rows, model) if host else []),
        compiler_params=pltpu.CompilerParams(
            collective_id=2 if host else 1, has_side_effects=True, vmem_limit_bytes=62 << 20
        ),
        cost_estimate=pl.CostEstimate(
            flops=flops, bytes_accessed=8 * dp * rows * (model + units), transcendentals=dp * rows * units
        ),
        name="ffn_plane",
    )(*operands)


def body(
    tokens,
    parents,
    cotangent,
    first_gain,
    first_shift,
    w_query,
    b_query,
    w_key,
    w_value,
    b_value,
    w_out,
    b_out,
    second_gain,
    second_shift,
    w_expand,
    b_expand,
    w_reduce,
    b_reduce,
):
    dp = lax.axis_size("dp")
    tn = lax.axis_size("tensor")
    dp_me = lax.axis_index("dp")
    tn_me = lax.axis_index("tensor")
    width = w_query.shape[1]
    model = w_query.shape[0] * dp
    units = w_expand.shape[1]
    mine = units // dp
    micros = range(tokens.shape[0])
    last = tokens.shape[0] - 1
    x_low = [tokens[m, 0] for m in micros]
    dy_low = [cotangent[m, 0] for m in micros]
    rows_here = x_low[0].shape[0]
    total = rows_here * tn

    cut = first_gain.shape[0]
    bq_rows, bq_cols = b_query.shape
    be_rows, be_cols = b_expand.shape
    small = jnp.concatenate(
        [first_gain, first_shift, b_out, second_gain, second_shift, b_reduce]
        + [b_query.reshape(-1), b_value.reshape(-1), b_expand.reshape(-1)]
    )
    used = small.shape[0]
    small = jnp.pad(small, (0, -used % 2048)).reshape(-1, 128)
    w_qkv = jnp.concatenate([w_query, w_key, w_value], axis=1)
    seq_x0, w_qkv, w_ot, w_e, w_r, small = front(
        x_low[0], w_qkv, w_out.T, w_expand, w_reduce, small
    )
    small = small.reshape(dp, -1)[:, :used]
    gain_one, shift_one, bias_out, gain_two, shift_two, bias_red = [
        small[:, i * cut : (i + 1) * cut].reshape(1, model).astype(F32) for i in range(6)
    ]
    at = 6 * cut
    bias_qkv = []
    for i in range(2):
        part = small[:, at : at + bq_rows * bq_cols].reshape(dp, bq_rows, bq_cols)
        bias_qkv.append(part.transpose(1, 0, 2).reshape(1, width).astype(F32))
        at += bq_rows * bq_cols
    bias_qkv = jnp.concatenate([bias_qkv[0], jnp.zeros((1, width), F32), bias_qkv[1]], 1)
    bias_e = small[:, at:].reshape(dp, dp, be_rows // dp, be_cols)
    bias_e = lax.dynamic_index_in_dim(bias_e, dp_me, 1, keepdims=False)
    bias_e = bias_e.transpose(1, 0, 2).reshape(mine)
    bias_e = jnp.pad(bias_e, (0, -mine % 2048)).reshape(-1, 128)

    seq_x = [seq_x0]
    w_r = lax.all_gather(w_r, "tensor", axis=0, tiled=True)
    w_e = lax.all_gather(w_e, "tensor", axis=1 if mine % 128 else 0, tiled=True)

    def outer(left, right):
        out = None
        for a, b in zip(left, right):
            term = over(a, b, 0, 0)
            out = term if out is None else out + term
        return out.astype(BF16)

    normal_one, seq_one, qkv, attended, hidden, normed_two = [], [], [], [], [], []
    out_part, seq_two, activated, d_pre, d_hidden, d_branch, out_sum = [], [], [], [], [], [], []
    d_qkv, d_one, d_att, row_attended = [], [], [], []
    g_gain_two = g_shift_two = g_bias_red = g_bias_out = g_bias_e = 0.0
    g_gain_one = g_shift_one = g_bias_qkv = 0.0
    for m in micros:
        normal_one.append(layer_norm(seq_x[m].astype(F32), 1.0, 0.0))
        seq_one.append((normal_one[m] * gain_one + shift_one).astype(BF16))
        qkv.append(
            (jnp.dot(seq_one[m], w_qkv, preferred_element_type=F32) + bias_qkv).astype(BF16)
        )
        attended.append(attend(parents[m, 0], qkv[m], width))
        if m == 0:
            bias_e, w_ot, grad, row_att = exchange(
                3, gathers=[bias_e], cubes=[w_ot, dy_low[m]], outs=[attended[m]]
            )
            seq_grad = [grad]
            bias_e = bias_e.reshape(tn, -1)[:, :mine].reshape(1, tn * mine).astype(F32)
        else:
            part, row_att, col_grad = exchange(
                4, planes=[out_part[m - 1]], outs=[attended[m]], backs=[d_att[m - 1]]
            )
            out_sum.append(part)
            d_att[m - 1] = col_grad
        if m < last:
            next_x, row_att = lax.optimization_barrier((x_low[m + 1], row_att))
            next_x = lax.all_gather(next_x, "tensor", axis=0, tiled=True)
        row_attended.append(row_att)
        branch = over(row_att, w_ot, 1, 1)
        hidden.append(x_low[m].astype(F32) + (branch + bias_out))
        normed_two.append(layer_norm(hidden[m], gain_two, shift_two).astype(BF16))
        if m < last:
            grad, normed_two[m] = lax.optimization_barrier((dy_low[m + 1], normed_two[m]))
            seq_grad.append(lax.all_gather(grad, "dp", axis=0, tiled=True))

        def attention_back(k):
            d_qkv.append(attend_back(parents[k, 0], qkv[k], d_att[k], width))
            d_one.append(over(d_qkv[k], w_qkv, 1, 1).astype(BF16))
            part = d_one[k].astype(F32)
            return (
                jnp.sum(part * normal_one[k], 0, keepdims=True),
                jnp.sum(part, 0, keepdims=True),
                jnp.sum(d_qkv[k].astype(F32), 0),
            )

        own = None
        if m:
            gain, shift, bias = attention_back(m - 1)
            g_gain_one, g_shift_one = g_gain_one + gain, g_shift_one + shift
            g_bias_qkv = g_bias_qkv + bias
            own = d_one[m - 1]

        if m == 0:
            (seq,) = exchange(7, cubes=[normed_two[m]])
        else:
            seq = lax.all_gather(normed_two[m], "dp", axis=0, tiled=True)
        d_two, act, dpre, part, *line = ffn(seq, seq_grad[m], w_e, w_r, bias_e, own)
        if m:
            d_one[m - 1] = line[0]
        seq_two.append(seq)
        activated.append(act)
        d_pre.append(dpre)
        out_part.append(part)
        if m == last:
            g_r = outer(activated, seq_grad)
            d_two, g_r = lax.optimization_barrier((d_two, g_r))
            g_r = lax.psum_scatter(g_r, "tensor", scatter_dimension=0, tiled=True)
        grad32 = dy_low[m].astype(F32)
        norm_value, norm_pull = jax.vjp(layer_norm, hidden[m], gain_two, shift_two)
        d_norm, g_gain, g_shift = norm_pull(d_two)
        d_hidden.append(grad32 + d_norm)
        d_branch.append(d_hidden[m].astype(BF16))
        d_att.append(jnp.dot(d_branch[m], w_ot, preferred_element_type=F32).astype(BF16))
        g_gain_two = g_gain_two + g_gain
        g_shift_two = g_shift_two + g_shift
        g_bias_red = g_bias_red + jnp.sum(grad32, 0, keepdims=True)
        g_bias_out = g_bias_out + jnp.sum(d_branch[m].astype(F32), 0, keepdims=True)
        g_bias_e = g_bias_e + jnp.sum(dpre.astype(F32), 0)
        if m < last:
            next_x, d_branch[m] = lax.optimization_barrier((next_x, d_branch[m]))
            seq_x.append(next_x)

    g_ot = outer([jnp.concatenate(d_branch, 0)], [jnp.concatenate(row_attended, 0)])
    g_ot, d_att[last] = exchange(6, planes=[g_ot], backs=[d_att[last]], weight=15)
    d_att[last], *d_pre = lax.optimization_barrier((d_att[last], *d_pre))
    g_et = outer(d_pre, seq_two)
    d_att[last], g_r = lax.optimization_barrier((d_att[last], g_r))
    g_et = lax.psum_scatter(g_et, "tensor", scatter_dimension=0, tiled=True)
    gain, shift, bias = attention_back(last)
    g_gain_one, g_shift_one = g_gain_one + gain, g_shift_one + shift
    g_bias_qkv = g_bias_qkv + bias

    rows = jnp.concatenate(
        [g_gain_one, g_shift_one, g_bias_out, g_gain_two, g_shift_two, g_bias_red], 0
    )
    rows = rows.reshape(6, dp, cut).transpose(1, 0, 2).reshape(dp, 6 * cut)
    row_qv = jnp.concatenate([g_bias_qkv[:width], g_bias_qkv[2 * width :]])
    row_qv = row_qv.reshape(2 * bq_rows, dp, bq_cols).transpose(1, 0, 2)[:, None]
    row_qv = lax.dynamic_update_slice(
        jnp.zeros((dp, tn, 2 * bq_rows, bq_cols), F32), row_qv, (0, tn_me, 0, 0)
    ).reshape(dp, -1)
    row_e = g_bias_e.reshape(tn, be_rows // dp, dp, be_cols).transpose(2, 0, 1, 3)[:, :, None]
    row_e = lax.dynamic_update_slice(
        jnp.zeros((dp, tn, dp, be_rows // dp, be_cols), F32), row_e, (0, 0, dp_me, 0, 0)
    ).reshape(dp, -1)
    little = jnp.concatenate([rows, row_qv, row_e], 1)
    little = jnp.pad(little, ((0, 0), (0, -little.shape[1] % 1024))).reshape(dp, -1, 128)

    g_qkv = outer(seq_one, d_qkv)
    g_ot = g_ot.astype(BF16).reshape(-1, tn, width).transpose(1, 0, 2).reshape(-1, width)
    d_one[last], g_ot, g_qkv, out_last, g_expand, g_reduce, little = exchange(
        5,
        lines=[d_one[last], g_ot],
        planes=[g_qkv, out_part[last]],
        swaps=[g_et, g_r],
        small=[little],
    )
    out_sum.append(out_last)
    g_query, g_key, g_value = [g_qkv[:, i * width : (i + 1) * width] for i in range(3)]
    g_out = g_ot.T
    g_expand = g_expand.T.astype(F32)
    g_reduce = g_reduce.astype(F32)
    layer_out = [(hidden[m] + (out_sum[m] + bias_red)).astype(BF16) for m in micros]
    little = little.reshape(-1)
    six = little[: 6 * cut].reshape(6, cut)
    at = 6 * cut
    g_bqv = little[at : at + tn * 2 * bq_rows * bq_cols].reshape(tn, 2 * bq_rows, bq_cols)
    g_bqv = lax.dynamic_index_in_dim(g_bqv, tn_me, 0, keepdims=False)
    g_bq, g_bv = g_bqv[:bq_rows], g_bqv[bq_rows:]
    at += tn * 2 * bq_rows * bq_cols
    g_be = little[at : at + tn * be_rows * be_cols].reshape(tn, be_rows, be_cols)
    g_be = lax.dynamic_index_in_dim(g_be, tn_me, 0, keepdims=False)
    input_grad = []
    for m in micros:
        first_value, first_pull = jax.vjp(
            lambda rows: layer_norm(rows, gain_one, shift_one), x_low[m].astype(F32)
        )
        input_grad.append((d_hidden[m] + first_pull(d_one[m])[0]).astype(BF16))

    return (
        jnp.stack(layer_out, 0)[:, None],
        jnp.stack(input_grad, 0)[:, None],
        six[0],
        six[1],
        g_query,
        g_bq,
        g_key,
        g_value,
        g_bv,
        g_out,
        six[2],
        six[3],
        six[4],
        g_expand,
        g_be,
        g_reduce,
        six[5],
    )


def solution(mesh):
    in_specs = (
        P(None, "dp", "tensor", None),
        P(None, "dp", None),
        P(None, "dp", "tensor", None),
        P("dp"),
        P("dp"),
        P("dp", "tensor"),
        P("tensor", "dp"),
        P("dp", "tensor"),
        P("dp", "tensor"),
        P("tensor", "dp"),
        P("tensor", "dp"),
        P("dp"),
        P("dp"),
        P("dp"),
        P("dp", "tensor"),
        P("tensor", "dp"),
        P("tensor", "dp"),
        P("dp"),
    )
    out_specs = (
        P(None, "dp", "tensor", None),
        P(None, "dp", "tensor", None),
        P("dp"),
        P("dp"),
        P("dp", "tensor"),
        P("tensor", "dp"),
        P("dp", "tensor"),
        P("dp", "tensor"),
        P("tensor", "dp"),
        P("tensor", "dp"),
        P("dp"),
        P("dp"),
        P("dp"),
        P("dp", "tensor"),
        P("tensor", "dp"),
        P("tensor", "dp"),
        P("dp"),
    )
    return jax.shard_map(body, mesh=mesh, in_specs=in_specs, out_specs=out_specs, check_vma=False)
```

```python
import functools
import math

import jax
import jax.numpy as jnp
from jax import lax
from jax.experimental import pallas as pl
from jax.experimental.pallas import tpu as pltpu
from jax.sharding import PartitionSpec as P

HEAD_DIM = 64
BLOCK = 256

F32 = jnp.float32
BF16 = jnp.bfloat16
MESH = pl.DeviceIdType.MESH
DMA = pltpu.SemaphoreType.DMA
GELU = math.sqrt(2.0 / math.pi)


def layer_norm(rows, gain, shift):
    center = rows - jnp.mean(rows, -1, keepdims=True)
    spread = jnp.mean(center * center, -1, keepdims=True)
    return center * lax.rsqrt(spread + 1e-05) * gain + shift


def after(value, *others):
    return lax.optimization_barrier((value,) + others)[0]


def over(left, right, on_left, on_right):
    return lax.dot_general(
        left, right, (((on_left,), (on_right,)), ((), ())), preferred_element_type=F32
    )


def window(index, rows):
    return pl.ds(pl.multiple_of(index * rows, rows), rows)


def remote(src, dst, send, recv, to):
    return pltpu.make_async_remote_copy(
        src_ref=src, dst_ref=dst, send_sem=send, recv_sem=recv,
        device_id=to, device_id_type=MESH,
    )


class Line:
    def __init__(self):
        self.n = lax.axis_size("tensor")
        self.me = lax.axis_index("tensor")
        self.dp = lax.axis_index("dp")

    def at(self, index):
        return (self.dp, index)

    def greet(self, barrier):
        @pl.when(self.me > 0)
        def _():
            pl.semaphore_signal(barrier, inc=1, device_id=self.at(self.me - 1), device_id_type=MESH)

        @pl.when(self.me < self.n - 1)
        def _():
            pl.semaphore_signal(barrier, inc=1, device_id=self.at(self.me + 1), device_id_type=MESH)

    @property
    def size(self):
        return self.n

    def greet_all(self, barrier):
        for k in range(1, self.n):
            pl.semaphore_signal(
                barrier, inc=1, device_id=self.at((self.me + k) % self.n), device_id_type=MESH
            )

    def peers(self):
        return (self.me + self.n - 1) // self.n + (2 * self.n - 2 - self.me) // self.n


class LineGather:
    def __init__(self, line, own, full, sems):
        self.line, self.own, self.full = line, own, full
        self.side = own.shape[0] == full.shape[0]
        self.local, self.up_send, self.up_recv, self.down_send, self.down_recv = sems

    @staticmethod
    def sems(n):
        return [DMA, DMA((n - 1,)), DMA((n - 1,)), DMA((n - 1,)), DMA((n - 1,))]

    def slot(self, index):
        if self.side:
            return self.full.at[:, window(index, self.own.shape[1])]
        return self.full.at[window(index, self.own.shape[0])]

    def hop(self, step, up):
        line = self.line
        if up:
            shard, to = line.me - (step - 1), line.me + 1
            send, recv = self.up_send, self.up_recv
        else:
            shard, to = line.me + (step - 1), line.me - 1
            send, recv = self.down_send, self.down_recv
        there = self.slot(shard)
        src = self.own if step == 1 else there
        return remote(src, there, send.at[step - 1], recv.at[step - 1], line.at(to))

    def sends(self, step, up):
        line = self.line
        if up:
            return (line.me < line.n - 1) & (line.me >= step - 1)
        return (line.me > 0) & (line.me + step - 1 < line.n)

    def takes(self, step, up):
        line = self.line
        return (line.me >= step) if up else (line.me + step < line.n)

    def send(self, step):
        for up in (True, False):
            @pl.when(self.sends(step, up))
            def _():
                self.hop(step, up).start()

    def start(self):
        pltpu.make_async_copy(self.own, self.slot(self.line.me), self.local).start()
        self.send(1)

    def take(self, step):
        for up in (True, False):
            @pl.when(self.takes(step, up))
            def _():
                line = self.line
                shard = (line.me - step) if up else (line.me + step)
                here = self.slot(shard)
                send, recv = (
                    (self.up_send, self.up_recv) if up else (self.down_send, self.down_recv)
                )
                remote(
                    here, here, send.at[step - 1], recv.at[step - 1], line.at(line.me)
                ).wait_recv()
        if step < self.line.n - 1:
            self.send(step + 1)

    def finish(self):
        for step in range(1, self.line.n):
            for up in (True, False):
                @pl.when(self.sends(step, up))
                def _():
                    self.hop(step, up).wait_send()
        pltpu.make_async_copy(self.own, self.slot(self.line.me), self.local).wait()


class LineScatter:
    def __init__(self, line, parts, out, scratch):
        self.line, self.parts, self.out = line, parts, out
        self.rows = out.shape[0]
        (self.own, self.sum, self.come, self.load, self.own_sem, self.send_sem, self.recv_sem) = scratch

    @staticmethod
    def scratch(n, rows, d):
        return [
            pltpu.VMEM((rows, d), BF16),
            pltpu.VMEM((2, n - 1, rows, d), BF16),
            pltpu.VMEM((2, n - 1, rows, d), BF16),
            DMA((2, n - 1)), DMA, DMA((2, n - 1)), DMA((2, n - 1)),
        ]

    def sends(self, step, up):
        line = self.line
        return (line.me <= step - 1) if up else (line.n - 1 - line.me <= step - 1)

    def load_of(self, step, up):
        line = self.line
        chunk = (line.me + line.n - step) if up else (line.me - line.n + step)
        way = 0 if up else 1
        return pltpu.make_async_copy(
            self.parts.at[window(chunk, self.rows)], self.sum.at[way, step - 1], self.load.at[way, step - 1]
        )

    def hop(self, step, up):
        line, way = self.line, 0 if up else 1
        return remote(
            self.sum.at[way, step - 1], self.come.at[way, step - 1],
            self.send_sem.at[way, step - 1], self.recv_sem.at[way, step - 1],
            line.at(line.me + 1 if up else line.me - 1),
        )

    def wait_from(self, step, up):
        line, way = self.line, 0 if up else 1
        remote(
            self.come.at[way, step - 1], self.come.at[way, step - 1],
            self.send_sem.at[way, step - 1], self.recv_sem.at[way, step - 1],
            line.at(line.me),
        ).wait_recv()

    def own_load(self):
        return pltpu.make_async_copy(
            self.parts.at[window(self.line.me, self.rows)], self.own, self.own_sem
        )

    def prepare(self):
        self.own_load().start()
        for step in range(1, self.line.n):
            for up in (True, False):
                @pl.when(self.sends(step, up))
                def _():
                    self.load_of(step, up).start()

    def step(self, step):
        line = self.line
        for up in (True, False):
            way = 0 if up else 1

            @pl.when(self.sends(step, up))
            def _():
                self.load_of(step, up).wait()
                if step > 1:
                    inner = (line.me > 0) if up else (line.me < line.n - 1)

                    @pl.when(inner)
                    def _():
                        self.wait_from(step - 1, up)

                        @pl.loop(0, self.rows // 16)
                        def _(i):
                            part = window(i, 16)
                            self.sum[way, step - 1, part] = (
                                self.sum[way, step - 1, part].astype(F32)
                                + self.come[way, step - 2, part].astype(F32)
                            ).astype(BF16)

                if step > 1:

                    @pl.when(self.sends(step - 1, up))
                    def _():
                        self.hop(step - 1, up).wait_send()

                self.hop(step, up).start()

    def finish(self):
        line, n = self.line, self.line.n
        self.own_load().wait()

        @pl.loop(0, self.rows // 16)
        def _(i):
            part = window(i, 16)
            self.out[part] = self.own[part].astype(F32)

        for up in (True, False):
            way = 0 if up else 1

            @pl.when((line.me > 0) if up else (line.me < n - 1))
            def _():
                self.wait_from(n - 1, up)

                @pl.loop(0, self.rows // 16)
                def _(i):
                    part = window(i, 16)
                    self.out[part] += self.come[way, n - 2, part].astype(F32)

        for up in (True, False):
            @pl.when(self.sends(n - 1, up))
            def _():
                self.hop(n - 1, up).wait_send()


class Cube:
    def __init__(self):
        self.dp = lax.axis_size("dp")
        self.levels = levels = self.dp.bit_length() - 2
        self.count = 1 << levels
        self.me = me = lax.axis_index("dp")
        self.tensor = lax.axis_index("tensor")
        core = me % 2
        flips = []
        for bit in range(1, levels + 1):
            flips.append((1 << bit) * (1 - 2 * ((me // (1 << bit)) % 2)))
        self.steps = [
            flips[l] * (1 - core) + flips[levels - 1 - l] * core for l in range(levels)
        ]
        self.core_step = 1 - 2 * core

    def at(self, index):
        return (index, self.tensor)

    def owner(self, piece):
        mine, other = self.me, self.me + self.core_step
        for l in range(self.levels):
            if piece >> l & 1:
                mine = mine + self.steps[l]
                other = other + self.steps[self.levels - 1 - l]
        return mine, other

    def greet(self, barrier):
        for step in self.steps + [self.core_step]:
            pl.semaphore_signal(
                barrier, inc=1, device_id=self.at(self.me + step), device_id_type=MESH
            )

    @property
    def size(self):
        return self.dp

    def greet_all(self, barrier):
        for k in range(1, self.dp):
            pl.semaphore_signal(
                barrier, inc=1, device_id=self.at((self.me + k) % self.dp), device_id_type=MESH
            )

    def peers(self):
        return self.levels + 1


class CubeGather:
    def __init__(self, cube, own, full, sems):
        self.cube, self.own, self.full = cube, own, full
        self.rows = own.shape[0]
        self.local, self.send_sem, self.recv_sem, self.core_send, self.core_recv = sems
        self.arrived, self.sent = {0}, []

    @staticmethod
    def sems(count):
        return [DMA, DMA((count,)), DMA((count,)), DMA((count,)), DMA((count,))]

    def slot(self, index):
        return self.full.at[window(index, self.rows)]

    def src(self, piece):
        return self.own if piece == 0 else self.slot(self.cube.owner(piece)[0])

    def hop(self, piece, level):
        cube, there = self.cube, piece + (1 << level)
        return remote(
            self.src(piece), self.slot(cube.owner(piece)[0]),
            self.send_sem.at[there], self.recv_sem.at[there], cube.at(cube.me + cube.steps[level]),
        )

    def core(self, piece):
        cube = self.cube
        return remote(
            self.src(piece), self.slot(cube.owner(piece)[0]),
            self.core_send.at[piece], self.core_recv.at[piece], cube.at(cube.me + cube.core_step),
        )

    def give(self, piece):
        for level in range(piece.bit_length(), self.cube.levels):
            self.sent.append(self.hop(piece, level))
            self.sent[-1].start()
        self.sent.append(self.core(piece))
        self.sent[-1].start()

    def start(self):
        self.place = pltpu.make_async_copy(self.own, self.slot(self.cube.me), self.local)
        self.place.start()
        self.give(0)

    def take(self, piece):
        if piece in self.arrived:
            return
        here = self.slot(self.cube.owner(piece)[0])
        remote(
            here, here, self.send_sem.at[piece], self.recv_sem.at[piece], self.cube.at(self.cube.me)
        ).wait_recv()
        self.arrived.add(piece)
        self.give(piece)

    def take_core(self, piece):
        here = self.slot(self.cube.owner(piece)[1])
        remote(
            here, here, self.core_send.at[piece], self.core_recv.at[piece], self.cube.at(self.cube.me)
        ).wait_recv()

    def finish(self):
        for piece in range(self.cube.count):
            self.take(piece)
            self.take_core(piece)
        for copy in self.sent:
            copy.wait_send()
        self.place.wait()


class CubeScatter:
    def __init__(self, cube, parts, out, scratch):
        self.cube, self.parts, self.out = cube, parts, out
        self.rows = out.shape[0]
        (self.keep, self.core_in, self.fold_in, self.load_sem,
         self.core_send, self.core_recv, self.send_sem, self.recv_sem) = scratch

    @staticmethod
    def scratch(count, rows, d):
        return [
            pltpu.VMEM((count, rows, d), BF16),
            pltpu.VMEM((count, rows, d), BF16),
            pltpu.VMEM((count - 1, rows, d), BF16),
            DMA((count,)), DMA((count,)), DMA((count,)), DMA((count - 1,)), DMA((count - 1,)),
        ]

    def load(self, piece):
        return pltpu.make_async_copy(
            self.parts.at[window(self.cube.owner(piece)[0], self.rows)],
            self.keep.at[piece], self.load_sem.at[piece],
        )

    def core(self, piece):
        cube = self.cube
        return remote(
            self.parts.at[window(cube.owner(piece)[1], self.rows)], self.core_in.at[piece],
            self.core_send.at[piece], self.core_recv.at[piece], cube.at(cube.me + cube.core_step),
        )

    def hop(self, piece):
        cube, level = self.cube, piece.bit_length() - 1
        return remote(
            self.keep.at[piece], self.fold_in.at[piece - 1],
            self.send_sem.at[piece - 1], self.recv_sem.at[piece - 1],
            cube.at(cube.me + cube.steps[level]),
        )

    def order(self):
        return sorted(range(self.cube.count), key=lambda p: (-(p.bit_length()), p))

    def start(self):
        for piece in self.order():
            self.core(piece).start()
            self.load(piece).start()

    def add(self, piece, other):
        @pl.loop(0, self.rows // 16)
        def _(i):
            part = window(i, 16)
            self.keep[piece, part] = (
                self.keep[piece, part].astype(F32) + other[part].astype(F32)
            ).astype(BF16)

    def fold(self, piece):
        self.load(piece).wait()
        self.core(piece).wait_recv()
        self.add(piece, self.core_in.at[piece])
        for level in range(self.cube.levels - 1, piece.bit_length() - 1, -1):
            above = piece + (1 << level)
            self.hop(above).wait_recv()
            self.add(piece, self.fold_in.at[above - 1])
        if piece:
            self.hop(piece).start()

    def finish(self):
        self.fold(0)

        @pl.loop(0, self.rows // 16)
        def _(i):
            part = window(i, 16)
            self.out[part] = self.keep[0, part].astype(F32)

        for piece in range(self.cube.count):
            self.core(piece).wait_send()
            if piece:
                self.hop(piece).wait_send()


class Swap:
    def __init__(self, place, moves, sems):
        self.place, self.moves = place, moves
        self.send_sem, self.recv_sem, self.local = sems

    @staticmethod
    def sems(size, moves):
        return [DMA((moves, size)), DMA((moves, size)), DMA((moves,))]

    def copies(self):
        place = self.place
        out = []
        for k in range(1, place.size):
            to = (place.me + k) % place.size
            for m, (src, dst) in enumerate(self.moves):
                out.append(
                    remote(src(to), dst(place.me), self.send_sem.at[m, k], self.recv_sem.at[m, k], place.at(to))
                )
        return out

    def locals(self):
        return [
            pltpu.make_async_copy(src(self.place.me), dst(self.place.me), self.local.at[m])
            for m, (src, dst) in enumerate(self.moves)
        ]

    def start(self):
        for copy in self.copies() + self.locals():
            copy.start()

    def finish(self):
        place = self.place
        for copy in self.copies():
            copy.wait_send()
        for k in range(1, place.size):
            of = (place.me - k + place.size) % place.size
            for m, (src, dst) in enumerate(self.moves):
                here = dst(of)
                remote(here, here, self.send_sem.at[m, k], self.recv_sem.at[m, k], place.at(of)).wait_recv()
        for copy in self.locals():
            copy.wait()


def rows_to_side(src, dst):
    rows, cols = dst.shape[0], src.shape[1]
    return (lambda d: src.at[window(d, rows)], lambda d: dst.at[:, window(d, cols)])


def side_to_rows(src, dst):
    rows, cols = src.shape[0], dst.shape[1]
    return (lambda d: src.at[:, window(d, cols)], lambda d: dst.at[window(d, rows)])


ANY = pl.BlockSpec(memory_space=pl.ANY)
VMEM = pl.BlockSpec(memory_space=pltpu.VMEM)


def front_kernel(
    x_ref, w_ref, we_ref, wr_ref, small_ref, seq_ref, w_out, we_out, wr_out, small_out, *sems
):
    line, cube = Line(), Cube()
    gather = LineGather(line, x_ref, seq_ref, sems[:5])
    weights = CubeGather(cube, w_ref, w_out, sems[5:10])
    tile = small_ref.shape[0]
    moves = [
        (lambda d: small_ref, lambda d: small_out.at[window(d, tile)]),
        rows_to_side(wr_ref, wr_out),
    ]
    if wr_out.shape[0] % 128 == 0:
        moves.append(side_to_rows(we_ref, we_out))
    swap = Swap(cube, moves, sems[10:13])
    barrier = pltpu.get_barrier_semaphore()
    line.greet(barrier)
    cube.greet_all(barrier)
    pl.semaphore_wait(barrier, cube.dp - 1 + line.peers())
    gather.start()
    weights.start()
    gather.take(1)
    for piece in range(1, cube.count):
        if piece.bit_length() < cube.levels:
            weights.take(piece)
    swap.start()
    gather.take(2)
    for piece in range(1, cube.count):
        weights.take(piece)
    for step in range(3, line.n):
        gather.take(step)
    weights.finish()
    swap.finish()
    gather.finish()


def front(x, w, w_e, w_r, small):
    dp, n = lax.axis_size("dp"), lax.axis_size("tensor")
    rows, model = x.shape
    seq, w_all, e_all, r_all, small_all = pl.pallas_call(
        front_kernel,
        out_shape=(
            jax.ShapeDtypeStruct((n * rows, model), BF16),
            jax.ShapeDtypeStruct((dp * w.shape[0], w.shape[1]), BF16),
            jax.ShapeDtypeStruct((dp * w_e.shape[0], w_e.shape[1] // dp), BF16),
            jax.ShapeDtypeStruct((w_r.shape[0] // dp, w_r.shape[1] * dp), BF16),
            jax.ShapeDtypeStruct((dp * small.shape[0], small.shape[1]), BF16),
        ),
        in_specs=[ANY] * 5,
        out_specs=(ANY,) * 5,
        scratch_shapes=LineGather.sems(n) + CubeGather.sems(dp // 2) + Swap.sems(dp, 3),
        compiler_params=pltpu.CompilerParams(collective_id=0, has_side_effects=True),
        cost_estimate=pl.CostEstimate(flops=80 * 10**9, bytes_accessed=10**7, transcendentals=0),
        name="front",
    )(x, w, w_e, w_r, small)
    if r_all.shape[0] % 128:
        e_all = lax.all_to_all(w_e, "dp", split_axis=1, concat_axis=0, tiled=True)
    return seq, w_all, e_all, r_all, small_all


class SmallSum:
    def __init__(self, line, cube, parts, out, scratch):
        self.line, self.cube, self.parts, self.out = line, cube, parts, out
        self.come, self.gather, self.sems, self.line_send, self.line_recv = (
            scratch[0], scratch[1], scratch[2:5], scratch[5], scratch[6]
        )
        moves = [(lambda d: parts.at[d], lambda d: self.come.at[d])]
        self.swap = Swap(cube, moves, self.sems)

    @staticmethod
    def scratch(dp, n, rows, d):
        return [
            pltpu.VMEM((dp, rows, d), F32),
            pltpu.VMEM((n, rows, d), F32),
            *Swap.sems(dp, 1),
            DMA((n,)), DMA((n,)),
        ]

    def hop(self, k):
        line = self.line
        here = self.gather.at[line.me]
        return remote(
            here, here, self.line_send.at[k], self.line_recv.at[k], line.at((line.me + k) % line.n)
        )

    def middle(self):
        self.swap.finish()
        total = self.come[0]
        for d in range(1, self.cube.dp):
            total = total + self.come[d]
        self.gather[self.line.me] = total
        for k in range(1, self.line.n):
            self.hop(k).start()

    def finish(self):
        line = self.line
        for k in range(1, line.n):
            here = self.gather.at[(line.me - k + line.n) % line.n]
            remote(
                here, here, self.line_send.at[k], self.line_recv.at[k], line.at(line.me)
            ).wait_recv()
            self.hop(k).wait_send()
        total = self.gather[0]
        for z in range(1, line.n):
            total = total + self.gather[z]
        self.out[...] = total


def exchange_kernel(counts, *refs):
    lines, planes, gathers, cubes, swaps, outs, backs, small, spreads = counts
    line, cube = Line(), Cube()
    count = sum(counts)
    pairs, scratch = list(zip(refs[:count], refs[count : 2 * count])), list(refs[2 * count :])
    whole_refs = [scratch.pop(0) for _ in range(spreads)]

    def take(number):
        taken = tuple(scratch[:number])
        del scratch[:number]
        return taken

    sums = [LineScatter(line, *pairs.pop(0), take(7)) for _ in range(lines)]
    folds = [CubeScatter(cube, *pairs.pop(0), take(8)) for _ in range(planes)]
    lanes = [LineGather(line, *pairs.pop(0), take(5)) for _ in range(gathers)]
    wholes = [CubeGather(cube, *pairs.pop(0), take(5)) for _ in range(cubes)]
    moves = [side_to_rows(*pairs.pop(0)) for _ in range(swaps)]
    swap = Swap(cube, moves, take(3)) if swaps else None
    turns = [rows_to_side(*pairs.pop(0)) for _ in range(outs)]
    turns += [side_to_rows(*pairs.pop(0)) for _ in range(backs)]
    turn = Swap(line, turns, take(3)) if turns else None
    little = SmallSum(line, cube, *pairs.pop(0), take(7)) if small else None
    for whole_ref in whole_refs:
        own, side = pairs.pop(0)
        lanes.append(LineGather(line, own, side, take(5)))
        wholes.append(CubeGather(cube, side, whole_ref, take(5)))
    barrier = pltpu.get_barrier_semaphore()
    peers = 0
    if small or turns:
        line.greet_all(barrier)
        peers = line.n - 1
    elif lanes or lines:
        line.greet(barrier)
        peers = line.peers()
    if small or swaps:
        cube.greet_all(barrier)
        peers = peers + cube.dp - 1
    elif planes or wholes:
        cube.greet(barrier)
        peers = peers + cube.peers()
    for s in sums:
        s.prepare()
    pl.semaphore_wait(barrier, peers)
    if turns:
        turn.start()
    if small:
        little.swap.start()
    for s in sums:
        s.step(1)
    for lane in lanes:
        lane.start()
    for whole in wholes[:1]:
        whole.start()
    for f in folds:
        f.start()
    if small:
        little.middle()
    if spreads:
        for step in range(1, line.n):
            for lane in lanes:
                lane.take(step)
        for lane in lanes:
            lane.finish()
        for whole in wholes[1:]:
            whole.start()
        lanes = []
    pieces = [p for p in folds[0].order() if p] if planes else []
    per = -(-len(pieces) // (line.n - 1))
    for step in range(1, line.n):
        for whole in wholes[step - 1 : step]:
            for piece in range(1, cube.count):
                if piece.bit_length() < cube.levels:
                    whole.take(piece)
        if step > 1:
            for s in sums:
                s.step(step)
            for lane in lanes:
                lane.take(step - 1)
        for piece in pieces[:per]:
            for f in folds:
                f.fold(piece)
        pieces = pieces[per:]
        if step == 1 and swaps:
            swap.start()
        for whole in wholes[step - 1 : step]:
            whole.finish()
        for whole in wholes[step : step + 1]:
            if not spreads:
                whole.start()
    for f in folds:
        f.finish()
    for lane in lanes:
        lane.take(line.n - 1)
        lane.finish()
    for s in sums:
        s.finish()
    if turns:
        turn.finish()
    if swaps:
        swap.finish()
    if small:
        little.finish()


def exchange(
    collective_id, lines=(), planes=(), gathers=(), cubes=(), swaps=(), outs=(), backs=(), small=(),
    spreads=(), weight=80,
):
    dp, n = lax.axis_size("dp"), lax.axis_size("tensor")
    groups = (lines, planes, gathers, cubes, swaps, outs, backs, small, spreads)
    counts = tuple(len(group) for group in groups)
    operands = [part for group in groups for part in group]
    out_shape, out_specs, scratch = [], [], []

    def result(rows, d, kind, spec):
        out_shape.append(jax.ShapeDtypeStruct((rows, d), kind))
        out_specs.append(spec)

    for part in lines:
        rows, d = part.shape[0] // n, part.shape[1]
        result(rows, d, F32, VMEM)
        scratch += LineScatter.scratch(n, rows, d)
    for part in planes:
        rows, d = part.shape[0] // dp, part.shape[1]
        result(rows, d, F32, VMEM)
        scratch += CubeScatter.scratch(dp // 2, rows, d)
    for part in gathers:
        result(n * part.shape[0], part.shape[1], BF16, ANY)
        scratch += LineGather.sems(n)
    for part in cubes:
        result(dp * part.shape[0], part.shape[1], BF16, ANY)
        scratch += CubeGather.sems(dp // 2)
    for part in swaps:
        result(dp * part.shape[0], part.shape[1] // dp, BF16, ANY)
    if swaps:
        scratch += Swap.sems(dp, len(swaps))
    for part in outs:
        result(part.shape[0] // n, part.shape[1] * n, BF16, ANY)
    for part in backs:
        result(part.shape[0] * n, part.shape[1] // n, BF16, ANY)
    if outs or backs:
        scratch += Swap.sems(n, len(outs) + len(backs))
    for part in small:
        rows, d = part.shape[1:]
        result(rows, d, F32, VMEM)
        scratch += SmallSum.scratch(dp, n, rows, d)
    for part in spreads:
        result(part.shape[0], n * part.shape[1], BF16, ANY)
        scratch += LineGather.sems(n) + CubeGather.sems(dp // 2)
    for part in spreads:
        result(dp * part.shape[0], n * part.shape[1], BF16, ANY)
    return pl.pallas_call(
        functools.partial(exchange_kernel, counts),
        out_shape=tuple(out_shape),
        in_specs=[ANY] * len(operands),
        out_specs=tuple(out_specs),
        scratch_shapes=scratch,
        compiler_params=pltpu.CompilerParams(
            collective_id=collective_id, has_side_effects=True, vmem_limit_bytes=60 << 20
        ),
        cost_estimate=pl.CostEstimate(flops=weight * 10**9, bytes_accessed=10**7, transcendentals=0),
        name="exchange",
    )(*operands)


PAIR = 2 * HEAD_DIM
NEVER = -1e30


def lane_of(shape, head):
    lane = lax.broadcasted_iota(jnp.int32, shape, 1)
    return (lane < HEAD_DIM) if head == 0 else (lane >= HEAD_DIM)


def sight(parents_ref, row, col):
    at = jnp.int32(row)
    seen = at == col
    for hop in range(row - col):
        at = parents_ref[at]
        seen = seen | (at == col)
    return jnp.where(seen, 0.0, NEVER).astype(F32)


def masked_scores(parents_ref, q_head, k_ref, row):
    scores = []
    for col in range(row + 1):
        part = over(q_head, k_ref[col * BLOCK : (col + 1) * BLOCK, :], 1, 1)
        if col == row:
            below = lax.broadcasted_iota(jnp.int32, part.shape, 1) <= lax.broadcasted_iota(
                jnp.int32, part.shape, 0
            )
            part = jnp.where(below, part, NEVER)
        else:
            part = part + sight(parents_ref, row, col)
        scores.append(part)
    return scores


def row_reduce(parts, fold, reduce):
    return reduce(functools.reduce(fold, parts), axis=-1, keepdims=True)


def attend_kernel(parents_ref, q_ref, k_ref, v_ref, out_ref):
    blocks = q_ref.shape[0] // BLOCK
    scale = 1.0 / math.sqrt(HEAD_DIM)
    for row in range(blocks):
        here = slice(row * BLOCK, (row + 1) * BLOCK)
        heads = []
        for head in range(2):
            q_head = q_ref[here, :].astype(F32) * scale
            q_head = jnp.where(lane_of(q_head.shape, head), q_head, 0.0).astype(BF16)
            scores = masked_scores(parents_ref, q_head, k_ref, row)
            top = row_reduce(scores, jnp.maximum, jnp.max)
            probs = [jnp.exp(s - top) for s in scores]
            total = row_reduce(probs, jnp.add, jnp.sum)
            out = None
            for col in range(row + 1):
                term = over(
                    probs[col].astype(BF16), v_ref[col * BLOCK : (col + 1) * BLOCK, :], 1, 0
                )
                out = term if out is None else out + term
            heads.append(out / total)
        mixed = jnp.where(lane_of(heads[0].shape, 0), heads[0], heads[1])
        out_ref[here, :] = mixed.astype(out_ref.dtype)


def attend(parents, qkv, width):
    rows = qkv.shape[0]
    pairs = width // PAIR
    spec = lambda part: pl.BlockSpec((rows, PAIR), lambda p, parents: (0, part * pairs + p))
    blocks = rows // BLOCK
    work = pairs * 2 * (blocks * (blocks + 1) // 2) * BLOCK * BLOCK
    return pl.pallas_call(
        attend_kernel,
        out_shape=jax.ShapeDtypeStruct((rows, width), BF16),
        grid_spec=pltpu.PrefetchScalarGridSpec(
            num_scalar_prefetch=1,
            grid=(pairs,),
            in_specs=[spec(0), spec(1), spec(2)],
            out_specs=pl.BlockSpec((rows, PAIR), lambda p, parents: (0, p)),
        ),
        compiler_params=pltpu.CompilerParams(vmem_limit_bytes=48 << 20),
        cost_estimate=pl.CostEstimate(
            flops=work * PAIR * 24, bytes_accessed=rows * width * 8, transcendentals=work
        ),
        name="attend",
    )(parents, qkv, qkv, qkv)


def attend_back_kernel(parents_ref, q_ref, k_ref, v_ref, g_ref, out_ref, dq_s, dk_s, dv_s):
    part = pl.program_id(1)
    blocks = q_ref.shape[0] // BLOCK
    scale = 1.0 / math.sqrt(HEAD_DIM)

    @pl.when(part == 0)
    def _():
        for row in range(blocks):
            here = slice(row * BLOCK, (row + 1) * BLOCK)
            dq_heads = []
            for head in range(2):
                lanes = lane_of((BLOCK, PAIR), head)
                q_head = jnp.where(lanes, q_ref[here, :].astype(F32) * scale, 0.0).astype(BF16)
                g_head = jnp.where(lanes, g_ref[here, :].astype(F32), 0.0).astype(BF16)
                scores = masked_scores(parents_ref, q_head, k_ref, row)
                top = row_reduce(scores, jnp.maximum, jnp.max)
                probs = [jnp.exp(s - top) for s in scores]
                rest = 1.0 / row_reduce(probs, jnp.add, jnp.sum)
                probs = [p * rest for p in probs]
                d_probs = [
                    over(g_head, v_ref[col * BLOCK : (col + 1) * BLOCK, :], 1, 1)
                    for col in range(row + 1)
                ]
                level = row_reduce([p * d for p, d in zip(probs, d_probs)], jnp.add, jnp.sum)
                dq = None
                for col in range(row + 1):
                    there = slice(col * BLOCK, (col + 1) * BLOCK)
                    d_scores = (probs[col] * (d_probs[col] - level)).astype(BF16)
                    term = over(d_scores, k_ref[there, :], 1, 0)
                    dq = term if dq is None else dq + term
                    dk = over(d_scores, q_head, 0, 0)
                    dv = over(probs[col].astype(BF16), g_head, 0, 0)
                    if row == col and head == 0:
                        dk_s[there, :] = dk
                        dv_s[there, :] = dv
                    else:
                        dk_s[there, :] += dk
                        dv_s[there, :] += dv
                dq_heads.append(dq * scale)
            dq_s[here, :] = jnp.where(lane_of((BLOCK, PAIR), 0), dq_heads[0], dq_heads[1]).astype(
                BF16
            )
        out_ref[...] = dq_s[...]

    @pl.when(part == 1)
    def _():
        out_ref[...] = dk_s[...].astype(BF16)

    @pl.when(part == 2)
    def _():
        out_ref[...] = dv_s[...].astype(BF16)


def attend_back(parents, qkv, grad, width):
    rows = qkv.shape[0]
    pairs = width // PAIR
    spec = lambda part: pl.BlockSpec((rows, PAIR), lambda p, c, parents: (0, part * pairs + p))
    blocks = rows // BLOCK
    work = pairs * 2 * (blocks * (blocks + 1) // 2) * BLOCK * BLOCK
    return pl.pallas_call(
        attend_back_kernel,
        out_shape=jax.ShapeDtypeStruct((rows, 3 * width), BF16),
        grid_spec=pltpu.PrefetchScalarGridSpec(
            num_scalar_prefetch=1,
            grid=(pairs, 3),
            in_specs=[
                spec(0),
                spec(1),
                spec(2),
                pl.BlockSpec((rows, PAIR), lambda p, c, parents: (0, p)),
            ],
            out_specs=pl.BlockSpec((rows, PAIR), lambda p, c, parents: (0, c * pairs + p)),
            scratch_shapes=[
                pltpu.VMEM((rows, PAIR), BF16),
                pltpu.VMEM((rows, PAIR), F32),
                pltpu.VMEM((rows, PAIR), F32),
            ],
        ),
        compiler_params=pltpu.CompilerParams(vmem_limit_bytes=48 << 20),
        cost_estimate=pl.CostEstimate(
            flops=work * PAIR * 60, bytes_accessed=rows * width * 14, transcendentals=work
        ),
        name="attend_back",
    )(parents, qkv, qkv, qkv, grad)


def ffn_kernel(n2_ref, dy_ref, we_ref, wr_ref, be_ref, *refs):
    sum_ref, act_ref, dpre_ref, part_ref = refs[:4]
    refs = refs[4:]
    we, wr, seq_st, dy_st, act_st, dpre_st, part_st, keep, give, core_in, fold_in = refs[:11]
    w_sem, load_sem, st_sem, rsc_send, rsc_recv, fold_send, fold_recv = refs[11:18]
    cube = Cube()
    levels, count, owner = cube.levels, cube.count, cube.owner
    rows, model = sum_ref.shape
    units = wr_ref.shape[0]
    barrier = pltpu.get_barrier_semaphore()
    cube.greet(barrier)
    parts = we_ref.shape[0] // model
    mine_units = we_ref.shape[1]
    loads_w = [pltpu.make_async_copy(wr_ref, wr, w_sem.at[parts])]
    for part in range(parts):
        loads_w.append(
            pltpu.make_async_copy(
                we_ref.at[pl.ds(part * model, model)],
                we.at[:, pl.ds(part * mine_units, mine_units)],
                w_sem.at[part],
            )
        )

    def load(piece, slot):
        out = []
        for half, index in enumerate(owner(piece)):
            for kind, (ref, stage) in enumerate(((n2_ref, seq_st), (dy_ref, dy_st))):
                out.append(
                    pltpu.make_async_copy(
                        ref.at[window(index, rows)],
                        stage.at[slot, pl.ds(half * rows, rows)],
                        load_sem.at[kind, slot, half],
                    )
                )
        return out

    order = sorted(range(count), key=lambda p: (-(p.bit_length()), p))
    slots = {piece: i % 2 for i, piece in enumerate(order)}
    loads = {order[0]: load(order[0], 0)}
    for c in loads[order[0]] + loads_w:
        c.start()
    pl.semaphore_wait(barrier, cube.peers())
    for c in loads_w:
        c.wait()
    stores, core_sends, folds = {}, {}, {}

    def add(piece, other):
        @pl.loop(0, rows // 16)
        def _(i):
            part = window(i, 16)
            keep[piece, part] = (
                keep[piece, part].astype(F32) + other[part].astype(F32)
            ).astype(BF16)

    def core_copy(piece):
        return remote(
            give.at[slots[piece]], core_in.at[piece],
            rsc_send.at[piece], rsc_recv.at[piece], cube.at(cube.me + cube.core_step),
        )

    def fold_copy(piece):
        return remote(
            keep.at[piece], fold_in.at[piece - 1], fold_send.at[piece - 1], fold_recv.at[piece - 1],
            cube.at(cube.me + cube.steps[piece.bit_length() - 1]),
        )

    def fold(piece):
        core_copy(piece).wait_recv()
        add(piece, core_in.at[piece])
        for level in range(levels - 1, piece.bit_length() - 1, -1):
            above = piece + (1 << level)
            fold_copy(above).wait_recv()
            add(piece, fold_in.at[above - 1])
        folds[piece] = fold_copy(piece)
        folds[piece].start()

    chunk = 256
    wide = 512
    for turn, piece in enumerate(order):
        slot = turn % 2
        for c in loads[piece]:
            c.wait()
        if turn + 1 < count:
            loads[order[turn + 1]] = load(order[turn + 1], 1 - slot)
            for c in loads[order[turn + 1]]:
                c.start()
        if turn >= 2:
            for c in stores[turn - 2]:
                c.wait()
            core_sends[order[turn - 2]].wait_send()

        @pl.loop(0, units // chunk)
        def _(i):
            cols = window(i, chunk)
            pre = over(seq_st[slot], we[:, cols], 1, 0) + be_ref[:, cols]
            d_act = over(dy_st[slot], wr[cols, :], 1, 1)
            square = pre * pre
            t = jnp.tanh(GELU * pre * (1.0 + 0.044715 * square))
            act_st[slot, :, cols] = (0.5 * pre * (1.0 + t)).astype(BF16)
            slope = 0.5 * (1.0 + t) + (0.5 * GELU) * pre * (1.0 - t * t) * (
                1.0 + (3 * 0.044715) * square
            )
            dpre_st[slot, :, cols] = (d_act * slope).astype(BF16)

        if turn:
            fold(order[turn - 1])

        @pl.loop(0, model // wide)
        def _(i):
            cols = window(i, wide)
            d_two = over(dpre_st[slot], we[cols, :], 1, 1).astype(BF16)
            keep[piece, :, cols] = d_two[:rows]
            give[slot, :, cols] = d_two[rows:]
            part_st[slot, :, cols] = over(act_st[slot], wr[:, cols], 1, 0).astype(BF16)

        core_sends[piece] = core_copy(piece)
        core_sends[piece].start()
        stores[turn] = []
        for half, index in enumerate(owner(piece)):
            to, part = window(index, rows), pl.ds(half * rows, rows)
            for kind, (stage, ref) in enumerate(
                ((act_st, act_ref), (dpre_st, dpre_ref), (part_st, part_ref))
            ):
                stores[turn].append(
                    pltpu.make_async_copy(stage.at[slot, part], ref.at[to], st_sem.at[kind, slot, half])
                )
        for c in stores[turn]:
            c.start()
    core_copy(0).wait_recv()
    for level in range(levels):
        fold_copy(1 << level).wait_recv()

    @pl.loop(0, rows // 16)
    def _(i):
        part = window(i, 16)
        total = keep[0, part].astype(F32) + core_in[0, part].astype(F32)
        for level in range(levels):
            total = total + fold_in[(1 << level) - 1, part].astype(F32)
        sum_ref[part] = total

    for turn in range(max(0, count - 2), count):
        for c in stores[turn]:
            c.wait()
        core_sends[order[turn]].wait_send()
    for s in folds.values():
        s.wait_send()


def ffn(n2, dy, we, wr, bias_e):
    n, dp = lax.axis_size("tensor"), lax.axis_size("dp")
    rows, model = n2.shape[0] // dp, n2.shape[1]
    units, count = wr.shape[0], dp // 2
    flops = 30 * dp * rows * model * units
    return pl.pallas_call(
        ffn_kernel,
        out_shape=(
            jax.ShapeDtypeStruct((rows, model), F32),
            jax.ShapeDtypeStruct((dp * rows, units), BF16),
            jax.ShapeDtypeStruct((dp * rows, units), BF16),
            jax.ShapeDtypeStruct((dp * rows, model), BF16),
        ),
        in_specs=[ANY] * 4 + [VMEM],
        out_specs=(VMEM, ANY, ANY, ANY),
        scratch_shapes=[
            pltpu.VMEM((model, units), BF16),
            pltpu.VMEM((units, model), BF16),
            pltpu.VMEM((2, 2 * rows, model), BF16),
            pltpu.VMEM((2, 2 * rows, model), BF16),
            pltpu.VMEM((2, 2 * rows, units), BF16),
            pltpu.VMEM((2, 2 * rows, units), BF16),
            pltpu.VMEM((2, 2 * rows, model), BF16),
            pltpu.VMEM((count, rows, model), BF16),
            pltpu.VMEM((2, rows, model), BF16),
            pltpu.VMEM((count, rows, model), BF16),
            pltpu.VMEM((count - 1, rows, model), BF16),
            DMA((n + 1,)), DMA((2, 2, 2)), DMA((3, 2, 2)),
            DMA((count,)), DMA((count,)), DMA((count - 1,)), DMA((count - 1,)),
        ],
        compiler_params=pltpu.CompilerParams(
            collective_id=1, has_side_effects=True, vmem_limit_bytes=62 << 20
        ),
        cost_estimate=pl.CostEstimate(
            flops=flops, bytes_accessed=8 * dp * rows * (model + units), transcendentals=dp * rows * units
        ),
        name="ffn_plane",
    )(n2, dy, we, wr, bias_e)


def body(
    tokens,
    parents,
    cotangent,
    first_gain,
    first_shift,
    w_query,
    b_query,
    w_key,
    w_value,
    b_value,
    w_out,
    b_out,
    second_gain,
    second_shift,
    w_expand,
    b_expand,
    w_reduce,
    b_reduce,
):
    dp = lax.axis_size("dp")
    tn = lax.axis_size("tensor")
    dp_me = lax.axis_index("dp")
    tn_me = lax.axis_index("tensor")
    width = w_query.shape[1]
    model = w_query.shape[0] * dp
    units = w_expand.shape[1]
    mine = units // dp
    micros = range(tokens.shape[0])
    last = tokens.shape[0] - 1
    x_low = [tokens[m, 0] for m in micros]
    dy_low = [cotangent[m, 0] for m in micros]
    rows_here = x_low[0].shape[0]
    total = rows_here * tn

    cut = first_gain.shape[0]
    bq_rows, bq_cols = b_query.shape
    be_rows, be_cols = b_expand.shape
    small = jnp.concatenate(
        [first_gain, first_shift, b_out, second_gain, second_shift, b_reduce]
        + [b_query.reshape(-1), b_value.reshape(-1), b_expand.reshape(-1)]
    )
    used = small.shape[0]
    small = jnp.pad(small, (0, -used % 2048)).reshape(-1, 128)
    w_qkv = jnp.concatenate([w_query, w_key, w_value], axis=1)
    seq_x0, w_qkv, w_e, w_r, small = front(x_low[0], w_qkv, w_expand, w_reduce, small)
    small = small.reshape(dp, -1)[:, :used]
    gain_one, shift_one, bias_out, gain_two, shift_two, bias_red = [
        small[:, i * cut : (i + 1) * cut].reshape(1, model).astype(F32) for i in range(6)
    ]
    at = 6 * cut
    bias_qkv = []
    for i in range(2):
        part = small[:, at : at + bq_rows * bq_cols].reshape(dp, bq_rows, bq_cols)
        bias_qkv.append(part.transpose(1, 0, 2).reshape(1, width).astype(F32))
        at += bq_rows * bq_cols
    bias_qkv = jnp.concatenate([bias_qkv[0], jnp.zeros((1, width), F32), bias_qkv[1]], 1)
    bias_e = small[:, at:].reshape(dp, dp, be_rows // dp, be_cols)
    bias_e = lax.dynamic_index_in_dim(bias_e, dp_me, 1, keepdims=False)
    bias_e = bias_e.transpose(1, 0, 2).reshape(mine)
    bias_e = jnp.pad(bias_e, (0, -mine % 2048)).reshape(-1, 128)

    seq_x = [seq_x0]
    w_r = lax.all_gather(w_r, "tensor", axis=0, tiled=True)
    w_e = lax.all_gather(w_e, "tensor", axis=1 if mine % 128 else 0, tiled=True)

    def outer(left, right):
        out = None
        for a, b in zip(left, right):
            term = over(a, b, 0, 0)
            out = term if out is None else out + term
        return out.astype(BF16)

    normal_one, seq_one, qkv, attended, hidden, normed_two = [], [], [], [], [], []
    out_part, seq_two, activated, d_pre, d_hidden, d_branch, out_sum = [], [], [], [], [], [], []
    d_qkv, d_one, d_att, row_attended = [], [], [], []
    g_gain_two = g_shift_two = g_bias_red = g_bias_out = g_bias_e = 0.0
    g_gain_one = g_shift_one = g_bias_qkv = 0.0
    for m in micros:
        normal_one.append(layer_norm(seq_x[m].astype(F32), 1.0, 0.0))
        seq_one.append((normal_one[m] * gain_one + shift_one).astype(BF16))
        qkv.append(
            (jnp.dot(seq_one[m], w_qkv, preferred_element_type=F32) + bias_qkv).astype(BF16)
        )
        attended.append(attend(parents[m, 0], qkv[m], width))
        if m == 0:
            bias_e, grad, row_att, _, w_ot = exchange(
                3, gathers=[bias_e], cubes=[dy_low[m]], outs=[attended[m]], spreads=[w_out.T]
            )
            seq_grad = [grad]
            bias_e = bias_e.reshape(tn, -1)[:, :mine].reshape(1, tn * mine).astype(F32)
        else:
            part, row_att, col_grad = exchange(
                4, planes=[out_part[m - 1]], outs=[attended[m]], backs=[d_att[m - 1]]
            )
            out_sum.append(part)
            d_att[m - 1] = col_grad
        if m < last:
            next_x, row_att = lax.optimization_barrier((x_low[m + 1], row_att))
            next_x = lax.all_gather(next_x, "tensor", axis=0, tiled=True)
        row_attended.append(row_att)
        branch = over(row_att, w_ot, 1, 1)
        hidden.append(x_low[m].astype(F32) + (branch + bias_out))
        normed_two.append(layer_norm(hidden[m], gain_two, shift_two).astype(BF16))
        if m < last:
            grad, normed_two[m] = lax.optimization_barrier((dy_low[m + 1], normed_two[m]))
            seq_grad.append(lax.all_gather(grad, "dp", axis=0, tiled=True))

        def attention_back(k):
            d_qkv.append(attend_back(parents[k, 0], qkv[k], d_att[k], width))
            d_one.append(over(d_qkv[k], w_qkv, 1, 1).astype(BF16))
            part = d_one[k].astype(F32)
            return (
                jnp.sum(part * normal_one[k], 0, keepdims=True),
                jnp.sum(part, 0, keepdims=True),
                jnp.sum(d_qkv[k].astype(F32), 0),
            )

        if m:
            normed_two[m], seq_grad[m] = lax.optimization_barrier((normed_two[m], seq_grad[m]))
            next_two = lax.all_gather(normed_two[m], "dp", axis=0, tiled=True)
            gain, shift, bias = attention_back(m - 1)
            g_gain_one, g_shift_one = g_gain_one + gain, g_shift_one + shift
            g_bias_qkv = g_bias_qkv + bias
            next_two, d_one[m - 1] = lax.optimization_barrier((next_two, d_one[m - 1]))
            d_one[m - 1] = lax.psum_scatter(
                d_one[m - 1], "tensor", scatter_dimension=0, tiled=True
            )

        if m == 0:
            (seq,) = exchange(7, cubes=[normed_two[m]])
        else:
            seq = next_two
        d_two, act, dpre, part = ffn(seq, seq_grad[m], w_e, w_r, bias_e)
        seq_two.append(seq)
        activated.append(act)
        d_pre.append(dpre)
        out_part.append(part)
        if m == last:
            g_r = outer(activated, seq_grad)
            d_two, g_r, *d_one = lax.optimization_barrier((d_two, g_r, *d_one))
            g_r = lax.psum_scatter(g_r, "tensor", scatter_dimension=0, tiled=True)
        grad32 = dy_low[m].astype(F32)
        norm_value, norm_pull = jax.vjp(layer_norm, hidden[m], gain_two, shift_two)
        d_norm, g_gain, g_shift = norm_pull(d_two)
        d_hidden.append(grad32 + d_norm)
        d_branch.append(d_hidden[m].astype(BF16))
        d_att.append(jnp.dot(d_branch[m], w_ot, preferred_element_type=F32).astype(BF16))
        g_gain_two = g_gain_two + g_gain
        g_shift_two = g_shift_two + g_shift
        g_bias_red = g_bias_red + jnp.sum(grad32, 0, keepdims=True)
        g_bias_out = g_bias_out + jnp.sum(d_branch[m].astype(F32), 0, keepdims=True)
        g_bias_e = g_bias_e + jnp.sum(dpre.astype(F32), 0)
        if m < last:
            next_x, d_branch[m] = lax.optimization_barrier((next_x, d_branch[m]))
            seq_x.append(next_x)

    g_ot = outer([jnp.concatenate(d_branch, 0)], [jnp.concatenate(row_attended, 0)])
    g_ot, d_att[last] = exchange(6, planes=[g_ot], backs=[d_att[last]], weight=15)
    d_att[last], *d_pre = lax.optimization_barrier((d_att[last], *d_pre))
    g_et = outer(d_pre, seq_two)
    d_att[last], g_r = lax.optimization_barrier((d_att[last], g_r))
    g_et = lax.psum_scatter(g_et, "tensor", scatter_dimension=0, tiled=True)
    gain, shift, bias = attention_back(last)
    g_gain_one, g_shift_one = g_gain_one + gain, g_shift_one + shift
    g_bias_qkv = g_bias_qkv + bias

    rows = jnp.concatenate(
        [g_gain_one, g_shift_one, g_bias_out, g_gain_two, g_shift_two, g_bias_red], 0
    )
    rows = rows.reshape(6, dp, cut).transpose(1, 0, 2).reshape(dp, 6 * cut)
    row_qv = jnp.concatenate([g_bias_qkv[:width], g_bias_qkv[2 * width :]])
    row_qv = row_qv.reshape(2 * bq_rows, dp, bq_cols).transpose(1, 0, 2)[:, None]
    row_qv = lax.dynamic_update_slice(
        jnp.zeros((dp, tn, 2 * bq_rows, bq_cols), F32), row_qv, (0, tn_me, 0, 0)
    ).reshape(dp, -1)
    row_e = g_bias_e.reshape(tn, be_rows // dp, dp, be_cols).transpose(2, 0, 1, 3)[:, :, None]
    row_e = lax.dynamic_update_slice(
        jnp.zeros((dp, tn, dp, be_rows // dp, be_cols), F32), row_e, (0, 0, dp_me, 0, 0)
    ).reshape(dp, -1)
    little = jnp.concatenate([rows, row_qv, row_e], 1)
    little = jnp.pad(little, ((0, 0), (0, -little.shape[1] % 1024))).reshape(dp, -1, 128)

    d_one[last], *d_qkv = lax.optimization_barrier((d_one[last], *d_qkv))
    g_qkv = outer(seq_one, d_qkv)
    g_ot = g_ot.astype(BF16).reshape(-1, tn, width).transpose(1, 0, 2).reshape(-1, width)
    d_one[last], g_ot, g_qkv, out_last, g_expand, g_reduce, little = exchange(
        5,
        lines=[d_one[last], g_ot],
        planes=[g_qkv, out_part[last]],
        swaps=[g_et, g_r],
        small=[little],
    )
    out_sum.append(out_last)
    g_query, g_key, g_value = [g_qkv[:, i * width : (i + 1) * width] for i in range(3)]
    g_out = g_ot.T
    g_expand = g_expand.T.astype(F32)
    g_reduce = g_reduce.astype(F32)
    layer_out = [(hidden[m] + (out_sum[m] + bias_red)).astype(BF16) for m in micros]
    little = little.reshape(-1)
    six = little[: 6 * cut].reshape(6, cut)
    at = 6 * cut
    g_bqv = little[at : at + tn * 2 * bq_rows * bq_cols].reshape(tn, 2 * bq_rows, bq_cols)
    g_bqv = lax.dynamic_index_in_dim(g_bqv, tn_me, 0, keepdims=False)
    g_bq, g_bv = g_bqv[:bq_rows], g_bqv[bq_rows:]
    at += tn * 2 * bq_rows * bq_cols
    g_be = little[at : at + tn * be_rows * be_cols].reshape(tn, be_rows, be_cols)
    g_be = lax.dynamic_index_in_dim(g_be, tn_me, 0, keepdims=False)
    input_grad = []
    for m in micros:
        first_value, first_pull = jax.vjp(
            lambda rows: layer_norm(rows, gain_one, shift_one), x_low[m].astype(F32)
        )
        input_grad.append((d_hidden[m] + first_pull(d_one[m].astype(F32))[0]).astype(BF16))

    return (
        jnp.stack(layer_out, 0)[:, None],
        jnp.stack(input_grad, 0)[:, None],
        six[0],
        six[1],
        g_query,
        g_bq,
        g_key,
        g_value,
        g_bv,
        g_out,
        six[2],
        six[3],
        six[4],
        g_expand,
        g_be,
        g_reduce,
        six[5],
    )


def solution(mesh):
    in_specs = (
        P(None, "dp", "tensor", None),
        P(None, "dp", None),
        P(None, "dp", "tensor", None),
        P("dp"),
        P("dp"),
        P("dp", "tensor"),
        P("tensor", "dp"),
        P("dp", "tensor"),
        P("dp", "tensor"),
        P("tensor", "dp"),
        P("tensor", "dp"),
        P("dp"),
        P("dp"),
        P("dp"),
        P("dp", "tensor"),
        P("tensor", "dp"),
        P("tensor", "dp"),
        P("dp"),
    )
    out_specs = (
        P(None, "dp", "tensor", None),
        P(None, "dp", "tensor", None),
        P("dp"),
        P("dp"),
        P("dp", "tensor"),
        P("tensor", "dp"),
        P("dp", "tensor"),
        P("dp", "tensor"),
        P("tensor", "dp"),
        P("tensor", "dp"),
        P("dp"),
        P("dp"),
        P("dp"),
        P("dp", "tensor"),
        P("tensor", "dp"),
        P("tensor", "dp"),
        P("dp"),
    )
    return jax.shard_map(body, mesh=mesh, in_specs=in_specs, out_specs=out_specs, check_vma=False)
```

```python
import functools
import math

import jax
import jax.numpy as jnp
from jax import lax
from jax.experimental import pallas as pl
from jax.experimental.pallas import tpu as pltpu
from jax.sharding import PartitionSpec as P

HEAD_DIM = 64
BLOCK = 256

F32 = jnp.float32
BF16 = jnp.bfloat16
MESH = pl.DeviceIdType.MESH
DMA = pltpu.SemaphoreType.DMA
GELU = math.sqrt(2.0 / math.pi)


def layer_norm(rows, gain, shift):
    center = rows - jnp.mean(rows, -1, keepdims=True)
    spread = jnp.mean(center * center, -1, keepdims=True)
    return center * lax.rsqrt(spread + 1e-05) * gain + shift


def after(value, *others):
    return lax.optimization_barrier((value,) + others)[0]


def over(left, right, on_left, on_right):
    return lax.dot_general(
        left, right, (((on_left,), (on_right,)), ((), ())), preferred_element_type=F32
    )


def window(index, rows):
    return pl.ds(pl.multiple_of(index * rows, rows), rows)


def remote(src, dst, send, recv, to):
    return pltpu.make_async_remote_copy(
        src_ref=src, dst_ref=dst, send_sem=send, recv_sem=recv,
        device_id=to, device_id_type=MESH,
    )


class Line:
    def __init__(self):
        self.n = lax.axis_size("tensor")
        self.me = lax.axis_index("tensor")
        self.dp = lax.axis_index("dp")

    def at(self, index):
        return (self.dp, index)

    def greet(self, barrier):
        @pl.when(self.me > 0)
        def _():
            pl.semaphore_signal(barrier, inc=1, device_id=self.at(self.me - 1), device_id_type=MESH)

        @pl.when(self.me < self.n - 1)
        def _():
            pl.semaphore_signal(barrier, inc=1, device_id=self.at(self.me + 1), device_id_type=MESH)

    @property
    def size(self):
        return self.n

    def greet_all(self, barrier):
        for k in range(1, self.n):
            pl.semaphore_signal(
                barrier, inc=1, device_id=self.at((self.me + k) % self.n), device_id_type=MESH
            )

    def peers(self):
        return (self.me + self.n - 1) // self.n + (2 * self.n - 2 - self.me) // self.n


class LineGather:
    def __init__(self, line, own, full, sems):
        self.line, self.own, self.full = line, own, full
        self.side = own.shape[0] == full.shape[0]
        self.local, self.up_send, self.up_recv, self.down_send, self.down_recv = sems

    @staticmethod
    def sems(n):
        return [DMA, DMA((n - 1,)), DMA((n - 1,)), DMA((n - 1,)), DMA((n - 1,))]

    def slot(self, index):
        if self.side:
            return self.full.at[:, window(index, self.own.shape[1])]
        return self.full.at[window(index, self.own.shape[0])]

    def hop(self, step, up):
        line = self.line
        if up:
            shard, to = line.me - (step - 1), line.me + 1
            send, recv = self.up_send, self.up_recv
        else:
            shard, to = line.me + (step - 1), line.me - 1
            send, recv = self.down_send, self.down_recv
        there = self.slot(shard)
        src = self.own if step == 1 else there
        return remote(src, there, send.at[step - 1], recv.at[step - 1], line.at(to))

    def sends(self, step, up):
        line = self.line
        if up:
            return (line.me < line.n - 1) & (line.me >= step - 1)
        return (line.me > 0) & (line.me + step - 1 < line.n)

    def takes(self, step, up):
        line = self.line
        return (line.me >= step) if up else (line.me + step < line.n)

    def send(self, step):
        for up in (True, False):
            @pl.when(self.sends(step, up))
            def _():
                self.hop(step, up).start()

    def start(self):
        pltpu.make_async_copy(self.own, self.slot(self.line.me), self.local).start()
        self.send(1)

    def take(self, step):
        for up in (True, False):
            @pl.when(self.takes(step, up))
            def _():
                line = self.line
                shard = (line.me - step) if up else (line.me + step)
                here = self.slot(shard)
                send, recv = (
                    (self.up_send, self.up_recv) if up else (self.down_send, self.down_recv)
                )
                remote(
                    here, here, send.at[step - 1], recv.at[step - 1], line.at(line.me)
                ).wait_recv()
        if step < self.line.n - 1:
            self.send(step + 1)

    def finish(self):
        for step in range(1, self.line.n):
            for up in (True, False):
                @pl.when(self.sends(step, up))
                def _():
                    self.hop(step, up).wait_send()
        pltpu.make_async_copy(self.own, self.slot(self.line.me), self.local).wait()


class LineScatter:
    def __init__(self, line, parts, out, scratch):
        self.line, self.parts, self.out = line, parts, out
        self.rows = out.shape[0]
        (self.own, self.sum, self.come, self.load, self.own_sem, self.send_sem, self.recv_sem) = scratch

    @staticmethod
    def scratch(n, rows, d):
        return [
            pltpu.VMEM((rows, d), BF16),
            pltpu.VMEM((2, n - 1, rows, d), BF16),
            pltpu.VMEM((2, n - 1, rows, d), BF16),
            DMA((2, n - 1)), DMA, DMA((2, n - 1)), DMA((2, n - 1)),
        ]

    def sends(self, step, up):
        line = self.line
        return (line.me <= step - 1) if up else (line.n - 1 - line.me <= step - 1)

    def load_of(self, step, up):
        line = self.line
        chunk = (line.me + line.n - step) if up else (line.me - line.n + step)
        way = 0 if up else 1
        return pltpu.make_async_copy(
            self.parts.at[window(chunk, self.rows)], self.sum.at[way, step - 1], self.load.at[way, step - 1]
        )

    def hop(self, step, up):
        line, way = self.line, 0 if up else 1
        return remote(
            self.sum.at[way, step - 1], self.come.at[way, step - 1],
            self.send_sem.at[way, step - 1], self.recv_sem.at[way, step - 1],
            line.at(line.me + 1 if up else line.me - 1),
        )

    def wait_from(self, step, up):
        line, way = self.line, 0 if up else 1
        remote(
            self.come.at[way, step - 1], self.come.at[way, step - 1],
            self.send_sem.at[way, step - 1], self.recv_sem.at[way, step - 1],
            line.at(line.me),
        ).wait_recv()

    def own_load(self):
        return pltpu.make_async_copy(
            self.parts.at[window(self.line.me, self.rows)], self.own, self.own_sem
        )

    def prepare(self):
        self.own_load().start()
        for step in range(1, self.line.n):
            for up in (True, False):
                @pl.when(self.sends(step, up))
                def _():
                    self.load_of(step, up).start()

    def step(self, step):
        line = self.line
        for up in (True, False):
            way = 0 if up else 1

            @pl.when(self.sends(step, up))
            def _():
                self.load_of(step, up).wait()
                if step > 1:
                    inner = (line.me > 0) if up else (line.me < line.n - 1)

                    @pl.when(inner)
                    def _():
                        self.wait_from(step - 1, up)

                        @pl.loop(0, self.rows // 16)
                        def _(i):
                            part = window(i, 16)
                            self.sum[way, step - 1, part] = (
                                self.sum[way, step - 1, part].astype(F32)
                                + self.come[way, step - 2, part].astype(F32)
                            ).astype(BF16)

                if step > 1:

                    @pl.when(self.sends(step - 1, up))
                    def _():
                        self.hop(step - 1, up).wait_send()

                self.hop(step, up).start()

    def finish(self):
        line, n = self.line, self.line.n
        self.own_load().wait()

        @pl.loop(0, self.rows // 16)
        def _(i):
            part = window(i, 16)
            self.out[part] = self.own[part].astype(F32)

        for up in (True, False):
            way = 0 if up else 1

            @pl.when((line.me > 0) if up else (line.me < n - 1))
            def _():
                self.wait_from(n - 1, up)

                @pl.loop(0, self.rows // 16)
                def _(i):
                    part = window(i, 16)
                    self.out[part] += self.come[way, n - 2, part].astype(F32)

        for up in (True, False):
            @pl.when(self.sends(n - 1, up))
            def _():
                self.hop(n - 1, up).wait_send()


class Cube:
    def __init__(self):
        self.dp = lax.axis_size("dp")
        self.levels = levels = self.dp.bit_length() - 2
        self.count = 1 << levels
        self.me = me = lax.axis_index("dp")
        self.tensor = lax.axis_index("tensor")
        core = me % 2
        flips = []
        for bit in range(1, levels + 1):
            flips.append((1 << bit) * (1 - 2 * ((me // (1 << bit)) % 2)))
        self.steps = [
            flips[l] * (1 - core) + flips[levels - 1 - l] * core for l in range(levels)
        ]
        self.core_step = 1 - 2 * core

    def at(self, index):
        return (index, self.tensor)

    def owner(self, piece):
        mine, other = self.me, self.me + self.core_step
        for l in range(self.levels):
            if piece >> l & 1:
                mine = mine + self.steps[l]
                other = other + self.steps[self.levels - 1 - l]
        return mine, other

    def greet(self, barrier):
        for step in self.steps + [self.core_step]:
            pl.semaphore_signal(
                barrier, inc=1, device_id=self.at(self.me + step), device_id_type=MESH
            )

    @property
    def size(self):
        return self.dp

    def greet_all(self, barrier):
        for k in range(1, self.dp):
            pl.semaphore_signal(
                barrier, inc=1, device_id=self.at((self.me + k) % self.dp), device_id_type=MESH
            )

    def peers(self):
        return self.levels + 1


class CubeGather:
    def __init__(self, cube, own, full, sems):
        self.cube, self.own, self.full = cube, own, full
        self.rows = own.shape[0]
        self.local, self.send_sem, self.recv_sem, self.core_send, self.core_recv = sems
        self.arrived, self.sent = {0}, []

    @staticmethod
    def sems(count):
        return [DMA, DMA((count,)), DMA((count,)), DMA((count,)), DMA((count,))]

    def slot(self, index):
        return self.full.at[window(index, self.rows)]

    def src(self, piece):
        return self.own if piece == 0 else self.slot(self.cube.owner(piece)[0])

    def hop(self, piece, level):
        cube, there = self.cube, piece + (1 << level)
        return remote(
            self.src(piece), self.slot(cube.owner(piece)[0]),
            self.send_sem.at[there], self.recv_sem.at[there], cube.at(cube.me + cube.steps[level]),
        )

    def core(self, piece):
        cube = self.cube
        return remote(
            self.src(piece), self.slot(cube.owner(piece)[0]),
            self.core_send.at[piece], self.core_recv.at[piece], cube.at(cube.me + cube.core_step),
        )

    def give(self, piece):
        for level in range(piece.bit_length(), self.cube.levels):
            self.sent.append(self.hop(piece, level))
            self.sent[-1].start()
        self.sent.append(self.core(piece))
        self.sent[-1].start()

    def start(self):
        self.place = pltpu.make_async_copy(self.own, self.slot(self.cube.me), self.local)
        self.place.start()
        self.give(0)

    def take(self, piece):
        if piece in self.arrived:
            return
        here = self.slot(self.cube.owner(piece)[0])
        remote(
            here, here, self.send_sem.at[piece], self.recv_sem.at[piece], self.cube.at(self.cube.me)
        ).wait_recv()
        self.arrived.add(piece)
        self.give(piece)

    def take_core(self, piece):
        here = self.slot(self.cube.owner(piece)[1])
        remote(
            here, here, self.core_send.at[piece], self.core_recv.at[piece], self.cube.at(self.cube.me)
        ).wait_recv()

    def finish(self):
        for piece in range(self.cube.count):
            self.take(piece)
            self.take_core(piece)
        for copy in self.sent:
            copy.wait_send()
        self.place.wait()


class CubeScatter:
    def __init__(self, cube, parts, out, scratch):
        self.cube, self.parts, self.out = cube, parts, out
        self.rows = out.shape[0]
        (self.keep, self.core_in, self.fold_in, self.load_sem,
         self.core_send, self.core_recv, self.send_sem, self.recv_sem) = scratch

    @staticmethod
    def scratch(count, rows, d):
        return [
            pltpu.VMEM((count, rows, d), BF16),
            pltpu.VMEM((count, rows, d), BF16),
            pltpu.VMEM((count - 1, rows, d), BF16),
            DMA((count,)), DMA((count,)), DMA((count,)), DMA((count - 1,)), DMA((count - 1,)),
        ]

    def load(self, piece):
        return pltpu.make_async_copy(
            self.parts.at[window(self.cube.owner(piece)[0], self.rows)],
            self.keep.at[piece], self.load_sem.at[piece],
        )

    def core(self, piece):
        cube = self.cube
        return remote(
            self.parts.at[window(cube.owner(piece)[1], self.rows)], self.core_in.at[piece],
            self.core_send.at[piece], self.core_recv.at[piece], cube.at(cube.me + cube.core_step),
        )

    def hop(self, piece):
        cube, level = self.cube, piece.bit_length() - 1
        return remote(
            self.keep.at[piece], self.fold_in.at[piece - 1],
            self.send_sem.at[piece - 1], self.recv_sem.at[piece - 1],
            cube.at(cube.me + cube.steps[level]),
        )

    def order(self):
        return sorted(range(self.cube.count), key=lambda p: (-(p.bit_length()), p))

    def start(self):
        for piece in self.order():
            self.core(piece).start()
            self.load(piece).start()

    def add(self, piece, other):
        @pl.loop(0, self.rows // 16)
        def _(i):
            part = window(i, 16)
            self.keep[piece, part] = (
                self.keep[piece, part].astype(F32) + other[part].astype(F32)
            ).astype(BF16)

    def fold(self, piece):
        self.load(piece).wait()
        self.core(piece).wait_recv()
        self.add(piece, self.core_in.at[piece])
        for level in range(self.cube.levels - 1, piece.bit_length() - 1, -1):
            above = piece + (1 << level)
            self.hop(above).wait_recv()
            self.add(piece, self.fold_in.at[above - 1])
        if piece:
            self.hop(piece).start()

    def finish(self):
        self.fold(0)

        @pl.loop(0, self.rows // 16)
        def _(i):
            part = window(i, 16)
            self.out[part] = self.keep[0, part].astype(F32)

        for piece in range(self.cube.count):
            self.core(piece).wait_send()
            if piece:
                self.hop(piece).wait_send()


class Swap:
    def __init__(self, place, moves, sems):
        self.place, self.moves = place, moves
        self.send_sem, self.recv_sem, self.local = sems

    @staticmethod
    def sems(size, moves):
        return [DMA((moves, size)), DMA((moves, size)), DMA((moves,))]

    def copies(self):
        place = self.place
        out = []
        for k in range(1, place.size):
            to = (place.me + k) % place.size
            for m, (src, dst) in enumerate(self.moves):
                out.append(
                    remote(src(to), dst(place.me), self.send_sem.at[m, k], self.recv_sem.at[m, k], place.at(to))
                )
        return out

    def locals(self):
        return [
            pltpu.make_async_copy(src(self.place.me), dst(self.place.me), self.local.at[m])
            for m, (src, dst) in enumerate(self.moves)
        ]

    def start(self):
        for copy in self.copies() + self.locals():
            copy.start()

    def finish(self):
        place = self.place
        for copy in self.copies():
            copy.wait_send()
        for k in range(1, place.size):
            of = (place.me - k + place.size) % place.size
            for m, (src, dst) in enumerate(self.moves):
                here = dst(of)
                remote(here, here, self.send_sem.at[m, k], self.recv_sem.at[m, k], place.at(of)).wait_recv()
        for copy in self.locals():
            copy.wait()


def rows_to_side(src, dst):
    rows, cols = dst.shape[0], src.shape[1]
    return (lambda d: src.at[window(d, rows)], lambda d: dst.at[:, window(d, cols)])


def side_to_rows(src, dst):
    rows, cols = src.shape[0], dst.shape[1]
    return (lambda d: src.at[:, window(d, cols)], lambda d: dst.at[window(d, rows)])


ANY = pl.BlockSpec(memory_space=pl.ANY)
VMEM = pl.BlockSpec(memory_space=pltpu.VMEM)


def front_kernel(
    x_ref, w_ref, wo_ref, we_ref, wr_ref, small_ref,
    seq_ref, w_out, wo_line, we_out, wr_out, small_out, *sems
):
    line, cube = Line(), Cube()
    gather = LineGather(line, x_ref, seq_ref, sems[:5])
    wide = LineGather(line, wo_ref, wo_line, sems[5:10])
    weights = CubeGather(cube, w_ref, w_out, sems[10:15])
    tile = small_ref.shape[0]
    moves = [
        (lambda d: small_ref, lambda d: small_out.at[window(d, tile)]),
        rows_to_side(wr_ref, wr_out),
    ]
    if wr_out.shape[0] % 128 == 0:
        moves.append(side_to_rows(we_ref, we_out))
    swap = Swap(cube, moves, sems[15:18])
    barrier = pltpu.get_barrier_semaphore()
    line.greet(barrier)
    cube.greet_all(barrier)
    pl.semaphore_wait(barrier, cube.dp - 1 + line.peers())
    gather.start()
    wide.start()
    weights.start()
    gather.take(1)
    wide.take(1)
    for piece in range(1, cube.count):
        if piece.bit_length() < cube.levels:
            weights.take(piece)
    swap.start()
    gather.take(2)
    wide.take(2)
    for piece in range(1, cube.count):
        weights.take(piece)
    for step in range(3, line.n):
        gather.take(step)
        wide.take(step)
    weights.finish()
    swap.finish()
    gather.finish()
    wide.finish()


def front(x, w, w_o, w_e, w_r, small):
    dp, n = lax.axis_size("dp"), lax.axis_size("tensor")
    rows, model = x.shape
    seq, w_all, o_line, e_all, r_all, small_all = pl.pallas_call(
        front_kernel,
        out_shape=(
            jax.ShapeDtypeStruct((n * rows, model), BF16),
            jax.ShapeDtypeStruct((dp * w.shape[0], w.shape[1]), BF16),
            jax.ShapeDtypeStruct((w_o.shape[0], n * w_o.shape[1]), BF16),
            jax.ShapeDtypeStruct((dp * w_e.shape[0], w_e.shape[1] // dp), BF16),
            jax.ShapeDtypeStruct((w_r.shape[0] // dp, w_r.shape[1] * dp), BF16),
            jax.ShapeDtypeStruct((dp * small.shape[0], small.shape[1]), BF16),
        ),
        in_specs=[ANY] * 6,
        out_specs=(ANY,) * 6,
        scratch_shapes=2 * LineGather.sems(n) + CubeGather.sems(dp // 2) + Swap.sems(dp, 3),
        compiler_params=pltpu.CompilerParams(collective_id=0, has_side_effects=True),
        cost_estimate=pl.CostEstimate(flops=80 * 10**9, bytes_accessed=10**7, transcendentals=0),
        name="front",
    )(x, w, w_o, w_e, w_r, small)
    if r_all.shape[0] % 128:
        e_all = lax.all_to_all(w_e, "dp", split_axis=1, concat_axis=0, tiled=True)
    return seq, w_all, o_line, e_all, r_all, small_all


class SmallSum:
    def __init__(self, line, cube, parts, out, scratch):
        self.line, self.cube, self.parts, self.out = line, cube, parts, out
        self.come, self.gather, self.sems, self.line_send, self.line_recv = (
            scratch[0], scratch[1], scratch[2:5], scratch[5], scratch[6]
        )
        moves = [(lambda d: parts.at[d], lambda d: self.come.at[d])]
        self.swap = Swap(cube, moves, self.sems)

    @staticmethod
    def scratch(dp, n, rows, d):
        return [
            pltpu.VMEM((dp, rows, d), F32),
            pltpu.VMEM((n, rows, d), F32),
            *Swap.sems(dp, 1),
            DMA((n,)), DMA((n,)),
        ]

    def hop(self, k):
        line = self.line
        here = self.gather.at[line.me]
        return remote(
            here, here, self.line_send.at[k], self.line_recv.at[k], line.at((line.me + k) % line.n)
        )

    def middle(self):
        self.swap.finish()
        total = self.come[0]
        for d in range(1, self.cube.dp):
            total = total + self.come[d]
        self.gather[self.line.me] = total
        for k in range(1, self.line.n):
            self.hop(k).start()

    def finish(self):
        line = self.line
        for k in range(1, line.n):
            here = self.gather.at[(line.me - k + line.n) % line.n]
            remote(
                here, here, self.line_send.at[k], self.line_recv.at[k], line.at(line.me)
            ).wait_recv()
            self.hop(k).wait_send()
        total = self.gather[0]
        for z in range(1, line.n):
            total = total + self.gather[z]
        self.out[...] = total


def exchange_kernel(counts, *refs):
    lines, planes, gathers, cubes, swaps, outs, backs, small = counts
    line, cube = Line(), Cube()
    count = sum(counts)
    pairs, scratch = list(zip(refs[:count], refs[count : 2 * count])), list(refs[2 * count :])

    def take(number):
        taken = tuple(scratch[:number])
        del scratch[:number]
        return taken

    sums = [LineScatter(line, *pairs.pop(0), take(7)) for _ in range(lines)]
    folds = [CubeScatter(cube, *pairs.pop(0), take(8)) for _ in range(planes)]
    lanes = [LineGather(line, *pairs.pop(0), take(5)) for _ in range(gathers)]
    wholes = [CubeGather(cube, *pairs.pop(0), take(5)) for _ in range(cubes)]
    moves = [side_to_rows(*pairs.pop(0)) for _ in range(swaps)]
    swap = Swap(cube, moves, take(3)) if swaps else None
    turns = [rows_to_side(*pairs.pop(0)) for _ in range(outs)]
    turns += [side_to_rows(*pairs.pop(0)) for _ in range(backs)]
    turn = Swap(line, turns, take(3)) if turns else None
    little = SmallSum(line, cube, *pairs.pop(0), take(7)) if small else None
    barrier = pltpu.get_barrier_semaphore()
    peers = 0
    if small or turns:
        line.greet_all(barrier)
        peers = line.n - 1
    elif lines or gathers:
        line.greet(barrier)
        peers = line.peers()
    if small or swaps:
        cube.greet_all(barrier)
        peers = peers + cube.dp - 1
    elif planes or cubes:
        cube.greet(barrier)
        peers = peers + cube.peers()
    for s in sums:
        s.prepare()
    pl.semaphore_wait(barrier, peers)
    if turns:
        turn.start()
    if small:
        little.swap.start()
    for s in sums:
        s.step(1)
    for lane in lanes:
        lane.start()
    for whole in wholes[:1]:
        whole.start()
    for f in folds:
        f.start()
    if small:
        little.middle()
    pieces = [p for p in folds[0].order() if p] if planes else []
    per = -(-len(pieces) // (line.n - 1))
    for step in range(1, line.n):
        for whole in wholes[step - 1 : step]:
            for piece in range(1, cube.count):
                if piece.bit_length() < cube.levels:
                    whole.take(piece)
        if step > 1:
            for s in sums:
                s.step(step)
            for lane in lanes:
                lane.take(step - 1)
        for piece in pieces[:per]:
            for f in folds:
                f.fold(piece)
        pieces = pieces[per:]
        if step == 1 and swaps:
            swap.start()
        for whole in wholes[step - 1 : step]:
            whole.finish()
        for whole in wholes[step : step + 1]:
            whole.start()
    for f in folds:
        f.finish()
    for lane in lanes:
        lane.take(line.n - 1)
        lane.finish()
    for s in sums:
        s.finish()
    if turns:
        turn.finish()
    if swaps:
        swap.finish()
    if small:
        little.finish()


def exchange(
    collective_id, lines=(), planes=(), gathers=(), cubes=(), swaps=(), outs=(), backs=(), small=(),
    weight=80,
):
    dp, n = lax.axis_size("dp"), lax.axis_size("tensor")
    groups = (lines, planes, gathers, cubes, swaps, outs, backs, small)
    counts = tuple(len(group) for group in groups)
    operands = [part for group in groups for part in group]
    out_shape, out_specs, scratch = [], [], []

    def result(rows, d, kind, spec):
        out_shape.append(jax.ShapeDtypeStruct((rows, d), kind))
        out_specs.append(spec)

    for part in lines:
        rows, d = part.shape[0] // n, part.shape[1]
        result(rows, d, F32, VMEM)
        scratch += LineScatter.scratch(n, rows, d)
    for part in planes:
        rows, d = part.shape[0] // dp, part.shape[1]
        result(rows, d, F32, VMEM)
        scratch += CubeScatter.scratch(dp // 2, rows, d)
    for part in gathers:
        result(n * part.shape[0], part.shape[1], BF16, ANY)
        scratch += LineGather.sems(n)
    for part in cubes:
        result(dp * part.shape[0], part.shape[1], BF16, ANY)
        scratch += CubeGather.sems(dp // 2)
    for part in swaps:
        result(dp * part.shape[0], part.shape[1] // dp, BF16, ANY)
    if swaps:
        scratch += Swap.sems(dp, len(swaps))
    for part in outs:
        result(part.shape[0] // n, part.shape[1] * n, BF16, ANY)
    for part in backs:
        result(part.shape[0] * n, part.shape[1] // n, BF16, ANY)
    if outs or backs:
        scratch += Swap.sems(n, len(outs) + len(backs))
    for part in small:
        rows, d = part.shape[1:]
        result(rows, d, F32, VMEM)
        scratch += SmallSum.scratch(dp, n, rows, d)
    return pl.pallas_call(
        functools.partial(exchange_kernel, counts),
        out_shape=tuple(out_shape),
        in_specs=[ANY] * len(operands),
        out_specs=tuple(out_specs),
        scratch_shapes=scratch,
        compiler_params=pltpu.CompilerParams(
            collective_id=collective_id, has_side_effects=True, vmem_limit_bytes=60 << 20
        ),
        cost_estimate=pl.CostEstimate(flops=weight * 10**9, bytes_accessed=10**7, transcendentals=0),
        name="exchange",
    )(*operands)


PAIR = 2 * HEAD_DIM
NEVER = -1e30


def lane_of(shape, head):
    lane = lax.broadcasted_iota(jnp.int32, shape, 1)
    return (lane < HEAD_DIM) if head == 0 else (lane >= HEAD_DIM)


def sight(parents_ref, row, col):
    at = jnp.int32(row)
    seen = at == col
    for hop in range(row - col):
        at = parents_ref[at]
        seen = seen | (at == col)
    return jnp.where(seen, 0.0, NEVER).astype(F32)


def masked_scores(parents_ref, q_head, k_ref, row):
    scores = []
    for col in range(row + 1):
        part = over(q_head, k_ref[col * BLOCK : (col + 1) * BLOCK, :], 1, 1)
        if col == row:
            below = lax.broadcasted_iota(jnp.int32, part.shape, 1) <= lax.broadcasted_iota(
                jnp.int32, part.shape, 0
            )
            part = jnp.where(below, part, NEVER)
        else:
            part = part + sight(parents_ref, row, col)
        scores.append(part)
    return scores


def row_reduce(parts, fold, reduce):
    return reduce(functools.reduce(fold, parts), axis=-1, keepdims=True)


def attend_kernel(parents_ref, q_ref, k_ref, v_ref, out_ref):
    blocks = q_ref.shape[0] // BLOCK
    scale = 1.0 / math.sqrt(HEAD_DIM)
    for row in range(blocks):
        here = slice(row * BLOCK, (row + 1) * BLOCK)
        heads = []
        for head in range(2):
            q_head = q_ref[here, :].astype(F32) * scale
            q_head = jnp.where(lane_of(q_head.shape, head), q_head, 0.0).astype(BF16)
            scores = masked_scores(parents_ref, q_head, k_ref, row)
            top = row_reduce(scores, jnp.maximum, jnp.max)
            probs = [jnp.exp(s - top) for s in scores]
            total = row_reduce(probs, jnp.add, jnp.sum)
            out = None
            for col in range(row + 1):
                term = over(
                    probs[col].astype(BF16), v_ref[col * BLOCK : (col + 1) * BLOCK, :], 1, 0
                )
                out = term if out is None else out + term
            heads.append(out / total)
        mixed = jnp.where(lane_of(heads[0].shape, 0), heads[0], heads[1])
        out_ref[here, :] = mixed.astype(out_ref.dtype)


def attend(parents, qkv, width):
    rows = qkv.shape[0]
    pairs = width // PAIR
    spec = lambda part: pl.BlockSpec((rows, PAIR), lambda p, parents: (0, part * pairs + p))
    blocks = rows // BLOCK
    work = pairs * 2 * (blocks * (blocks + 1) // 2) * BLOCK * BLOCK
    return pl.pallas_call(
        attend_kernel,
        out_shape=jax.ShapeDtypeStruct((rows, width), BF16),
        grid_spec=pltpu.PrefetchScalarGridSpec(
            num_scalar_prefetch=1,
            grid=(pairs,),
            in_specs=[spec(0), spec(1), spec(2)],
            out_specs=pl.BlockSpec((rows, PAIR), lambda p, parents: (0, p)),
        ),
        compiler_params=pltpu.CompilerParams(vmem_limit_bytes=48 << 20),
        cost_estimate=pl.CostEstimate(
            flops=work * PAIR * 24, bytes_accessed=rows * width * 8, transcendentals=work
        ),
        name="attend",
    )(parents, qkv, qkv, qkv)


def attend_back_kernel(parents_ref, q_ref, k_ref, v_ref, g_ref, out_ref, dq_s, dk_s, dv_s):
    part = pl.program_id(1)
    blocks = q_ref.shape[0] // BLOCK
    scale = 1.0 / math.sqrt(HEAD_DIM)

    @pl.when(part == 0)
    def _():
        for row in range(blocks):
            here = slice(row * BLOCK, (row + 1) * BLOCK)
            dq_heads = []
            for head in range(2):
                lanes = lane_of((BLOCK, PAIR), head)
                q_head = jnp.where(lanes, q_ref[here, :].astype(F32) * scale, 0.0).astype(BF16)
                g_head = jnp.where(lanes, g_ref[here, :].astype(F32), 0.0).astype(BF16)
                scores = masked_scores(parents_ref, q_head, k_ref, row)
                top = row_reduce(scores, jnp.maximum, jnp.max)
                probs = [jnp.exp(s - top) for s in scores]
                rest = 1.0 / row_reduce(probs, jnp.add, jnp.sum)
                probs = [p * rest for p in probs]
                d_probs = [
                    over(g_head, v_ref[col * BLOCK : (col + 1) * BLOCK, :], 1, 1)
                    for col in range(row + 1)
                ]
                level = row_reduce([p * d for p, d in zip(probs, d_probs)], jnp.add, jnp.sum)
                dq = None
                for col in range(row + 1):
                    there = slice(col * BLOCK, (col + 1) * BLOCK)
                    d_scores = (probs[col] * (d_probs[col] - level)).astype(BF16)
                    term = over(d_scores, k_ref[there, :], 1, 0)
                    dq = term if dq is None else dq + term
                    dk = over(d_scores, q_head, 0, 0)
                    dv = over(probs[col].astype(BF16), g_head, 0, 0)
                    if row == col and head == 0:
                        dk_s[there, :] = dk
                        dv_s[there, :] = dv
                    else:
                        dk_s[there, :] += dk
                        dv_s[there, :] += dv
                dq_heads.append(dq * scale)
            dq_s[here, :] = jnp.where(lane_of((BLOCK, PAIR), 0), dq_heads[0], dq_heads[1]).astype(
                BF16
            )
        out_ref[...] = dq_s[...]

    @pl.when(part == 1)
    def _():
        out_ref[...] = dk_s[...].astype(BF16)

    @pl.when(part == 2)
    def _():
        out_ref[...] = dv_s[...].astype(BF16)


def attend_back(parents, qkv, grad, width):
    rows = qkv.shape[0]
    pairs = width // PAIR
    spec = lambda part: pl.BlockSpec((rows, PAIR), lambda p, c, parents: (0, part * pairs + p))
    blocks = rows // BLOCK
    work = pairs * 2 * (blocks * (blocks + 1) // 2) * BLOCK * BLOCK
    return pl.pallas_call(
        attend_back_kernel,
        out_shape=jax.ShapeDtypeStruct((rows, 3 * width), BF16),
        grid_spec=pltpu.PrefetchScalarGridSpec(
            num_scalar_prefetch=1,
            grid=(pairs, 3),
            in_specs=[
                spec(0),
                spec(1),
                spec(2),
                pl.BlockSpec((rows, PAIR), lambda p, c, parents: (0, p)),
            ],
            out_specs=pl.BlockSpec((rows, PAIR), lambda p, c, parents: (0, c * pairs + p)),
            scratch_shapes=[
                pltpu.VMEM((rows, PAIR), BF16),
                pltpu.VMEM((rows, PAIR), F32),
                pltpu.VMEM((rows, PAIR), F32),
            ],
        ),
        compiler_params=pltpu.CompilerParams(vmem_limit_bytes=48 << 20),
        cost_estimate=pl.CostEstimate(
            flops=work * PAIR * 60, bytes_accessed=rows * width * 14, transcendentals=work
        ),
        name="attend_back",
    )(parents, qkv, qkv, qkv, grad)


def ffn_kernel(n2_ref, dy_ref, we_ref, wr_ref, be_ref, *refs):
    sum_ref, act_ref, dpre_ref, part_ref = refs[:4]
    refs = refs[4:]
    we, wr, seq_st, dy_st, act_st, dpre_st, part_st, keep, give, core_in, fold_in = refs[:11]
    w_sem, load_sem, st_sem, rsc_send, rsc_recv, fold_send, fold_recv = refs[11:18]
    cube = Cube()
    levels, count, owner = cube.levels, cube.count, cube.owner
    rows, model = sum_ref.shape
    units = wr_ref.shape[0]
    barrier = pltpu.get_barrier_semaphore()
    cube.greet(barrier)
    parts = we_ref.shape[0] // model
    mine_units = we_ref.shape[1]
    loads_w = [pltpu.make_async_copy(wr_ref, wr, w_sem.at[parts])]
    for part in range(parts):
        loads_w.append(
            pltpu.make_async_copy(
                we_ref.at[pl.ds(part * model, model)],
                we.at[:, pl.ds(part * mine_units, mine_units)],
                w_sem.at[part],
            )
        )

    def load(piece, slot):
        out = []
        for half, index in enumerate(owner(piece)):
            for kind, (ref, stage) in enumerate(((n2_ref, seq_st), (dy_ref, dy_st))):
                out.append(
                    pltpu.make_async_copy(
                        ref.at[window(index, rows)],
                        stage.at[slot, pl.ds(half * rows, rows)],
                        load_sem.at[kind, slot, half],
                    )
                )
        return out

    order = sorted(range(count), key=lambda p: (-(p.bit_length()), p))
    slots = {piece: i % 2 for i, piece in enumerate(order)}
    loads = {order[0]: load(order[0], 0)}
    for c in loads[order[0]] + loads_w:
        c.start()
    pl.semaphore_wait(barrier, cube.peers())
    for c in loads_w:
        c.wait()
    stores, core_sends, folds = {}, {}, {}

    def add(piece, other):
        @pl.loop(0, rows // 16)
        def _(i):
            part = window(i, 16)
            keep[piece, part] = (
                keep[piece, part].astype(F32) + other[part].astype(F32)
            ).astype(BF16)

    def core_copy(piece):
        return remote(
            give.at[slots[piece]], core_in.at[piece],
            rsc_send.at[piece], rsc_recv.at[piece], cube.at(cube.me + cube.core_step),
        )

    def fold_copy(piece):
        return remote(
            keep.at[piece], fold_in.at[piece - 1], fold_send.at[piece - 1], fold_recv.at[piece - 1],
            cube.at(cube.me + cube.steps[piece.bit_length() - 1]),
        )

    def fold(piece):
        core_copy(piece).wait_recv()
        add(piece, core_in.at[piece])
        for level in range(levels - 1, piece.bit_length() - 1, -1):
            above = piece + (1 << level)
            fold_copy(above).wait_recv()
            add(piece, fold_in.at[above - 1])
        folds[piece] = fold_copy(piece)
        folds[piece].start()

    chunk = 256
    wide = 512
    for turn, piece in enumerate(order):
        slot = turn % 2
        for c in loads[piece]:
            c.wait()
        if turn + 1 < count:
            loads[order[turn + 1]] = load(order[turn + 1], 1 - slot)
            for c in loads[order[turn + 1]]:
                c.start()
        if turn >= 2:
            for c in stores[turn - 2]:
                c.wait()
            core_sends[order[turn - 2]].wait_send()

        @pl.loop(0, units // chunk)
        def _(i):
            cols = window(i, chunk)
            pre = over(seq_st[slot], we[:, cols], 1, 0) + be_ref[:, cols]
            d_act = over(dy_st[slot], wr[cols, :], 1, 1)
            square = pre * pre
            t = jnp.tanh(GELU * pre * (1.0 + 0.044715 * square))
            act_st[slot, :, cols] = (0.5 * pre * (1.0 + t)).astype(BF16)
            slope = 0.5 * (1.0 + t) + (0.5 * GELU) * pre * (1.0 - t * t) * (
                1.0 + (3 * 0.044715) * square
            )
            dpre_st[slot, :, cols] = (d_act * slope).astype(BF16)

        if turn:
            fold(order[turn - 1])

        @pl.loop(0, model // wide)
        def _(i):
            cols = window(i, wide)
            d_two = over(dpre_st[slot], we[cols, :], 1, 1).astype(BF16)
            keep[piece, :, cols] = d_two[:rows]
            give[slot, :, cols] = d_two[rows:]
            part_st[slot, :, cols] = over(act_st[slot], wr[:, cols], 1, 0).astype(BF16)

        core_sends[piece] = core_copy(piece)
        core_sends[piece].start()
        stores[turn] = []
        for half, index in enumerate(owner(piece)):
            to, part = window(index, rows), pl.ds(half * rows, rows)
            for kind, (stage, ref) in enumerate(
                ((act_st, act_ref), (dpre_st, dpre_ref), (part_st, part_ref))
            ):
                stores[turn].append(
                    pltpu.make_async_copy(stage.at[slot, part], ref.at[to], st_sem.at[kind, slot, half])
                )
        for c in stores[turn]:
            c.start()
    core_copy(0).wait_recv()
    for level in range(levels):
        fold_copy(1 << level).wait_recv()

    @pl.loop(0, rows // 16)
    def _(i):
        part = window(i, 16)
        total = keep[0, part].astype(F32) + core_in[0, part].astype(F32)
        for level in range(levels):
            total = total + fold_in[(1 << level) - 1, part].astype(F32)
        sum_ref[part] = total

    for turn in range(max(0, count - 2), count):
        for c in stores[turn]:
            c.wait()
        core_sends[order[turn]].wait_send()
    for s in folds.values():
        s.wait_send()


def ffn(n2, dy, we, wr, bias_e):
    n, dp = lax.axis_size("tensor"), lax.axis_size("dp")
    rows, model = n2.shape[0] // dp, n2.shape[1]
    units, count = wr.shape[0], dp // 2
    flops = 30 * dp * rows * model * units
    return pl.pallas_call(
        ffn_kernel,
        out_shape=(
            jax.ShapeDtypeStruct((rows, model), F32),
            jax.ShapeDtypeStruct((dp * rows, units), BF16),
            jax.ShapeDtypeStruct((dp * rows, units), BF16),
            jax.ShapeDtypeStruct((dp * rows, model), BF16),
        ),
        in_specs=[ANY] * 4 + [VMEM],
        out_specs=(VMEM, ANY, ANY, ANY),
        scratch_shapes=[
            pltpu.VMEM((model, units), BF16),
            pltpu.VMEM((units, model), BF16),
            pltpu.VMEM((2, 2 * rows, model), BF16),
            pltpu.VMEM((2, 2 * rows, model), BF16),
            pltpu.VMEM((2, 2 * rows, units), BF16),
            pltpu.VMEM((2, 2 * rows, units), BF16),
            pltpu.VMEM((2, 2 * rows, model), BF16),
            pltpu.VMEM((count, rows, model), BF16),
            pltpu.VMEM((2, rows, model), BF16),
            pltpu.VMEM((count, rows, model), BF16),
            pltpu.VMEM((count - 1, rows, model), BF16),
            DMA((n + 1,)), DMA((2, 2, 2)), DMA((3, 2, 2)),
            DMA((count,)), DMA((count,)), DMA((count - 1,)), DMA((count - 1,)),
        ],
        compiler_params=pltpu.CompilerParams(
            collective_id=1, has_side_effects=True, vmem_limit_bytes=62 << 20
        ),
        cost_estimate=pl.CostEstimate(
            flops=flops, bytes_accessed=8 * dp * rows * (model + units), transcendentals=dp * rows * units
        ),
        name="ffn_plane",
    )(n2, dy, we, wr, bias_e)


def body(
    tokens,
    parents,
    cotangent,
    first_gain,
    first_shift,
    w_query,
    b_query,
    w_key,
    w_value,
    b_value,
    w_out,
    b_out,
    second_gain,
    second_shift,
    w_expand,
    b_expand,
    w_reduce,
    b_reduce,
):
    dp = lax.axis_size("dp")
    tn = lax.axis_size("tensor")
    dp_me = lax.axis_index("dp")
    tn_me = lax.axis_index("tensor")
    width = w_query.shape[1]
    model = w_query.shape[0] * dp
    units = w_expand.shape[1]
    mine = units // dp
    micros = range(tokens.shape[0])
    last = tokens.shape[0] - 1
    x_low = [tokens[m, 0] for m in micros]
    dy_low = [cotangent[m, 0] for m in micros]
    rows_here = x_low[0].shape[0]
    total = rows_here * tn

    cut = first_gain.shape[0]
    bq_rows, bq_cols = b_query.shape
    be_rows, be_cols = b_expand.shape
    small = jnp.concatenate(
        [first_gain, first_shift, b_out, second_gain, second_shift, b_reduce]
        + [b_query.reshape(-1), b_value.reshape(-1), b_expand.reshape(-1)]
    )
    used = small.shape[0]
    small = jnp.pad(small, (0, -used % 2048)).reshape(-1, 128)
    w_qkv = jnp.concatenate([w_query, w_key, w_value], axis=1)
    seq_x0, w_qkv, w_ot, w_e, w_r, small = front(
        x_low[0], w_qkv, w_out.T, w_expand, w_reduce, small
    )
    small = small.reshape(dp, -1)[:, :used]
    gain_one, shift_one, bias_out, gain_two, shift_two, bias_red = [
        small[:, i * cut : (i + 1) * cut].reshape(1, model).astype(F32) for i in range(6)
    ]
    at = 6 * cut
    bias_qkv = []
    for i in range(2):
        part = small[:, at : at + bq_rows * bq_cols].reshape(dp, bq_rows, bq_cols)
        bias_qkv.append(part.transpose(1, 0, 2).reshape(1, width).astype(F32))
        at += bq_rows * bq_cols
    bias_qkv = jnp.concatenate([bias_qkv[0], jnp.zeros((1, width), F32), bias_qkv[1]], 1)
    bias_e = small[:, at:].reshape(dp, dp, be_rows // dp, be_cols)
    bias_e = lax.dynamic_index_in_dim(bias_e, dp_me, 1, keepdims=False)
    bias_e = bias_e.transpose(1, 0, 2).reshape(mine)
    bias_e = jnp.pad(bias_e, (0, -mine % 2048)).reshape(-1, 128)

    seq_x = [seq_x0]
    w_r = lax.all_gather(w_r, "tensor", axis=0, tiled=True)
    w_e = lax.all_gather(w_e, "tensor", axis=1 if mine % 128 else 0, tiled=True)

    def outer(left, right):
        out = None
        for a, b in zip(left, right):
            term = over(a, b, 0, 0)
            out = term if out is None else out + term
        return out.astype(BF16)

    normal_one, seq_one, qkv, attended, hidden, normed_two = [], [], [], [], [], []
    out_part, seq_two, activated, d_pre, d_hidden, d_branch, out_sum = [], [], [], [], [], [], []
    d_qkv, d_one, d_att, row_attended = [], [], [], []
    g_gain_two = g_shift_two = g_bias_red = g_bias_out = g_bias_e = 0.0
    g_gain_one = g_shift_one = g_bias_qkv = 0.0
    for m in micros:
        normal_one.append(layer_norm(seq_x[m].astype(F32), 1.0, 0.0))
        seq_one.append((normal_one[m] * gain_one + shift_one).astype(BF16))
        qkv.append(
            (jnp.dot(seq_one[m], w_qkv, preferred_element_type=F32) + bias_qkv).astype(BF16)
        )
        attended.append(attend(parents[m, 0], qkv[m], width))
        if m == 0:
            bias_e, w_ot, grad, row_att = exchange(
                3, gathers=[bias_e], cubes=[w_ot, dy_low[m]], outs=[attended[m]]
            )
            seq_grad = [grad]
            bias_e = bias_e.reshape(tn, -1)[:, :mine].reshape(1, tn * mine).astype(F32)
        else:
            part, row_att, col_grad = exchange(
                4, planes=[out_part[m - 1]], outs=[attended[m]], backs=[d_att[m - 1]]
            )
            out_sum.append(part)
            d_att[m - 1] = col_grad
        if m < last:
            next_x, row_att = lax.optimization_barrier((x_low[m + 1], row_att))
            next_x = lax.all_gather(next_x, "tensor", axis=0, tiled=True)
        row_attended.append(row_att)
        branch = over(row_att, w_ot, 1, 1)
        hidden.append(x_low[m].astype(F32) + (branch + bias_out))
        normed_two.append(layer_norm(hidden[m], gain_two, shift_two).astype(BF16))
        if m < last:
            grad, normed_two[m] = lax.optimization_barrier((dy_low[m + 1], normed_two[m]))
            seq_grad.append(lax.all_gather(grad, "dp", axis=0, tiled=True))

        def attention_back(k):
            d_qkv.append(attend_back(parents[k, 0], qkv[k], d_att[k], width))
            d_one.append(over(d_qkv[k], w_qkv, 1, 1).astype(BF16))
            part = d_one[k].astype(F32)
            return (
                jnp.sum(part * normal_one[k], 0, keepdims=True),
                jnp.sum(part, 0, keepdims=True),
                jnp.sum(d_qkv[k].astype(F32), 0),
            )

        if m:
            normed_two[m], seq_grad[m] = lax.optimization_barrier((normed_two[m], seq_grad[m]))
            next_two = lax.all_gather(normed_two[m], "dp", axis=0, tiled=True)
            gain, shift, bias = attention_back(m - 1)
            g_gain_one, g_shift_one = g_gain_one + gain, g_shift_one + shift
            g_bias_qkv = g_bias_qkv + bias
            next_two, d_one[m - 1] = lax.optimization_barrier((next_two, d_one[m - 1]))
            d_one[m - 1] = lax.psum_scatter(
                d_one[m - 1], "tensor", scatter_dimension=0, tiled=True
            )

        if m == 0:
            (seq,) = exchange(7, cubes=[normed_two[m]])
        else:
            seq = next_two
        d_two, act, dpre, part = ffn(seq, seq_grad[m], w_e, w_r, bias_e)
        seq_two.append(seq)
        activated.append(act)
        d_pre.append(dpre)
        out_part.append(part)
        if m == last:
            g_r = outer(activated, seq_grad)
            d_two, g_r, *d_one = lax.optimization_barrier((d_two, g_r, *d_one))
            g_r = lax.psum_scatter(g_r, "tensor", scatter_dimension=0, tiled=True)
        grad32 = dy_low[m].astype(F32)
        norm_value, norm_pull = jax.vjp(layer_norm, hidden[m], gain_two, shift_two)
        d_norm, g_gain, g_shift = norm_pull(d_two)
        d_hidden.append(grad32 + d_norm)
        d_branch.append(d_hidden[m].astype(BF16))
        d_att.append(jnp.dot(d_branch[m], w_ot, preferred_element_type=F32).astype(BF16))
        g_gain_two = g_gain_two + g_gain
        g_shift_two = g_shift_two + g_shift
        g_bias_red = g_bias_red + jnp.sum(grad32, 0, keepdims=True)
        g_bias_out = g_bias_out + jnp.sum(d_branch[m].astype(F32), 0, keepdims=True)
        g_bias_e = g_bias_e + jnp.sum(dpre.astype(F32), 0)
        if m < last:
            next_x, d_branch[m] = lax.optimization_barrier((next_x, d_branch[m]))
            seq_x.append(next_x)

    g_ot = outer([jnp.concatenate(d_branch, 0)], [jnp.concatenate(row_attended, 0)])
    g_ot, d_att[last] = exchange(6, planes=[g_ot], backs=[d_att[last]], weight=15)
    d_att[last], *d_pre = lax.optimization_barrier((d_att[last], *d_pre))
    g_et = outer(d_pre, seq_two)
    d_att[last], g_r = lax.optimization_barrier((d_att[last], g_r))
    g_et = lax.psum_scatter(g_et, "tensor", scatter_dimension=0, tiled=True)
    gain, shift, bias = attention_back(last)
    g_gain_one, g_shift_one = g_gain_one + gain, g_shift_one + shift
    g_bias_qkv = g_bias_qkv + bias

    rows = jnp.concatenate(
        [g_gain_one, g_shift_one, g_bias_out, g_gain_two, g_shift_two, g_bias_red], 0
    )
    rows = rows.reshape(6, dp, cut).transpose(1, 0, 2).reshape(dp, 6 * cut)
    row_qv = jnp.concatenate([g_bias_qkv[:width], g_bias_qkv[2 * width :]])
    row_qv = row_qv.reshape(2 * bq_rows, dp, bq_cols).transpose(1, 0, 2)[:, None]
    row_qv = lax.dynamic_update_slice(
        jnp.zeros((dp, tn, 2 * bq_rows, bq_cols), F32), row_qv, (0, tn_me, 0, 0)
    ).reshape(dp, -1)
    row_e = g_bias_e.reshape(tn, be_rows // dp, dp, be_cols).transpose(2, 0, 1, 3)[:, :, None]
    row_e = lax.dynamic_update_slice(
        jnp.zeros((dp, tn, dp, be_rows // dp, be_cols), F32), row_e, (0, 0, dp_me, 0, 0)
    ).reshape(dp, -1)
    little = jnp.concatenate([rows, row_qv, row_e], 1)
    little = jnp.pad(little, ((0, 0), (0, -little.shape[1] % 1024))).reshape(dp, -1, 128)

    layer_out, input_grad = [], []

    def done(m):
        layer_out.append((hidden[m] + (out_sum[m] + bias_red)).astype(BF16))
        first_value, first_pull = jax.vjp(
            lambda rows: layer_norm(rows, gain_one, shift_one), x_low[m].astype(F32)
        )
        input_grad.append((d_hidden[m] + first_pull(d_one[m].astype(F32))[0]).astype(BF16))

    d_one[last], *d_qkv = lax.optimization_barrier((d_one[last], *d_qkv))
    g_qkv = outer(seq_one, d_qkv)
    for m in micros[:last]:
        done(m)
    d_one[last], *finished = lax.optimization_barrier((d_one[last], *layer_out, *input_grad))
    layer_out, input_grad = finished[:last], finished[last:]
    g_ot = g_ot.astype(BF16).reshape(-1, tn, width).transpose(1, 0, 2).reshape(-1, width)
    d_one[last], g_ot, g_qkv, out_last, g_expand, g_reduce, little = exchange(
        5,
        lines=[d_one[last], g_ot],
        planes=[g_qkv, out_part[last]],
        swaps=[g_et, g_r],
        small=[little],
    )
    out_sum.append(out_last)
    g_query, g_key, g_value = [g_qkv[:, i * width : (i + 1) * width] for i in range(3)]
    g_out = g_ot.T
    g_expand = g_expand.T.astype(F32)
    g_reduce = g_reduce.astype(F32)
    little = little.reshape(-1)
    six = little[: 6 * cut].reshape(6, cut)
    at = 6 * cut
    g_bqv = little[at : at + tn * 2 * bq_rows * bq_cols].reshape(tn, 2 * bq_rows, bq_cols)
    g_bqv = lax.dynamic_index_in_dim(g_bqv, tn_me, 0, keepdims=False)
    g_bq, g_bv = g_bqv[:bq_rows], g_bqv[bq_rows:]
    at += tn * 2 * bq_rows * bq_cols
    g_be = little[at : at + tn * be_rows * be_cols].reshape(tn, be_rows, be_cols)
    g_be = lax.dynamic_index_in_dim(g_be, tn_me, 0, keepdims=False)
    done(last)

    return (
        jnp.stack(layer_out, 0)[:, None],
        jnp.stack(input_grad, 0)[:, None],
        six[0],
        six[1],
        g_query,
        g_bq,
        g_key,
        g_value,
        g_bv,
        g_out,
        six[2],
        six[3],
        six[4],
        g_expand,
        g_be,
        g_reduce,
        six[5],
    )


def solution(mesh):
    in_specs = (
        P(None, "dp", "tensor", None),
        P(None, "dp", None),
        P(None, "dp", "tensor", None),
        P("dp"),
        P("dp"),
        P("dp", "tensor"),
        P("tensor", "dp"),
        P("dp", "tensor"),
        P("dp", "tensor"),
        P("tensor", "dp"),
        P("tensor", "dp"),
        P("dp"),
        P("dp"),
        P("dp"),
        P("dp", "tensor"),
        P("tensor", "dp"),
        P("tensor", "dp"),
        P("dp"),
    )
    out_specs = (
        P(None, "dp", "tensor", None),
        P(None, "dp", "tensor", None),
        P("dp"),
        P("dp"),
        P("dp", "tensor"),
        P("tensor", "dp"),
        P("dp", "tensor"),
        P("dp", "tensor"),
        P("tensor", "dp"),
        P("tensor", "dp"),
        P("dp"),
        P("dp"),
        P("dp"),
        P("dp", "tensor"),
        P("tensor", "dp"),
        P("tensor", "dp"),
        P("dp"),
    )
    return jax.shard_map(body, mesh=mesh, in_specs=in_specs, out_specs=out_specs, check_vma=False)
```

```python
import functools
import math

import jax
import jax.numpy as jnp
from jax import lax
from jax.experimental import pallas as pl
from jax.experimental.pallas import tpu as pltpu
from jax.sharding import PartitionSpec as P

HEAD_DIM = 64
BLOCK = 256

F32 = jnp.float32
BF16 = jnp.bfloat16
MESH = pl.DeviceIdType.MESH
DMA = pltpu.SemaphoreType.DMA
GELU = math.sqrt(2.0 / math.pi)


def layer_norm(rows, gain, shift):
    center = rows - jnp.mean(rows, -1, keepdims=True)
    spread = jnp.mean(center * center, -1, keepdims=True)
    return center * lax.rsqrt(spread + 1e-05) * gain + shift


def after(value, *others):
    return lax.optimization_barrier((value,) + others)[0]


def over(left, right, on_left, on_right):
    return lax.dot_general(
        left, right, (((on_left,), (on_right,)), ((), ())), preferred_element_type=F32
    )


def window(index, rows):
    return pl.ds(pl.multiple_of(index * rows, rows), rows)


def remote(src, dst, send, recv, to):
    return pltpu.make_async_remote_copy(
        src_ref=src, dst_ref=dst, send_sem=send, recv_sem=recv,
        device_id=to, device_id_type=MESH,
    )


class Line:
    def __init__(self):
        self.n = lax.axis_size("tensor")
        self.me = lax.axis_index("tensor")
        self.dp = lax.axis_index("dp")

    def at(self, index):
        return (self.dp, index)

    def greet(self, barrier):
        @pl.when(self.me > 0)
        def _():
            pl.semaphore_signal(barrier, inc=1, device_id=self.at(self.me - 1), device_id_type=MESH)

        @pl.when(self.me < self.n - 1)
        def _():
            pl.semaphore_signal(barrier, inc=1, device_id=self.at(self.me + 1), device_id_type=MESH)

    @property
    def size(self):
        return self.n

    def greet_all(self, barrier):
        for k in range(1, self.n):
            pl.semaphore_signal(
                barrier, inc=1, device_id=self.at((self.me + k) % self.n), device_id_type=MESH
            )

    def peers(self):
        return (self.me + self.n - 1) // self.n + (2 * self.n - 2 - self.me) // self.n


class LineGather:
    def __init__(self, line, own, full, sems):
        self.line, self.own, self.full = line, own, full
        self.side = own.shape[0] == full.shape[0]
        self.local, self.up_send, self.up_recv, self.down_send, self.down_recv = sems

    @staticmethod
    def sems(n):
        return [DMA, DMA((n - 1,)), DMA((n - 1,)), DMA((n - 1,)), DMA((n - 1,))]

    def slot(self, index):
        if self.side:
            return self.full.at[:, window(index, self.own.shape[1])]
        return self.full.at[window(index, self.own.shape[0])]

    def hop(self, step, up):
        line = self.line
        if up:
            shard, to = line.me - (step - 1), line.me + 1
            send, recv = self.up_send, self.up_recv
        else:
            shard, to = line.me + (step - 1), line.me - 1
            send, recv = self.down_send, self.down_recv
        there = self.slot(shard)
        src = self.own if step == 1 else there
        return remote(src, there, send.at[step - 1], recv.at[step - 1], line.at(to))

    def sends(self, step, up):
        line = self.line
        if up:
            return (line.me < line.n - 1) & (line.me >= step - 1)
        return (line.me > 0) & (line.me + step - 1 < line.n)

    def takes(self, step, up):
        line = self.line
        return (line.me >= step) if up else (line.me + step < line.n)

    def send(self, step):
        for up in (True, False):
            @pl.when(self.sends(step, up))
            def _():
                self.hop(step, up).start()

    def start(self):
        pltpu.make_async_copy(self.own, self.slot(self.line.me), self.local).start()
        self.send(1)

    def take(self, step):
        for up in (True, False):
            @pl.when(self.takes(step, up))
            def _():
                line = self.line
                shard = (line.me - step) if up else (line.me + step)
                here = self.slot(shard)
                send, recv = (
                    (self.up_send, self.up_recv) if up else (self.down_send, self.down_recv)
                )
                remote(
                    here, here, send.at[step - 1], recv.at[step - 1], line.at(line.me)
                ).wait_recv()
        if step < self.line.n - 1:
            self.send(step + 1)

    def finish(self):
        for step in range(1, self.line.n):
            for up in (True, False):
                @pl.when(self.sends(step, up))
                def _():
                    self.hop(step, up).wait_send()
        pltpu.make_async_copy(self.own, self.slot(self.line.me), self.local).wait()


class LineScatter:
    def __init__(self, line, parts, out, scratch):
        self.line, self.parts, self.out = line, parts, out
        self.rows = out.shape[0]
        (self.own, self.sum, self.come, self.load, self.own_sem, self.send_sem, self.recv_sem) = scratch

    @staticmethod
    def scratch(n, rows, d):
        return [
            pltpu.VMEM((rows, d), BF16),
            pltpu.VMEM((2, n - 1, rows, d), BF16),
            pltpu.VMEM((2, n - 1, rows, d), BF16),
            DMA((2, n - 1)), DMA, DMA((2, n - 1)), DMA((2, n - 1)),
        ]

    def sends(self, step, up):
        line = self.line
        return (line.me <= step - 1) if up else (line.n - 1 - line.me <= step - 1)

    def load_of(self, step, up):
        line = self.line
        chunk = (line.me + line.n - step) if up else (line.me - line.n + step)
        way = 0 if up else 1
        return pltpu.make_async_copy(
            self.parts.at[window(chunk, self.rows)], self.sum.at[way, step - 1], self.load.at[way, step - 1]
        )

    def hop(self, step, up):
        line, way = self.line, 0 if up else 1
        return remote(
            self.sum.at[way, step - 1], self.come.at[way, step - 1],
            self.send_sem.at[way, step - 1], self.recv_sem.at[way, step - 1],
            line.at(line.me + 1 if up else line.me - 1),
        )

    def wait_from(self, step, up):
        line, way = self.line, 0 if up else 1
        remote(
            self.come.at[way, step - 1], self.come.at[way, step - 1],
            self.send_sem.at[way, step - 1], self.recv_sem.at[way, step - 1],
            line.at(line.me),
        ).wait_recv()

    def own_load(self):
        return pltpu.make_async_copy(
            self.parts.at[window(self.line.me, self.rows)], self.own, self.own_sem
        )

    def prepare(self):
        self.own_load().start()
        for step in range(1, self.line.n):
            for up in (True, False):
                @pl.when(self.sends(step, up))
                def _():
                    self.load_of(step, up).start()

    def step(self, step):
        line = self.line
        for up in (True, False):
            way = 0 if up else 1

            @pl.when(self.sends(step, up))
            def _():
                self.load_of(step, up).wait()
                if step > 1:
                    inner = (line.me > 0) if up else (line.me < line.n - 1)

                    @pl.when(inner)
                    def _():
                        self.wait_from(step - 1, up)

                        @pl.loop(0, self.rows // 16)
                        def _(i):
                            part = window(i, 16)
                            self.sum[way, step - 1, part] = (
                                self.sum[way, step - 1, part].astype(F32)
                                + self.come[way, step - 2, part].astype(F32)
                            ).astype(BF16)

                if step > 1:

                    @pl.when(self.sends(step - 1, up))
                    def _():
                        self.hop(step - 1, up).wait_send()

                self.hop(step, up).start()

    def finish(self):
        line, n = self.line, self.line.n
        self.own_load().wait()

        @pl.loop(0, self.rows // 16)
        def _(i):
            part = window(i, 16)
            self.out[part] = self.own[part].astype(F32)

        for up in (True, False):
            way = 0 if up else 1

            @pl.when((line.me > 0) if up else (line.me < n - 1))
            def _():
                self.wait_from(n - 1, up)

                @pl.loop(0, self.rows // 16)
                def _(i):
                    part = window(i, 16)
                    self.out[part] += self.come[way, n - 2, part].astype(F32)

        for up in (True, False):
            @pl.when(self.sends(n - 1, up))
            def _():
                self.hop(n - 1, up).wait_send()


class Cube:
    def __init__(self):
        self.dp = lax.axis_size("dp")
        self.levels = levels = self.dp.bit_length() - 2
        self.count = 1 << levels
        self.me = me = lax.axis_index("dp")
        self.tensor = lax.axis_index("tensor")
        core = me % 2
        flips = []
        for bit in range(1, levels + 1):
            flips.append((1 << bit) * (1 - 2 * ((me // (1 << bit)) % 2)))
        self.steps = [
            flips[l] * (1 - core) + flips[levels - 1 - l] * core for l in range(levels)
        ]
        self.core_step = 1 - 2 * core

    def at(self, index):
        return (index, self.tensor)

    def owner(self, piece):
        mine, other = self.me, self.me + self.core_step
        for l in range(self.levels):
            if piece >> l & 1:
                mine = mine + self.steps[l]
                other = other + self.steps[self.levels - 1 - l]
        return mine, other

    def greet(self, barrier):
        for step in self.steps + [self.core_step]:
            pl.semaphore_signal(
                barrier, inc=1, device_id=self.at(self.me + step), device_id_type=MESH
            )

    @property
    def size(self):
        return self.dp

    def greet_all(self, barrier):
        for k in range(1, self.dp):
            pl.semaphore_signal(
                barrier, inc=1, device_id=self.at((self.me + k) % self.dp), device_id_type=MESH
            )

    def peers(self):
        return self.levels + 1


class CubeGather:
    def __init__(self, cube, own, full, sems):
        self.cube, self.own, self.full = cube, own, full
        self.rows = own.shape[0]
        self.local, self.send_sem, self.recv_sem, self.core_send, self.core_recv = sems
        self.arrived, self.sent = {0}, []

    @staticmethod
    def sems(count):
        return [DMA, DMA((count,)), DMA((count,)), DMA((count,)), DMA((count,))]

    def slot(self, index):
        return self.full.at[window(index, self.rows)]

    def src(self, piece):
        return self.own if piece == 0 else self.slot(self.cube.owner(piece)[0])

    def hop(self, piece, level):
        cube, there = self.cube, piece + (1 << level)
        return remote(
            self.src(piece), self.slot(cube.owner(piece)[0]),
            self.send_sem.at[there], self.recv_sem.at[there], cube.at(cube.me + cube.steps[level]),
        )

    def core(self, piece):
        cube = self.cube
        return remote(
            self.src(piece), self.slot(cube.owner(piece)[0]),
            self.core_send.at[piece], self.core_recv.at[piece], cube.at(cube.me + cube.core_step),
        )

    def give(self, piece):
        for level in range(piece.bit_length(), self.cube.levels):
            self.sent.append(self.hop(piece, level))
            self.sent[-1].start()
        self.sent.append(self.core(piece))
        self.sent[-1].start()

    def start(self):
        self.place = pltpu.make_async_copy(self.own, self.slot(self.cube.me), self.local)
        self.place.start()
        self.give(0)

    def take(self, piece):
        if piece in self.arrived:
            return
        here = self.slot(self.cube.owner(piece)[0])
        remote(
            here, here, self.send_sem.at[piece], self.recv_sem.at[piece], self.cube.at(self.cube.me)
        ).wait_recv()
        self.arrived.add(piece)
        self.give(piece)

    def take_core(self, piece):
        here = self.slot(self.cube.owner(piece)[1])
        remote(
            here, here, self.core_send.at[piece], self.core_recv.at[piece], self.cube.at(self.cube.me)
        ).wait_recv()

    def finish(self):
        for piece in range(self.cube.count):
            self.take(piece)
            self.take_core(piece)
        for copy in self.sent:
            copy.wait_send()
        self.place.wait()


class CubeScatter:
    def __init__(self, cube, parts, out, scratch):
        self.cube, self.parts, self.out = cube, parts, out
        self.rows = out.shape[0]
        (self.keep, self.core_in, self.fold_in, self.load_sem,
         self.core_send, self.core_recv, self.send_sem, self.recv_sem) = scratch

    @staticmethod
    def scratch(count, rows, d):
        return [
            pltpu.VMEM((count, rows, d), BF16),
            pltpu.VMEM((count, rows, d), BF16),
            pltpu.VMEM((count - 1, rows, d), BF16),
            DMA((count,)), DMA((count,)), DMA((count,)), DMA((count - 1,)), DMA((count - 1,)),
        ]

    def load(self, piece):
        return pltpu.make_async_copy(
            self.parts.at[window(self.cube.owner(piece)[0], self.rows)],
            self.keep.at[piece], self.load_sem.at[piece],
        )

    def core(self, piece):
        cube = self.cube
        return remote(
            self.parts.at[window(cube.owner(piece)[1], self.rows)], self.core_in.at[piece],
            self.core_send.at[piece], self.core_recv.at[piece], cube.at(cube.me + cube.core_step),
        )

    def hop(self, piece):
        cube, level = self.cube, piece.bit_length() - 1
        return remote(
            self.keep.at[piece], self.fold_in.at[piece - 1],
            self.send_sem.at[piece - 1], self.recv_sem.at[piece - 1],
            cube.at(cube.me + cube.steps[level]),
        )

    def order(self):
        return sorted(range(self.cube.count), key=lambda p: (-(p.bit_length()), p))

    def start(self):
        for piece in self.order():
            self.core(piece).start()
            self.load(piece).start()

    def add(self, piece, other):
        @pl.loop(0, self.rows // 16)
        def _(i):
            part = window(i, 16)
            self.keep[piece, part] = (
                self.keep[piece, part].astype(F32) + other[part].astype(F32)
            ).astype(BF16)

    def fold(self, piece):
        self.load(piece).wait()
        self.core(piece).wait_recv()
        self.add(piece, self.core_in.at[piece])
        for level in range(self.cube.levels - 1, piece.bit_length() - 1, -1):
            above = piece + (1 << level)
            self.hop(above).wait_recv()
            self.add(piece, self.fold_in.at[above - 1])
        if piece:
            self.hop(piece).start()

    def finish(self):
        self.fold(0)

        @pl.loop(0, self.rows // 16)
        def _(i):
            part = window(i, 16)
            self.out[part] = self.keep[0, part].astype(F32)

        for piece in range(self.cube.count):
            self.core(piece).wait_send()
            if piece:
                self.hop(piece).wait_send()


class Swap:
    def __init__(self, place, moves, sems):
        self.place, self.moves = place, moves
        self.send_sem, self.recv_sem, self.local = sems

    @staticmethod
    def sems(size, moves):
        return [DMA((moves, size)), DMA((moves, size)), DMA((moves,))]

    def copies(self):
        place = self.place
        out = []
        for k in range(1, place.size):
            to = (place.me + k) % place.size
            for m, (src, dst) in enumerate(self.moves):
                out.append(
                    remote(src(to), dst(place.me), self.send_sem.at[m, k], self.recv_sem.at[m, k], place.at(to))
                )
        return out

    def locals(self):
        return [
            pltpu.make_async_copy(src(self.place.me), dst(self.place.me), self.local.at[m])
            for m, (src, dst) in enumerate(self.moves)
        ]

    def start(self):
        for copy in self.copies() + self.locals():
            copy.start()

    def finish(self):
        place = self.place
        for copy in self.copies():
            copy.wait_send()
        for k in range(1, place.size):
            of = (place.me - k + place.size) % place.size
            for m, (src, dst) in enumerate(self.moves):
                here = dst(of)
                remote(here, here, self.send_sem.at[m, k], self.recv_sem.at[m, k], place.at(of)).wait_recv()
        for copy in self.locals():
            copy.wait()


def rows_to_side(src, dst):
    rows, cols = dst.shape[0], src.shape[1]
    return (lambda d: src.at[window(d, rows)], lambda d: dst.at[:, window(d, cols)])


def side_to_rows(src, dst):
    rows, cols = src.shape[0], dst.shape[1]
    return (lambda d: src.at[:, window(d, cols)], lambda d: dst.at[window(d, rows)])


ANY = pl.BlockSpec(memory_space=pl.ANY)
VMEM = pl.BlockSpec(memory_space=pltpu.VMEM)


def front_kernel(
    x_ref, w_ref, wo_ref, we_ref, wr_ref, small_ref,
    seq_ref, w_out, wo_line, we_out, wr_out, small_out, *sems
):
    line, cube = Line(), Cube()
    gather = LineGather(line, x_ref, seq_ref, sems[:5])
    wide = LineGather(line, wo_ref, wo_line, sems[5:10])
    weights = CubeGather(cube, w_ref, w_out, sems[10:15])
    tile = small_ref.shape[0]
    moves = [
        (lambda d: small_ref, lambda d: small_out.at[window(d, tile)]),
        rows_to_side(wr_ref, wr_out),
    ]
    if wr_out.shape[0] % 128 == 0:
        moves.append(side_to_rows(we_ref, we_out))
    swap = Swap(cube, moves, sems[15:18])
    barrier = pltpu.get_barrier_semaphore()
    line.greet(barrier)
    cube.greet_all(barrier)
    pl.semaphore_wait(barrier, cube.dp - 1 + line.peers())
    gather.start()
    wide.start()
    weights.start()
    gather.take(1)
    wide.take(1)
    for piece in range(1, cube.count):
        if piece.bit_length() < cube.levels:
            weights.take(piece)
    swap.start()
    gather.take(2)
    wide.take(2)
    for piece in range(1, cube.count):
        weights.take(piece)
    for step in range(3, line.n):
        gather.take(step)
        wide.take(step)
    weights.finish()
    swap.finish()
    gather.finish()
    wide.finish()


def front(x, w, w_o, w_e, w_r, small):
    dp, n = lax.axis_size("dp"), lax.axis_size("tensor")
    rows, model = x.shape
    seq, w_all, o_line, e_all, r_all, small_all = pl.pallas_call(
        front_kernel,
        out_shape=(
            jax.ShapeDtypeStruct((n * rows, model), BF16),
            jax.ShapeDtypeStruct((dp * w.shape[0], w.shape[1]), BF16),
            jax.ShapeDtypeStruct((w_o.shape[0], n * w_o.shape[1]), BF16),
            jax.ShapeDtypeStruct((dp * w_e.shape[0], w_e.shape[1] // dp), BF16),
            jax.ShapeDtypeStruct((w_r.shape[0] // dp, w_r.shape[1] * dp), BF16),
            jax.ShapeDtypeStruct((dp * small.shape[0], small.shape[1]), BF16),
        ),
        in_specs=[ANY] * 6,
        out_specs=(ANY,) * 6,
        scratch_shapes=2 * LineGather.sems(n) + CubeGather.sems(dp // 2) + Swap.sems(dp, 3),
        compiler_params=pltpu.CompilerParams(collective_id=0, has_side_effects=True),
        cost_estimate=pl.CostEstimate(flops=80 * 10**9, bytes_accessed=10**7, transcendentals=0),
        name="front",
    )(x, w, w_o, w_e, w_r, small)
    if r_all.shape[0] % 128:
        e_all = lax.all_to_all(w_e, "dp", split_axis=1, concat_axis=0, tiled=True)
    return seq, w_all, o_line, e_all, r_all, small_all


class SmallSum:
    def __init__(self, line, cube, parts, out, scratch):
        self.line, self.cube, self.parts, self.out = line, cube, parts, out
        self.come, self.gather, self.sems, self.line_send, self.line_recv = (
            scratch[0], scratch[1], scratch[2:5], scratch[5], scratch[6]
        )
        moves = [(lambda d: parts.at[d], lambda d: self.come.at[d])]
        self.swap = Swap(cube, moves, self.sems)

    @staticmethod
    def scratch(dp, n, rows, d):
        return [
            pltpu.VMEM((dp, rows, d), F32),
            pltpu.VMEM((n, rows, d), F32),
            *Swap.sems(dp, 1),
            DMA((n,)), DMA((n,)),
        ]

    def hop(self, k):
        line = self.line
        here = self.gather.at[line.me]
        return remote(
            here, here, self.line_send.at[k], self.line_recv.at[k], line.at((line.me + k) % line.n)
        )

    def middle(self):
        self.swap.finish()
        total = self.come[0]
        for d in range(1, self.cube.dp):
            total = total + self.come[d]
        self.gather[self.line.me] = total
        for k in range(1, self.line.n):
            self.hop(k).start()

    def finish(self):
        line = self.line
        for k in range(1, line.n):
            here = self.gather.at[(line.me - k + line.n) % line.n]
            remote(
                here, here, self.line_send.at[k], self.line_recv.at[k], line.at(line.me)
            ).wait_recv()
            self.hop(k).wait_send()
        total = self.gather[0]
        for z in range(1, line.n):
            total = total + self.gather[z]
        self.out[...] = total


def exchange_kernel(counts, *refs):
    lines, planes, gathers, cubes, swaps, outs, backs, small = counts
    line, cube = Line(), Cube()
    count = sum(counts)
    pairs, scratch = list(zip(refs[:count], refs[count : 2 * count])), list(refs[2 * count :])

    def take(number):
        taken = tuple(scratch[:number])
        del scratch[:number]
        return taken

    sums = [LineScatter(line, *pairs.pop(0), take(7)) for _ in range(lines)]
    folds = [CubeScatter(cube, *pairs.pop(0), take(8)) for _ in range(planes)]
    lanes = [LineGather(line, *pairs.pop(0), take(5)) for _ in range(gathers)]
    wholes = [CubeGather(cube, *pairs.pop(0), take(5)) for _ in range(cubes)]
    moves = [side_to_rows(*pairs.pop(0)) for _ in range(swaps)]
    swap = Swap(cube, moves, take(3)) if swaps else None
    turns = [rows_to_side(*pairs.pop(0)) for _ in range(outs)]
    turns += [side_to_rows(*pairs.pop(0)) for _ in range(backs)]
    turn = Swap(line, turns, take(3)) if turns else None
    little = SmallSum(line, cube, *pairs.pop(0), take(7)) if small else None
    barrier = pltpu.get_barrier_semaphore()
    peers = 0
    if small or turns:
        line.greet_all(barrier)
        peers = line.n - 1
    elif lines or gathers:
        line.greet(barrier)
        peers = line.peers()
    if small or swaps:
        cube.greet_all(barrier)
        peers = peers + cube.dp - 1
    elif planes or cubes:
        cube.greet(barrier)
        peers = peers + cube.peers()
    for s in sums:
        s.prepare()
    pl.semaphore_wait(barrier, peers)
    if turns:
        turn.start()
    if small:
        little.swap.start()
    for s in sums:
        s.step(1)
    for lane in lanes:
        lane.start()
    for whole in wholes[:1]:
        whole.start()
    for f in folds:
        f.start()
    if small:
        little.middle()
    pieces = [p for p in folds[0].order() if p] if planes else []
    per = -(-len(pieces) // (line.n - 1))
    for step in range(1, line.n):
        for whole in wholes[step - 1 : step]:
            for piece in range(1, cube.count):
                if piece.bit_length() < cube.levels:
                    whole.take(piece)
        if step > 1:
            for s in sums:
                s.step(step)
            for lane in lanes:
                lane.take(step - 1)
        for piece in pieces[:per]:
            for f in folds:
                f.fold(piece)
        pieces = pieces[per:]
        if step == 1 and swaps:
            swap.start()
        for whole in wholes[step - 1 : step]:
            whole.finish()
        for whole in wholes[step : step + 1]:
            whole.start()
    for f in folds:
        f.finish()
    for lane in lanes:
        lane.take(line.n - 1)
        lane.finish()
    for s in sums:
        s.finish()
    if turns:
        turn.finish()
    if swaps:
        swap.finish()
    if small:
        little.finish()


def exchange(
    collective_id, lines=(), planes=(), gathers=(), cubes=(), swaps=(), outs=(), backs=(), small=(),
    weight=80,
):
    dp, n = lax.axis_size("dp"), lax.axis_size("tensor")
    groups = (lines, planes, gathers, cubes, swaps, outs, backs, small)
    counts = tuple(len(group) for group in groups)
    operands = [part for group in groups for part in group]
    out_shape, out_specs, scratch = [], [], []

    def result(rows, d, kind, spec):
        out_shape.append(jax.ShapeDtypeStruct((rows, d), kind))
        out_specs.append(spec)

    for part in lines:
        rows, d = part.shape[0] // n, part.shape[1]
        result(rows, d, F32, VMEM)
        scratch += LineScatter.scratch(n, rows, d)
    for part in planes:
        rows, d = part.shape[0] // dp, part.shape[1]
        result(rows, d, F32, VMEM)
        scratch += CubeScatter.scratch(dp // 2, rows, d)
    for part in gathers:
        result(n * part.shape[0], part.shape[1], BF16, ANY)
        scratch += LineGather.sems(n)
    for part in cubes:
        result(dp * part.shape[0], part.shape[1], BF16, ANY)
        scratch += CubeGather.sems(dp // 2)
    for part in swaps:
        result(dp * part.shape[0], part.shape[1] // dp, BF16, ANY)
    if swaps:
        scratch += Swap.sems(dp, len(swaps))
    for part in outs:
        result(part.shape[0] // n, part.shape[1] * n, BF16, ANY)
    for part in backs:
        result(part.shape[0] * n, part.shape[1] // n, BF16, ANY)
    if outs or backs:
        scratch += Swap.sems(n, len(outs) + len(backs))
    for part in small:
        rows, d = part.shape[1:]
        result(rows, d, F32, VMEM)
        scratch += SmallSum.scratch(dp, n, rows, d)
    return pl.pallas_call(
        functools.partial(exchange_kernel, counts),
        out_shape=tuple(out_shape),
        in_specs=[ANY] * len(operands),
        out_specs=tuple(out_specs),
        scratch_shapes=scratch,
        compiler_params=pltpu.CompilerParams(
            collective_id=collective_id, has_side_effects=True, vmem_limit_bytes=60 << 20
        ),
        cost_estimate=pl.CostEstimate(flops=weight * 10**9, bytes_accessed=10**7, transcendentals=0),
        name="exchange",
    )(*operands)


PAIR = 2 * HEAD_DIM
NEVER = -1e30


def lane_of(shape, head):
    lane = lax.broadcasted_iota(jnp.int32, shape, 1)
    return (lane < HEAD_DIM) if head == 0 else (lane >= HEAD_DIM)


def sight(parents_ref, row, col):
    at = jnp.int32(row)
    seen = at == col
    for hop in range(row - col):
        at = parents_ref[at]
        seen = seen | (at == col)
    return jnp.where(seen, 0.0, NEVER).astype(F32)


def masked_scores(parents_ref, q_head, k_ref, row):
    scores = []
    for col in range(row + 1):
        part = over(q_head, k_ref[col * BLOCK : (col + 1) * BLOCK, :], 1, 1)
        if col == row:
            below = lax.broadcasted_iota(jnp.int32, part.shape, 1) <= lax.broadcasted_iota(
                jnp.int32, part.shape, 0
            )
            part = jnp.where(below, part, NEVER)
        else:
            part = part + sight(parents_ref, row, col)
        scores.append(part)
    return scores


def row_reduce(parts, fold, reduce):
    return reduce(functools.reduce(fold, parts), axis=-1, keepdims=True)


def attend_kernel(parents_ref, q_ref, k_ref, v_ref, out_ref):
    blocks = q_ref.shape[0] // BLOCK
    scale = 1.0 / math.sqrt(HEAD_DIM)
    for row in range(blocks):
        here = slice(row * BLOCK, (row + 1) * BLOCK)
        heads = []
        for head in range(2):
            q_head = q_ref[here, :].astype(F32) * scale
            q_head = jnp.where(lane_of(q_head.shape, head), q_head, 0.0).astype(BF16)
            scores = masked_scores(parents_ref, q_head, k_ref, row)
            top = row_reduce(scores, jnp.maximum, jnp.max)
            probs = [jnp.exp(s - top) for s in scores]
            total = row_reduce(probs, jnp.add, jnp.sum)
            out = None
            for col in range(row + 1):
                term = over(
                    probs[col].astype(BF16), v_ref[col * BLOCK : (col + 1) * BLOCK, :], 1, 0
                )
                out = term if out is None else out + term
            heads.append(out / total)
        mixed = jnp.where(lane_of(heads[0].shape, 0), heads[0], heads[1])
        out_ref[here, :] = mixed.astype(out_ref.dtype)


def attend(parents, qkv, width):
    rows = qkv.shape[0]
    pairs = width // PAIR
    spec = lambda part: pl.BlockSpec((rows, PAIR), lambda p, parents: (0, part * pairs + p))
    blocks = rows // BLOCK
    work = pairs * 2 * (blocks * (blocks + 1) // 2) * BLOCK * BLOCK
    return pl.pallas_call(
        attend_kernel,
        out_shape=jax.ShapeDtypeStruct((rows, width), BF16),
        grid_spec=pltpu.PrefetchScalarGridSpec(
            num_scalar_prefetch=1,
            grid=(pairs,),
            in_specs=[spec(0), spec(1), spec(2)],
            out_specs=pl.BlockSpec((rows, PAIR), lambda p, parents: (0, p)),
        ),
        compiler_params=pltpu.CompilerParams(vmem_limit_bytes=48 << 20),
        cost_estimate=pl.CostEstimate(
            flops=work * PAIR * 24, bytes_accessed=rows * width * 8, transcendentals=work
        ),
        name="attend",
    )(parents, qkv, qkv, qkv)


def attend_back_kernel(parents_ref, q_ref, k_ref, v_ref, g_ref, out_ref, dq_s, dk_s, dv_s):
    part = pl.program_id(1)
    blocks = q_ref.shape[0] // BLOCK
    scale = 1.0 / math.sqrt(HEAD_DIM)

    @pl.when(part == 0)
    def _():
        for row in range(blocks):
            here = slice(row * BLOCK, (row + 1) * BLOCK)
            dq_heads = []
            for head in range(2):
                lanes = lane_of((BLOCK, PAIR), head)
                q_head = jnp.where(lanes, q_ref[here, :].astype(F32) * scale, 0.0).astype(BF16)
                g_head = jnp.where(lanes, g_ref[here, :].astype(F32), 0.0).astype(BF16)
                scores = masked_scores(parents_ref, q_head, k_ref, row)
                top = row_reduce(scores, jnp.maximum, jnp.max)
                probs = [jnp.exp(s - top) for s in scores]
                rest = 1.0 / row_reduce(probs, jnp.add, jnp.sum)
                probs = [p * rest for p in probs]
                d_probs = [
                    over(g_head, v_ref[col * BLOCK : (col + 1) * BLOCK, :], 1, 1)
                    for col in range(row + 1)
                ]
                level = row_reduce([p * d for p, d in zip(probs, d_probs)], jnp.add, jnp.sum)
                dq = None
                for col in range(row + 1):
                    there = slice(col * BLOCK, (col + 1) * BLOCK)
                    d_scores = (probs[col] * (d_probs[col] - level)).astype(BF16)
                    term = over(d_scores, k_ref[there, :], 1, 0)
                    dq = term if dq is None else dq + term
                    dk = over(d_scores, q_head, 0, 0)
                    dv = over(probs[col].astype(BF16), g_head, 0, 0)
                    if row == col and head == 0:
                        dk_s[there, :] = dk
                        dv_s[there, :] = dv
                    else:
                        dk_s[there, :] += dk
                        dv_s[there, :] += dv
                dq_heads.append(dq * scale)
            dq_s[here, :] = jnp.where(lane_of((BLOCK, PAIR), 0), dq_heads[0], dq_heads[1]).astype(
                BF16
            )
        out_ref[...] = dq_s[...]

    @pl.when(part == 1)
    def _():
        out_ref[...] = dk_s[...].astype(BF16)

    @pl.when(part == 2)
    def _():
        out_ref[...] = dv_s[...].astype(BF16)


def attend_back(parents, qkv, grad, width):
    rows = qkv.shape[0]
    pairs = width // PAIR
    spec = lambda part: pl.BlockSpec((rows, PAIR), lambda p, c, parents: (0, part * pairs + p))
    blocks = rows // BLOCK
    work = pairs * 2 * (blocks * (blocks + 1) // 2) * BLOCK * BLOCK
    return pl.pallas_call(
        attend_back_kernel,
        out_shape=jax.ShapeDtypeStruct((rows, 3 * width), BF16),
        grid_spec=pltpu.PrefetchScalarGridSpec(
            num_scalar_prefetch=1,
            grid=(pairs, 3),
            in_specs=[
                spec(0),
                spec(1),
                spec(2),
                pl.BlockSpec((rows, PAIR), lambda p, c, parents: (0, p)),
            ],
            out_specs=pl.BlockSpec((rows, PAIR), lambda p, c, parents: (0, c * pairs + p)),
            scratch_shapes=[
                pltpu.VMEM((rows, PAIR), BF16),
                pltpu.VMEM((rows, PAIR), F32),
                pltpu.VMEM((rows, PAIR), F32),
            ],
        ),
        compiler_params=pltpu.CompilerParams(vmem_limit_bytes=48 << 20),
        cost_estimate=pl.CostEstimate(
            flops=work * PAIR * 60, bytes_accessed=rows * width * 14, transcendentals=work
        ),
        name="attend_back",
    )(parents, qkv, qkv, qkv, grad)


def ffn_kernel(n2_ref, dy_ref, we_ref, wr_ref, be_ref, *refs):
    sum_ref, act_ref, dpre_ref, part_ref = refs[:4]
    refs = refs[4:]
    we, wr, seq_st, dy_st, act_st, dpre_st, part_st, keep, give, core_in, fold_in = refs[:11]
    w_sem, load_sem, st_sem, rsc_send, rsc_recv, fold_send, fold_recv = refs[11:18]
    cube = Cube()
    levels, count, owner = cube.levels, cube.count, cube.owner
    rows, model = sum_ref.shape
    units = wr_ref.shape[0]
    barrier = pltpu.get_barrier_semaphore()
    cube.greet(barrier)
    parts = we_ref.shape[0] // model
    mine_units = we_ref.shape[1]
    loads_w = [pltpu.make_async_copy(wr_ref, wr, w_sem.at[parts])]
    for part in range(parts):
        loads_w.append(
            pltpu.make_async_copy(
                we_ref.at[pl.ds(part * model, model)],
                we.at[:, pl.ds(part * mine_units, mine_units)],
                w_sem.at[part],
            )
        )

    def load(piece, slot):
        out = []
        for half, index in enumerate(owner(piece)):
            for kind, (ref, stage) in enumerate(((n2_ref, seq_st), (dy_ref, dy_st))):
                out.append(
                    pltpu.make_async_copy(
                        ref.at[window(index, rows)],
                        stage.at[slot, pl.ds(half * rows, rows)],
                        load_sem.at[kind, slot, half],
                    )
                )
        return out

    order = sorted(range(count), key=lambda p: (-(p.bit_length()), p))
    slots = {piece: i % 2 for i, piece in enumerate(order)}
    loads = {order[0]: load(order[0], 0)}
    for c in loads[order[0]] + loads_w:
        c.start()
    pl.semaphore_wait(barrier, cube.peers())
    for c in loads_w:
        c.wait()
    stores, core_sends, folds = {}, {}, {}

    def add(piece, other):
        @pl.loop(0, rows // 16)
        def _(i):
            part = window(i, 16)
            keep[piece, part] = (
                keep[piece, part].astype(F32) + other[part].astype(F32)
            ).astype(BF16)

    def core_copy(piece):
        return remote(
            give.at[slots[piece]], core_in.at[piece],
            rsc_send.at[piece], rsc_recv.at[piece], cube.at(cube.me + cube.core_step),
        )

    def fold_copy(piece):
        return remote(
            keep.at[piece], fold_in.at[piece - 1], fold_send.at[piece - 1], fold_recv.at[piece - 1],
            cube.at(cube.me + cube.steps[piece.bit_length() - 1]),
        )

    def fold(piece):
        core_copy(piece).wait_recv()
        add(piece, core_in.at[piece])
        for level in range(levels - 1, piece.bit_length() - 1, -1):
            above = piece + (1 << level)
            fold_copy(above).wait_recv()
            add(piece, fold_in.at[above - 1])
        folds[piece] = fold_copy(piece)
        folds[piece].start()

    chunk = 512
    wide = 512
    for turn, piece in enumerate(order):
        slot = turn % 2
        for c in loads[piece]:
            c.wait()
        if turn + 1 < count:
            loads[order[turn + 1]] = load(order[turn + 1], 1 - slot)
            for c in loads[order[turn + 1]]:
                c.start()
        if turn >= 2:
            for c in stores[turn - 2]:
                c.wait()
            core_sends[order[turn - 2]].wait_send()

        @pl.loop(0, units // chunk)
        def _(i):
            cols = window(i, chunk)
            pre = over(seq_st[slot], we[:, cols], 1, 0) + be_ref[:, cols]
            d_act = over(dy_st[slot], wr[cols, :], 1, 1)
            square = pre * pre
            t = jnp.tanh(GELU * pre * (1.0 + 0.044715 * square))
            act_st[slot, :, cols] = (0.5 * pre * (1.0 + t)).astype(BF16)
            slope = 0.5 * (1.0 + t) + (0.5 * GELU) * pre * (1.0 - t * t) * (
                1.0 + (3 * 0.044715) * square
            )
            dpre_st[slot, :, cols] = (d_act * slope).astype(BF16)

        if turn:
            fold(order[turn - 1])

        @pl.loop(0, model // wide)
        def _(i):
            cols = window(i, wide)
            d_two = over(dpre_st[slot], we[cols, :], 1, 1).astype(BF16)
            keep[piece, :, cols] = d_two[:rows]
            give[slot, :, cols] = d_two[rows:]
            part_st[slot, :, cols] = over(act_st[slot], wr[:, cols], 1, 0).astype(BF16)

        core_sends[piece] = core_copy(piece)
        core_sends[piece].start()
        stores[turn] = []
        for half, index in enumerate(owner(piece)):
            to, part = window(index, rows), pl.ds(half * rows, rows)
            for kind, (stage, ref) in enumerate(
                ((act_st, act_ref), (dpre_st, dpre_ref), (part_st, part_ref))
            ):
                stores[turn].append(
                    pltpu.make_async_copy(stage.at[slot, part], ref.at[to], st_sem.at[kind, slot, half])
                )
        for c in stores[turn]:
            c.start()
    core_copy(0).wait_recv()
    for level in range(levels):
        fold_copy(1 << level).wait_recv()

    @pl.loop(0, rows // 16)
    def _(i):
        part = window(i, 16)
        total = keep[0, part].astype(F32) + core_in[0, part].astype(F32)
        for level in range(levels):
            total = total + fold_in[(1 << level) - 1, part].astype(F32)
        sum_ref[part] = total

    for turn in range(max(0, count - 2), count):
        for c in stores[turn]:
            c.wait()
        core_sends[order[turn]].wait_send()
    for s in folds.values():
        s.wait_send()


def ffn(n2, dy, we, wr, bias_e):
    n, dp = lax.axis_size("tensor"), lax.axis_size("dp")
    rows, model = n2.shape[0] // dp, n2.shape[1]
    units, count = wr.shape[0], dp // 2
    flops = 30 * dp * rows * model * units
    return pl.pallas_call(
        ffn_kernel,
        out_shape=(
            jax.ShapeDtypeStruct((rows, model), F32),
            jax.ShapeDtypeStruct((dp * rows, units), BF16),
            jax.ShapeDtypeStruct((dp * rows, units), BF16),
            jax.ShapeDtypeStruct((dp * rows, model), BF16),
        ),
        in_specs=[ANY] * 4 + [VMEM],
        out_specs=(VMEM, ANY, ANY, ANY),
        scratch_shapes=[
            pltpu.VMEM((model, units), BF16),
            pltpu.VMEM((units, model), BF16),
            pltpu.VMEM((2, 2 * rows, model), BF16),
            pltpu.VMEM((2, 2 * rows, model), BF16),
            pltpu.VMEM((2, 2 * rows, units), BF16),
            pltpu.VMEM((2, 2 * rows, units), BF16),
            pltpu.VMEM((2, 2 * rows, model), BF16),
            pltpu.VMEM((count, rows, model), BF16),
            pltpu.VMEM((2, rows, model), BF16),
            pltpu.VMEM((count, rows, model), BF16),
            pltpu.VMEM((count - 1, rows, model), BF16),
            DMA((n + 1,)), DMA((2, 2, 2)), DMA((3, 2, 2)),
            DMA((count,)), DMA((count,)), DMA((count - 1,)), DMA((count - 1,)),
        ],
        compiler_params=pltpu.CompilerParams(
            collective_id=1, has_side_effects=True, vmem_limit_bytes=62 << 20
        ),
        cost_estimate=pl.CostEstimate(
            flops=flops, bytes_accessed=8 * dp * rows * (model + units), transcendentals=dp * rows * units
        ),
        name="ffn_plane",
    )(n2, dy, we, wr, bias_e)


def body(
    tokens,
    parents,
    cotangent,
    first_gain,
    first_shift,
    w_query,
    b_query,
    w_key,
    w_value,
    b_value,
    w_out,
    b_out,
    second_gain,
    second_shift,
    w_expand,
    b_expand,
    w_reduce,
    b_reduce,
):
    dp = lax.axis_size("dp")
    tn = lax.axis_size("tensor")
    dp_me = lax.axis_index("dp")
    tn_me = lax.axis_index("tensor")
    width = w_query.shape[1]
    model = w_query.shape[0] * dp
    units = w_expand.shape[1]
    mine = units // dp
    micros = range(tokens.shape[0])
    last = tokens.shape[0] - 1
    x_low = [tokens[m, 0] for m in micros]
    dy_low = [cotangent[m, 0] for m in micros]
    rows_here = x_low[0].shape[0]
    total = rows_here * tn

    cut = first_gain.shape[0]
    bq_rows, bq_cols = b_query.shape
    be_rows, be_cols = b_expand.shape
    small = jnp.concatenate(
        [first_gain, first_shift, b_out, second_gain, second_shift, b_reduce]
        + [b_query.reshape(-1), b_value.reshape(-1), b_expand.reshape(-1)]
    )
    used = small.shape[0]
    small = jnp.pad(small, (0, -used % 2048)).reshape(-1, 128)
    w_qkv = jnp.concatenate([w_query, w_key, w_value], axis=1)
    seq_x0, w_qkv, w_ot, w_e, w_r, small = front(
        x_low[0], w_qkv, w_out.T, w_expand, w_reduce, small
    )
    small = small.reshape(dp, -1)[:, :used]
    gain_one, shift_one, bias_out, gain_two, shift_two, bias_red = [
        small[:, i * cut : (i + 1) * cut].reshape(1, model).astype(F32) for i in range(6)
    ]
    at = 6 * cut
    bias_qkv = []
    for i in range(2):
        part = small[:, at : at + bq_rows * bq_cols].reshape(dp, bq_rows, bq_cols)
        bias_qkv.append(part.transpose(1, 0, 2).reshape(1, width).astype(F32))
        at += bq_rows * bq_cols
    bias_qkv = jnp.concatenate([bias_qkv[0], jnp.zeros((1, width), F32), bias_qkv[1]], 1)
    bias_e = small[:, at:].reshape(dp, dp, be_rows // dp, be_cols)
    bias_e = lax.dynamic_index_in_dim(bias_e, dp_me, 1, keepdims=False)
    bias_e = bias_e.transpose(1, 0, 2).reshape(mine)
    bias_e = jnp.pad(bias_e, (0, -mine % 2048)).reshape(-1, 128)

    seq_x = [seq_x0]
    w_r = lax.all_gather(w_r, "tensor", axis=0, tiled=True)
    w_e = lax.all_gather(w_e, "tensor", axis=1 if mine % 128 else 0, tiled=True)

    def outer(left, right):
        out = None
        for a, b in zip(left, right):
            term = over(a, b, 0, 0)
            out = term if out is None else out + term
        return out.astype(BF16)

    normal_one, seq_one, qkv, attended, hidden, normed_two = [], [], [], [], [], []
    out_part, seq_two, activated, d_pre, d_hidden, d_branch, out_sum = [], [], [], [], [], [], []
    d_qkv, d_one, d_att, row_attended = [], [], [], []
    g_gain_two = g_shift_two = g_bias_red = g_bias_out = 0.0
    g_gain_one = g_shift_one = g_bias_qkv = 0.0
    for m in micros:
        normal_one.append(layer_norm(seq_x[m].astype(F32), 1.0, 0.0))
        seq_one.append((normal_one[m] * gain_one + shift_one).astype(BF16))
        qkv.append(
            (jnp.dot(seq_one[m], w_qkv, preferred_element_type=F32) + bias_qkv).astype(BF16)
        )
        attended.append(attend(parents[m, 0], qkv[m], width))
        if m == 0:
            bias_e, w_ot, grad, row_att = exchange(
                3, gathers=[bias_e], cubes=[w_ot, dy_low[m]], outs=[attended[m]]
            )
            seq_grad = [grad]
            bias_e = bias_e.reshape(tn, -1)[:, :mine].reshape(1, tn * mine).astype(F32)
        else:
            part, row_att, col_grad = exchange(
                4, planes=[out_part[m - 1]], outs=[attended[m]], backs=[d_att[m - 1]]
            )
            out_sum.append(part)
            d_att[m - 1] = col_grad
        if m < last:
            next_x, row_att = lax.optimization_barrier((x_low[m + 1], row_att))
            next_x = lax.all_gather(next_x, "tensor", axis=0, tiled=True)
        row_attended.append(row_att)
        branch = over(row_att, w_ot, 1, 1)
        hidden.append(x_low[m].astype(F32) + (branch + bias_out))
        normed_two.append(layer_norm(hidden[m], gain_two, shift_two).astype(BF16))
        if m < last:
            grad, normed_two[m] = lax.optimization_barrier((dy_low[m + 1], normed_two[m]))
            seq_grad.append(lax.all_gather(grad, "dp", axis=0, tiled=True))

        def attention_back(k):
            d_qkv.append(attend_back(parents[k, 0], qkv[k], d_att[k], width))
            d_one.append(over(d_qkv[k], w_qkv, 1, 1).astype(BF16))
            part = d_one[k].astype(F32)
            return (
                jnp.sum(part * normal_one[k], 0, keepdims=True),
                jnp.sum(part, 0, keepdims=True),
                jnp.sum(d_qkv[k].astype(F32), 0),
            )

        if m:
            normed_two[m], seq_grad[m] = lax.optimization_barrier((normed_two[m], seq_grad[m]))
            next_two = lax.all_gather(normed_two[m], "dp", axis=0, tiled=True)
            gain, shift, bias = attention_back(m - 1)
            g_gain_one, g_shift_one = g_gain_one + gain, g_shift_one + shift
            g_bias_qkv = g_bias_qkv + bias
            next_two, d_one[m - 1] = lax.optimization_barrier((next_two, d_one[m - 1]))
            d_one[m - 1] = lax.psum_scatter(
                d_one[m - 1], "tensor", scatter_dimension=0, tiled=True
            )

        if m == 0:
            (seq,) = exchange(7, cubes=[normed_two[m]])
        else:
            seq = next_two
        d_two, act, dpre, part = ffn(seq, seq_grad[m], w_e, w_r, bias_e)
        seq_two.append(seq)
        activated.append(act)
        d_pre.append(dpre)
        out_part.append(part)
        if m == last:
            g_r = outer(activated, seq_grad)
            d_two, g_r, *d_one = lax.optimization_barrier((d_two, g_r, *d_one))
            g_r = lax.psum_scatter(g_r, "tensor", scatter_dimension=0, tiled=True)
        grad32 = dy_low[m].astype(F32)
        norm_value, norm_pull = jax.vjp(layer_norm, hidden[m], gain_two, shift_two)
        d_norm, g_gain, g_shift = norm_pull(d_two)
        d_hidden.append(grad32 + d_norm)
        d_branch.append(d_hidden[m].astype(BF16))
        d_att.append(jnp.dot(d_branch[m], w_ot, preferred_element_type=F32).astype(BF16))
        g_gain_two = g_gain_two + g_gain
        g_shift_two = g_shift_two + g_shift
        g_bias_red = g_bias_red + jnp.sum(grad32, 0, keepdims=True)
        g_bias_out = g_bias_out + jnp.sum(d_branch[m].astype(F32), 0, keepdims=True)
        if m < last:
            next_x, d_branch[m] = lax.optimization_barrier((next_x, d_branch[m]))
            seq_x.append(next_x)

    g_ot = outer([jnp.concatenate(d_branch, 0)], [jnp.concatenate(row_attended, 0)])
    g_ot, d_att[last] = exchange(6, planes=[g_ot], backs=[d_att[last]], weight=15)
    d_att[last], *d_pre = lax.optimization_barrier((d_att[last], *d_pre))
    g_et = outer(d_pre, seq_two)
    d_att[last], g_r = lax.optimization_barrier((d_att[last], g_r))
    g_et = lax.psum_scatter(g_et, "tensor", scatter_dimension=0, tiled=True)
    gain, shift, bias = attention_back(last)
    d_one[last], *d_pre = lax.optimization_barrier((d_one[last], *d_pre))
    g_bias_e = sum(jnp.sum(part.astype(F32), 0) for part in d_pre)
    g_gain_one, g_shift_one = g_gain_one + gain, g_shift_one + shift
    g_bias_qkv = g_bias_qkv + bias

    rows = jnp.concatenate(
        [g_gain_one, g_shift_one, g_bias_out, g_gain_two, g_shift_two, g_bias_red], 0
    )
    rows = rows.reshape(6, dp, cut).transpose(1, 0, 2).reshape(dp, 6 * cut)
    row_qv = jnp.concatenate([g_bias_qkv[:width], g_bias_qkv[2 * width :]])
    row_qv = row_qv.reshape(2 * bq_rows, dp, bq_cols).transpose(1, 0, 2)[:, None]
    row_qv = lax.dynamic_update_slice(
        jnp.zeros((dp, tn, 2 * bq_rows, bq_cols), F32), row_qv, (0, tn_me, 0, 0)
    ).reshape(dp, -1)
    row_e = g_bias_e.reshape(tn, be_rows // dp, dp, be_cols).transpose(2, 0, 1, 3)[:, :, None]
    row_e = lax.dynamic_update_slice(
        jnp.zeros((dp, tn, dp, be_rows // dp, be_cols), F32), row_e, (0, 0, dp_me, 0, 0)
    ).reshape(dp, -1)
    little = jnp.concatenate([rows, row_qv, row_e], 1)
    little = jnp.pad(little, ((0, 0), (0, -little.shape[1] % 1024))).reshape(dp, -1, 128)

    layer_out, input_grad = [], []

    def done(m):
        layer_out.append((hidden[m] + (out_sum[m] + bias_red)).astype(BF16))
        first_value, first_pull = jax.vjp(
            lambda rows: layer_norm(rows, gain_one, shift_one), x_low[m].astype(F32)
        )
        input_grad.append((d_hidden[m] + first_pull(d_one[m].astype(F32))[0]).astype(BF16))

    d_one[last], *d_qkv = lax.optimization_barrier((d_one[last], *d_qkv))
    g_qkv = outer(seq_one, d_qkv)
    for m in micros[:last]:
        done(m)
    d_one[last], *finished = lax.optimization_barrier((d_one[last], *layer_out, *input_grad))
    layer_out, input_grad = finished[:last], finished[last:]
    g_ot = g_ot.astype(BF16).reshape(-1, tn, width).transpose(1, 0, 2).reshape(-1, width)
    d_one[last], g_ot, g_qkv, out_last, g_expand, g_reduce, little = exchange(
        5,
        lines=[d_one[last], g_ot],
        planes=[g_qkv, out_part[last]],
        swaps=[g_et, g_r],
        small=[little],
    )
    out_sum.append(out_last)
    g_query, g_key, g_value = [g_qkv[:, i * width : (i + 1) * width] for i in range(3)]
    g_out = g_ot.T
    g_expand = g_expand.T.astype(F32)
    g_reduce = g_reduce.astype(F32)
    little = little.reshape(-1)
    six = little[: 6 * cut].reshape(6, cut)
    at = 6 * cut
    g_bqv = little[at : at + tn * 2 * bq_rows * bq_cols].reshape(tn, 2 * bq_rows, bq_cols)
    g_bqv = lax.dynamic_index_in_dim(g_bqv, tn_me, 0, keepdims=False)
    g_bq, g_bv = g_bqv[:bq_rows], g_bqv[bq_rows:]
    at += tn * 2 * bq_rows * bq_cols
    g_be = little[at : at + tn * be_rows * be_cols].reshape(tn, be_rows, be_cols)
    g_be = lax.dynamic_index_in_dim(g_be, tn_me, 0, keepdims=False)
    done(last)

    return (
        jnp.stack(layer_out, 0)[:, None],
        jnp.stack(input_grad, 0)[:, None],
        six[0],
        six[1],
        g_query,
        g_bq,
        g_key,
        g_value,
        g_bv,
        g_out,
        six[2],
        six[3],
        six[4],
        g_expand,
        g_be,
        g_reduce,
        six[5],
    )


def solution(mesh):
    in_specs = (
        P(None, "dp", "tensor", None),
        P(None, "dp", None),
        P(None, "dp", "tensor", None),
        P("dp"),
        P("dp"),
        P("dp", "tensor"),
        P("tensor", "dp"),
        P("dp", "tensor"),
        P("dp", "tensor"),
        P("tensor", "dp"),
        P("tensor", "dp"),
        P("dp"),
        P("dp"),
        P("dp"),
        P("dp", "tensor"),
        P("tensor", "dp"),
        P("tensor", "dp"),
        P("dp"),
    )
    out_specs = (
        P(None, "dp", "tensor", None),
        P(None, "dp", "tensor", None),
        P("dp"),
        P("dp"),
        P("dp", "tensor"),
        P("tensor", "dp"),
        P("dp", "tensor"),
        P("dp", "tensor"),
        P("tensor", "dp"),
        P("tensor", "dp"),
        P("dp"),
        P("dp"),
        P("dp"),
        P("dp", "tensor"),
        P("tensor", "dp"),
        P("tensor", "dp"),
        P("dp"),
    )
    return jax.shard_map(body, mesh=mesh, in_specs=in_specs, out_specs=out_specs, check_vma=False)
```
